32 devices in a mesh: dp: 8 (over z, x), tensor: 4 (over y, core).
Axes of the slice: x: 2, y: 2, z: 4, core: 2. Of those that a mesh axis runs over, the one named last changes fastest.
Arguments:
- attn_out: bfloat16 [4096, 8192], P('dp', 'tensor'), may hold values from -6 to 6
- frozen_weight: bfloat16 [8192, 8192], P('tensor', 'dp'), may hold values from -0.0625 to 0.0625
- vector_bank: float32 [256, 256], replicated, may hold values from -0.18 to 0.18
- logits_a: float32 [16, 32, 2], P(None, 'tensor'), may hold values from -2 to 2
- index_a: int32 [16, 32, 2], P(None, 'tensor'), may hold values from 0 to 255, all different within a row
- logits_b: float32 [16, 32, 2], P(None, 'tensor'), may hold values from -2 to 2
- index_b: int32 [16, 32, 2], P(None, 'tensor'), may hold values from 0 to 255, all different within a row
- out_grad: bfloat16 [4096, 8192], P('dp'), may hold values from -6 to 6
Outputs:
- layer_out: bfloat16 [4096, 8192], P('dp', 'tensor')
- attn_grad: bfloat16 [4096, 8192], P('dp', 'tensor')
- bank_grad: float32 [256, 256], replicated
- logits_a_grad: float32 [16, 32, 2], P(None, 'tensor')
- logits_b_grad: float32 [16, 32, 2], P(None, 'tensor')
The draws below stay inside these ranges and needn't reach their ends.
Inputs may be any that keep to these rules, and one draw needn't show every extreme that they name: `index_a`: the 2 entries of one sub-vector differ. `index_b`: the 2 entries of one sub-vector differ.
All inputs are finite; a program needn't handle non-finite values.
Results may differ from the reference program's by a relative error of at most 0.014.
Values may be sent and summed in bfloat16 or wider, within the bound.
A program may use at most 128 MiB of HBM per device.

```python
import jax
import jax.numpy as jnp
from jax import lax

D = 8192
ATTN = 8192
RANK = 16
SUBLEN = 256
BANK = 256
TOP = 2
TOKENS = 4096
JA = 32
JB = 32
N_TENSOR = 4


def block_levels(own_key, extent, cuts, low, top_value):
    gain = 1.0
    for position, blocks in cuts:
        draws = jax.random.uniform(jax.random.fold_in(jax.random.fold_in(own_key, 6), position), (blocks,), jnp.float32, low / len(cuts), top_value / len(cuts))
        gain = gain * jnp.repeat(jnp.exp(draws), extent[position] // blocks).reshape((-1,) + (1,) * (len(extent) - 1 - position))
    return gain


def choose_distinct(stream_key, rows, number_of, top, lift):
    sequence = jax.random.permutation(jax.random.fold_in(stream_key, 1), number_of)
    boost = sequence
    for power in range(3):
        boost = boost * boost // number_of
    boost = boost * lift // number_of
    lots = jax.random.randint(jax.random.fold_in(stream_key, 2), (rows, number_of), 0, 4096) + boost
    fixed_rows = jax.random.permutation(jax.random.fold_in(stream_key, 3), rows)[jnp.arange(number_of) % rows]
    lots = jnp.where(jnp.arange(rows)[:, None] == fixed_rows[None, :], 1 << 14, lots)
    priority = lots * number_of + jnp.arange(number_of)
    return lax.top_k(priority.astype(jnp.int32), top)[1].astype(jnp.int32)


def normal_values(stream_key, shape, spread, bound, pieces=(), held_as=jnp.bfloat16):
    entries = jax.random.normal(stream_key, shape, jnp.float32) * spread
    if len(pieces) > 0:
        entries = block_levels(stream_key, shape, pieces, -0.22, 0.18) * entries
    return jnp.clip(entries, min=-bound, max=bound).astype(held_as)


def setup_inputs(seed: int = 0) -> dict:
    keys = jax.random.split(jax.random.key(seed), 9)
    attn_out = normal_values(keys[0], (TOKENS, ATTN), 1.0, 6.0, ((0, 8), (1, 4)))
    frozen_weight = normal_values(keys[1], (ATTN, D), ATTN ** -0.5, 0.0625, ((0, 4), (1, 8)))
    vector_bank = normal_values(keys[2], (BANK, SUBLEN), 0.03, 0.18, (), jnp.float32)
    logits_a = jnp.clip(jax.random.uniform(keys[3], (RANK, JA, TOP), jnp.float32, -2.0, 2.0) * block_levels(keys[3], (RANK, JA, TOP), ((1, 4),), -0.4, 0.0), -2.0, 2.0)
    index_a = choose_distinct(keys[4], RANK * JA, BANK, TOP, 64).reshape((RANK, JA, TOP))
    logits_b = jnp.clip(jax.random.uniform(keys[5], (RANK, JB, TOP), jnp.float32, -2.0, 2.0) * block_levels(keys[5], (RANK, JB, TOP), ((1, 4),), -0.4, 0.0), -2.0, 2.0)
    index_b = choose_distinct(keys[6], RANK * JB, BANK, TOP, 64).reshape((RANK, JB, TOP))
    out_grad = normal_values(keys[7], (TOKENS, D), 1.0, 6.0, ((0, 8),))
    return {"attn_out": attn_out, "frozen_weight": frozen_weight, "vector_bank": vector_bank, "logits_a": logits_a, "index_a": index_a, "logits_b": logits_b, "index_b": index_b, "out_grad": out_grad}


adapter_scale = 2.0


def compose(logits, indices, vector_bank):
    weights = jax.nn.sigmoid(logits - logits[..., ::-1])
    levels = jnp.arange(vector_bank.shape[0], dtype=jnp.int32)
    picked = (indices[..., None] == levels).astype(jnp.float32)
    mixing = jnp.sum(picked * weights[..., None], axis=2)
    blocks = jnp.einsum("rjb,bc->rjc", mixing, vector_bank, precision=lax.Precision.HIGHEST)
    return weights, picked, mixing, blocks.reshape(blocks.shape[0], -1)


def compose_back(grad_rows, weights, picked, mixing, vector_bank):
    blocks = grad_rows.reshape(mixing.shape[0], mixing.shape[1], -1)
    bank_part = jnp.einsum("rjb,rjc->bc", mixing, blocks, precision=lax.Precision.HIGHEST)
    projected = jnp.einsum("rjc,bc->rjb", blocks, vector_bank, precision=lax.Precision.HIGHEST)
    dots = jnp.sum(picked * projected[:, :, None, :], axis=3)
    logit_grad = weights * (dots - jnp.sum(weights * dots, axis=2, keepdims=True))
    return bank_part, logit_grad


def reference(attn_out, frozen_weight, vector_bank, logits_a, index_a, logits_b, index_b, out_grad):
    weights_a, picked_a, mixing_a, rows_a = compose(logits_a, index_a, vector_bank)
    weights_b, picked_b, mixing_b, rows_b = compose(logits_b, index_b, vector_bank)
    down_a = rows_a.astype(jnp.bfloat16)
    up_b = rows_b.astype(jnp.bfloat16)
    low_bf = jnp.dot(attn_out, down_a.T, preferred_element_type=jnp.float32).astype(jnp.bfloat16)
    back_bf = jnp.dot(out_grad, up_b.T, preferred_element_type=jnp.float32).astype(jnp.bfloat16)
    width = ATTN // N_TENSOR

    def add_block(carry, block):
        columns = lax.dynamic_slice_in_dim(attn_out, block * width, width, 1)
        weight_rows = lax.dynamic_slice_in_dim(frozen_weight, block * width, width, 0)
        partial_value = jnp.dot(columns, weight_rows, preferred_element_type=jnp.float32).astype(jnp.bfloat16)
        partial_value = lax.optimization_barrier(partial_value)
        return carry + partial_value.astype(jnp.float32), None

    summed, _ = lax.scan(add_block, jnp.zeros((attn_out.shape[0], D), jnp.float32), jnp.arange(N_TENSOR, dtype=jnp.int32))
    layer_out = (summed + adapter_scale * jnp.dot(low_bf, up_b, preferred_element_type=jnp.float32)).astype(jnp.bfloat16)
    main = lax.dot_general(out_grad, frozen_weight, (((1,), (1,)), ((), ())), preferred_element_type=jnp.float32)
    attn_grad = (main + adapter_scale * jnp.dot(back_bf, down_a, preferred_element_type=jnp.float32)).astype(jnp.bfloat16)
    factor = adapter_scale / TOKENS
    grad_a = factor * lax.dot_general(back_bf, attn_out, (((0,), (0,)), ((), ())), preferred_element_type=jnp.float32)
    grad_b = factor * lax.dot_general(low_bf, out_grad, (((0,), (0,)), ((), ())), preferred_element_type=jnp.float32)
    bank_a, logit_grad_a = compose_back(grad_a, weights_a, picked_a, mixing_a, vector_bank)
    bank_b, logit_grad_b = compose_back(grad_b, weights_b, picked_b, mixing_b, vector_bank)
    return layer_out, attn_grad, bank_a + bank_b, logit_grad_a, logit_grad_b
```

```python
import functools

import jax
import jax.numpy as jnp
from jax import lax
from jax.experimental import pallas as pl
from jax.experimental.pallas import tpu as pltpu
from jax.sharding import PartitionSpec as P

adapter_scale = 2.0
ROW_PIECES = 4


def compose(logits, indices, vector_bank):
    weights = jax.nn.sigmoid(logits - logits[..., ::-1])
    levels = jnp.arange(vector_bank.shape[0], dtype=jnp.int32)
    picked = (indices[..., None] == levels).astype(jnp.float32)
    mixing = jnp.sum(picked * weights[..., None], axis=2)
    blocks = jnp.einsum("rjb,bc->rjc", mixing, vector_bank, precision=lax.Precision.HIGHEST)
    return (weights, picked, mixing, blocks.reshape(blocks.shape[0], -1))


def compose_back(grad_rows, weights, picked, mixing, vector_bank):
    blocks = grad_rows.reshape(mixing.shape[0], mixing.shape[1], -1)
    bank_part = jnp.einsum("rjb,rjc->bc", mixing, blocks, precision=lax.Precision.HIGHEST)
    projected = jnp.einsum("rjc,bc->rjb", blocks, vector_bank, precision=lax.Precision.HIGHEST)
    dots = jnp.sum(picked * projected[:, :, None, :], axis=3)
    logit_grad = weights * (dots - jnp.sum(weights * dots, axis=2, keepdims=True))
    return (bank_part, logit_grad)


def local(attn_out, frozen_weight, vector_bank, logits_a, index_a, logits_b, index_b, out_grad):
    weights_a, picked_a, mixing_a, rows_a = compose(logits_a, index_a, vector_bank)
    weights_b, picked_b, mixing_b, rows_b = compose(logits_b, index_b, vector_bank)
    down_a = rows_a.astype(jnp.bfloat16)
    up_b = rows_b.astype(jnp.bfloat16)
    own_width = up_b.shape[1]
    grad_cols = lax.dynamic_slice_in_dim(
        out_grad, lax.axis_index("tensor") * own_width, own_width, 1
    )
    low_part = jnp.dot(attn_out, down_a.T, preferred_element_type=jnp.float32)
    back_part = jnp.dot(grad_cols, up_b.T, preferred_element_type=jnp.float32)
    low_total = lax.psum(low_part, "tensor")
    low_bf = low_total.astype(jnp.bfloat16)
    gathered = lax.all_gather(frozen_weight, "dp", axis=1, tiled=True)
    partial_value = jnp.dot(attn_out, gathered, preferred_element_type=jnp.float32).astype(
        jnp.bfloat16
    )
    summed = lax.psum_scatter(partial_value, "tensor", scatter_dimension=1, tiled=True).astype(
        jnp.float32
    )
    layer_out = (
        summed + adapter_scale * jnp.dot(low_bf, up_b, preferred_element_type=jnp.float32)
    ).astype(jnp.bfloat16)
    back_total = lax.psum(back_part, "tensor")
    back_bf = back_total.astype(jnp.bfloat16)
    main = lax.dot_general(
        out_grad, gathered, (((1,), (1,)), ((), ())), preferred_element_type=jnp.float32
    )
    attn_grad = (
        main + adapter_scale * jnp.dot(back_bf, down_a, preferred_element_type=jnp.float32)
    ).astype(jnp.bfloat16)
    factor = adapter_scale / (attn_out.shape[0] * lax.axis_size("dp"))
    grad_a = factor * lax.dot_general(
        back_bf, attn_out, (((0,), (0,)), ((), ())), preferred_element_type=jnp.float32
    )
    grad_b = factor * lax.dot_general(
        low_bf, grad_cols, (((0,), (0,)), ((), ())), preferred_element_type=jnp.float32
    )
    bank_a, logit_grad_a = compose_back(grad_a, weights_a, picked_a, mixing_a, vector_bank)
    bank_b, logit_grad_b = compose_back(grad_b, weights_b, picked_b, mixing_b, vector_bank)
    bank_part = bank_a + bank_b
    bank_group = lax.psum(bank_part, "tensor")
    bank_grad, logits_a_grad, logits_b_grad = lax.psum(
        (bank_group, logit_grad_a, logit_grad_b), "dp"
    )
    return (layer_out, attn_grad, bank_grad, logits_a_grad, logits_b_grad)


def ring_local(dp_size, tensor_size, attn_out, frozen_weight, vector_bank, logits_a, index_a, logits_b, index_b, out_grad):
    depth = tensor_size
    chips = tensor_size // 2
    rows = attn_out.shape[0]
    own_width = attn_out.shape[1]
    width = frozen_weight.shape[1]
    half = width // 2
    part = own_width // ROW_PIECES
    place = lax.axis_index("dp")
    level, side = place // 2, place % 2
    tensor_index = lax.axis_index("tensor")

    ring = [(d, (d + 2) % dp_size) for d in range(dp_size)]
    swap = [(d, d ^ 1) for d in range(dp_size)]

    def hop(value):
        return lax.ppermute(value, "dp", ring)

    def cross(value):
        return lax.ppermute(value, "dp", swap)

    def collect(partial_value, step):
        target = (level - step + depth) % depth
        pairs = []
        for d in range(dp_size):
            goal = (d // 2 - step) % depth
            for chip in range(chips):
                core = 2 * chip + goal % 2
                pairs.append((d * tensor_size + (core ^ 1), d * tensor_size + core))
        other = lax.ppermute(partial_value, ("dp", "tensor"), pairs)
        paired = partial_value.astype(jnp.float32) + other.astype(jnp.float32)
        sent = paired.astype(jnp.bfloat16)
        total = paired
        for k in range(1, chips):
            pairs = []
            for d in range(dp_size):
                goal = (d // 2 - step) % depth
                source = ((goal // 2 + k) % chips) * 2 + goal % 2
                pairs.append((d * tensor_size + source, d * tensor_size + goal))
            total = total + lax.ppermute(sent, ("dp", "tensor"), pairs).astype(jnp.float32)
        return jnp.where(tensor_index == target, total, 0.0)

    first = frozen_weight[:, :half]
    later = [frozen_weight[r * part : (r + 1) * part, half:] for r in range(ROW_PIECES)]
    held = [(first, later)]
    for step in range(1, depth):
        first = hop(first)
        later = [hop(v) for v in later]
        held.append((first, later))

    attn_two = jnp.concatenate([attn_out, cross(attn_out)], axis=0)
    attn_parts = [attn_two[:, r * part : (r + 1) * part] for r in range(ROW_PIECES)]

    def grad_pair(step):
        origin = (level - step + depth) % depth
        mine = lax.dynamic_slice_in_dim(out_grad, (origin * 2 + side) * width, width, 1)
        theirs = lax.dynamic_slice_in_dim(out_grad, (origin * 2 + 1 - side) * width, width, 1)
        return jnp.concatenate([mine, cross(theirs)], axis=0)

    weights_a, picked_a, mixing_a, rows_a = compose(logits_a, index_a, vector_bank)
    weights_b, picked_b, mixing_b, rows_b = compose(logits_b, index_b, vector_bank)
    down_a = rows_a.astype(jnp.bfloat16)
    up_b = rows_b.astype(jnp.bfloat16)
    rank = down_a.shape[0]
    grad_cols = lax.dynamic_slice_in_dim(out_grad, tensor_index * own_width, own_width, 1)
    low_part = jnp.dot(attn_out, down_a.T, preferred_element_type=jnp.float32)
    back_part = jnp.dot(grad_cols, up_b.T, preferred_element_type=jnp.float32)
    both = lax.psum(jnp.concatenate([low_part, back_part], axis=1), "tensor")
    low_bf = both[:, :rank].astype(jnp.bfloat16)
    back_bf = both[:, rank:].astype(jnp.bfloat16)

    sums = [None] * ROW_PIECES
    own_total = jnp.zeros((rows, width), jnp.float32)
    cross_total = jnp.zeros((rows, width), jnp.float32)
    for step in range(depth):
        first, later = held[step]
        grads = grad_pair(step)
        out_first = jnp.dot(attn_two, first, preferred_element_type=jnp.float32)
        for r in range(ROW_PIECES):
            term = lax.dot_general(
                grads[:, :half],
                first[r * part : (r + 1) * part],
                (((1,), (1,)), ((), ())),
                preferred_element_type=jnp.float32,
            )
            sums[r] = term if sums[r] is None else sums[r] + term
        out_later = None
        for r in range(ROW_PIECES):
            term = jnp.dot(attn_parts[r], later[r], preferred_element_type=jnp.float32)
            out_later = term if out_later is None else out_later + term
            sums[r] = sums[r] + lax.dot_general(
                grads[:, half:],
                later[r],
                (((1,), (1,)), ((), ())),
                preferred_element_type=jnp.float32,
            )
        out_first = out_first.astype(jnp.bfloat16)
        out_later = out_later.astype(jnp.bfloat16)
        if step < depth - 1:
            block = collect(jnp.concatenate([out_first, out_later], axis=1), step)
            own_total = own_total + block[:rows]
            cross_total = cross_total + block[rows:]
        if step == depth - 2:
            came = cross(cross_total.astype(jnp.bfloat16)).astype(jnp.float32)
        if step == depth - 1:
            ends = [collect(out_first, step), collect(out_later, step)]
            own_end = jnp.concatenate([v[:rows] for v in ends], axis=1)
            came_end = jnp.concatenate(
                [cross(v[rows:].astype(jnp.bfloat16)) for v in ends], axis=1
            ).astype(jnp.float32)
    own_half = own_total + own_end
    other_half = came + came_end
    summed = jnp.concatenate(
        [
            jnp.where(side == 0, own_half, other_half),
            jnp.where(side == 0, other_half, own_half),
        ],
        axis=1,
    )
    layer_out = (
        summed + adapter_scale * jnp.dot(low_bf, up_b, preferred_element_type=jnp.float32)
    ).astype(jnp.bfloat16)

    adapter = adapter_scale * jnp.dot(back_bf, down_a, preferred_element_type=jnp.float32)
    pieces = []
    for r in range(ROW_PIECES):
        came_grad = cross(sums[r][rows:].astype(jnp.bfloat16)).astype(jnp.float32)
        pieces.append(sums[r][:rows] + came_grad + adapter[:, r * part : (r + 1) * part])
    attn_grad = jnp.concatenate(pieces, axis=1).astype(jnp.bfloat16)

    factor = adapter_scale / (rows * dp_size)
    grad_a = factor * lax.dot_general(
        back_bf, attn_out, (((0,), (0,)), ((), ())), preferred_element_type=jnp.float32
    )
    grad_b = factor * lax.dot_general(
        low_bf, grad_cols, (((0,), (0,)), ((), ())), preferred_element_type=jnp.float32
    )
    bank_a, logit_grad_a = compose_back(grad_a, weights_a, picked_a, mixing_a, vector_bank)
    bank_b, logit_grad_b = compose_back(grad_b, weights_b, picked_b, mixing_b, vector_bank)
    bank_grad = lax.psum(bank_a + bank_b, ("dp", "tensor"))
    logits_a_grad, logits_b_grad = lax.psum((logit_grad_a, logit_grad_b), "dp")
    return (layer_out, attn_grad, bank_grad, logits_a_grad, logits_b_grad)


MESH_ID = pl.DeviceIdType.MESH
PIECES = 4


def dot_nn(a, b):
    return jnp.dot(a, b, preferred_element_type=jnp.float32)


def dot_nt(a, b):
    return lax.dot_general(a, b, (((1,), (1,)), ((), ())), preferred_element_type=jnp.float32)


def exchange_kernel(
    factor,
    attn, weight, grad, down, up,
    out_hbm, agrad_hbm, relay, gab,
    wbuf, abuf, gbuf, dacc, cbuf, ybuf, dsend, drecv, cacc, lb, low, back,
    load_sem, zs_send, relay_recv, relay_send, far_recv, xs_send, x_recv, xf_send, xf_recv,
    g_send, g_recv, gm_send, gm_recv, a_send, a_recv, lb_send, lb_recv,
    c_send, c_recv, y_send, y_recv, zc_send, zc_recv, d_send, d_recv, out_sem,
):
    rows, depth = attn.shape
    width = weight.shape[1]
    half = width // 2
    step = depth // PIECES
    tile = rows // 2
    rank = down.shape[0]
    own = up.shape[1]

    dp, t = lax.axis_index("dp"), lax.axis_index("tensor")
    z, x = dp // 2, dp % 2
    y, c = t // 2, t % 2
    zh, zl = z // 2, z % 2
    inner = (z == 1) | (z == 2)
    pz = zh * 2 + (1 - zl)
    mz = jnp.where(z == 1, 2, 1)
    x_dev = (z * 2 + (1 - x), t)
    p_dev = (pz * 2 + x, t)
    m_dev = (mz * 2 + x, t)
    c_dev = (dp, y * 2 + (1 - c))
    y_dev = (dp, (1 - y) * 2 + c)
    reduces = c == zl

    def remote(src, dst, send, recv, device):
        return pltpu.make_async_remote_copy(
            src_ref=src, dst_ref=dst, send_sem=send, recv_sem=recv,
            device_id=device, device_id_type=MESH_ID,
        )

    def rowsof(p):
        return pl.ds(pl.multiple_of(p * step, step), step)

    barrier = pltpu.get_barrier_semaphore()
    others = [(dp, (t + k) % 4) for k in (1, 2, 3)]
    for device in others + [x_dev, p_dev]:
        pl.semaphore_signal(barrier, inc=1, device_id=device, device_id_type=MESH_ID)

    @pl.when(inner)
    def _():
        pl.semaphore_signal(barrier, inc=1, device_id=m_dev, device_id_type=MESH_ID)

    def column_block(zz, b, xx):
        zb = jnp.where(b < 2, zz, (zz + 2) % 4)
        xb = jnp.where(b % 2 == 0, xx, 1 - xx)
        return zb * 2 + xb

    loads = [pltpu.make_async_copy(attn, abuf.at[0], load_sem.at[0])]
    gq = pltpu.make_async_copy(
        grad.at[:, pl.ds(pl.multiple_of(t * own, own), own)], dsend.at[:, pl.ds(0, own)], load_sem.at[1]
    )
    loads.append(gq)
    for n in range(2):
        loads.append(
            pltpu.make_async_copy(weight.at[:, pl.ds(n * half, half)], wbuf.at[n], load_sem.at[2 + n])
        )
    for s in range(8):
        col = column_block(z, s // 2, x) * width + (s % 2) * half
        loads.append(
            pltpu.make_async_copy(
                grad.at[:, pl.ds(pl.multiple_of(col, half), half)], gbuf.at[s, 0], load_sem.at[4 + s]
            )
        )
    for load in loads:
        load.start()

    @pl.when(inner)
    def _():
        pl.semaphore_wait(barrier, 6)

    @pl.when(jnp.logical_not(inner))
    def _():
        pl.semaphore_wait(barrier, 5)

    def x_own(i):
        n, p = i // 4, i % 4
        return remote(
            weight.at[rowsof(p), pl.ds(pl.multiple_of(n * half, half), half)],
            wbuf.at[2 + n, rowsof(p)], xs_send.at[i], x_recv.at[i], x_dev,
        )

    def z_own(i):
        n, p = i // 4, i % 4
        stream = jnp.where(inner, 0, 1)
        device = (jnp.where(inner, mz, pz) * 2 + x, t)
        return remote(
            weight.at[rowsof(p), pl.ds(pl.multiple_of(n * half, half), half)],
            relay.at[stream, n, rowsof(p)], zs_send.at[i], relay_recv.at[stream, i], device,
        )

    def g_own(n):
        col = column_block(pz, t, x) * width + n * half
        return remote(
            grad.at[:, pl.ds(pl.multiple_of(col, half), half)],
            gbuf.at[2 * t + n, 1], g_send.at[n], g_recv.at[n], p_dev,
        )

    a_own = remote(attn, abuf.at[1], a_send.at[0], a_recv.at[0], p_dev)

    for n in range(2):
        g_own(n).start()
    a_own.start()

    @pl.loop(0, 8)
    def _(i):
        x_own(i).start()
        z_own(i).start()

    loads[0].wait()
    loads[1].wait()
    lb[t, :rank] = dot_nt(down[...], abuf[0])
    lb[t, rank:] = dot_nt(up[...], dsend[:, :own])

    def lb_copy(k):
        device = (dp, (t + k) % 4)
        return remote(lb.at[t], lb.at[t], lb_send.at[k - 1], lb_recv.at[k - 1], device)

    for k in (1, 2, 3):
        lb_copy(k).start()
    for load in loads[2:]:
        load.wait()
    dacc[...] = jnp.zeros_like(dacc)
    for k in (1, 2, 3):
        lb_copy(k).wait()
    both = lb[0] + lb[1] + lb[2] + lb[3]
    low[...] = both[:rank].T.astype(jnp.bfloat16)
    back[...] = both[rank:].T.astype(jnp.bfloat16)
    both = both.astype(jnp.bfloat16)
    gab[:rank] = factor * dot_nn(both[rank:], abuf[0])
    gab[rank:] = factor * dot_nn(both[:rank], dsend[:, :own])

    def relay_on(stream, i):
        n, p = i // 4, i % 4
        device = (jnp.where(stream == 0, pz, mz) * 2 + x, t)
        return remote(
            relay.at[stream, n, rowsof(p)], wbuf.at[4 + n, rowsof(p)],
            relay_send.at[stream, i], far_recv.at[i], device,
        )

    def relay_wait(stream, i):
        n, p = i // 4, i % 4
        piece = relay.at[stream, n, rowsof(p)]
        remote(piece, piece, relay_send.at[stream, i], relay_recv.at[stream, i], p_dev).wait_recv()

    def x_far(i):
        n, p = i // 4, i % 4
        return remote(
            wbuf.at[4 + n, rowsof(p)], wbuf.at[6 + n, rowsof(p)], xf_send.at[i], xf_recv.at[i], x_dev
        )

    def far_wait(i):
        n, p = i // 4, i % 4
        piece = wbuf.at[4 + n, rowsof(p)]
        remote(piece, piece, xf_send.at[i], far_recv.at[i], x_dev).wait_recv()

    def g_spread(k, n):
        piece = gbuf.at[2 * t + n, 1]
        return remote(piece, piece, gm_send.at[k - 1, n], gm_recv.at[k - 1, n], (dp, (t + k) % 4))

    lag = jnp.where(inner, 9, 7)

    def tick(i, carry):
        @pl.when(i < 8)
        def _():
            x_own(i).wait_recv()

            @pl.when(inner)
            def _():
                relay_wait(0, i)
                relay_on(0, i).start()

        @pl.when(i == 2)
        def _():
            for n in range(2):
                g_own(n).wait_recv()
                for k in (1, 2, 3):
                    g_spread(k, n).start()

        @pl.when((i >= 7) & (i < 15) & inner)
        def _():
            relay_wait(1, i - 7)
            relay_on(1, i - 7).start()

        @pl.when((i >= lag) & (i < lag + 8))
        def _():
            far_wait(i - lag)
            x_far(i - lag).start()

        return carry

    def c_copy(s, r):
        return remote(cbuf.at[s, r], cbuf.at[s, r], c_send.at[s, r], c_recv.at[s, r], c_dev)

    def y_copy(s, r):
        return remote(cbuf.at[s, r], ybuf.at[s % 4, r], y_send.at[s % 4, r], y_recv.at[s % 4, r], y_dev)

    def z_copy(s):
        return remote(cbuf.at[s, 1], ybuf.at[s % 4, 0], zc_send.at[s % 4], zc_recv.at[s % 4], p_dev)

    def kept(s):
        return jnp.where(s < 4, zh, 1 - zh) == y

    def out_columns(j):
        xb = jnp.where(j < 2, x, 1 - x)
        return pl.ds(pl.multiple_of(xb * width + (j % 2) * half, half), half)

    def out_copy(j):
        return pltpu.make_async_copy(ybuf.at[j, 0], out_hbm.at[:, out_columns(j)], out_sem.at[j])

    def adapter_out(j):
        return 2.0 * dot_nn(low[...], up[:, out_columns(j)])

    def pass_core(s, r, partial):
        @pl.when(jnp.logical_not(reduces))
        def _():
            cbuf[s, r] = partial[...].astype(jnp.bfloat16)
            c_copy(s, r).start()

    def sum_core(s, r, partial):
        @pl.when(reduces)
        def _():
            c_copy(s, r).wait_recv()
            cbuf[s, r] = (partial[...] + cbuf[s, r].astype(jnp.float32)).astype(jnp.bfloat16)

            @pl.when(jnp.logical_not(kept(s)))
            def _():
                y_copy(s, r).start()

    def sum_y(s, r):
        @pl.when(reduces & kept(s))
        def _():
            j = s % 4
            y_copy(s, r).wait_recv()
            total = cbuf[s, r].astype(jnp.float32) + ybuf[j, r].astype(jnp.float32)

            @pl.when(r == 0)
            def _():
                ybuf[j, 0] = (total + adapter_out(j)).astype(jnp.bfloat16)
                out_copy(j).start()

            @pl.when(r == 1)
            def _():
                cbuf[s, 1] = total.astype(jnp.bfloat16)
                z_copy(s).start()

    def finish_other(j):
        @pl.when(jnp.logical_not(reduces))
        def _():
            z_copy(j).wait_recv()
            ybuf[j, 0] = (ybuf[j, 0].astype(jnp.float32) + adapter_out(j)).astype(jnp.bfloat16)
            out_copy(j).start()

    slots = (0, 1, 2, 0, 1, 2, 3, 3, 4, 4, 6, 6, 5, 5, 7, 7)
    sides = (0, 0, 0, 1, 1, 1, 0, 1, 0, 1, 0, 1, 0, 1, 0, 1)

    def pick(table, u):
        if isinstance(u, int):
            return table[u]
        value = table[0]
        for k in range(1, len(table)):
            if table[k] != table[k - 1]:
                value = jnp.where(u >= k, table[k], value)
        return value

    def ready(u):
        value = jnp.where(u >= 2, 4, 0)
        value = jnp.where(u >= 3, 7, value)
        value = jnp.where(u >= 6, 8, value)
        value = jnp.where(u >= 8, lag + 4, value)
        return jnp.where(u >= 10, lag + 5, value)

    def unit(u, carry):
        s, r = pick(slots, u), pick(sides, u)
        lax.fori_loop(ready(u - 1), ready(u), tick, 0)

        @pl.when(u == 3)
        def _():
            a_own.wait_recv()
            for n in range(2):
                for k in (1, 2, 3):
                    g_spread(k, n).wait_recv()

        @pl.when(u == 10)
        def _():
            for p in range(PIECES):
                x_far(p).wait_recv()

        partial = cacc.at[0, u % 2]
        for m in range(2):
            part = pl.ds(m * tile, tile)
            partial[part] = dot_nn(abuf[r, part], wbuf[s])
            dacc[r, part] += dot_nt(gbuf[s, r, part], wbuf[s])
        pass_core(s, r, partial)

        @pl.when(u >= 1)
        def _():
            sum_core(pick(slots, u - 1), pick(sides, u - 1), cacc.at[0, (u - 1) % 2])

        @pl.when(u >= 4)
        def _():
            sum_y(pick(slots, u - 4), pick(sides, u - 4))

        return carry

    lax.fori_loop(0, 12, unit, 0)
    sum_core(slots[11], sides[11], cacc.at[0, 1])
    cacc[...] = jnp.zeros_like(cacc)

    def d_copy(p):
        columns = pl.ds(pl.multiple_of(p * step, step), step)
        return remote(dsend.at[:, columns], drecv.at[:, columns], d_send.at[p], d_recv.at[p], p_dev)

    def last_piece(p, carry):
        lax.fori_loop(lag + 5 + p, jnp.where(p == 3, 17, lag + 6 + p), tick, 0)
        x_far(4 + p).wait_recv()
        columns = rowsof(p)
        for q in range(2):
            r = 1 - q
            for m in range(2):
                part = pl.ds(m * tile, tile)
                grown = dacc[r, part, columns]
                grown += dot_nt(gbuf[5, r, part], wbuf[5, columns])
                grown += dot_nt(gbuf[7, r, part], wbuf[7, columns])
                if r == 1:
                    dsend[part, columns] = grown.astype(jnp.bfloat16)
                else:
                    dacc[0, part, columns] = grown
            if r == 1:
                d_copy(p).start()
        for k in range(2):
            for r in range(2):
                cacc[k, r] += dot_nn(abuf[r, :, columns], wbuf[5 + 2 * k, columns])

        @pl.when(p < 2)
        def _():
            sum_y(pick(slots, 8 + 2 * p), 0)
            sum_y(pick(slots, 8 + 2 * p), 1)

        @pl.when(p >= 2)
        def _():
            finish_other(2 * (p - 2))

        return carry

    lax.fori_loop(0, PIECES, last_piece, 0)

    def agrad_copy(p):
        columns = pl.ds(pl.multiple_of(p * step, step), step)
        return pltpu.make_async_copy(drecv.at[:, columns], agrad_hbm.at[:, columns], out_sem.at[4 + p])

    def finish_grad(p, carry):
        columns = pl.ds(pl.multiple_of(p * step, step), step)
        d_copy(p).wait_recv()
        total = dacc[0, :, columns] + drecv[:, columns].astype(jnp.float32)
        drecv[:, columns] = (total + 2.0 * dot_nn(back[...], down[:, columns])).astype(jnp.bfloat16)
        agrad_copy(p).start()
        return carry

    for u in range(12, 16):
        pass_core(slots[u], sides[u], cacc.at[(u - 12) // 2, sides[u]])
    lax.fori_loop(0, 2, finish_grad, 0)
    for u in range(12, 16):
        sum_core(slots[u], sides[u], cacc.at[(u - 12) // 2, sides[u]])
    lax.fori_loop(2, 4, finish_grad, 0)
    for u in range(12, 16):
        sum_y(slots[u], sides[u])
    finish_other(1)
    finish_other(3)

    a_own.wait_send()
    for n in range(2):
        g_own(n).wait_send()
        for k in (1, 2, 3):
            g_spread(k, n).wait_send()

    @pl.loop(0, 8)
    def _(i):
        x_own(i).wait_send()
        z_own(i).wait_send()
        x_far(i).wait_send()

        @pl.when(inner)
        def _():
            relay_on(0, i).wait_send()
            relay_on(1, i).wait_send()

        @pl.when(jnp.logical_not(reduces))
        def _():
            for r in range(2):
                c_copy(i, r).wait_send()

        @pl.when(reduces & jnp.logical_not(kept(i)))
        def _():
            for r in range(2):
                y_copy(i, r).wait_send()

        @pl.when(reduces & kept(i))
        def _():
            z_copy(i).wait_send()

    @pl.loop(0, 4)
    def _(p):
        d_copy(p).wait_send()
        agrad_copy(p).wait()
        out_copy(p).wait()


def exchange(attn_out, frozen_weight, out_grad, down, up, factor):
    rows, depth = attn_out.shape
    width = frozen_weight.shape[1]
    half = width // 2
    rank, own = up.shape
    bf16, f32 = jnp.bfloat16, jnp.float32
    dma = pltpu.SemaphoreType.DMA
    hbm = pl.BlockSpec(memory_space=pl.ANY)
    vmem = pl.BlockSpec(memory_space=pltpu.VMEM)
    return pl.pallas_call(
        functools.partial(exchange_kernel, factor),
        name="exchange",
        out_shape=(
            jax.ShapeDtypeStruct((rows, own), bf16),
            jax.ShapeDtypeStruct((rows, depth), bf16),
            jax.ShapeDtypeStruct((2, 2, depth, half), bf16),
            jax.ShapeDtypeStruct((2 * rank, depth), f32),
        ),
        in_specs=[hbm, hbm, hbm, vmem, vmem],
        out_specs=(hbm, hbm, hbm, vmem),
        scratch_shapes=[
            pltpu.VMEM((8, depth, half), bf16),
            pltpu.VMEM((2, rows, depth), bf16),
            pltpu.VMEM((8, 2, rows, half), bf16),
            pltpu.VMEM((2, rows, depth), f32),
            pltpu.VMEM((8, 2, rows, half), bf16),
            pltpu.VMEM((4, 2, rows, half), bf16),
            pltpu.VMEM((rows, depth), bf16),
            pltpu.VMEM((rows, depth), bf16),
            pltpu.VMEM((2, 2, rows, half), f32),
            pltpu.VMEM((4, 2 * rank, rows), f32),
            pltpu.VMEM((rows, rank), bf16),
            pltpu.VMEM((rows, rank), bf16),
            dma((12,)), dma((8,)), dma((2, 8)), dma((2, 8)), dma((8,)),
            dma((8,)), dma((8,)), dma((8,)), dma((8,)),
            dma((2,)), dma((2,)), dma((3, 2)), dma((3, 2)), dma((1,)), dma((1,)),
            dma((3,)), dma((3,)),
            dma((8, 2)), dma((8, 2)), dma((4, 2)), dma((4, 2)), dma((4,)), dma((4,)),
            dma((4,)), dma((4,)), dma((8,)),
        ],
        compiler_params=pltpu.CompilerParams(
            collective_id=0, has_side_effects=True, vmem_limit_bytes=67043328
        ),
    )(attn_out, frozen_weight, out_grad, down, up)


def fused_local(dp_size, attn_out, frozen_weight, vector_bank, logits_a, index_a, logits_b, index_b, out_grad):
    weights_a, picked_a, mixing_a, rows_a = compose(logits_a, index_a, vector_bank)
    weights_b, picked_b, mixing_b, rows_b = compose(logits_b, index_b, vector_bank)
    down_a = rows_a.astype(jnp.bfloat16)
    up_b = rows_b.astype(jnp.bfloat16)
    rank = down_a.shape[0]
    factor = adapter_scale / (attn_out.shape[0] * dp_size)
    layer_out, attn_grad, _, grads = exchange(attn_out, frozen_weight, out_grad, down_a, up_b, factor)
    bank_a, logit_grad_a = compose_back(grads[:rank], weights_a, picked_a, mixing_a, vector_bank)
    bank_b, logit_grad_b = compose_back(grads[rank:], weights_b, picked_b, mixing_b, vector_bank)
    bank_grad = lax.psum(bank_a + bank_b, ("dp", "tensor"))
    logits_a_grad, logits_b_grad = lax.psum((logit_grad_a, logit_grad_b), "dp")
    return (layer_out, attn_grad, bank_grad, logits_a_grad, logits_b_grad)


def solution(mesh):
    dp_size, tensor_size = mesh.shape["dp"], mesh.shape["tensor"]
    paired = dp_size == 2 * tensor_size and tensor_size % 2 == 0
    body = functools.partial(ring_local, dp_size, tensor_size) if paired else local
    if paired and tensor_size == 4:
        body = functools.partial(fused_local, dp_size)
    return jax.shard_map(
        body,
        mesh=mesh,
        in_specs=(
            P("dp", "tensor"),
            P("tensor", "dp"),
            P(),
            P(None, "tensor", None),
            P(None, "tensor", None),
            P(None, "tensor", None),
            P(None, "tensor", None),
            P("dp", None),
        ),
        out_specs=(
            P("dp", "tensor"),
            P("dp", "tensor"),
            P(),
            P(None, "tensor", None),
            P(None, "tensor", None),
        ),
        check_vma=False,
    )
```

```python
import functools

import jax
import jax.numpy as jnp
from jax import lax
from jax.experimental import pallas as pl
from jax.experimental.pallas import tpu as pltpu
from jax.sharding import PartitionSpec as P

adapter_scale = 2.0
ROW_PIECES = 4


def compose(logits, indices, vector_bank):
    weights = jax.nn.sigmoid(logits - logits[..., ::-1])
    levels = jnp.arange(vector_bank.shape[0], dtype=jnp.int32)
    picked = (indices[..., None] == levels).astype(jnp.float32)
    mixing = jnp.sum(picked * weights[..., None], axis=2)
    blocks = jnp.einsum("rjb,bc->rjc", mixing, vector_bank, precision=lax.Precision.HIGHEST)
    return (weights, picked, mixing, blocks.reshape(blocks.shape[0], -1))


def compose_back(grad_rows, weights, picked, mixing, vector_bank):
    blocks = grad_rows.reshape(mixing.shape[0], mixing.shape[1], -1)
    bank_part = jnp.einsum("rjb,rjc->bc", mixing, blocks, precision=lax.Precision.HIGHEST)
    projected = jnp.einsum("rjc,bc->rjb", blocks, vector_bank, precision=lax.Precision.HIGHEST)
    dots = jnp.sum(picked * projected[:, :, None, :], axis=3)
    logit_grad = weights * (dots - jnp.sum(weights * dots, axis=2, keepdims=True))
    return (bank_part, logit_grad)


def local(attn_out, frozen_weight, vector_bank, logits_a, index_a, logits_b, index_b, out_grad):
    weights_a, picked_a, mixing_a, rows_a = compose(logits_a, index_a, vector_bank)
    weights_b, picked_b, mixing_b, rows_b = compose(logits_b, index_b, vector_bank)
    down_a = rows_a.astype(jnp.bfloat16)
    up_b = rows_b.astype(jnp.bfloat16)
    own_width = up_b.shape[1]
    grad_cols = lax.dynamic_slice_in_dim(
        out_grad, lax.axis_index("tensor") * own_width, own_width, 1
    )
    low_part = jnp.dot(attn_out, down_a.T, preferred_element_type=jnp.float32)
    back_part = jnp.dot(grad_cols, up_b.T, preferred_element_type=jnp.float32)
    low_total = lax.psum(low_part, "tensor")
    low_bf = low_total.astype(jnp.bfloat16)
    gathered = lax.all_gather(frozen_weight, "dp", axis=1, tiled=True)
    partial_value = jnp.dot(attn_out, gathered, preferred_element_type=jnp.float32).astype(
        jnp.bfloat16
    )
    summed = lax.psum_scatter(partial_value, "tensor", scatter_dimension=1, tiled=True).astype(
        jnp.float32
    )
    layer_out = (
        summed + adapter_scale * jnp.dot(low_bf, up_b, preferred_element_type=jnp.float32)
    ).astype(jnp.bfloat16)
    back_total = lax.psum(back_part, "tensor")
    back_bf = back_total.astype(jnp.bfloat16)
    main = lax.dot_general(
        out_grad, gathered, (((1,), (1,)), ((), ())), preferred_element_type=jnp.float32
    )
    attn_grad = (
        main + adapter_scale * jnp.dot(back_bf, down_a, preferred_element_type=jnp.float32)
    ).astype(jnp.bfloat16)
    factor = adapter_scale / (attn_out.shape[0] * lax.axis_size("dp"))
    grad_a = factor * lax.dot_general(
        back_bf, attn_out, (((0,), (0,)), ((), ())), preferred_element_type=jnp.float32
    )
    grad_b = factor * lax.dot_general(
        low_bf, grad_cols, (((0,), (0,)), ((), ())), preferred_element_type=jnp.float32
    )
    bank_a, logit_grad_a = compose_back(grad_a, weights_a, picked_a, mixing_a, vector_bank)
    bank_b, logit_grad_b = compose_back(grad_b, weights_b, picked_b, mixing_b, vector_bank)
    bank_part = bank_a + bank_b
    bank_group = lax.psum(bank_part, "tensor")
    bank_grad, logits_a_grad, logits_b_grad = lax.psum(
        (bank_group, logit_grad_a, logit_grad_b), "dp"
    )
    return (layer_out, attn_grad, bank_grad, logits_a_grad, logits_b_grad)


def ring_local(dp_size, tensor_size, attn_out, frozen_weight, vector_bank, logits_a, index_a, logits_b, index_b, out_grad):
    depth = tensor_size
    chips = tensor_size // 2
    rows = attn_out.shape[0]
    own_width = attn_out.shape[1]
    width = frozen_weight.shape[1]
    half = width // 2
    part = own_width // ROW_PIECES
    place = lax.axis_index("dp")
    level, side = place // 2, place % 2
    tensor_index = lax.axis_index("tensor")

    ring = [(d, (d + 2) % dp_size) for d in range(dp_size)]
    swap = [(d, d ^ 1) for d in range(dp_size)]

    def hop(value):
        return lax.ppermute(value, "dp", ring)

    def cross(value):
        return lax.ppermute(value, "dp", swap)

    def collect(partial_value, step):
        target = (level - step + depth) % depth
        pairs = []
        for d in range(dp_size):
            goal = (d // 2 - step) % depth
            for chip in range(chips):
                core = 2 * chip + goal % 2
                pairs.append((d * tensor_size + (core ^ 1), d * tensor_size + core))
        other = lax.ppermute(partial_value, ("dp", "tensor"), pairs)
        paired = partial_value.astype(jnp.float32) + other.astype(jnp.float32)
        sent = paired.astype(jnp.bfloat16)
        total = paired
        for k in range(1, chips):
            pairs = []
            for d in range(dp_size):
                goal = (d // 2 - step) % depth
                source = ((goal // 2 + k) % chips) * 2 + goal % 2
                pairs.append((d * tensor_size + source, d * tensor_size + goal))
            total = total + lax.ppermute(sent, ("dp", "tensor"), pairs).astype(jnp.float32)
        return jnp.where(tensor_index == target, total, 0.0)

    first = frozen_weight[:, :half]
    later = [frozen_weight[r * part : (r + 1) * part, half:] for r in range(ROW_PIECES)]
    held = [(first, later)]
    for step in range(1, depth):
        first = hop(first)
        later = [hop(v) for v in later]
        held.append((first, later))

    attn_two = jnp.concatenate([attn_out, cross(attn_out)], axis=0)
    attn_parts = [attn_two[:, r * part : (r + 1) * part] for r in range(ROW_PIECES)]

    def grad_pair(step):
        origin = (level - step + depth) % depth
        mine = lax.dynamic_slice_in_dim(out_grad, (origin * 2 + side) * width, width, 1)
        theirs = lax.dynamic_slice_in_dim(out_grad, (origin * 2 + 1 - side) * width, width, 1)
        return jnp.concatenate([mine, cross(theirs)], axis=0)

    weights_a, picked_a, mixing_a, rows_a = compose(logits_a, index_a, vector_bank)
    weights_b, picked_b, mixing_b, rows_b = compose(logits_b, index_b, vector_bank)
    down_a = rows_a.astype(jnp.bfloat16)
    up_b = rows_b.astype(jnp.bfloat16)
    rank = down_a.shape[0]
    grad_cols = lax.dynamic_slice_in_dim(out_grad, tensor_index * own_width, own_width, 1)
    low_part = jnp.dot(attn_out, down_a.T, preferred_element_type=jnp.float32)
    back_part = jnp.dot(grad_cols, up_b.T, preferred_element_type=jnp.float32)
    both = lax.psum(jnp.concatenate([low_part, back_part], axis=1), "tensor")
    low_bf = both[:, :rank].astype(jnp.bfloat16)
    back_bf = both[:, rank:].astype(jnp.bfloat16)

    sums = [None] * ROW_PIECES
    own_total = jnp.zeros((rows, width), jnp.float32)
    cross_total = jnp.zeros((rows, width), jnp.float32)
    for step in range(depth):
        first, later = held[step]
        grads = grad_pair(step)
        out_first = jnp.dot(attn_two, first, preferred_element_type=jnp.float32)
        for r in range(ROW_PIECES):
            term = lax.dot_general(
                grads[:, :half],
                first[r * part : (r + 1) * part],
                (((1,), (1,)), ((), ())),
                preferred_element_type=jnp.float32,
            )
            sums[r] = term if sums[r] is None else sums[r] + term
        out_later = None
        for r in range(ROW_PIECES):
            term = jnp.dot(attn_parts[r], later[r], preferred_element_type=jnp.float32)
            out_later = term if out_later is None else out_later + term
            sums[r] = sums[r] + lax.dot_general(
                grads[:, half:],
                later[r],
                (((1,), (1,)), ((), ())),
                preferred_element_type=jnp.float32,
            )
        out_first = out_first.astype(jnp.bfloat16)
        out_later = out_later.astype(jnp.bfloat16)
        if step < depth - 1:
            block = collect(jnp.concatenate([out_first, out_later], axis=1), step)
            own_total = own_total + block[:rows]
            cross_total = cross_total + block[rows:]
        if step == depth - 2:
            came = cross(cross_total.astype(jnp.bfloat16)).astype(jnp.float32)
        if step == depth - 1:
            ends = [collect(out_first, step), collect(out_later, step)]
            own_end = jnp.concatenate([v[:rows] for v in ends], axis=1)
            came_end = jnp.concatenate(
                [cross(v[rows:].astype(jnp.bfloat16)) for v in ends], axis=1
            ).astype(jnp.float32)
    own_half = own_total + own_end
    other_half = came + came_end
    summed = jnp.concatenate(
        [
            jnp.where(side == 0, own_half, other_half),
            jnp.where(side == 0, other_half, own_half),
        ],
        axis=1,
    )
    layer_out = (
        summed + adapter_scale * jnp.dot(low_bf, up_b, preferred_element_type=jnp.float32)
    ).astype(jnp.bfloat16)

    adapter = adapter_scale * jnp.dot(back_bf, down_a, preferred_element_type=jnp.float32)
    pieces = []
    for r in range(ROW_PIECES):
        came_grad = cross(sums[r][rows:].astype(jnp.bfloat16)).astype(jnp.float32)
        pieces.append(sums[r][:rows] + came_grad + adapter[:, r * part : (r + 1) * part])
    attn_grad = jnp.concatenate(pieces, axis=1).astype(jnp.bfloat16)

    factor = adapter_scale / (rows * dp_size)
    grad_a = factor * lax.dot_general(
        back_bf, attn_out, (((0,), (0,)), ((), ())), preferred_element_type=jnp.float32
    )
    grad_b = factor * lax.dot_general(
        low_bf, grad_cols, (((0,), (0,)), ((), ())), preferred_element_type=jnp.float32
    )
    bank_a, logit_grad_a = compose_back(grad_a, weights_a, picked_a, mixing_a, vector_bank)
    bank_b, logit_grad_b = compose_back(grad_b, weights_b, picked_b, mixing_b, vector_bank)
    bank_grad = lax.psum(bank_a + bank_b, ("dp", "tensor"))
    logits_a_grad, logits_b_grad = lax.psum((logit_grad_a, logit_grad_b), "dp")
    return (layer_out, attn_grad, bank_grad, logits_a_grad, logits_b_grad)


MESH_ID = pl.DeviceIdType.MESH
PIECES = 4


def dot_nn(a, b):
    return jnp.dot(a, b, preferred_element_type=jnp.float32)


def dot_nt(a, b):
    return lax.dot_general(a, b, (((1,), (1,)), ((), ())), preferred_element_type=jnp.float32)


def exchange_kernel(
    factor,
    attn, weight, grad, bank, table,
    out_hbm, agrad_hbm, relay, bank_out, slope_out,
    wbuf, abuf, gbuf, dacc, cbuf, ybuf, dsend, drecv, cacc, lb, low, back,
    down, up, blocks, mixing, sums, came,
    load_sem, zs_send, relay_recv, relay_send, far_recv, xs_send, x_recv, xf_send, xf_recv,
    g_send, g_recv, gm_send, gm_recv, a_send, a_recv, lb_send, lb_recv,
    c_send, c_recv, y_send, y_recv, zc_send, zc_recv, d_send, d_recv, out_sem,
    sum_send, sum_recv,
):
    rows, depth = attn.shape
    width = weight.shape[1]
    half = width // 2
    step = depth // PIECES
    tile = rows // 2
    rank = down.shape[0]
    own = up.shape[1]

    dp, t = lax.axis_index("dp"), lax.axis_index("tensor")
    z, x = dp // 2, dp % 2
    y, c = t // 2, t % 2
    zh, zl = z // 2, z % 2
    inner = (z == 1) | (z == 2)
    pz = zh * 2 + (1 - zl)
    mz = jnp.where(z == 1, 2, 1)
    x_dev = (z * 2 + (1 - x), t)
    p_dev = (pz * 2 + x, t)
    m_dev = (mz * 2 + x, t)
    c_dev = (dp, y * 2 + (1 - c))
    y_dev = (dp, (1 - y) * 2 + c)
    reduces = c == zl

    def remote(src, dst, send, recv, device):
        return pltpu.make_async_remote_copy(
            src_ref=src, dst_ref=dst, send_sem=send, recv_sem=recv,
            device_id=device, device_id_type=MESH_ID,
        )

    def rowsof(p):
        return pl.ds(pl.multiple_of(p * step, step), step)

    barrier = pltpu.get_barrier_semaphore()
    others = [(dp, (t + k) % 4) for k in (1, 2, 3)]
    for device in others + [x_dev, p_dev]:
        pl.semaphore_signal(barrier, inc=1, device_id=device, device_id_type=MESH_ID)

    @pl.when(inner)
    def _():
        pl.semaphore_signal(barrier, inc=1, device_id=m_dev, device_id_type=MESH_ID)

    def column_block(zz, b, xx):
        zb = jnp.where(b < 2, zz, (zz + 2) % 4)
        xb = jnp.where(b % 2 == 0, xx, 1 - xx)
        return zb * 2 + xb

    loads = [pltpu.make_async_copy(attn, abuf.at[0], load_sem.at[0])]
    gq = pltpu.make_async_copy(
        grad.at[:, pl.ds(pl.multiple_of(t * own, own), own)], dsend.at[:, pl.ds(0, own)], load_sem.at[1]
    )
    loads.append(gq)
    for n in range(2):
        loads.append(
            pltpu.make_async_copy(weight.at[:, pl.ds(n * half, half)], wbuf.at[n], load_sem.at[2 + n])
        )
    for s in range(8):
        col = column_block(z, s // 2, x) * width + (s % 2) * half
        loads.append(
            pltpu.make_async_copy(
                grad.at[:, pl.ds(pl.multiple_of(col, half), half)], gbuf.at[s, 0], load_sem.at[4 + s]
            )
        )
    for load in loads:
        load.start()

    @pl.when(inner)
    def _():
        pl.semaphore_wait(barrier, 6)

    @pl.when(jnp.logical_not(inner))
    def _():
        pl.semaphore_wait(barrier, 5)

    def x_own(i):
        n, p = i // 4, i % 4
        return remote(
            weight.at[rowsof(p), pl.ds(pl.multiple_of(n * half, half), half)],
            wbuf.at[2 + n, rowsof(p)], xs_send.at[i], x_recv.at[i], x_dev,
        )

    def z_own(i):
        n, p = i // 4, i % 4
        stream = jnp.where(inner, 0, 1)
        device = (jnp.where(inner, mz, pz) * 2 + x, t)
        return remote(
            weight.at[rowsof(p), pl.ds(pl.multiple_of(n * half, half), half)],
            relay.at[stream, n, rowsof(p)], zs_send.at[i], relay_recv.at[stream, i], device,
        )

    def g_own(n):
        col = column_block(pz, t, x) * width + n * half
        return remote(
            grad.at[:, pl.ds(pl.multiple_of(col, half), half)],
            gbuf.at[2 * t + n, 1], g_send.at[n], g_recv.at[n], p_dev,
        )

    a_own = remote(attn, abuf.at[1], a_send.at[0], a_recv.at[0], p_dev)

    for n in range(2):
        g_own(n).start()
    a_own.start()

    @pl.loop(0, 4)
    def _(i):
        x_own(i).start()

    @pl.when(inner)
    def _():
        @pl.loop(0, 8)
        def _(i):
            z_own(i).start()

    levels = bank.shape[0]
    sublen = bank.shape[1]
    vectors = mixing.shape[1]
    per_row = vectors // rank
    exact = dict(preferred_element_type=jnp.float32, precision=lax.Precision.HIGHEST)

    def chosen(k):
        first, second = table[:, 2 * k : 2 * k + 1], table[:, 2 * k + 1 : 2 * k + 2]
        place = lax.broadcasted_iota(jnp.int32, (vectors, levels), 1)
        picks = [table[:, 4 + 2 * k + m : 5 + 2 * k + m].astype(jnp.int32) for m in range(2)]
        shares = (1.0 / (1.0 + jnp.exp(second - first)), 1.0 / (1.0 + jnp.exp(first - second)))
        return shares, (place == picks[0], place == picks[1])

    for k, target in enumerate((down, up)):
        (first, second), (at_first, at_second) = chosen(k)
        mixing[k] = jnp.where(at_first, first, 0.0) + jnp.where(at_second, second, 0.0)
        blocks[k] = jnp.dot(mixing[k], bank[...], **exact)
        for j in range(per_row):
            row = blocks[k, j * rank : (j + 1) * rank]
            target[:, j * sublen : (j + 1) * sublen] = row.astype(jnp.bfloat16)

    loads[0].wait()
    loads[1].wait()
    lb[t, :rank] = dot_nt(down[...], abuf[0])
    lb[t, rank:] = dot_nt(up[...], dsend[:, :own])

    def lb_copy(k):
        device = (dp, (t + k) % 4)
        return remote(lb.at[t], lb.at[t], lb_send.at[k - 1], lb_recv.at[k - 1], device)

    for k in (1, 2, 3):
        lb_copy(k).start()
    for load in loads[2:]:
        load.wait()
    dacc[...] = jnp.zeros_like(dacc)
    for k in (1, 2, 3):
        lb_copy(k).wait()
    both = lb[0] + lb[1] + lb[2] + lb[3]
    low[...] = both[:rank].T.astype(jnp.bfloat16)
    back[...] = both[rank:].T.astype(jnp.bfloat16)
    both = both.astype(jnp.bfloat16)
    slopes = (
        factor * dot_nn(both[rank:], abuf[0]),
        factor * dot_nn(both[:rank], dsend[:, :own]),
    )
    wide = levels // 2
    for k in range(2):
        for j in range(per_row):
            blocks[k, j * rank : (j + 1) * rank] = slopes[k][:, j * sublen : (j + 1) * sublen]
    for h in range(2):
        part = pl.ds(h * wide, wide)
        piece = 0.0
        for k in range(2):
            piece += lax.dot_general(
                mixing[k, :, h * wide : (h + 1) * wide], blocks[k], (((0,), (0,)), ((), ())), **exact
            )
        bank_out[part] = piece
    lane = lax.broadcasted_iota(jnp.int32, (vectors, 128), 1)
    dots = jnp.zeros((vectors, 128), jnp.float32)
    for k in range(2):
        _, found = chosen(k)
        projected = lax.dot_general(blocks[k], bank[...], (((1,), (1,)), ((), ())), **exact)
        for m in range(2):
            value = jnp.sum(jnp.where(found[m], projected, 0.0), axis=1, keepdims=True)
            dots = jnp.where(lane == 2 * k + m, value, dots)

    own_half = pl.ds(pl.multiple_of(c * wide, wide), wide)
    other_half = pl.ds(pl.multiple_of((1 - c) * wide, wide), wide)

    def sum_copy(k, device, columns):
        return remote(
            sums.at[:, pl.ds(0, columns)], came.at[k, :, pl.ds(0, columns)],
            sum_send.at[k], sum_recv.at[k], device,
        )

    full = sublen + 128
    sums[:, :sublen] = bank_out[other_half]
    core_sum = sum_copy(0, c_dev, sublen)
    y_sum = sum_copy(1, y_dev, sublen)
    x_sum = sum_copy(2, x_dev, full)
    p_sum = sum_copy(3, p_dev, full)
    m_sum = sum_copy(4, m_dev, full)
    out_sum = sum_copy(5, p_dev, full)
    last_sum = sum_copy(6, c_dev, sublen)
    core_sum.start()
    core_sum.wait()
    sums[:, :sublen] = bank_out[own_half] + came[0, :, :sublen]
    y_sum.start()
    y_sum.wait()
    sums[:, :sublen] += came[1, :, :sublen]
    sums[:, sublen:] = dots
    x_sum.start()

    @pl.loop(4, 8)
    def _(i):
        x_own(i).start()

    def relay_on(stream, i):
        n, p = i // 4, i % 4
        device = (jnp.where(stream == 0, pz, mz) * 2 + x, t)
        return remote(
            relay.at[stream, n, rowsof(p)], wbuf.at[4 + n, rowsof(p)],
            relay_send.at[stream, i], far_recv.at[i], device,
        )

    def relay_wait(stream, i):
        n, p = i // 4, i % 4
        piece = relay.at[stream, n, rowsof(p)]
        remote(piece, piece, relay_send.at[stream, i], relay_recv.at[stream, i], p_dev).wait_recv()

    def x_far(i):
        n, p = i // 4, i % 4
        return remote(
            wbuf.at[4 + n, rowsof(p)], wbuf.at[6 + n, rowsof(p)], xf_send.at[i], xf_recv.at[i], x_dev
        )

    def far_wait(i):
        n, p = i // 4, i % 4
        piece = wbuf.at[4 + n, rowsof(p)]
        remote(piece, piece, xf_send.at[i], far_recv.at[i], x_dev).wait_recv()

    def g_spread(k, n):
        piece = gbuf.at[2 * t + n, 1]
        return remote(piece, piece, gm_send.at[k - 1, n], gm_recv.at[k - 1, n], (dp, (t + k) % 4))

    lag = jnp.where(inner, 9, 7)

    def tick(i, carry):
        @pl.when(i < 8)
        def _():
            x_own(i).wait_recv()

            @pl.when(inner)
            def _():
                relay_wait(0, i)
                relay_on(0, i).start()

        @pl.when(i == 4)
        def _():
            x_sum.wait()
            sums[...] += came[2]
            p_sum.start()

            @pl.when(jnp.logical_not(inner))
            def _():
                @pl.loop(0, 8)
                def _(k):
                    z_own(k).start()

        @pl.when(i == 7)
        def _():
            p_sum.wait()
            sums[...] += came[3]

            @pl.when(inner)
            def _():
                m_sum.start()

        @pl.when((i == 9) & inner)
        def _():
            m_sum.wait()
            sums[...] += came[4]
            out_sum.start()

        @pl.when(i == 2)
        def _():
            for n in range(2):
                g_own(n).wait_recv()
                for k in (1, 2, 3):
                    g_spread(k, n).start()

        @pl.when((i >= 7) & (i < 15) & inner)
        def _():
            relay_wait(1, i - 7)
            relay_on(1, i - 7).start()

        @pl.when((i >= lag) & (i < lag + 8))
        def _():
            far_wait(i - lag)
            x_far(i - lag).start()

        return carry

    def c_copy(s, r):
        return remote(cbuf.at[s, r], cbuf.at[s, r], c_send.at[s, r], c_recv.at[s, r], c_dev)

    def y_copy(s, r):
        return remote(cbuf.at[s, r], ybuf.at[s % 4, r], y_send.at[s % 4, r], y_recv.at[s % 4, r], y_dev)

    def z_copy(s):
        return remote(cbuf.at[s, 1], ybuf.at[s % 4, 0], zc_send.at[s % 4], zc_recv.at[s % 4], p_dev)

    def kept(s):
        return jnp.where(s < 4, zh, 1 - zh) == y

    def out_columns(j):
        xb = jnp.where(j < 2, x, 1 - x)
        return pl.ds(pl.multiple_of(xb * width + (j % 2) * half, half), half)

    def out_copy(j):
        return pltpu.make_async_copy(ybuf.at[j, 0], out_hbm.at[:, out_columns(j)], out_sem.at[j])

    def adapter_out(j):
        return 2.0 * dot_nn(low[...], up[:, out_columns(j)])

    def pass_core(s, r, partial):
        @pl.when(jnp.logical_not(reduces))
        def _():
            cbuf[s, r] = partial[...].astype(jnp.bfloat16)
            c_copy(s, r).start()

    def sum_core(s, r, partial):
        @pl.when(reduces)
        def _():
            c_copy(s, r).wait_recv()
            cbuf[s, r] = (partial[...] + cbuf[s, r].astype(jnp.float32)).astype(jnp.bfloat16)

            @pl.when(jnp.logical_not(kept(s)))
            def _():
                y_copy(s, r).start()

    def sum_y(s, r):
        @pl.when(reduces & kept(s))
        def _():
            j = s % 4
            y_copy(s, r).wait_recv()
            total = cbuf[s, r].astype(jnp.float32) + ybuf[j, r].astype(jnp.float32)

            @pl.when(r == 0)
            def _():
                ybuf[j, 0] = (total + adapter_out(j)).astype(jnp.bfloat16)
                out_copy(j).start()

            @pl.when(r == 1)
            def _():
                cbuf[s, 1] = total.astype(jnp.bfloat16)
                z_copy(s).start()

    def finish_other(j):
        @pl.when(jnp.logical_not(reduces))
        def _():
            z_copy(j).wait_recv()
            ybuf[j, 0] = (ybuf[j, 0].astype(jnp.float32) + adapter_out(j)).astype(jnp.bfloat16)
            out_copy(j).start()

    slots = (0, 1, 2, 0, 1, 2, 3, 3, 4, 4, 6, 6, 5, 5, 7, 7)
    sides = (0, 0, 0, 1, 1, 1, 0, 1, 0, 1, 0, 1, 0, 1, 0, 1)

    def pick(table, u):
        if isinstance(u, int):
            return table[u]
        value = table[0]
        for k in range(1, len(table)):
            if table[k] != table[k - 1]:
                value = jnp.where(u >= k, table[k], value)
        return value

    def ready(u):
        value = jnp.where(u >= 2, 4, 0)
        value = jnp.where(u >= 3, 7, value)
        value = jnp.where(u >= 6, 8, value)
        value = jnp.where(u >= 8, lag + 4, value)
        return jnp.where(u >= 10, lag + 5, value)

    def unit(u, carry):
        s, r = pick(slots, u), pick(sides, u)
        lax.fori_loop(ready(u - 1), ready(u), tick, 0)

        @pl.when(u == 3)
        def _():
            a_own.wait_recv()
            for n in range(2):
                for k in (1, 2, 3):
                    g_spread(k, n).wait_recv()

        @pl.when(u == 10)
        def _():
            for p in range(PIECES):
                x_far(p).wait_recv()

        partial = cacc.at[0, u % 2]
        for m in range(2):
            part = pl.ds(m * tile, tile)
            partial[part] = dot_nn(abuf[r, part], wbuf[s])
            dacc[r, part] += dot_nt(gbuf[s, r, part], wbuf[s])
        pass_core(s, r, partial)

        @pl.when(u >= 1)
        def _():
            sum_core(pick(slots, u - 1), pick(sides, u - 1), cacc.at[0, (u - 1) % 2])

        @pl.when(u >= 4)
        def _():
            sum_y(pick(slots, u - 4), pick(sides, u - 4))

        return carry

    lax.fori_loop(0, 12, unit, 0)
    sum_core(slots[11], sides[11], cacc.at[0, 1])
    cacc[...] = jnp.zeros_like(cacc)

    def d_copy(p):
        columns = pl.ds(pl.multiple_of(p * step, step), step)
        return remote(dsend.at[:, columns], drecv.at[:, columns], d_send.at[p], d_recv.at[p], p_dev)

    def last_piece(p, carry):
        lax.fori_loop(lag + 5 + p, jnp.where(p == 3, 17, lag + 6 + p), tick, 0)
        x_far(4 + p).wait_recv()
        columns = rowsof(p)
        for q in range(2):
            r = 1 - q
            for m in range(2):
                part = pl.ds(m * tile, tile)
                grown = dacc[r, part, columns]
                grown += dot_nt(gbuf[5, r, part], wbuf[5, columns])
                grown += dot_nt(gbuf[7, r, part], wbuf[7, columns])
                if r == 1:
                    dsend[part, columns] = grown.astype(jnp.bfloat16)
                else:
                    dacc[0, part, columns] = grown
            if r == 1:
                d_copy(p).start()
        for k in range(2):
            for r in range(2):
                cacc[k, r] += dot_nn(abuf[r, :, columns], wbuf[5 + 2 * k, columns])

        @pl.when(p == 1)
        def _():
            @pl.when(inner)
            def _():
                out_sum.wait_send()

            @pl.when(jnp.logical_not(inner))
            def _():
                out_sum.wait_recv()
                sums[...] = came[5]

            last_sum.start()

        @pl.when(p < 2)
        def _():
            sum_y(pick(slots, 8 + 2 * p), 0)
            sum_y(pick(slots, 8 + 2 * p), 1)

        @pl.when(p >= 2)
        def _():
            finish_other(2 * (p - 2))

        return carry

    lax.fori_loop(0, PIECES, last_piece, 0)

    def agrad_copy(p):
        columns = pl.ds(pl.multiple_of(p * step, step), step)
        return pltpu.make_async_copy(drecv.at[:, columns], agrad_hbm.at[:, columns], out_sem.at[4 + p])

    def finish_grad(p, carry):
        columns = pl.ds(pl.multiple_of(p * step, step), step)
        d_copy(p).wait_recv()
        total = dacc[0, :, columns] + drecv[:, columns].astype(jnp.float32)
        drecv[:, columns] = (total + 2.0 * dot_nn(back[...], down[:, columns])).astype(jnp.bfloat16)
        agrad_copy(p).start()
        return carry

    for u in range(12, 16):
        pass_core(slots[u], sides[u], cacc.at[(u - 12) // 2, sides[u]])
    last_sum.wait()
    bank_out[own_half] = sums[:, :sublen]
    bank_out[other_half] = came[6, :, :sublen]
    changes = []
    for k in range(2):
        shares, _ = chosen(k)
        values = [sums[:, sublen + 2 * k + m : sublen + 2 * k + m + 1] for m in range(2)]
        mean = shares[0] * values[0] + shares[1] * values[1]
        changes += [shares[m] * (values[m] - mean) for m in range(2)]
    slope_out[...] = jnp.concatenate(changes, axis=1)
    lax.fori_loop(0, 2, finish_grad, 0)
    for u in range(12, 16):
        sum_core(slots[u], sides[u], cacc.at[(u - 12) // 2, sides[u]])
    lax.fori_loop(2, 4, finish_grad, 0)
    for u in range(12, 16):
        sum_y(slots[u], sides[u])
    finish_other(1)
    finish_other(3)

    a_own.wait_send()
    for n in range(2):
        g_own(n).wait_send()
        for k in (1, 2, 3):
            g_spread(k, n).wait_send()

    @pl.loop(0, 8)
    def _(i):
        x_own(i).wait_send()
        z_own(i).wait_send()
        x_far(i).wait_send()

        @pl.when(inner)
        def _():
            relay_on(0, i).wait_send()
            relay_on(1, i).wait_send()

        @pl.when(jnp.logical_not(reduces))
        def _():
            for r in range(2):
                c_copy(i, r).wait_send()

        @pl.when(reduces & jnp.logical_not(kept(i)))
        def _():
            for r in range(2):
                y_copy(i, r).wait_send()

        @pl.when(reduces & kept(i))
        def _():
            z_copy(i).wait_send()

    @pl.loop(0, 4)
    def _(p):
        d_copy(p).wait_send()
        agrad_copy(p).wait()
        out_copy(p).wait()


def fused_local(dp_size, attn_out, frozen_weight, vector_bank, logits_a, index_a, logits_b, index_b, out_grad):
    rows, depth = attn_out.shape
    width = frozen_weight.shape[1]
    half = width // 2
    levels, sublen = vector_bank.shape
    rank, per_row, _ = logits_a.shape
    vectors = rank * per_row
    own = logits_b.shape[1] * sublen
    wide = levels // 2
    factor = adapter_scale / (rows * dp_size)
    columns = [v.transpose(1, 0, 2).reshape(vectors, 2) for v in (logits_a, logits_b, index_a, index_b)]
    table = jnp.concatenate([v.astype(jnp.float32) for v in columns], axis=1)
    bf16, f32 = jnp.bfloat16, jnp.float32
    dma = pltpu.SemaphoreType.DMA
    hbm = pl.BlockSpec(memory_space=pl.ANY)
    vmem = pl.BlockSpec(memory_space=pltpu.VMEM)
    layer_out, attn_grad, _, bank_grad, slopes = pl.pallas_call(
        functools.partial(exchange_kernel, factor),
        name="exchange",
        out_shape=(
            jax.ShapeDtypeStruct((rows, own), bf16),
            jax.ShapeDtypeStruct((rows, depth), bf16),
            jax.ShapeDtypeStruct((2, 2, depth, half), bf16),
            jax.ShapeDtypeStruct((levels, sublen), f32),
            jax.ShapeDtypeStruct((vectors, 4), f32),
        ),
        in_specs=[hbm, hbm, hbm, vmem, vmem],
        out_specs=(hbm, hbm, hbm, vmem, vmem),
        scratch_shapes=[
            pltpu.VMEM((8, depth, half), bf16),
            pltpu.VMEM((2, rows, depth), bf16),
            pltpu.VMEM((8, 2, rows, half), bf16),
            pltpu.VMEM((2, rows, depth), f32),
            pltpu.VMEM((8, 2, rows, half), bf16),
            pltpu.VMEM((4, 2, rows, half), bf16),
            pltpu.VMEM((rows, depth), bf16),
            pltpu.VMEM((rows, depth), bf16),
            pltpu.VMEM((2, 2, rows, half), f32),
            pltpu.VMEM((4, 2 * rank, rows), f32),
            pltpu.VMEM((rows, rank), bf16),
            pltpu.VMEM((rows, rank), bf16),
            pltpu.VMEM((rank, depth), bf16),
            pltpu.VMEM((rank, own), bf16),
            pltpu.VMEM((2, vectors, sublen), f32),
            pltpu.VMEM((2, vectors, levels), f32),
            pltpu.VMEM((wide, sublen + 128), f32),
            pltpu.VMEM((7, wide, sublen + 128), f32),
            dma((12,)), dma((8,)), dma((2, 8)), dma((2, 8)), dma((8,)),
            dma((8,)), dma((8,)), dma((8,)), dma((8,)),
            dma((2,)), dma((2,)), dma((3, 2)), dma((3, 2)), dma((1,)), dma((1,)),
            dma((3,)), dma((3,)),
            dma((8, 2)), dma((8, 2)), dma((4, 2)), dma((4, 2)), dma((4,)), dma((4,)),
            dma((4,)), dma((4,)), dma((8,)), dma((7,)), dma((7,)),
        ],
        compiler_params=pltpu.CompilerParams(
            collective_id=0, has_side_effects=True, vmem_limit_bytes=67043328
        ),
    )(attn_out, frozen_weight, out_grad, vector_bank, table)
    slopes = slopes.reshape(per_row, rank, 4).transpose(1, 0, 2)
    return (layer_out, attn_grad, bank_grad, slopes[..., :2], slopes[..., 2:])


def solution(mesh):
    dp_size, tensor_size = mesh.shape["dp"], mesh.shape["tensor"]
    paired = dp_size == 2 * tensor_size and tensor_size % 2 == 0
    body = functools.partial(ring_local, dp_size, tensor_size) if paired else local
    if paired and tensor_size == 4:
        body = functools.partial(fused_local, dp_size)
    return jax.shard_map(
        body,
        mesh=mesh,
        in_specs=(
            P("dp", "tensor"),
            P("tensor", "dp"),
            P(),
            P(None, "tensor", None),
            P(None, "tensor", None),
            P(None, "tensor", None),
            P(None, "tensor", None),
            P("dp", None),
        ),
        out_specs=(
            P("dp", "tensor"),
            P("dp", "tensor"),
            P(),
            P(None, "tensor", None),
            P(None, "tensor", None),
        ),
        check_vma=False,
    )
```

```python
import functools

import jax
import jax.numpy as jnp
from jax import lax
from jax.experimental import pallas as pl
from jax.experimental.pallas import tpu as pltpu
from jax.sharding import PartitionSpec as P

adapter_scale = 2.0
ROW_PIECES = 4


def compose(logits, indices, vector_bank):
    weights = jax.nn.sigmoid(logits - logits[..., ::-1])
    levels = jnp.arange(vector_bank.shape[0], dtype=jnp.int32)
    picked = (indices[..., None] == levels).astype(jnp.float32)
    mixing = jnp.sum(picked * weights[..., None], axis=2)
    blocks = jnp.einsum("rjb,bc->rjc", mixing, vector_bank, precision=lax.Precision.HIGHEST)
    return (weights, picked, mixing, blocks.reshape(blocks.shape[0], -1))


def compose_back(grad_rows, weights, picked, mixing, vector_bank):
    blocks = grad_rows.reshape(mixing.shape[0], mixing.shape[1], -1)
    bank_part = jnp.einsum("rjb,rjc->bc", mixing, blocks, precision=lax.Precision.HIGHEST)
    projected = jnp.einsum("rjc,bc->rjb", blocks, vector_bank, precision=lax.Precision.HIGHEST)
    dots = jnp.sum(picked * projected[:, :, None, :], axis=3)
    logit_grad = weights * (dots - jnp.sum(weights * dots, axis=2, keepdims=True))
    return (bank_part, logit_grad)


def local(attn_out, frozen_weight, vector_bank, logits_a, index_a, logits_b, index_b, out_grad):
    weights_a, picked_a, mixing_a, rows_a = compose(logits_a, index_a, vector_bank)
    weights_b, picked_b, mixing_b, rows_b = compose(logits_b, index_b, vector_bank)
    down_a = rows_a.astype(jnp.bfloat16)
    up_b = rows_b.astype(jnp.bfloat16)
    own_width = up_b.shape[1]
    grad_cols = lax.dynamic_slice_in_dim(
        out_grad, lax.axis_index("tensor") * own_width, own_width, 1
    )
    low_part = jnp.dot(attn_out, down_a.T, preferred_element_type=jnp.float32)
    back_part = jnp.dot(grad_cols, up_b.T, preferred_element_type=jnp.float32)
    low_total = lax.psum(low_part, "tensor")
    low_bf = low_total.astype(jnp.bfloat16)
    gathered = lax.all_gather(frozen_weight, "dp", axis=1, tiled=True)
    partial_value = jnp.dot(attn_out, gathered, preferred_element_type=jnp.float32).astype(
        jnp.bfloat16
    )
    summed = lax.psum_scatter(partial_value, "tensor", scatter_dimension=1, tiled=True).astype(
        jnp.float32
    )
    layer_out = (
        summed + adapter_scale * jnp.dot(low_bf, up_b, preferred_element_type=jnp.float32)
    ).astype(jnp.bfloat16)
    back_total = lax.psum(back_part, "tensor")
    back_bf = back_total.astype(jnp.bfloat16)
    main = lax.dot_general(
        out_grad, gathered, (((1,), (1,)), ((), ())), preferred_element_type=jnp.float32
    )
    attn_grad = (
        main + adapter_scale * jnp.dot(back_bf, down_a, preferred_element_type=jnp.float32)
    ).astype(jnp.bfloat16)
    factor = adapter_scale / (attn_out.shape[0] * lax.axis_size("dp"))
    grad_a = factor * lax.dot_general(
        back_bf, attn_out, (((0,), (0,)), ((), ())), preferred_element_type=jnp.float32
    )
    grad_b = factor * lax.dot_general(
        low_bf, grad_cols, (((0,), (0,)), ((), ())), preferred_element_type=jnp.float32
    )
    bank_a, logit_grad_a = compose_back(grad_a, weights_a, picked_a, mixing_a, vector_bank)
    bank_b, logit_grad_b = compose_back(grad_b, weights_b, picked_b, mixing_b, vector_bank)
    bank_part = bank_a + bank_b
    bank_group = lax.psum(bank_part, "tensor")
    bank_grad, logits_a_grad, logits_b_grad = lax.psum(
        (bank_group, logit_grad_a, logit_grad_b), "dp"
    )
    return (layer_out, attn_grad, bank_grad, logits_a_grad, logits_b_grad)


def ring_local(dp_size, tensor_size, attn_out, frozen_weight, vector_bank, logits_a, index_a, logits_b, index_b, out_grad):
    depth = tensor_size
    chips = tensor_size // 2
    rows = attn_out.shape[0]
    own_width = attn_out.shape[1]
    width = frozen_weight.shape[1]
    half = width // 2
    part = own_width // ROW_PIECES
    place = lax.axis_index("dp")
    level, side = place // 2, place % 2
    tensor_index = lax.axis_index("tensor")

    ring = [(d, (d + 2) % dp_size) for d in range(dp_size)]
    swap = [(d, d ^ 1) for d in range(dp_size)]

    def hop(value):
        return lax.ppermute(value, "dp", ring)

    def cross(value):
        return lax.ppermute(value, "dp", swap)

    def collect(partial_value, step):
        target = (level - step + depth) % depth
        pairs = []
        for d in range(dp_size):
            goal = (d // 2 - step) % depth
            for chip in range(chips):
                core = 2 * chip + goal % 2
                pairs.append((d * tensor_size + (core ^ 1), d * tensor_size + core))
        other = lax.ppermute(partial_value, ("dp", "tensor"), pairs)
        paired = partial_value.astype(jnp.float32) + other.astype(jnp.float32)
        sent = paired.astype(jnp.bfloat16)
        total = paired
        for k in range(1, chips):
            pairs = []
            for d in range(dp_size):
                goal = (d // 2 - step) % depth
                source = ((goal // 2 + k) % chips) * 2 + goal % 2
                pairs.append((d * tensor_size + source, d * tensor_size + goal))
            total = total + lax.ppermute(sent, ("dp", "tensor"), pairs).astype(jnp.float32)
        return jnp.where(tensor_index == target, total, 0.0)

    first = frozen_weight[:, :half]
    later = [frozen_weight[r * part : (r + 1) * part, half:] for r in range(ROW_PIECES)]
    held = [(first, later)]
    for step in range(1, depth):
        first = hop(first)
        later = [hop(v) for v in later]
        held.append((first, later))

    attn_two = jnp.concatenate([attn_out, cross(attn_out)], axis=0)
    attn_parts = [attn_two[:, r * part : (r + 1) * part] for r in range(ROW_PIECES)]

    def grad_pair(step):
        origin = (level - step + depth) % depth
        mine = lax.dynamic_slice_in_dim(out_grad, (origin * 2 + side) * width, width, 1)
        theirs = lax.dynamic_slice_in_dim(out_grad, (origin * 2 + 1 - side) * width, width, 1)
        return jnp.concatenate([mine, cross(theirs)], axis=0)

    weights_a, picked_a, mixing_a, rows_a = compose(logits_a, index_a, vector_bank)
    weights_b, picked_b, mixing_b, rows_b = compose(logits_b, index_b, vector_bank)
    down_a = rows_a.astype(jnp.bfloat16)
    up_b = rows_b.astype(jnp.bfloat16)
    rank = down_a.shape[0]
    grad_cols = lax.dynamic_slice_in_dim(out_grad, tensor_index * own_width, own_width, 1)
    low_part = jnp.dot(attn_out, down_a.T, preferred_element_type=jnp.float32)
    back_part = jnp.dot(grad_cols, up_b.T, preferred_element_type=jnp.float32)
    both = lax.psum(jnp.concatenate([low_part, back_part], axis=1), "tensor")
    low_bf = both[:, :rank].astype(jnp.bfloat16)
    back_bf = both[:, rank:].astype(jnp.bfloat16)

    sums = [None] * ROW_PIECES
    own_total = jnp.zeros((rows, width), jnp.float32)
    cross_total = jnp.zeros((rows, width), jnp.float32)
    for step in range(depth):
        first, later = held[step]
        grads = grad_pair(step)
        out_first = jnp.dot(attn_two, first, preferred_element_type=jnp.float32)
        for r in range(ROW_PIECES):
            term = lax.dot_general(
                grads[:, :half],
                first[r * part : (r + 1) * part],
                (((1,), (1,)), ((), ())),
                preferred_element_type=jnp.float32,
            )
            sums[r] = term if sums[r] is None else sums[r] + term
        out_later = None
        for r in range(ROW_PIECES):
            term = jnp.dot(attn_parts[r], later[r], preferred_element_type=jnp.float32)
            out_later = term if out_later is None else out_later + term
            sums[r] = sums[r] + lax.dot_general(
                grads[:, half:],
                later[r],
                (((1,), (1,)), ((), ())),
                preferred_element_type=jnp.float32,
            )
        out_first = out_first.astype(jnp.bfloat16)
        out_later = out_later.astype(jnp.bfloat16)
        if step < depth - 1:
            block = collect(jnp.concatenate([out_first, out_later], axis=1), step)
            own_total = own_total + block[:rows]
            cross_total = cross_total + block[rows:]
        if step == depth - 2:
            came = cross(cross_total.astype(jnp.bfloat16)).astype(jnp.float32)
        if step == depth - 1:
            ends = [collect(out_first, step), collect(out_later, step)]
            own_end = jnp.concatenate([v[:rows] for v in ends], axis=1)
            came_end = jnp.concatenate(
                [cross(v[rows:].astype(jnp.bfloat16)) for v in ends], axis=1
            ).astype(jnp.float32)
    own_half = own_total + own_end
    other_half = came + came_end
    summed = jnp.concatenate(
        [
            jnp.where(side == 0, own_half, other_half),
            jnp.where(side == 0, other_half, own_half),
        ],
        axis=1,
    )
    layer_out = (
        summed + adapter_scale * jnp.dot(low_bf, up_b, preferred_element_type=jnp.float32)
    ).astype(jnp.bfloat16)

    adapter = adapter_scale * jnp.dot(back_bf, down_a, preferred_element_type=jnp.float32)
    pieces = []
    for r in range(ROW_PIECES):
        came_grad = cross(sums[r][rows:].astype(jnp.bfloat16)).astype(jnp.float32)
        pieces.append(sums[r][:rows] + came_grad + adapter[:, r * part : (r + 1) * part])
    attn_grad = jnp.concatenate(pieces, axis=1).astype(jnp.bfloat16)

    factor = adapter_scale / (rows * dp_size)
    grad_a = factor * lax.dot_general(
        back_bf, attn_out, (((0,), (0,)), ((), ())), preferred_element_type=jnp.float32
    )
    grad_b = factor * lax.dot_general(
        low_bf, grad_cols, (((0,), (0,)), ((), ())), preferred_element_type=jnp.float32
    )
    bank_a, logit_grad_a = compose_back(grad_a, weights_a, picked_a, mixing_a, vector_bank)
    bank_b, logit_grad_b = compose_back(grad_b, weights_b, picked_b, mixing_b, vector_bank)
    bank_grad = lax.psum(bank_a + bank_b, ("dp", "tensor"))
    logits_a_grad, logits_b_grad = lax.psum((logit_grad_a, logit_grad_b), "dp")
    return (layer_out, attn_grad, bank_grad, logits_a_grad, logits_b_grad)


MESH_ID = pl.DeviceIdType.MESH
PIECES = 8


def dot_nn(a, b):
    return jnp.dot(a, b, preferred_element_type=jnp.float32)


def dot_nt(a, b):
    return lax.dot_general(a, b, (((1,), (1,)), ((), ())), preferred_element_type=jnp.float32)


def exchange_kernel(
    factor,
    attn, weight, grad, bank, logits_a, index_a, logits_b, index_b,
    out_hbm, agrad_hbm, relay, bank_out, slope_a, slope_b,
    wbuf, abuf, gbuf, dacc, cbuf, ybuf, dsend, drecv, cacc, lb, low, back,
    down, up, mixing, sums, came,
    load_sem, zs_send, relay_recv, relay_send, far_recv, xs_send, x_recv, xf_send, xf_recv,
    g_send, g_recv, gm_send, gm_recv, a_send, a_recv, lb_send, lb_recv,
    c_send, c_recv, y_send, y_recv, zc_send, zc_recv, d_send, d_recv, out_sem,
    sum_send, sum_recv,
):
    rows, depth = attn.shape
    width = weight.shape[1]
    half = width // 2
    step = depth // PIECES
    tile = rows // 2
    rank = down.shape[0]
    own = up.shape[1]

    dp, t = lax.axis_index("dp"), lax.axis_index("tensor")
    z, x = dp // 2, dp % 2
    y, c = t // 2, t % 2
    zh, zl = z // 2, z % 2
    inner = (z == 1) | (z == 2)
    pz = zh * 2 + (1 - zl)
    mz = jnp.where(z == 1, 2, 1)
    x_dev = (z * 2 + (1 - x), t)
    p_dev = (pz * 2 + x, t)
    m_dev = (mz * 2 + x, t)
    c_dev = (dp, y * 2 + (1 - c))
    y_dev = (dp, (1 - y) * 2 + c)
    reduces = c == zl

    def remote(src, dst, send, recv, device):
        return pltpu.make_async_remote_copy(
            src_ref=src, dst_ref=dst, send_sem=send, recv_sem=recv,
            device_id=device, device_id_type=MESH_ID,
        )

    def rowsof(p):
        return pl.ds(pl.multiple_of(p * step, step), step)

    barrier = pltpu.get_barrier_semaphore()
    others = [(dp, (t + k) % 4) for k in (1, 2, 3)]
    for device in others + [x_dev, p_dev]:
        pl.semaphore_signal(barrier, inc=1, device_id=device, device_id_type=MESH_ID)

    @pl.when(inner)
    def _():
        pl.semaphore_signal(barrier, inc=1, device_id=m_dev, device_id_type=MESH_ID)

    def column_block(zz, b, xx):
        zb = jnp.where(b < 2, zz, (zz + 2) % 4)
        xb = jnp.where(b % 2 == 0, xx, 1 - xx)
        return zb * 2 + xb

    loads = [pltpu.make_async_copy(attn, abuf.at[0], load_sem.at[0])]
    gq = pltpu.make_async_copy(
        grad.at[:, pl.ds(pl.multiple_of(t * own, own), own)], dsend.at[:, pl.ds(0, own)], load_sem.at[1]
    )
    loads.append(gq)
    for n in range(2):
        loads.append(
            pltpu.make_async_copy(weight.at[:, pl.ds(n * half, half)], wbuf.at[n], load_sem.at[2 + n])
        )
    for s in range(8):
        col = column_block(z, s // 2, x) * width + (s % 2) * half
        loads.append(
            pltpu.make_async_copy(
                grad.at[:, pl.ds(pl.multiple_of(col, half), half)], gbuf.at[s, 0], load_sem.at[4 + s]
            )
        )
    for load in loads:
        load.start()

    @pl.when(inner)
    def _():
        pl.semaphore_wait(barrier, 6)

    @pl.when(jnp.logical_not(inner))
    def _():
        pl.semaphore_wait(barrier, 5)

    def x_own(i):
        n, p = i // PIECES, i % PIECES
        return remote(
            weight.at[rowsof(p), pl.ds(pl.multiple_of(n * half, half), half)],
            wbuf.at[2 + n, rowsof(p)], xs_send.at[i], x_recv.at[i], x_dev,
        )

    def z_own(i):
        n, p = i // PIECES, i % PIECES
        stream = jnp.where(inner, 0, 1)
        device = (jnp.where(inner, mz, pz) * 2 + x, t)
        return remote(
            weight.at[rowsof(p), pl.ds(pl.multiple_of(n * half, half), half)],
            relay.at[stream, n, rowsof(p)], zs_send.at[i], relay_recv.at[stream, i], device,
        )

    def g_own(n):
        col = column_block(pz, t, x) * width + n * half
        return remote(
            grad.at[:, pl.ds(pl.multiple_of(col, half), half)],
            gbuf.at[2 * t + n, 1], g_send.at[n], g_recv.at[n], p_dev,
        )

    a_own = remote(attn, abuf.at[1], a_send.at[0], a_recv.at[0], p_dev)

    for n in range(2):
        g_own(n).start()
    a_own.start()

    @pl.loop(0, PIECES)
    def _(i):
        x_own(i).start()

    @pl.when(inner)
    def _():
        @pl.loop(0, 2 * PIECES)
        def _(i):
            z_own(i).start()

    levels = bank.shape[0]
    sublen = bank.shape[1]
    vectors = mixing.shape[2]
    per_row = vectors // rank
    exact = dict(preferred_element_type=jnp.float32, precision=lax.Precision.HIGHEST)

    place = lax.broadcasted_iota(jnp.int32, (rank, vectors), 1)
    spread = (place % rank == lax.broadcasted_iota(jnp.int32, (rank, vectors), 0)).astype(jnp.float32)
    place = lax.broadcasted_iota(jnp.int32, (per_row, vectors), 1)
    keep = place // rank == lax.broadcasted_iota(jnp.int32, (per_row, vectors), 0)
    level = lax.broadcasted_iota(jnp.int32, (levels, vectors), 0)

    def as_row(value):
        wide_value = jnp.dot(value.astype(jnp.float32), spread, **exact)
        return jnp.sum(jnp.where(keep, wide_value, 0.0), axis=0, keepdims=True)

    def from_row(row):
        return lax.dot_general(jnp.where(keep, row, 0.0), spread, (((1,), (1,)), ((), ())), **exact)

    shares, found = [], []
    for k, (logits, indices) in enumerate(((logits_a, index_a), (logits_b, index_b))):
        first, second = as_row(logits[:, 0, :]), as_row(logits[:, 1, :])
        shares.append((1.0 / (1.0 + jnp.exp(second - first)), 1.0 / (1.0 + jnp.exp(first - second))))
        picks = [(as_row(indices[:, m, :]) + 0.5).astype(jnp.int32) for m in range(2)]
        found.append([level == pick for pick in picks])

    for k, target in enumerate((down, up)):
        mixing[k] = sum(jnp.where(found[k][m], shares[k][m], 0.0) for m in range(2))
        blocks = lax.dot_general(mixing[k], bank[...], (((0,), (0,)), ((), ())), **exact)
        for j in range(per_row):
            row = blocks[j * rank : (j + 1) * rank]
            target[:, j * sublen : (j + 1) * sublen] = row.astype(jnp.bfloat16)

    loads[0].wait()
    loads[1].wait()
    lb[t, :rank] = dot_nt(down[...], abuf[0])
    lb[t, rank:] = dot_nt(up[...], dsend[:, :own])

    def lb_copy(k):
        device = (dp, (t + k) % 4)
        return remote(lb.at[t], lb.at[t], lb_send.at[k - 1], lb_recv.at[k - 1], device)

    for k in (1, 2, 3):
        lb_copy(k).start()
    for load in loads[2:]:
        load.wait()
    dacc[...] = jnp.zeros_like(dacc)
    for k in (1, 2, 3):
        lb_copy(k).wait()
    both = lb[0] + lb[1] + lb[2] + lb[3]
    low[...] = both[:rank].T.astype(jnp.bfloat16)
    back[...] = both[rank:].T.astype(jnp.bfloat16)
    both = both.astype(jnp.bfloat16)
    slopes = (
        factor * dot_nn(both[rank:], abuf[0]),
        factor * dot_nn(both[:rank], dsend[:, :own]),
    )
    wide = levels // 2
    bank_out[...] = jnp.zeros_like(bank_out)
    dots = []
    for k in range(2):
        pieces = [slopes[k][:, j * sublen : (j + 1) * sublen] for j in range(per_row)]
        stacked = jnp.concatenate(pieces, axis=0)
        bank_out[...] += jnp.dot(mixing[k], stacked, **exact)
        projected = lax.dot_general(bank[...], stacked, (((1,), (1,)), ((), ())), **exact)
        for m in range(2):
            dots.append(jnp.sum(jnp.where(found[k][m], projected, 0.0), axis=0, keepdims=True))

    own_half = pl.ds(pl.multiple_of(c * wide, wide), wide)
    other_half = pl.ds(pl.multiple_of((1 - c) * wide, wide), wide)

    def sum_copy(k, device, count):
        return remote(
            sums.at[pl.ds(0, count)], came.at[k, pl.ds(0, count)],
            sum_send.at[k], sum_recv.at[k], device,
        )

    full = sums.shape[0]
    sums[:wide] = bank_out[other_half]
    core_sum = sum_copy(0, c_dev, wide)
    y_sum = sum_copy(1, y_dev, wide)
    x_sum = sum_copy(2, x_dev, full)
    p_sum = sum_copy(3, p_dev, full)
    m_sum = sum_copy(4, m_dev, full)
    out_sum = sum_copy(5, p_dev, full)
    last_sum = sum_copy(6, c_dev, wide)
    core_sum.start()
    core_sum.wait()
    sums[:wide] = bank_out[own_half] + came[0, :wide]
    y_sum.start()
    y_sum.wait()
    sums[:wide] += came[1, :wide]
    sums[wide:] = jnp.zeros_like(sums[wide:])
    for k in range(4):
        sums[wide + k : wide + k + 1, :vectors] = dots[k]
    x_sum.start()

    @pl.loop(PIECES, 2 * PIECES)
    def _(i):
        x_own(i).start()

    def relay_on(stream, i):
        n, p = i // PIECES, i % PIECES
        device = (jnp.where(stream == 0, pz, mz) * 2 + x, t)
        return remote(
            relay.at[stream, n, rowsof(p)], wbuf.at[4 + n, rowsof(p)],
            relay_send.at[stream, i], far_recv.at[i], device,
        )

    def relay_wait(stream, i):
        n, p = i // PIECES, i % PIECES
        piece = relay.at[stream, n, rowsof(p)]
        remote(piece, piece, relay_send.at[stream, i], relay_recv.at[stream, i], p_dev).wait_recv()

    def x_far(i):
        n, p = i // PIECES, i % PIECES
        return remote(
            wbuf.at[4 + n, rowsof(p)], wbuf.at[6 + n, rowsof(p)], xf_send.at[i], xf_recv.at[i], x_dev
        )

    def far_wait(i):
        n, p = i // PIECES, i % PIECES
        piece = wbuf.at[4 + n, rowsof(p)]
        remote(piece, piece, xf_send.at[i], far_recv.at[i], x_dev).wait_recv()

    def g_spread(k, n):
        piece = gbuf.at[2 * t + n, 1]
        return remote(piece, piece, gm_send.at[k - 1, n], gm_recv.at[k - 1, n], (dp, (t + k) % 4))

    lag = jnp.where(inner, 17, 13)
    late = 12
    total = 2 * PIECES

    def tick(i, carry):
        @pl.when(i < total)
        def _():
            x_own(i).wait_recv()

            @pl.when(inner)
            def _():
                relay_wait(0, i)

                @pl.when(i > PIECES)
                def _():
                    relay_on(0, i).start()

        @pl.when(i == PIECES)
        def _():
            x_sum.wait()
            sums[...] += came[2]
            p_sum.start()

            @pl.when(jnp.logical_not(inner))
            def _():
                @pl.loop(0, total)
                def _(k):
                    z_own(k).start()

            @pl.when(inner)
            def _():
                @pl.loop(0, PIECES + 1)
                def _(k):
                    relay_on(0, k).start()

        @pl.when(i == late)
        def _():
            p_sum.wait()
            sums[...] += came[3]

            @pl.when(inner)
            def _():
                m_sum.start()

        @pl.when((i == 17) & inner)
        def _():
            m_sum.wait()
            sums[...] += came[4]
            out_sum.start()

        @pl.when(i == 4)
        def _():
            for n in range(2):
                g_own(n).wait_recv()
                for k in (1, 2, 3):
                    g_spread(k, n).start()

        @pl.when((i >= late) & (i < late + total) & inner)
        def _():
            relay_wait(1, i - late)
            relay_on(1, i - late).start()

        @pl.when((i >= lag) & (i < lag + total))
        def _():
            far_wait(i - lag)
            x_far(i - lag).start()

        return carry

    def c_copy(s, r):
        return remote(cbuf.at[s, r], cbuf.at[s, r], c_send.at[s, r], c_recv.at[s, r], c_dev)

    def y_copy(s, r):
        return remote(cbuf.at[s, r], ybuf.at[s % 4, r], y_send.at[s % 4, r], y_recv.at[s % 4, r], y_dev)

    def z_copy(s):
        return remote(cbuf.at[s, 1], ybuf.at[s % 4, 0], zc_send.at[s % 4], zc_recv.at[s % 4], p_dev)

    def kept(s):
        return jnp.where(s < 4, zh, 1 - zh) == y

    def out_columns(j):
        xb = jnp.where(j < 2, x, 1 - x)
        return pl.ds(pl.multiple_of(xb * width + (j % 2) * half, half), half)

    def out_copy(j):
        return pltpu.make_async_copy(ybuf.at[j, 0], out_hbm.at[:, out_columns(j)], out_sem.at[j])

    def adapter_out(j):
        return 2.0 * dot_nn(low[...], up[:, out_columns(j)])

    def pass_core(s, r, partial):
        @pl.when(jnp.logical_not(reduces))
        def _():
            cbuf[s, r] = partial[...].astype(jnp.bfloat16)
            c_copy(s, r).start()

    def sum_core(s, r, partial):
        @pl.when(reduces)
        def _():
            c_copy(s, r).wait_recv()
            cbuf[s, r] = (partial[...] + cbuf[s, r].astype(jnp.float32)).astype(jnp.bfloat16)

            @pl.when(jnp.logical_not(kept(s)))
            def _():
                y_copy(s, r).start()

    def sum_y(s, r):
        @pl.when(reduces & kept(s))
        def _():
            j = s % 4
            y_copy(s, r).wait_recv()
            total = cbuf[s, r].astype(jnp.float32) + ybuf[j, r].astype(jnp.float32)

            @pl.when(r == 0)
            def _():
                ybuf[j, 0] = (total + adapter_out(j)).astype(jnp.bfloat16)
                out_copy(j).start()

            @pl.when(r == 1)
            def _():
                cbuf[s, 1] = total.astype(jnp.bfloat16)
                z_copy(s).start()

    def finish_other(j):
        @pl.when(jnp.logical_not(reduces))
        def _():
            z_copy(j).wait_recv()
            ybuf[j, 0] = (ybuf[j, 0].astype(jnp.float32) + adapter_out(j)).astype(jnp.bfloat16)
            out_copy(j).start()

    slots = (0, 1, 2, 0, 1, 2, 3, 3, 4, 4, 6, 6)
    sides = (0, 0, 0, 1, 1, 1, 0, 1, 0, 1, 0, 1)

    def pick(table, u):
        if isinstance(u, int):
            return table[u]
        value = table[0]
        for k in range(1, len(table)):
            if table[k] != table[k - 1]:
                value = jnp.where(u >= k, table[k], value)
        return value

    def ready(u):
        value = jnp.where(u >= 2, PIECES, 0)
        value = jnp.where(u >= 3, 12, value)
        value = jnp.where(u >= 6, total, value)
        value = jnp.where(u >= 8, lag + PIECES, value)
        return jnp.where(u >= 10, lag + PIECES + 2, value)

    def unit(u, carry):
        s, r = pick(slots, u), pick(sides, u)
        lax.fori_loop(ready(u - 1), ready(u), tick, 0)

        @pl.when(u == 3)
        def _():
            a_own.wait_recv()
            for n in range(2):
                for k in (1, 2, 3):
                    g_spread(k, n).wait_recv()

        @pl.when(u == 10)
        def _():
            for p in range(PIECES):
                x_far(p).wait_recv()

        partial = cacc.at[0, u % 2]
        for m in range(2):
            part = pl.ds(m * tile, tile)
            partial[part] = dot_nn(abuf[r, part], wbuf[s])
            dacc[r, part] += dot_nt(gbuf[s, r, part], wbuf[s])
        pass_core(s, r, partial)

        @pl.when(u >= 1)
        def _():
            sum_core(pick(slots, u - 1), pick(sides, u - 1), cacc.at[0, (u - 1) % 2])

        @pl.when(u >= 4)
        def _():
            sum_y(pick(slots, u - 4), pick(sides, u - 4))

        return carry

    lax.fori_loop(0, 12, unit, 0)
    sum_core(slots[11], sides[11], cacc.at[0, 1])
    cacc[...] = jnp.zeros_like(cacc)

    def d_copy(p):
        columns = pl.ds(pl.multiple_of(p * step, step), step)
        return remote(dsend.at[:, columns], drecv.at[:, columns], d_send.at[p], d_recv.at[p], p_dev)

    def last_piece(p, carry):
        done = lag + PIECES + 2 + p
        lax.fori_loop(jnp.minimum(done, lag + total), jnp.minimum(done + 1, lag + total), tick, 0)
        x_far(PIECES + p).wait_recv()
        columns = rowsof(p)
        for q in range(2):
            r = 1 - q
            for m in range(2):
                part = pl.ds(m * tile, tile)
                grown = dacc[r, part, columns]
                grown += dot_nt(gbuf[5, r, part], wbuf[5, columns])
                grown += dot_nt(gbuf[7, r, part], wbuf[7, columns])
                if r == 1:
                    dsend[part, columns] = grown.astype(jnp.bfloat16)
                else:
                    dacc[0, part, columns] = grown
            if r == 1:
                d_copy(p).start()
        for k in range(2):
            for r in range(2):
                cacc[k, r] += dot_nn(abuf[r, :, columns], wbuf[5 + 2 * k, columns])

        @pl.when(p == 1)
        def _():
            @pl.when(inner)
            def _():
                out_sum.wait_send()

            @pl.when(jnp.logical_not(inner))
            def _():
                out_sum.wait_recv()
                sums[...] = came[5]

            last_sum.start()

        @pl.when((p >= 1) & (p < 5))
        def _():
            sum_y(pick(slots, 7 + p), (p - 1) % 2)

        return carry

    lax.fori_loop(0, PIECES, last_piece, 0)

    def agrad_copy(p):
        columns = pl.ds(pl.multiple_of(p * step, step), step)
        return pltpu.make_async_copy(drecv.at[:, columns], agrad_hbm.at[:, columns], out_sem.at[4 + p])

    def finish_grad(p, carry):
        columns = pl.ds(pl.multiple_of(p * step, step), step)
        d_copy(p).wait_recv()
        total = dacc[0, :, columns] + drecv[:, columns].astype(jnp.float32)
        drecv[:, columns] = (total + 2.0 * dot_nn(back[...], down[:, columns])).astype(jnp.bfloat16)
        agrad_copy(p).start()
        return carry

    final = ((5, 1), (7, 1), (5, 0), (7, 0))
    for slot, side in final:
        pass_core(slot, side, cacc.at[(slot - 5) // 2, side])
    last_sum.wait()
    bank_out[own_half] = sums[:wide]
    bank_out[other_half] = came[6, :wide]
    for k, target in enumerate((slope_a, slope_b)):
        values = [sums[wide + 2 * k + m : wide + 2 * k + m + 1, :vectors] for m in range(2)]
        mean = shares[k][0] * values[0] + shares[k][1] * values[1]
        for m in range(2):
            target[:, m, :] = from_row(shares[k][m] * (values[m] - mean))
    for slot, side in final:
        sum_core(slot, side, cacc.at[(slot - 5) // 2, side])
    lax.fori_loop(0, PIECES, finish_grad, 0)
    for slot, side in final:
        sum_y(slot, side)
    for j in (0, 2, 1, 3):
        finish_other(j)
    a_own.wait_send()
    for n in range(2):
        g_own(n).wait_send()
        for k in (1, 2, 3):
            g_spread(k, n).wait_send()

    @pl.loop(0, total)
    def _(i):
        x_own(i).wait_send()
        z_own(i).wait_send()
        x_far(i).wait_send()

        @pl.when(inner)
        def _():
            relay_on(0, i).wait_send()
            relay_on(1, i).wait_send()

    @pl.loop(0, 8)
    def _(i):
        @pl.when(jnp.logical_not(reduces))
        def _():
            for r in range(2):
                c_copy(i, r).wait_send()

        @pl.when(reduces & jnp.logical_not(kept(i)))
        def _():
            for r in range(2):
                y_copy(i, r).wait_send()

        @pl.when(reduces & kept(i))
        def _():
            z_copy(i).wait_send()

    @pl.loop(0, PIECES)
    def _(p):
        d_copy(p).wait_send()
        agrad_copy(p).wait()

    @pl.loop(0, 4)
    def _(j):
        out_copy(j).wait()


def fused_local(dp_size, attn_out, frozen_weight, vector_bank, logits_a, index_a, logits_b, index_b, out_grad):
    rows, depth = attn_out.shape
    width = frozen_weight.shape[1]
    half = width // 2
    levels, sublen = vector_bank.shape
    rank, per_row, _ = logits_a.shape
    vectors = rank * per_row
    own = logits_b.shape[1] * sublen
    wide = levels // 2
    factor = adapter_scale / (rows * dp_size)
    total = 2 * PIECES
    small = [v.transpose(1, 2, 0) for v in (logits_a, index_a, logits_b, index_b)]
    bf16, f32 = jnp.bfloat16, jnp.float32
    dma = pltpu.SemaphoreType.DMA
    hbm = pl.BlockSpec(memory_space=pl.ANY)
    vmem = pl.BlockSpec(memory_space=pltpu.VMEM)
    layer_out, attn_grad, _, bank_grad, slope_a, slope_b = pl.pallas_call(
        functools.partial(exchange_kernel, factor),
        name="exchange",
        out_shape=(
            jax.ShapeDtypeStruct((rows, own), bf16),
            jax.ShapeDtypeStruct((rows, depth), bf16),
            jax.ShapeDtypeStruct((2, 2, depth, half), bf16),
            jax.ShapeDtypeStruct((levels, sublen), f32),
            jax.ShapeDtypeStruct((per_row, 2, rank), f32),
            jax.ShapeDtypeStruct((per_row, 2, rank), f32),
        ),
        in_specs=[hbm, hbm, hbm, vmem, vmem, vmem, vmem, vmem],
        out_specs=(hbm, hbm, hbm, vmem, vmem, vmem),
        scratch_shapes=[
            pltpu.VMEM((8, depth, half), bf16),
            pltpu.VMEM((2, rows, depth), bf16),
            pltpu.VMEM((8, 2, rows, half), bf16),
            pltpu.VMEM((2, rows, depth), f32),
            pltpu.VMEM((8, 2, rows, half), bf16),
            pltpu.VMEM((4, 2, rows, half), bf16),
            pltpu.VMEM((rows, depth), bf16),
            pltpu.VMEM((rows, depth), bf16),
            pltpu.VMEM((2, 2, rows, half), f32),
            pltpu.VMEM((4, 2 * rank, rows), f32),
            pltpu.VMEM((rows, rank), bf16),
            pltpu.VMEM((rows, rank), bf16),
            pltpu.VMEM((rank, depth), bf16),
            pltpu.VMEM((rank, own), bf16),
            pltpu.VMEM((2, levels, vectors), f32),
            pltpu.VMEM((wide + 8, sublen), f32),
            pltpu.VMEM((7, wide + 8, sublen), f32),
            dma((12,)), dma((total,)), dma((2, total)), dma((2, total)), dma((total,)),
            dma((total,)), dma((total,)), dma((total,)), dma((total,)),
            dma((2,)), dma((2,)), dma((3, 2)), dma((3, 2)), dma((1,)), dma((1,)),
            dma((3,)), dma((3,)),
            dma((8, 2)), dma((8, 2)), dma((4, 2)), dma((4, 2)), dma((4,)), dma((4,)),
            dma((PIECES,)), dma((PIECES,)), dma((4 + PIECES,)), dma((7,)), dma((7,)),
        ],
        compiler_params=pltpu.CompilerParams(
            collective_id=0, has_side_effects=True, vmem_limit_bytes=67043328
        ),
    )(attn_out, frozen_weight, out_grad, vector_bank, *small)
    return (layer_out, attn_grad, bank_grad, slope_a.transpose(2, 0, 1), slope_b.transpose(2, 0, 1))


def solution(mesh):
    dp_size, tensor_size = mesh.shape["dp"], mesh.shape["tensor"]
    paired = dp_size == 2 * tensor_size and tensor_size % 2 == 0
    body = functools.partial(ring_local, dp_size, tensor_size) if paired else local
    if paired and tensor_size == 4:
        body = functools.partial(fused_local, dp_size)
    return jax.shard_map(
        body,
        mesh=mesh,
        in_specs=(
            P("dp", "tensor"),
            P("tensor", "dp"),
            P(),
            P(None, "tensor", None),
            P(None, "tensor", None),
            P(None, "tensor", None),
            P(None, "tensor", None),
            P("dp", None),
        ),
        out_specs=(
            P("dp", "tensor"),
            P("dp", "tensor"),
            P(),
            P(None, "tensor", None),
            P(None, "tensor", None),
        ),
        check_vma=False,
    )
```

```python
import functools

import jax
import jax.numpy as jnp
from jax import lax
from jax.experimental import pallas as pl
from jax.experimental.pallas import tpu as pltpu
from jax.sharding import PartitionSpec as P

adapter_scale = 2.0
ROW_PIECES = 4


def compose(logits, indices, vector_bank):
    weights = jax.nn.sigmoid(logits - logits[..., ::-1])
    levels = jnp.arange(vector_bank.shape[0], dtype=jnp.int32)
    picked = (indices[..., None] == levels).astype(jnp.float32)
    mixing = jnp.sum(picked * weights[..., None], axis=2)
    blocks = jnp.einsum("rjb,bc->rjc", mixing, vector_bank, precision=lax.Precision.HIGHEST)
    return (weights, picked, mixing, blocks.reshape(blocks.shape[0], -1))


def compose_back(grad_rows, weights, picked, mixing, vector_bank):
    blocks = grad_rows.reshape(mixing.shape[0], mixing.shape[1], -1)
    bank_part = jnp.einsum("rjb,rjc->bc", mixing, blocks, precision=lax.Precision.HIGHEST)
    projected = jnp.einsum("rjc,bc->rjb", blocks, vector_bank, precision=lax.Precision.HIGHEST)
    dots = jnp.sum(picked * projected[:, :, None, :], axis=3)
    logit_grad = weights * (dots - jnp.sum(weights * dots, axis=2, keepdims=True))
    return (bank_part, logit_grad)


def local(attn_out, frozen_weight, vector_bank, logits_a, index_a, logits_b, index_b, out_grad):
    weights_a, picked_a, mixing_a, rows_a = compose(logits_a, index_a, vector_bank)
    weights_b, picked_b, mixing_b, rows_b = compose(logits_b, index_b, vector_bank)
    down_a = rows_a.astype(jnp.bfloat16)
    up_b = rows_b.astype(jnp.bfloat16)
    own_width = up_b.shape[1]
    grad_cols = lax.dynamic_slice_in_dim(
        out_grad, lax.axis_index("tensor") * own_width, own_width, 1
    )
    low_part = jnp.dot(attn_out, down_a.T, preferred_element_type=jnp.float32)
    back_part = jnp.dot(grad_cols, up_b.T, preferred_element_type=jnp.float32)
    low_total = lax.psum(low_part, "tensor")
    low_bf = low_total.astype(jnp.bfloat16)
    gathered = lax.all_gather(frozen_weight, "dp", axis=1, tiled=True)
    partial_value = jnp.dot(attn_out, gathered, preferred_element_type=jnp.float32).astype(
        jnp.bfloat16
    )
    summed = lax.psum_scatter(partial_value, "tensor", scatter_dimension=1, tiled=True).astype(
        jnp.float32
    )
    layer_out = (
        summed + adapter_scale * jnp.dot(low_bf, up_b, preferred_element_type=jnp.float32)
    ).astype(jnp.bfloat16)
    back_total = lax.psum(back_part, "tensor")
    back_bf = back_total.astype(jnp.bfloat16)
    main = lax.dot_general(
        out_grad, gathered, (((1,), (1,)), ((), ())), preferred_element_type=jnp.float32
    )
    attn_grad = (
        main + adapter_scale * jnp.dot(back_bf, down_a, preferred_element_type=jnp.float32)
    ).astype(jnp.bfloat16)
    factor = adapter_scale / (attn_out.shape[0] * lax.axis_size("dp"))
    grad_a = factor * lax.dot_general(
        back_bf, attn_out, (((0,), (0,)), ((), ())), preferred_element_type=jnp.float32
    )
    grad_b = factor * lax.dot_general(
        low_bf, grad_cols, (((0,), (0,)), ((), ())), preferred_element_type=jnp.float32
    )
    bank_a, logit_grad_a = compose_back(grad_a, weights_a, picked_a, mixing_a, vector_bank)
    bank_b, logit_grad_b = compose_back(grad_b, weights_b, picked_b, mixing_b, vector_bank)
    bank_part = bank_a + bank_b
    bank_group = lax.psum(bank_part, "tensor")
    bank_grad, logits_a_grad, logits_b_grad = lax.psum(
        (bank_group, logit_grad_a, logit_grad_b), "dp"
    )
    return (layer_out, attn_grad, bank_grad, logits_a_grad, logits_b_grad)


def ring_local(dp_size, tensor_size, attn_out, frozen_weight, vector_bank, logits_a, index_a, logits_b, index_b, out_grad):
    depth = tensor_size
    chips = tensor_size // 2
    rows = attn_out.shape[0]
    own_width = attn_out.shape[1]
    width = frozen_weight.shape[1]
    half = width // 2
    part = own_width // ROW_PIECES
    place = lax.axis_index("dp")
    level, side = place // 2, place % 2
    tensor_index = lax.axis_index("tensor")

    ring = [(d, (d + 2) % dp_size) for d in range(dp_size)]
    swap = [(d, d ^ 1) for d in range(dp_size)]

    def hop(value):
        return lax.ppermute(value, "dp", ring)

    def cross(value):
        return lax.ppermute(value, "dp", swap)

    def collect(partial_value, step):
        target = (level - step + depth) % depth
        pairs = []
        for d in range(dp_size):
            goal = (d // 2 - step) % depth
            for chip in range(chips):
                core = 2 * chip + goal % 2
                pairs.append((d * tensor_size + (core ^ 1), d * tensor_size + core))
        other = lax.ppermute(partial_value, ("dp", "tensor"), pairs)
        paired = partial_value.astype(jnp.float32) + other.astype(jnp.float32)
        sent = paired.astype(jnp.bfloat16)
        total = paired
        for k in range(1, chips):
            pairs = []
            for d in range(dp_size):
                goal = (d // 2 - step) % depth
                source = ((goal // 2 + k) % chips) * 2 + goal % 2
                pairs.append((d * tensor_size + source, d * tensor_size + goal))
            total = total + lax.ppermute(sent, ("dp", "tensor"), pairs).astype(jnp.float32)
        return jnp.where(tensor_index == target, total, 0.0)

    first = frozen_weight[:, :half]
    later = [frozen_weight[r * part : (r + 1) * part, half:] for r in range(ROW_PIECES)]
    held = [(first, later)]
    for step in range(1, depth):
        first = hop(first)
        later = [hop(v) for v in later]
        held.append((first, later))

    attn_two = jnp.concatenate([attn_out, cross(attn_out)], axis=0)
    attn_parts = [attn_two[:, r * part : (r + 1) * part] for r in range(ROW_PIECES)]

    def grad_pair(step):
        origin = (level - step + depth) % depth
        mine = lax.dynamic_slice_in_dim(out_grad, (origin * 2 + side) * width, width, 1)
        theirs = lax.dynamic_slice_in_dim(out_grad, (origin * 2 + 1 - side) * width, width, 1)
        return jnp.concatenate([mine, cross(theirs)], axis=0)

    weights_a, picked_a, mixing_a, rows_a = compose(logits_a, index_a, vector_bank)
    weights_b, picked_b, mixing_b, rows_b = compose(logits_b, index_b, vector_bank)
    down_a = rows_a.astype(jnp.bfloat16)
    up_b = rows_b.astype(jnp.bfloat16)
    rank = down_a.shape[0]
    grad_cols = lax.dynamic_slice_in_dim(out_grad, tensor_index * own_width, own_width, 1)
    low_part = jnp.dot(attn_out, down_a.T, preferred_element_type=jnp.float32)
    back_part = jnp.dot(grad_cols, up_b.T, preferred_element_type=jnp.float32)
    both = lax.psum(jnp.concatenate([low_part, back_part], axis=1), "tensor")
    low_bf = both[:, :rank].astype(jnp.bfloat16)
    back_bf = both[:, rank:].astype(jnp.bfloat16)

    sums = [None] * ROW_PIECES
    own_total = jnp.zeros((rows, width), jnp.float32)
    cross_total = jnp.zeros((rows, width), jnp.float32)
    for step in range(depth):
        first, later = held[step]
        grads = grad_pair(step)
        out_first = jnp.dot(attn_two, first, preferred_element_type=jnp.float32)
        for r in range(ROW_PIECES):
            term = lax.dot_general(
                grads[:, :half],
                first[r * part : (r + 1) * part],
                (((1,), (1,)), ((), ())),
                preferred_element_type=jnp.float32,
            )
            sums[r] = term if sums[r] is None else sums[r] + term
        out_later = None
        for r in range(ROW_PIECES):
            term = jnp.dot(attn_parts[r], later[r], preferred_element_type=jnp.float32)
            out_later = term if out_later is None else out_later + term
            sums[r] = sums[r] + lax.dot_general(
                grads[:, half:],
                later[r],
                (((1,), (1,)), ((), ())),
                preferred_element_type=jnp.float32,
            )
        out_first = out_first.astype(jnp.bfloat16)
        out_later = out_later.astype(jnp.bfloat16)
        if step < depth - 1:
            block = collect(jnp.concatenate([out_first, out_later], axis=1), step)
            own_total = own_total + block[:rows]
            cross_total = cross_total + block[rows:]
        if step == depth - 2:
            came = cross(cross_total.astype(jnp.bfloat16)).astype(jnp.float32)
        if step == depth - 1:
            ends = [collect(out_first, step), collect(out_later, step)]
            own_end = jnp.concatenate([v[:rows] for v in ends], axis=1)
            came_end = jnp.concatenate(
                [cross(v[rows:].astype(jnp.bfloat16)) for v in ends], axis=1
            ).astype(jnp.float32)
    own_half = own_total + own_end
    other_half = came + came_end
    summed = jnp.concatenate(
        [
            jnp.where(side == 0, own_half, other_half),
            jnp.where(side == 0, other_half, own_half),
        ],
        axis=1,
    )
    layer_out = (
        summed + adapter_scale * jnp.dot(low_bf, up_b, preferred_element_type=jnp.float32)
    ).astype(jnp.bfloat16)

    adapter = adapter_scale * jnp.dot(back_bf, down_a, preferred_element_type=jnp.float32)
    pieces = []
    for r in range(ROW_PIECES):
        came_grad = cross(sums[r][rows:].astype(jnp.bfloat16)).astype(jnp.float32)
        pieces.append(sums[r][:rows] + came_grad + adapter[:, r * part : (r + 1) * part])
    attn_grad = jnp.concatenate(pieces, axis=1).astype(jnp.bfloat16)

    factor = adapter_scale / (rows * dp_size)
    grad_a = factor * lax.dot_general(
        back_bf, attn_out, (((0,), (0,)), ((), ())), preferred_element_type=jnp.float32
    )
    grad_b = factor * lax.dot_general(
        low_bf, grad_cols, (((0,), (0,)), ((), ())), preferred_element_type=jnp.float32
    )
    bank_a, logit_grad_a = compose_back(grad_a, weights_a, picked_a, mixing_a, vector_bank)
    bank_b, logit_grad_b = compose_back(grad_b, weights_b, picked_b, mixing_b, vector_bank)
    bank_grad = lax.psum(bank_a + bank_b, ("dp", "tensor"))
    logits_a_grad, logits_b_grad = lax.psum((logit_grad_a, logit_grad_b), "dp")
    return (layer_out, attn_grad, bank_grad, logits_a_grad, logits_b_grad)


MESH_ID = pl.DeviceIdType.MESH
PIECES = 8


def dot_nn(a, b):
    return jnp.dot(a, b, preferred_element_type=jnp.float32)


def dot_nt(a, b):
    return lax.dot_general(a, b, (((1,), (1,)), ((), ())), preferred_element_type=jnp.float32)


def exchange_kernel(
    factor,
    attn, weight, grad, bank, logits_a, index_a, logits_b, index_b,
    out_hbm, agrad_hbm, relay, bank_out, slope_a, slope_b,
    wbuf, abuf, gbuf, dacc, cbuf, ybuf, dsend, drecv, cacc, lb, low, back,
    down, up, mixing, sums, came,
    load_sem, zs_send, relay_recv, relay_send, far_recv, xs_send, x_recv, xf_send, xf_recv,
    g_send, g_recv, gm_send, gm_recv, a_send, a_recv, lb_send, lb_recv,
    c_send, c_recv, y_send, y_recv, zc_send, zc_recv, d_send, d_recv, out_sem, grad_sem,
    sum_send, sum_recv,
):
    rows, depth = attn.shape
    width = weight.shape[1]
    half = width // 2
    step = depth // PIECES
    tile = rows // 2
    rank = down.shape[0]
    own = up.shape[1]

    dp, t = lax.axis_index("dp"), lax.axis_index("tensor")
    z, x = dp // 2, dp % 2
    y, c = t // 2, t % 2
    zh, zl = z // 2, z % 2
    inner = (z == 1) | (z == 2)
    pz = zh * 2 + (1 - zl)
    mz = jnp.where(z == 1, 2, 1)
    x_dev = (z * 2 + (1 - x), t)
    p_dev = (pz * 2 + x, t)
    m_dev = (mz * 2 + x, t)
    c_dev = (dp, y * 2 + (1 - c))
    y_dev = (dp, (1 - y) * 2 + c)
    reduces = c == zl

    def remote(src, dst, send, recv, device):
        return pltpu.make_async_remote_copy(
            src_ref=src, dst_ref=dst, send_sem=send, recv_sem=recv,
            device_id=device, device_id_type=MESH_ID,
        )

    def rowsof(p):
        return pl.ds(pl.multiple_of(p * step, step), step)

    barrier = pltpu.get_barrier_semaphore()
    others = [(dp, (t + k) % 4) for k in (1, 2, 3)]
    for device in others + [x_dev, p_dev]:
        pl.semaphore_signal(barrier, inc=1, device_id=device, device_id_type=MESH_ID)

    @pl.when(inner)
    def _():
        pl.semaphore_signal(barrier, inc=1, device_id=m_dev, device_id_type=MESH_ID)

    def column_block(zz, b, xx):
        zb = jnp.where(b < 2, zz, (zz + 2) % 4)
        xb = jnp.where(b % 2 == 0, xx, 1 - xx)
        return zb * 2 + xb

    loads = [pltpu.make_async_copy(attn, abuf.at[0], load_sem.at[0])]
    gq = pltpu.make_async_copy(
        grad.at[:, pl.ds(pl.multiple_of(t * own, own), own)], dsend.at[:, pl.ds(0, own)], load_sem.at[1]
    )
    loads.append(gq)
    for n in range(2):
        loads.append(
            pltpu.make_async_copy(weight.at[:, pl.ds(n * half, half)], wbuf.at[n], load_sem.at[2 + n])
        )
    for s in range(8):
        col = column_block(z, s // 2, x) * width + (s % 2) * half
        loads.append(
            pltpu.make_async_copy(
                grad.at[:, pl.ds(pl.multiple_of(col, half), half)], gbuf.at[s, 0], load_sem.at[4 + s]
            )
        )
    for load in loads[:2]:
        load.start()

    @pl.when(inner)
    def _():
        pl.semaphore_wait(barrier, 6)

    @pl.when(jnp.logical_not(inner))
    def _():
        pl.semaphore_wait(barrier, 5)

    total = 2 * PIECES
    narrow = half // 2

    def area(n, p):
        return pl.ds(pl.multiple_of(p * step, step), step), pl.ds(0, half)

    def weight_area(n, p):
        return weight.at[area(n, p)[0], pl.ds(n * half, half)]

    def by_half(i, act):
        for n in range(2):

            @pl.when(i // PIECES == n)
            def _():
                act(n, i % PIECES)

    def x_own(n, p):
        i = n * PIECES + p
        return remote(weight_area(n, p), wbuf.at[(2 + n, *area(n, p))], xs_send.at[i], x_recv.at[i], x_dev)

    def z_own(n, p):
        i = n * PIECES + p
        stream = jnp.where(inner, 0, 1)
        device = (jnp.where(inner, mz, pz) * 2 + x, t)
        return remote(
            weight_area(n, p), relay.at[(stream, n, *area(n, p))],
            zs_send.at[i], relay_recv.at[stream, i], device,
        )

    def g_own(n):
        col = column_block(pz, t, x) * width + n * half
        return remote(
            grad.at[:, pl.ds(pl.multiple_of(col, half), half)],
            gbuf.at[2 * t + n, 1], g_send.at[n], g_recv.at[n], p_dev,
        )

    held = 2
    a_own = remote(attn, abuf.at[1], a_send.at[0], a_recv.at[0], p_dev)

    for n in range(2):
        g_own(n).start()
    a_own.start()

    @pl.loop(0, PIECES)
    def _(i):
        x_own(0, i).start()

        @pl.when(inner)
        def _():
            z_own(0, i).start()

    @pl.when(inner)
    def _():
        @pl.loop(0, PIECES - held)
        def _(i):
            z_own(1, i).start()

    for load in loads[2:]:
        load.start()

    levels = bank.shape[0]
    sublen = bank.shape[1]
    vectors = mixing.shape[2]
    per_row = vectors // rank
    exact = dict(preferred_element_type=jnp.float32, precision=lax.Precision.HIGHEST)

    place = lax.broadcasted_iota(jnp.int32, (rank, vectors), 1)
    spread = (place % rank == lax.broadcasted_iota(jnp.int32, (rank, vectors), 0)).astype(jnp.float32)
    place = lax.broadcasted_iota(jnp.int32, (per_row, vectors), 1)
    keep = place // rank == lax.broadcasted_iota(jnp.int32, (per_row, vectors), 0)
    level = lax.broadcasted_iota(jnp.int32, (levels, vectors), 0)

    def as_row(value):
        wide_value = jnp.dot(value.astype(jnp.float32), spread, **exact)
        return jnp.sum(jnp.where(keep, wide_value, 0.0), axis=0, keepdims=True)

    def from_row(row):
        return lax.dot_general(jnp.where(keep, row, 0.0), spread, (((1,), (1,)), ((), ())), **exact)

    shares, found = [], []
    for k, (logits, indices) in enumerate(((logits_a, index_a), (logits_b, index_b))):
        first, second = as_row(logits[:, 0, :]), as_row(logits[:, 1, :])
        shares.append((1.0 / (1.0 + jnp.exp(second - first)), 1.0 / (1.0 + jnp.exp(first - second))))
        picks = [(as_row(indices[:, m, :]) + 0.5).astype(jnp.int32) for m in range(2)]
        found.append([level == pick for pick in picks])

    for k, target in enumerate((down, up)):
        mixing[k] = sum(jnp.where(found[k][m], shares[k][m], 0.0) for m in range(2))
        blocks = lax.dot_general(mixing[k], bank[...], (((0,), (0,)), ((), ())), **exact)
        for j in range(per_row):
            row = blocks[j * rank : (j + 1) * rank]
            target[:, j * sublen : (j + 1) * sublen] = row.astype(jnp.bfloat16)

    loads[0].wait()
    loads[1].wait()
    lb[t, :rank] = dot_nt(down[...], abuf[0])
    lb[t, rank:] = dot_nt(up[...], dsend[:, :own])

    def lb_copy(k):
        device = (dp, (t + k) % 4)
        return remote(lb.at[t], lb.at[t], lb_send.at[k - 1], lb_recv.at[k - 1], device)

    for k in (1, 2, 3):
        lb_copy(k).start()
    for load in loads[2:]:
        load.wait()
    dacc[...] = jnp.zeros_like(dacc)
    for k in (1, 2, 3):
        lb_copy(k).wait()
    both = lb[0] + lb[1] + lb[2] + lb[3]
    low[...] = both[:rank].T.astype(jnp.bfloat16)
    back[...] = both[rank:].T.astype(jnp.bfloat16)
    both = both.astype(jnp.bfloat16)
    slopes = (
        factor * dot_nn(both[rank:], abuf[0]),
        factor * dot_nn(both[:rank], dsend[:, :own]),
    )
    bank_out[...] = jnp.zeros_like(bank_out)
    dots = []
    for k in range(2):
        pieces = [slopes[k][:, j * sublen : (j + 1) * sublen] for j in range(per_row)]
        stacked = jnp.concatenate(pieces, axis=0)
        bank_out[...] += jnp.dot(mixing[k], stacked, **exact)
        projected = lax.dot_general(bank[...], stacked, (((1,), (1,)), ((), ())), **exact)
        for m in range(2):
            dots.append(jnp.sum(jnp.where(found[k][m], projected, 0.0), axis=0, keepdims=True))

    q1, q2, q3 = levels // 2, levels // 4, levels // 8
    pack = q3 + 8
    at_c = c * q1
    at_y = at_c + y * q2
    at_x = at_y + x * q3
    counts = (q1, q2, pack, pack, pack, q3, q2, q1)
    places = [pl.ds(sum(counts[:k]), counts[k]) for k in range(8)]

    def bank_rows(start, count):
        return pl.ds(pl.multiple_of(start, 8), count)

    def sum_copy(k, source, device):
        return remote(source, came.at[places[k]], sum_send.at[k], sum_recv.at[k], device)

    core_sum = sum_copy(0, bank_out.at[bank_rows((1 - c) * q1, q1)], c_dev)
    y_sum = sum_copy(1, bank_out.at[bank_rows(at_c + (1 - y) * q2, q2)], y_dev)
    x_sum = sum_copy(2, sums, x_dev)
    p_sum = sum_copy(3, sums, p_dev)
    m_sum = sum_copy(4, sums, m_dev)
    x_all = sum_copy(5, bank_out.at[bank_rows(at_x, q3)], x_dev)
    y_all = sum_copy(6, bank_out.at[bank_rows(at_y, q2)], y_dev)
    c_all = sum_copy(7, bank_out.at[bank_rows(at_c, q1)], c_dev)
    core_sum.start()
    core_sum.wait()
    bank_out[bank_rows(at_c, q1)] += came[places[0]]
    y_sum.start()
    y_sum.wait()
    bank_out[bank_rows(at_y, q2)] += came[places[1]]
    sums[:q3] = bank_out[bank_rows(at_y + (1 - x) * q3, q3)]
    sums[q3:] = jnp.zeros_like(sums[q3:])
    for k in range(4):
        sums[q3 + k : q3 + k + 1, :vectors] = dots[k]
    x_sum.start()

    @pl.loop(0, PIECES)
    def _(i):
        x_own(1, i).start()

    def relay_on(stream, n, p):
        i = n * PIECES + p
        device = (jnp.where(stream == 0, pz, mz) * 2 + x, t)
        return remote(
            relay.at[(stream, n, *area(n, p))], wbuf.at[(4 + n, *area(n, p))],
            relay_send.at[stream, i], far_recv.at[i], device,
        )

    def relay_wait(stream, n, p):
        i = n * PIECES + p
        piece = relay.at[(stream, n, *area(n, p))]
        remote(piece, piece, relay_send.at[stream, i], relay_recv.at[stream, i], p_dev).wait_recv()

    def x_far(n, p):
        i = n * PIECES + p
        return remote(
            wbuf.at[(4 + n, *area(n, p))], wbuf.at[(6 + n, *area(n, p))], xf_send.at[i], xf_recv.at[i], x_dev
        )

    def far_wait(n, p):
        i = n * PIECES + p
        piece = wbuf.at[(4 + n, *area(n, p))]
        remote(piece, piece, xf_send.at[i], far_recv.at[i], x_dev).wait_recv()

    def g_spread(k, n):
        piece = gbuf.at[2 * t + n, 1]
        return remote(piece, piece, gm_send.at[k - 1, n], gm_recv.at[k - 1, n], (dp, (t + k) % 4))

    lag = jnp.where(inner, 15, 13)
    late, later = 12, 17

    def tick(i, carry):
        def near(n, p):
            x_own(n, p).wait_recv()

            @pl.when(inner & (i < total - held))
            def _():
                relay_wait(0, n, p)

                @pl.when(i > PIECES)
                def _():
                    relay_on(0, n, p).start()

        @pl.when(i < total)
        def _():
            by_half(i, near)

        @pl.when(i == PIECES)
        def _():
            x_sum.wait()
            sums[:q3] = bank_out[bank_rows(at_x, q3)] + came[places[2]][:q3]
            sums[q3:] += came[places[2]][q3:]

            @pl.when(jnp.logical_not(inner))
            def _():
                p_sum.start()
                for n in range(2):

                    @pl.loop(0, PIECES)
                    def _(k):
                        z_own(n, k).start()

            @pl.when(inner)
            def _():
                @pl.loop(0, PIECES)
                def _(k):
                    relay_on(0, 0, k).start()

                relay_on(0, 1, 0).start()

        @pl.when(i == late)
        def _():
            @pl.when(jnp.logical_not(inner))
            def _():
                p_sum.wait_send()

            @pl.when(inner)
            def _():
                p_sum.wait_recv()
                sums[...] += came[places[3]]
                m_sum.start()

        @pl.when((i >= later) & (i < later + held) & inner)
        def _():
            p = PIECES - held + i - later
            relay_wait(0, 1, p)
            relay_on(0, 1, p).start()

        @pl.when((i == later) & inner)
        def _():
            m_sum.wait()
            sums[...] += came[places[4]]
            p_sum.start()

        @pl.when(i == 4)
        def _():
            for n in range(2):
                g_own(n).wait_recv()
                for k in (1, 2, 3):
                    g_spread(k, n).start()

        def onward(n, p):
            relay_wait(1, n, p)
            relay_on(1, n, p).start()
            if n == 0:

                @pl.when(p < held)
                def _():
                    z_own(1, PIECES - held + p).start()

        @pl.when((i >= late) & (i < late + total) & inner)
        def _():
            by_half(i - late, onward)

        def far(n, p):
            far_wait(n, p)
            x_far(n, p).start()

        @pl.when((i >= lag) & (i < lag + total))
        def _():
            by_half(i - lag, far)

        return carry

    def part_of(h):
        return pl.ds(h * narrow, narrow)

    def c_copy(s, r, h):
        piece = cbuf.at[s, r, :, part_of(h)]
        return remote(piece, piece, c_send.at[s, r, h], c_recv.at[s, r, h], c_dev)

    def y_copy(s, r, h):
        j = s % 4
        return remote(
            cbuf.at[s, r, :, part_of(h)], ybuf.at[j, r, :, part_of(h)],
            y_send.at[j, r, h], y_recv.at[j, r, h], y_dev,
        )

    def z_copy(s, h):
        j = s % 4
        return remote(
            cbuf.at[s, 1, :, part_of(h)], ybuf.at[j, 0, :, part_of(h)],
            zc_send.at[j, h], zc_recv.at[j, h], p_dev,
        )

    def kept(s):
        return jnp.where(s < 4, zh, 1 - zh) == y

    def out_columns(j, h):
        xb = jnp.where(j < 2, x, 1 - x)
        return pl.ds(pl.multiple_of(xb * width + (j % 2) * half + h * narrow, narrow), narrow)

    def out_copy(j, h):
        return pltpu.make_async_copy(
            ybuf.at[j, 0, :, part_of(h)], out_hbm.at[:, out_columns(j, h)], out_sem.at[j, h]
        )

    def adapter_out(j, h):
        return 2.0 * dot_nn(low[...], up[:, out_columns(j, h)])

    def pass_core(s, r, partial, hs=(0, 1)):
        @pl.when(jnp.logical_not(reduces))
        def _():
            for h in hs:
                cbuf[s, r, :, part_of(h)] = partial[:, part_of(h)].astype(jnp.bfloat16)
                c_copy(s, r, h).start()

    def sum_core(s, r, partial, hs=(0, 1)):
        @pl.when(reduces)
        def _():
            for h in hs:
                part = part_of(h)
                c_copy(s, r, h).wait_recv()
                total_here = partial[:, part] + cbuf[s, r, :, part].astype(jnp.float32)
                cbuf[s, r, :, part] = total_here.astype(jnp.bfloat16)

                @pl.when(jnp.logical_not(kept(s)))
                def _():
                    y_copy(s, r, h).start()

    def sum_y(s, r, hs=(0, 1)):
        @pl.when(reduces & kept(s))
        def _():
            j = s % 4
            for h in hs:
                part = part_of(h)
                y_copy(s, r, h).wait_recv()
                total_here = cbuf[s, r, :, part].astype(jnp.float32) + ybuf[j, r, :, part].astype(jnp.float32)

                @pl.when(r == 0)
                def _():
                    ybuf[j, 0, :, part] = (total_here + adapter_out(j, h)).astype(jnp.bfloat16)
                    out_copy(j, h).start()

                @pl.when(r == 1)
                def _():
                    cbuf[s, 1, :, part] = total_here.astype(jnp.bfloat16)
                    z_copy(s, h).start()

    def finish_other(j, h):
        @pl.when(jnp.logical_not(reduces))
        def _():
            part = part_of(h)
            z_copy(j, h).wait_recv()
            ybuf[j, 0, :, part] = (ybuf[j, 0, :, part].astype(jnp.float32) + adapter_out(j, h)).astype(jnp.bfloat16)
            out_copy(j, h).start()

    slots = (0, 1, 2, 0, 1, 2, 3, 3, 4, 4, 6, 6)
    sides = (0, 0, 0, 1, 1, 1, 0, 1, 0, 1, 0, 1)

    def pick(table, u):
        if isinstance(u, int):
            return table[u]
        value = table[0]
        for k in range(1, len(table)):
            if table[k] != table[k - 1]:
                value = jnp.where(u >= k, table[k], value)
        return value

    def ready(u):
        value = jnp.where(u >= 2, PIECES, 0)
        value = jnp.where(u >= 3, 12, value)
        value = jnp.where(u >= 6, total, value)
        value = jnp.where(u >= 8, lag + PIECES, value)
        return jnp.where(u >= 10, lag + PIECES + 2, value)

    def unit(u, carry):
        s, r = pick(slots, u), pick(sides, u)
        lax.fori_loop(ready(u - 1), ready(u), tick, 0)

        @pl.when(u == 3)
        def _():
            a_own.wait_recv()
            for n in range(2):
                for k in (1, 2, 3):
                    g_spread(k, n).wait_recv()

        @pl.when(u == 10)
        def _():
            for p in range(PIECES):
                x_far(0, p).wait_recv()

        partial = cacc.at[0, u % 2]
        for m in range(2):
            part = pl.ds(m * tile, tile)
            partial[part] = dot_nn(abuf[r, part], wbuf[s])
            dacc[r, part] += dot_nt(gbuf[s, r, part], wbuf[s])
        pass_core(s, r, partial)

        @pl.when(u >= 1)
        def _():
            sum_core(pick(slots, u - 1), pick(sides, u - 1), cacc.at[0, (u - 1) % 2])

        @pl.when(u >= 4)
        def _():
            sum_y(pick(slots, u - 4), pick(sides, u - 4))

        return carry

    lax.fori_loop(0, 12, unit, 0)
    sum_core(slots[11], sides[11], cacc.at[0, 1])
    cacc[...] = jnp.zeros_like(cacc)

    final = ((5, 1), (7, 1), (5, 0), (7, 0))

    def grad_part(p):
        return pl.ds(pl.multiple_of(p * step, step), step)

    def d_copy(p):
        columns = grad_part(p)
        return remote(dsend.at[:, columns], drecv.at[:, columns], d_send.at[p], d_recv.at[p], p_dev)

    def last_piece(p, carry):
        done = lag + PIECES + 2 + p
        lax.fori_loop(jnp.minimum(done, lag + total), jnp.minimum(done + 1, lag + total), tick, 0)
        x_far(1, p).wait_recv()
        columns = grad_part(p)
        for r in (1, 0):
            for m in range(2):
                part = pl.ds(m * tile, tile)
                grown = dacc[r, part, columns]
                grown += dot_nt(gbuf[5, r, part], wbuf[5, columns])
                grown += dot_nt(gbuf[7, r, part], wbuf[7, columns])
                if r == 1:
                    dsend[part, columns] = grown.astype(jnp.bfloat16)
                else:
                    dacc[0, part, columns] = grown
            if r == 1:
                d_copy(p).start()
        for k in range(2):
            for r in range(2):
                cacc[k, r] += dot_nn(abuf[r, :, columns], wbuf[5 + 2 * k, columns])


        @pl.when(p == 1)
        def _():
            @pl.when(inner)
            def _():
                p_sum.wait_send()

            @pl.when(jnp.logical_not(inner))
            def _():
                p_sum.wait_recv()
                sums[...] = came[places[3]]

            bank_out[bank_rows(at_x, q3)] = sums[:q3]
            x_all.start()

        @pl.when(p == 3)
        def _():
            x_all.wait()
            bank_out[bank_rows(at_y + (1 - x) * q3, q3)] = came[places[5]]
            y_all.start()

        @pl.when((p >= 1) & (p < 5))
        def _():
            sum_y(pick(slots, 7 + p), (p - 1) % 2)

        @pl.when(p == 5)
        def _():
            y_all.wait()
            bank_out[bank_rows(at_c + (1 - y) * q2, q2)] = came[places[6]]
            c_all.start()

        return carry

    lax.fori_loop(0, PIECES, last_piece, 0)

    def agrad_copy(p):
        columns = grad_part(p)
        return pltpu.make_async_copy(drecv.at[:, columns], agrad_hbm.at[:, columns], grad_sem.at[p])

    def finish_grad(p, carry):
        columns = grad_part(p)
        d_copy(p).wait_recv()
        total_here = dacc[0, :, columns] + drecv[:, columns].astype(jnp.float32)
        drecv[:, columns] = (total_here + 2.0 * dot_nn(back[...], down[:, columns])).astype(jnp.bfloat16)
        agrad_copy(p).start()
        return carry

    for slot, side in final:
        pass_core(slot, side, cacc.at[(slot - 5) // 2, side])
    for slot, side in final:
        sum_core(slot, side, cacc.at[(slot - 5) // 2, side])
    c_all.wait()
    bank_out[bank_rows((1 - c) * q1, q1)] = came[places[7]]
    for k, target in enumerate((slope_a, slope_b)):
        values = [sums[q3 + 2 * k + m : q3 + 2 * k + m + 1, :vectors] for m in range(2)]
        mean = shares[k][0] * values[0] + shares[k][1] * values[1]
        for m in range(2):
            target[:, m, :] = from_row(shares[k][m] * (values[m] - mean))
    for j in (0, 2):
        for h in range(2):
            finish_other(j, h)
    for slot, side in final:
        sum_y(slot, side)
    lax.fori_loop(0, PIECES, finish_grad, 0)
    for h in range(2):
        for j in (1, 3):
            finish_other(j, h)
    a_own.wait_send()
    for n in range(2):
        g_own(n).wait_send()
        for k in (1, 2, 3):
            g_spread(k, n).wait_send()

    for n in range(2):

        @pl.loop(0, PIECES)
        def _(p):
            x_own(n, p).wait_send()
            z_own(n, p).wait_send()
            x_far(n, p).wait_send()

            @pl.when(inner)
            def _():
                relay_on(0, n, p).wait_send()
                relay_on(1, n, p).wait_send()

    @pl.loop(0, 8)
    def _(i):
        for h in range(2):

            @pl.when(jnp.logical_not(reduces))
            def _():
                for r in range(2):
                    c_copy(i, r, h).wait_send()

            @pl.when(reduces & jnp.logical_not(kept(i)))
            def _():
                for r in range(2):
                    y_copy(i, r, h).wait_send()

            @pl.when(reduces & kept(i))
            def _():
                z_copy(i, h).wait_send()

    @pl.loop(0, PIECES)
    def _(p):
        d_copy(p).wait_send()
        agrad_copy(p).wait()

    @pl.loop(0, 4)
    def _(j):
        for h in range(2):
            out_copy(j, h).wait()


def settle_kernel(out_in, agrad_in, bank_in, slope_a_in, slope_b_in, out, agrad, bank, slope_a, slope_b, held, sem_in, sem_out):
    pieces = sem_in.shape[1]
    part = held.shape[1] // pieces
    pairs = ((out_in, out), (agrad_in, agrad))

    def copy_in(k, p):
        rows = pl.ds(p * part, part)
        return pltpu.make_async_copy(pairs[k][0].at[rows], held.at[k, rows], sem_in.at[k, p])

    def copy_out(k, p):
        rows = pl.ds(p * part, part)
        return pltpu.make_async_copy(held.at[k, rows], pairs[k][1].at[rows], sem_out.at[k, p])

    order = [(k, p) for p in range(pieces) for k in range(2)]
    for k, p in order:
        copy_in(k, p).start()
    bank[...] = bank_in[...]
    slope_a[...] = slope_a_in[...]
    slope_b[...] = slope_b_in[...]
    for k, p in order:
        copy_in(k, p).wait()
        copy_out(k, p).start()
    for k, p in order:
        copy_out(k, p).wait()


def fused_local(dp_size, attn_out, frozen_weight, vector_bank, logits_a, index_a, logits_b, index_b, out_grad):
    rows, depth = attn_out.shape
    width = frozen_weight.shape[1]
    half = width // 2
    levels, sublen = vector_bank.shape
    rank, per_row, _ = logits_a.shape
    vectors = rank * per_row
    own = logits_b.shape[1] * sublen
    factor = adapter_scale / (rows * dp_size)
    total = 2 * PIECES
    small = [v.transpose(1, 2, 0) for v in (logits_a, index_a, logits_b, index_b)]
    bf16, f32 = jnp.bfloat16, jnp.float32
    dma = pltpu.SemaphoreType.DMA
    hbm = pl.BlockSpec(memory_space=pl.ANY)
    vmem = pl.BlockSpec(memory_space=pltpu.VMEM)
    layer_out, attn_grad, _, bank_grad, slope_a, slope_b = pl.pallas_call(
        functools.partial(exchange_kernel, factor),
        name="exchange",
        out_shape=(
            jax.ShapeDtypeStruct((rows, own), bf16),
            jax.ShapeDtypeStruct((rows, depth), bf16),
            jax.ShapeDtypeStruct((2, 2, depth, half), bf16),
            jax.ShapeDtypeStruct((levels, sublen), f32),
            jax.ShapeDtypeStruct((per_row, 2, rank), f32),
            jax.ShapeDtypeStruct((per_row, 2, rank), f32),
        ),
        in_specs=[hbm, hbm, hbm, vmem, vmem, vmem, vmem, vmem],
        out_specs=(hbm, hbm, hbm, vmem, vmem, vmem),
        scratch_shapes=[
            pltpu.VMEM((8, depth, half), bf16),
            pltpu.VMEM((2, rows, depth), bf16),
            pltpu.VMEM((8, 2, rows, half), bf16),
            pltpu.VMEM((2, rows, depth), f32),
            pltpu.VMEM((8, 2, rows, half), bf16),
            pltpu.VMEM((4, 2, rows, half), bf16),
            pltpu.VMEM((rows, depth), bf16),
            pltpu.VMEM((rows, depth), bf16),
            pltpu.VMEM((2, 2, rows, half), f32),
            pltpu.VMEM((4, 2 * rank, rows), f32),
            pltpu.VMEM((rows, rank), bf16),
            pltpu.VMEM((rows, rank), bf16),
            pltpu.VMEM((rank, depth), bf16),
            pltpu.VMEM((rank, own), bf16),
            pltpu.VMEM((2, levels, vectors), f32),
            pltpu.VMEM((levels // 8 + 8, sublen), f32),
            pltpu.VMEM((2 * levels + 24, sublen), f32),
            dma((12,)), dma((total,)), dma((2, total)), dma((2, total)), dma((total,)),
            dma((total,)), dma((total,)), dma((total,)), dma((total,)),
            dma((2,)), dma((2,)), dma((3, 2)), dma((3, 2)), dma((1,)), dma((1,)),
            dma((3,)), dma((3,)),
            dma((8, 2, 2)), dma((8, 2, 2)), dma((4, 2, 2)), dma((4, 2, 2)), dma((4, 2)), dma((4, 2)),
            dma((PIECES,)), dma((PIECES,)), dma((4, 2)), dma((PIECES,)), dma((8,)), dma((8,)),
        ],
        compiler_params=pltpu.CompilerParams(
            collective_id=0, has_side_effects=True, vmem_limit_bytes=67043328
        ),
    )(attn_out, frozen_weight, out_grad, vector_bank, *small)
    layer_out, attn_grad, bank_grad, slope_a, slope_b = pl.pallas_call(
        settle_kernel,
        name="settle",
        out_shape=[jax.ShapeDtypeStruct(v.shape, v.dtype) for v in (layer_out, attn_grad, bank_grad, slope_a, slope_b)],
        in_specs=[hbm, hbm, vmem, vmem, vmem],
        out_specs=[hbm, hbm, vmem, vmem, vmem],
        scratch_shapes=[pltpu.VMEM((2, rows, depth), bf16), dma((2, 4)), dma((2, 4))],
    )(layer_out, attn_grad, bank_grad, slope_a, slope_b)
    return (layer_out, attn_grad, bank_grad, slope_a.transpose(2, 0, 1), slope_b.transpose(2, 0, 1))


def solution(mesh):
    dp_size, tensor_size = mesh.shape["dp"], mesh.shape["tensor"]
    paired = dp_size == 2 * tensor_size and tensor_size % 2 == 0
    body = functools.partial(ring_local, dp_size, tensor_size) if paired else local
    if paired and tensor_size == 4:
        body = functools.partial(fused_local, dp_size)
    return jax.shard_map(
        body,
        mesh=mesh,
        in_specs=(
            P("dp", "tensor"),
            P("tensor", "dp"),
            P(),
            P(None, "tensor", None),
            P(None, "tensor", None),
            P(None, "tensor", None),
            P(None, "tensor", None),
            P("dp", None),
        ),
        out_specs=(
            P("dp", "tensor"),
            P("dp", "tensor"),
            P(),
            P(None, "tensor", None),
            P(None, "tensor", None),
        ),
        check_vma=False,
    )
```

```python
import functools

import jax
import jax.numpy as jnp
from jax import lax
from jax.experimental import pallas as pl
from jax.experimental.pallas import tpu as pltpu
from jax.sharding import PartitionSpec as P

adapter_scale = 2.0
ROW_PIECES = 4


def compose(logits, indices, vector_bank):
    weights = jax.nn.sigmoid(logits - logits[..., ::-1])
    levels = jnp.arange(vector_bank.shape[0], dtype=jnp.int32)
    picked = (indices[..., None] == levels).astype(jnp.float32)
    mixing = jnp.sum(picked * weights[..., None], axis=2)
    blocks = jnp.einsum("rjb,bc->rjc", mixing, vector_bank, precision=lax.Precision.HIGHEST)
    return (weights, picked, mixing, blocks.reshape(blocks.shape[0], -1))


def compose_back(grad_rows, weights, picked, mixing, vector_bank):
    blocks = grad_rows.reshape(mixing.shape[0], mixing.shape[1], -1)
    bank_part = jnp.einsum("rjb,rjc->bc", mixing, blocks, precision=lax.Precision.HIGHEST)
    projected = jnp.einsum("rjc,bc->rjb", blocks, vector_bank, precision=lax.Precision.HIGHEST)
    dots = jnp.sum(picked * projected[:, :, None, :], axis=3)
    logit_grad = weights * (dots - jnp.sum(weights * dots, axis=2, keepdims=True))
    return (bank_part, logit_grad)


def local(attn_out, frozen_weight, vector_bank, logits_a, index_a, logits_b, index_b, out_grad):
    weights_a, picked_a, mixing_a, rows_a = compose(logits_a, index_a, vector_bank)
    weights_b, picked_b, mixing_b, rows_b = compose(logits_b, index_b, vector_bank)
    down_a = rows_a.astype(jnp.bfloat16)
    up_b = rows_b.astype(jnp.bfloat16)
    own_width = up_b.shape[1]
    grad_cols = lax.dynamic_slice_in_dim(
        out_grad, lax.axis_index("tensor") * own_width, own_width, 1
    )
    low_part = jnp.dot(attn_out, down_a.T, preferred_element_type=jnp.float32)
    back_part = jnp.dot(grad_cols, up_b.T, preferred_element_type=jnp.float32)
    low_total = lax.psum(low_part, "tensor")
    low_bf = low_total.astype(jnp.bfloat16)
    gathered = lax.all_gather(frozen_weight, "dp", axis=1, tiled=True)
    partial_value = jnp.dot(attn_out, gathered, preferred_element_type=jnp.float32).astype(
        jnp.bfloat16
    )
    summed = lax.psum_scatter(partial_value, "tensor", scatter_dimension=1, tiled=True).astype(
        jnp.float32
    )
    layer_out = (
        summed + adapter_scale * jnp.dot(low_bf, up_b, preferred_element_type=jnp.float32)
    ).astype(jnp.bfloat16)
    back_total = lax.psum(back_part, "tensor")
    back_bf = back_total.astype(jnp.bfloat16)
    main = lax.dot_general(
        out_grad, gathered, (((1,), (1,)), ((), ())), preferred_element_type=jnp.float32
    )
    attn_grad = (
        main + adapter_scale * jnp.dot(back_bf, down_a, preferred_element_type=jnp.float32)
    ).astype(jnp.bfloat16)
    factor = adapter_scale / (attn_out.shape[0] * lax.axis_size("dp"))
    grad_a = factor * lax.dot_general(
        back_bf, attn_out, (((0,), (0,)), ((), ())), preferred_element_type=jnp.float32
    )
    grad_b = factor * lax.dot_general(
        low_bf, grad_cols, (((0,), (0,)), ((), ())), preferred_element_type=jnp.float32
    )
    bank_a, logit_grad_a = compose_back(grad_a, weights_a, picked_a, mixing_a, vector_bank)
    bank_b, logit_grad_b = compose_back(grad_b, weights_b, picked_b, mixing_b, vector_bank)
    bank_part = bank_a + bank_b
    bank_group = lax.psum(bank_part, "tensor")
    bank_grad, logits_a_grad, logits_b_grad = lax.psum(
        (bank_group, logit_grad_a, logit_grad_b), "dp"
    )
    return (layer_out, attn_grad, bank_grad, logits_a_grad, logits_b_grad)


def ring_local(dp_size, tensor_size, attn_out, frozen_weight, vector_bank, logits_a, index_a, logits_b, index_b, out_grad):
    depth = tensor_size
    chips = tensor_size // 2
    rows = attn_out.shape[0]
    own_width = attn_out.shape[1]
    width = frozen_weight.shape[1]
    half = width // 2
    part = own_width // ROW_PIECES
    place = lax.axis_index("dp")
    level, side = place // 2, place % 2
    tensor_index = lax.axis_index("tensor")

    ring = [(d, (d + 2) % dp_size) for d in range(dp_size)]
    swap = [(d, d ^ 1) for d in range(dp_size)]

    def hop(value):
        return lax.ppermute(value, "dp", ring)

    def cross(value):
        return lax.ppermute(value, "dp", swap)

    def collect(partial_value, step):
        target = (level - step + depth) % depth
        pairs = []
        for d in range(dp_size):
            goal = (d // 2 - step) % depth
            for chip in range(chips):
                core = 2 * chip + goal % 2
                pairs.append((d * tensor_size + (core ^ 1), d * tensor_size + core))
        other = lax.ppermute(partial_value, ("dp", "tensor"), pairs)
        paired = partial_value.astype(jnp.float32) + other.astype(jnp.float32)
        sent = paired.astype(jnp.bfloat16)
        total = paired
        for k in range(1, chips):
            pairs = []
            for d in range(dp_size):
                goal = (d // 2 - step) % depth
                source = ((goal // 2 + k) % chips) * 2 + goal % 2
                pairs.append((d * tensor_size + source, d * tensor_size + goal))
            total = total + lax.ppermute(sent, ("dp", "tensor"), pairs).astype(jnp.float32)
        return jnp.where(tensor_index == target, total, 0.0)

    first = frozen_weight[:, :half]
    later = [frozen_weight[r * part : (r + 1) * part, half:] for r in range(ROW_PIECES)]
    held = [(first, later)]
    for step in range(1, depth):
        first = hop(first)
        later = [hop(v) for v in later]
        held.append((first, later))

    attn_two = jnp.concatenate([attn_out, cross(attn_out)], axis=0)
    attn_parts = [attn_two[:, r * part : (r + 1) * part] for r in range(ROW_PIECES)]

    def grad_pair(step):
        origin = (level - step + depth) % depth
        mine = lax.dynamic_slice_in_dim(out_grad, (origin * 2 + side) * width, width, 1)
        theirs = lax.dynamic_slice_in_dim(out_grad, (origin * 2 + 1 - side) * width, width, 1)
        return jnp.concatenate([mine, cross(theirs)], axis=0)

    weights_a, picked_a, mixing_a, rows_a = compose(logits_a, index_a, vector_bank)
    weights_b, picked_b, mixing_b, rows_b = compose(logits_b, index_b, vector_bank)
    down_a = rows_a.astype(jnp.bfloat16)
    up_b = rows_b.astype(jnp.bfloat16)
    rank = down_a.shape[0]
    grad_cols = lax.dynamic_slice_in_dim(out_grad, tensor_index * own_width, own_width, 1)
    low_part = jnp.dot(attn_out, down_a.T, preferred_element_type=jnp.float32)
    back_part = jnp.dot(grad_cols, up_b.T, preferred_element_type=jnp.float32)
    both = lax.psum(jnp.concatenate([low_part, back_part], axis=1), "tensor")
    low_bf = both[:, :rank].astype(jnp.bfloat16)
    back_bf = both[:, rank:].astype(jnp.bfloat16)

    sums = [None] * ROW_PIECES
    own_total = jnp.zeros((rows, width), jnp.float32)
    cross_total = jnp.zeros((rows, width), jnp.float32)
    for step in range(depth):
        first, later = held[step]
        grads = grad_pair(step)
        out_first = jnp.dot(attn_two, first, preferred_element_type=jnp.float32)
        for r in range(ROW_PIECES):
            term = lax.dot_general(
                grads[:, :half],
                first[r * part : (r + 1) * part],
                (((1,), (1,)), ((), ())),
                preferred_element_type=jnp.float32,
            )
            sums[r] = term if sums[r] is None else sums[r] + term
        out_later = None
        for r in range(ROW_PIECES):
            term = jnp.dot(attn_parts[r], later[r], preferred_element_type=jnp.float32)
            out_later = term if out_later is None else out_later + term
            sums[r] = sums[r] + lax.dot_general(
                grads[:, half:],
                later[r],
                (((1,), (1,)), ((), ())),
                preferred_element_type=jnp.float32,
            )
        out_first = out_first.astype(jnp.bfloat16)
        out_later = out_later.astype(jnp.bfloat16)
        if step < depth - 1:
            block = collect(jnp.concatenate([out_first, out_later], axis=1), step)
            own_total = own_total + block[:rows]
            cross_total = cross_total + block[rows:]
        if step == depth - 2:
            came = cross(cross_total.astype(jnp.bfloat16)).astype(jnp.float32)
        if step == depth - 1:
            ends = [collect(out_first, step), collect(out_later, step)]
            own_end = jnp.concatenate([v[:rows] for v in ends], axis=1)
            came_end = jnp.concatenate(
                [cross(v[rows:].astype(jnp.bfloat16)) for v in ends], axis=1
            ).astype(jnp.float32)
    own_half = own_total + own_end
    other_half = came + came_end
    summed = jnp.concatenate(
        [
            jnp.where(side == 0, own_half, other_half),
            jnp.where(side == 0, other_half, own_half),
        ],
        axis=1,
    )
    layer_out = (
        summed + adapter_scale * jnp.dot(low_bf, up_b, preferred_element_type=jnp.float32)
    ).astype(jnp.bfloat16)

    adapter = adapter_scale * jnp.dot(back_bf, down_a, preferred_element_type=jnp.float32)
    pieces = []
    for r in range(ROW_PIECES):
        came_grad = cross(sums[r][rows:].astype(jnp.bfloat16)).astype(jnp.float32)
        pieces.append(sums[r][:rows] + came_grad + adapter[:, r * part : (r + 1) * part])
    attn_grad = jnp.concatenate(pieces, axis=1).astype(jnp.bfloat16)

    factor = adapter_scale / (rows * dp_size)
    grad_a = factor * lax.dot_general(
        back_bf, attn_out, (((0,), (0,)), ((), ())), preferred_element_type=jnp.float32
    )
    grad_b = factor * lax.dot_general(
        low_bf, grad_cols, (((0,), (0,)), ((), ())), preferred_element_type=jnp.float32
    )
    bank_a, logit_grad_a = compose_back(grad_a, weights_a, picked_a, mixing_a, vector_bank)
    bank_b, logit_grad_b = compose_back(grad_b, weights_b, picked_b, mixing_b, vector_bank)
    bank_grad = lax.psum(bank_a + bank_b, ("dp", "tensor"))
    logits_a_grad, logits_b_grad = lax.psum((logit_grad_a, logit_grad_b), "dp")
    return (layer_out, attn_grad, bank_grad, logits_a_grad, logits_b_grad)


MESH_ID = pl.DeviceIdType.MESH
PIECES = 8


def dot_nn(a, b):
    return jnp.dot(a, b, preferred_element_type=jnp.float32)


def dot_nt(a, b):
    return lax.dot_general(a, b, (((1,), (1,)), ((), ())), preferred_element_type=jnp.float32)


def exchange_kernel(
    factor,
    attn, weight, grad, bank_hbm, logits_a, index_a, logits_b, index_b,
    out_hbm, agrad_hbm, relay, bank_hbm_out, slope_a, slope_b,
    wbuf, abuf, gbuf, dacc, cbuf, ybuf, dsend, drecv, cacc, lb, low, back,
    down, up, bank, bank_out, mixing, sums, came,
    load_sem, zs_send, relay_recv, relay_send, far_recv, xs_send, x_recv, xf_send, xf_recv,
    g_send, g_recv, gm_send, gm_recv, a_send, a_recv, lb_send, lb_recv,
    c_send, c_recv, y_send, y_recv, zc_send, zc_recv, d_send, d_recv, out_sem, grad_sem,
    sum_send, sum_recv,
):
    rows, depth = attn.shape
    width = weight.shape[1]
    half = width // 2
    step = depth // PIECES
    tile = rows // 2
    rank = down.shape[0]
    own = up.shape[1]

    dp, t = lax.axis_index("dp"), lax.axis_index("tensor")
    z, x = dp // 2, dp % 2
    y, c = t // 2, t % 2
    zh, zl = z // 2, z % 2
    inner = (z == 1) | (z == 2)
    pz = zh * 2 + (1 - zl)
    mz = jnp.where(z == 1, 2, 1)
    x_dev = (z * 2 + (1 - x), t)
    p_dev = (pz * 2 + x, t)
    m_dev = (mz * 2 + x, t)
    c_dev = (dp, y * 2 + (1 - c))
    y_dev = (dp, (1 - y) * 2 + c)
    reduces = c == zl

    def remote(src, dst, send, recv, device):
        return pltpu.make_async_remote_copy(
            src_ref=src, dst_ref=dst, send_sem=send, recv_sem=recv,
            device_id=device, device_id_type=MESH_ID,
        )

    def rowsof(p):
        return pl.ds(pl.multiple_of(p * step, step), step)

    barrier = pltpu.get_barrier_semaphore()
    others = [(dp, (t + k) % 4) for k in (1, 2, 3)]
    for device in others + [x_dev, p_dev]:
        pl.semaphore_signal(barrier, inc=1, device_id=device, device_id_type=MESH_ID)

    @pl.when(inner)
    def _():
        pl.semaphore_signal(barrier, inc=1, device_id=m_dev, device_id_type=MESH_ID)

    def column_block(zz, b, xx):
        zb = jnp.where(b < 2, zz, (zz + 2) % 4)
        xb = jnp.where(b % 2 == 0, xx, 1 - xx)
        return zb * 2 + xb

    loads = [pltpu.make_async_copy(attn, abuf.at[0], load_sem.at[0])]
    gq = pltpu.make_async_copy(
        grad.at[:, pl.ds(pl.multiple_of(t * own, own), own)], dsend.at[:, pl.ds(0, own)], load_sem.at[1]
    )
    loads.append(gq)
    bank_load = pltpu.make_async_copy(bank_hbm, bank, load_sem.at[5])
    bank_load.start()
    for n in range(2):
        loads.append(
            pltpu.make_async_copy(weight.at[:, pl.ds(n * half, half)], wbuf.at[n], load_sem.at[2 + n])
        )
    for s in range(8):
        col = column_block(z, s // 2, x) * width + (s % 2) * half
        loads.append(
            pltpu.make_async_copy(
                grad.at[:, pl.ds(pl.multiple_of(col, half), half)], gbuf.at[s, 0], load_sem.at[4]
            )
        )
    for load in loads[:2]:
        load.start()

    @pl.when(inner)
    def _():
        pl.semaphore_wait(barrier, 6)

    @pl.when(jnp.logical_not(inner))
    def _():
        pl.semaphore_wait(barrier, 5)

    total = 2 * PIECES
    narrow = half // 2

    def area(n, p):
        return pl.ds(pl.multiple_of(p * step, step), step), pl.ds(0, half)

    def weight_area(n, p):
        return weight.at[area(n, p)[0], pl.ds(n * half, half)]

    def by_half(i, act):
        for n in range(2):

            @pl.when(i // PIECES == n)
            def _():
                act(n, i % PIECES)

    def x_own(n, p):
        i = n * PIECES + p
        return remote(weight_area(n, p), wbuf.at[(2 + n, *area(n, p))], xs_send.at[0], x_recv.at[i], x_dev)

    def z_own(n, p):
        i = n * PIECES + p
        stream = jnp.where(inner, 0, 1)
        device = (jnp.where(inner, mz, pz) * 2 + x, t)
        return remote(
            weight_area(n, p), relay.at[(stream, n, *area(n, p))],
            zs_send.at[0], relay_recv.at[stream, i], device,
        )

    def g_own(n):
        col = column_block(pz, t, x) * width + n * half
        return remote(
            grad.at[:, pl.ds(pl.multiple_of(col, half), half)],
            gbuf.at[2 * t + n, 1], g_send.at[0], g_recv.at[n], p_dev,
        )

    held = 2
    a_own = remote(attn, abuf.at[1], a_send.at[0], a_recv.at[0], p_dev)

    for n in range(2):
        g_own(n).start()
    a_own.start()

    @pl.loop(0, PIECES)
    def _(i):
        x_own(0, i).start()

        @pl.when(inner)
        def _():
            z_own(0, i).start()

    @pl.when(inner)
    def _():
        @pl.loop(0, PIECES - held)
        def _(i):
            z_own(1, i).start()

    for load in loads[2:]:
        load.start()

    bank_load.wait()
    levels = bank.shape[0]
    sublen = bank.shape[1]
    vectors = mixing.shape[2]
    per_row = vectors // rank
    exact = dict(preferred_element_type=jnp.float32, precision=lax.Precision.HIGHEST)

    place = lax.broadcasted_iota(jnp.int32, (rank, vectors), 1)
    spread = (place % rank == lax.broadcasted_iota(jnp.int32, (rank, vectors), 0)).astype(jnp.float32)
    place = lax.broadcasted_iota(jnp.int32, (per_row, vectors), 1)
    keep = place // rank == lax.broadcasted_iota(jnp.int32, (per_row, vectors), 0)
    level = lax.broadcasted_iota(jnp.int32, (levels, vectors), 0)

    def as_row(value):
        wide_value = jnp.dot(value.astype(jnp.float32), spread, **exact)
        return jnp.sum(jnp.where(keep, wide_value, 0.0), axis=0, keepdims=True)

    def from_row(row):
        return lax.dot_general(jnp.where(keep, row, 0.0), spread, (((1,), (1,)), ((), ())), **exact)

    shares, found = [], []
    for k, (logits, indices) in enumerate(((logits_a, index_a), (logits_b, index_b))):
        first, second = as_row(logits[:, 0, :]), as_row(logits[:, 1, :])
        shares.append((1.0 / (1.0 + jnp.exp(second - first)), 1.0 / (1.0 + jnp.exp(first - second))))
        picks = [(as_row(indices[:, m, :]) + 0.5).astype(jnp.int32) for m in range(2)]
        found.append([level == pick for pick in picks])

    for k, target in enumerate((down, up)):
        mixing[k] = sum(jnp.where(found[k][m], shares[k][m], 0.0) for m in range(2))
        blocks = lax.dot_general(mixing[k], bank[...], (((0,), (0,)), ((), ())), **exact)
        for j in range(per_row):
            row = blocks[j * rank : (j + 1) * rank]
            target[:, j * sublen : (j + 1) * sublen] = row.astype(jnp.bfloat16)

    loads[0].wait()
    loads[1].wait()
    lb[t, :rank] = dot_nt(down[...], abuf[0])
    lb[t, rank:] = dot_nt(up[...], dsend[:, :own])

    def lb_copy(k):
        device = (dp, (t + k) % 4)
        return remote(lb.at[t], lb.at[t], lb_send.at[0], lb_recv.at[0], device)

    for k in (1, 2, 3):
        lb_copy(k).start()
    for load in loads[2:4]:
        load.wait()
    pltpu.make_async_copy(gbuf.at[pl.ds(0, 4)], gbuf.at[pl.ds(0, 4)], load_sem.at[4]).wait()
    dacc[...] = jnp.zeros_like(dacc)
    three = lb.at[pl.ds(0, 3)]
    remote(three, three, lb_send.at[0], lb_recv.at[0], y_dev).wait()
    both = lb[0] + lb[1] + lb[2] + lb[3]
    low[...] = both[:rank].T.astype(jnp.bfloat16)
    back[...] = both[rank:].T.astype(jnp.bfloat16)
    both = both.astype(jnp.bfloat16)
    slopes = (
        factor * dot_nn(both[rank:], abuf[0]),
        factor * dot_nn(both[:rank], dsend[:, :own]),
    )
    bank_out[...] = jnp.zeros_like(bank_out)
    dots = []
    for k in range(2):
        pieces = [slopes[k][:, j * sublen : (j + 1) * sublen] for j in range(per_row)]
        stacked = jnp.concatenate(pieces, axis=0)
        bank_out[...] += jnp.dot(mixing[k], stacked, **exact)
        projected = lax.dot_general(bank[...], stacked, (((1,), (1,)), ((), ())), **exact)
        for m in range(2):
            dots.append(jnp.sum(jnp.where(found[k][m], projected, 0.0), axis=0, keepdims=True))

    q1, q2, q3 = levels // 2, levels // 4, levels // 8
    pack = q3 + 8
    at_c = c * q1
    at_y = at_c + y * q2
    at_x = at_y + x * q3
    counts = (q1, q2, pack, pack, pack, q3, q2, q1)
    places = [pl.ds(sum(counts[:k]), counts[k]) for k in range(8)]

    def bank_rows(start, count):
        return pl.ds(pl.multiple_of(start, 8), count)

    def sum_copy(k, source, device):
        return remote(source, came.at[places[k]], sum_send.at[k], sum_recv.at[k], device)

    core_sum = sum_copy(0, bank_out.at[bank_rows((1 - c) * q1, q1)], c_dev)
    y_sum = sum_copy(1, bank_out.at[bank_rows(at_c + (1 - y) * q2, q2)], y_dev)
    x_sum = sum_copy(2, sums, x_dev)
    p_sum = sum_copy(3, sums, p_dev)
    m_sum = sum_copy(4, sums, m_dev)
    x_all = sum_copy(5, bank_out.at[bank_rows(at_x, q3)], x_dev)
    y_all = sum_copy(6, bank_out.at[bank_rows(at_y, q2)], y_dev)
    c_all = sum_copy(7, bank_out.at[bank_rows(at_c, q1)], c_dev)
    core_sum.start()
    core_sum.wait()
    bank_out[bank_rows(at_c, q1)] += came[places[0]]
    y_sum.start()
    y_sum.wait()
    bank_out[bank_rows(at_y, q2)] += came[places[1]]
    sums[:q3] = bank_out[bank_rows(at_y + (1 - x) * q3, q3)]
    sums[q3:] = jnp.zeros_like(sums[q3:])
    for k in range(4):
        sums[q3 + k : q3 + k + 1, :vectors] = dots[k]
    x_sum.start()

    @pl.loop(0, PIECES)
    def _(i):
        x_own(1, i).start()

    def relay_on(stream, n, p):
        i = n * PIECES + p
        device = (jnp.where(stream == 0, pz, mz) * 2 + x, t)
        return remote(
            relay.at[(stream, n, *area(n, p))], wbuf.at[(4 + n, *area(n, p))],
            relay_send.at[stream], far_recv.at[i], device,
        )

    def relay_wait(stream, n, p):
        i = n * PIECES + p
        piece = relay.at[(stream, n, *area(n, p))]
        remote(piece, piece, relay_send.at[stream], relay_recv.at[stream, i], p_dev).wait_recv()

    def x_far(n, p):
        i = n * PIECES + p
        return remote(
            wbuf.at[(4 + n, *area(n, p))], wbuf.at[(6 + n, *area(n, p))], xf_send.at[0], xf_recv.at[i], x_dev
        )

    def far_wait(n, p):
        i = n * PIECES + p
        piece = wbuf.at[(4 + n, *area(n, p))]
        remote(piece, piece, xf_send.at[0], far_recv.at[i], x_dev).wait_recv()

    def g_spread(k, n):
        piece = gbuf.at[2 * t + n, 1]
        return remote(piece, piece, gm_send.at[0], gm_recv.at[0], (dp, (t + k) % 4))

    lag = jnp.where(inner, 15, 13)
    late, msum, later = 12, 17, 17

    def tick(i, carry):
        def near(n, p):
            x_own(n, p).wait_recv()

            @pl.when(inner & (i < total - held))
            def _():
                relay_wait(0, n, p)

                @pl.when(i > PIECES)
                def _():
                    relay_on(0, n, p).start()

        @pl.when(i < total)
        def _():
            by_half(i, near)

        @pl.when(i == PIECES)
        def _():
            x_sum.wait()
            sums[:q3] = bank_out[bank_rows(at_x, q3)] + came[places[2]][:q3]
            sums[q3:] += came[places[2]][q3:]

            @pl.when(jnp.logical_not(inner))
            def _():
                p_sum.start()
                for n in range(2):

                    @pl.loop(0, PIECES)
                    def _(k):
                        z_own(n, k).start()

            @pl.when(inner)
            def _():
                @pl.loop(0, PIECES)
                def _(k):
                    relay_on(0, 0, k).start()

                relay_on(0, 1, 0).start()

        @pl.when(i == late)
        def _():
            @pl.when(jnp.logical_not(inner))
            def _():
                p_sum.wait_send()

            @pl.when(inner)
            def _():
                p_sum.wait_recv()
                sums[...] += came[places[3]]
                m_sum.start()

        @pl.when((i >= later) & (i < later + held) & inner)
        def _():
            p = PIECES - held + i - later
            relay_wait(0, 1, p)
            relay_on(0, 1, p).start()

        @pl.when((i == msum) & inner)
        def _():
            m_sum.wait()
            sums[...] += came[places[4]]
            p_sum.start()

        @pl.when(i == 4)
        def _():
            for n in range(2):
                g_own(n).wait_recv()
                for k in (1, 2, 3):
                    g_spread(k, n).start()

        def onward(n, p):
            relay_wait(1, n, p)
            relay_on(1, n, p).start()
            if n == 0:

                @pl.when(p < held)
                def _():
                    z_own(1, PIECES - held + p).start()

        @pl.when((i >= late) & (i < late + total) & inner)
        def _():
            by_half(i - late, onward)

        def far(n, p):
            far_wait(n, p)
            x_far(n, p).start()

        @pl.when((i >= lag) & (i < lag + total))
        def _():
            by_half(i - lag, far)

        return carry

    def c_copy(s, r):
        return remote(cbuf.at[s, r], cbuf.at[s, r], c_send.at[0], c_recv.at[s, r], c_dev)

    def y_copy(s, r):
        j = s % 4
        return remote(cbuf.at[s, r], ybuf.at[j, r], y_send.at[0], y_recv.at[j, r], y_dev)

    def z_copy(s):
        j = s % 4
        return remote(cbuf.at[s, 1], ybuf.at[j, 0], zc_send.at[0], zc_recv.at[j], p_dev)

    def kept(s):
        return jnp.where(s < 4, zh, 1 - zh) == y

    def out_columns(j):
        xb = jnp.where(j < 2, x, 1 - x)
        return pl.ds(pl.multiple_of(xb * width + (j % 2) * half, half), half)

    def out_copy(j):
        return pltpu.make_async_copy(ybuf.at[j, 0], out_hbm.at[:, out_columns(j)], out_sem.at[0])

    def adapter_out(j):
        return 2.0 * dot_nn(low[...], up[:, out_columns(j)])

    def pass_core(s, r, partial):
        @pl.when(jnp.logical_not(reduces))
        def _():
            cbuf[s, r] = partial[...].astype(jnp.bfloat16)
            c_copy(s, r).start()

    def sum_core(s, r, partial):
        @pl.when(reduces)
        def _():
            c_copy(s, r).wait_recv()
            cbuf[s, r] = (partial[...] + cbuf[s, r].astype(jnp.float32)).astype(jnp.bfloat16)

            @pl.when(jnp.logical_not(kept(s)))
            def _():
                y_copy(s, r).start()

    def sum_y(s, r):
        @pl.when(reduces & kept(s))
        def _():
            j = s % 4
            y_copy(s, r).wait_recv()
            total_here = cbuf[s, r].astype(jnp.float32) + ybuf[j, r].astype(jnp.float32)

            @pl.when(r == 0)
            def _():
                ybuf[j, 0] = (total_here + adapter_out(j)).astype(jnp.bfloat16)
                out_copy(j).start()

            @pl.when(r == 1)
            def _():
                cbuf[s, 1] = total_here.astype(jnp.bfloat16)
                z_copy(s).start()

    def finish_other(j):
        @pl.when(jnp.logical_not(reduces))
        def _():
            z_copy(j).wait_recv()
            ybuf[j, 0] = (ybuf[j, 0].astype(jnp.float32) + adapter_out(j)).astype(jnp.bfloat16)
            out_copy(j).start()

    slots = (0, 1, 2, 0, 1, 2, 3, 3, 4, 4, 6, 6)
    sides = (0, 0, 0, 1, 1, 1, 0, 1, 0, 1, 0, 1)

    def pick(table, u):
        if isinstance(u, int):
            return table[u]
        value = table[0]
        for k in range(1, len(table)):
            if table[k] != table[k - 1]:
                value = jnp.where(u >= k, table[k], value)
        return value

    def ready(u):
        value = jnp.where(u >= 2, PIECES, 0)
        value = jnp.where(u >= 3, 12, value)
        value = jnp.where(u >= 6, total, value)
        value = jnp.where(u >= 8, lag + PIECES, value)
        return jnp.where(u >= 10, lag + PIECES + 2, value)

    def unit(u, carry):
        s, r = pick(slots, u), pick(sides, u)
        lax.fori_loop(ready(u - 1), ready(u), tick, 0)

        @pl.when(u == 3)
        def _():
            a_own.wait_recv()
            everything = gbuf.at[pl.ds(0, 3)]
            remote(everything, everything, gm_send.at[0], gm_recv.at[0], y_dev).wait_recv()

        @pl.when(u == 10)
        def _():
            for p in range(PIECES):
                x_far(0, p).wait_recv()

        partial = cacc.at[0, u % 2]
        for m in range(2):
            part = pl.ds(m * tile, tile)
            partial[part] = dot_nn(abuf[r, part], wbuf[s])
            dacc[r, part] += dot_nt(gbuf[s, r, part], wbuf[s])
        pass_core(s, r, partial)

        @pl.when(u >= 1)
        def _():
            sum_core(pick(slots, u - 1), pick(sides, u - 1), cacc.at[0, (u - 1) % 2])

        @pl.when(u >= 4)
        def _():
            sum_y(pick(slots, u - 4), pick(sides, u - 4))

        return carry

    lax.fori_loop(0, 12, unit, 0)
    sum_core(slots[11], sides[11], cacc.at[0, 1])
    cacc[...] = jnp.zeros_like(cacc)

    final = ((5, 1), (7, 1), (5, 0), (7, 0))

    def grad_part(p):
        return pl.ds(pl.multiple_of(p * step, step), step)

    def d_copy(p):
        columns = grad_part(p)
        return remote(dsend.at[:, columns], drecv.at[:, columns], d_send.at[0], d_recv.at[p], p_dev)

    def last_piece(p, carry):
        done = lag + PIECES + 2 + p
        lax.fori_loop(jnp.minimum(done, lag + total), jnp.minimum(done + 1, lag + total), tick, 0)
        x_far(1, p).wait_recv()
        columns = grad_part(p)
        for r in (1, 0):
            for m in range(2):
                part = pl.ds(m * tile, tile)
                grown = dacc[r, part, columns]
                grown += dot_nt(gbuf[5, r, part], wbuf[5, columns])
                grown += dot_nt(gbuf[7, r, part], wbuf[7, columns])
                if r == 1:
                    dsend[part, columns] = grown.astype(jnp.bfloat16)
                else:
                    dacc[0, part, columns] = grown
            if r == 1:
                d_copy(p).start()
        for k in range(2):
            for r in range(2):
                cacc[k, r] += dot_nn(abuf[r, :, columns], wbuf[5 + 2 * k, columns])


        @pl.when(p == 1)
        def _():
            @pl.when(inner)
            def _():
                p_sum.wait_send()

            @pl.when(jnp.logical_not(inner))
            def _():
                p_sum.wait_recv()
                sums[...] = came[places[3]]

            bank_out[bank_rows(at_x, q3)] = sums[:q3]
            x_all.start()

        @pl.when(p == 3)
        def _():
            x_all.wait()
            bank_out[bank_rows(at_y + (1 - x) * q3, q3)] = came[places[5]]
            y_all.start()

        @pl.when((p >= 1) & (p < 5))
        def _():
            sum_y(pick(slots, 7 + p), (p - 1) % 2)

        @pl.when(p == 5)
        def _():
            y_all.wait()
            bank_out[bank_rows(at_c + (1 - y) * q2, q2)] = came[places[6]]
            c_all.start()

        return carry

    lax.fori_loop(0, PIECES, last_piece, 0)

    def agrad_copy(p):
        columns = grad_part(p)
        return pltpu.make_async_copy(drecv.at[:, columns], agrad_hbm.at[:, columns], grad_sem.at[0])

    def finish_grad(p, carry):
        columns = grad_part(p)
        d_copy(p).wait_recv()
        total_here = dacc[0, :, columns] + drecv[:, columns].astype(jnp.float32)
        drecv[:, columns] = (total_here + 2.0 * dot_nn(back[...], down[:, columns])).astype(jnp.bfloat16)
        agrad_copy(p).start()
        return carry

    for slot, side in final:
        pass_core(slot, side, cacc.at[(slot - 5) // 2, side])
    for slot, side in final:
        sum_core(slot, side, cacc.at[(slot - 5) // 2, side])
    c_all.wait()
    bank_out[bank_rows((1 - c) * q1, q1)] = came[places[7]]
    bank_copy = pltpu.make_async_copy(bank_out, bank_hbm_out, load_sem.at[5])
    bank_copy.start()
    for k, target in enumerate((slope_a, slope_b)):
        values = [sums[q3 + 2 * k + m : q3 + 2 * k + m + 1, :vectors] for m in range(2)]
        mean = shares[k][0] * values[0] + shares[k][1] * values[1]
        for m in range(2):
            target[:, m, :] = from_row(shares[k][m] * (values[m] - mean))
    finish_other(0)
    finish_other(2)
    for slot, side in final:
        sum_y(slot, side)
    lax.fori_loop(0, PIECES, finish_grad, 0)
    finish_other(1)
    finish_other(3)
    def drain(buffer, semaphore):
        remote(buffer, buffer, semaphore, a_recv.at[0], p_dev).wait_send()

    a_own.wait_send()
    drain(gbuf.at[0], g_send.at[0])
    drain(gbuf.at[pl.ds(0, 3)], gm_send.at[0])
    drain(weight, xs_send.at[0])
    drain(weight, zs_send.at[0])
    drain(weight, xf_send.at[0])
    drain(dsend, d_send.at[0])

    @pl.when(inner)
    def _():
        drain(relay.at[0], relay_send.at[0])
        drain(relay.at[1], relay_send.at[1])

    @pl.when(jnp.logical_not(reduces))
    def _():
        drain(cbuf, c_send.at[0])

    @pl.when(reduces)
    def _():
        drain(cbuf.at[pl.ds(0, 4)], y_send.at[0])
        drain(cbuf.at[pl.ds(0, 2)], zc_send.at[0])

    bank_copy.wait()
    pltpu.make_async_copy(drecv, agrad_hbm, grad_sem.at[0]).wait()
    pltpu.make_async_copy(out_hbm, out_hbm, out_sem.at[0]).wait()


def settle_kernel(*refs):
    sources, targets = refs[:5], refs[5:10]
    held, held_bank, sem_in, sem_out = refs[10:]
    pieces = sem_in.shape[1]
    part = held.shape[1] // pieces

    def copies(k, p):
        rows = pl.ds(p * part, part)
        return (
            pltpu.make_async_copy(sources[k].at[rows], held.at[k, rows], sem_in.at[k, p]),
            pltpu.make_async_copy(held.at[k, rows], targets[k].at[rows], sem_out.at[k, p]),
        )

    order = [copies(k, p) for p in range(pieces) for k in range(2)]
    order.append(
        (
            pltpu.make_async_copy(sources[2], held_bank, sem_in.at[2, 0]),
            pltpu.make_async_copy(held_bank, targets[2], sem_out.at[2, 0]),
        )
    )
    for inward, _ in order:
        inward.start()
    for source, target in zip(sources[3:], targets[3:]):
        target[...] = source[...]
    for inward, outward in order:
        inward.wait()
        outward.start()
    for _, outward in order:
        outward.wait()


def fused_local(dp_size, attn_out, frozen_weight, vector_bank, logits_a, index_a, logits_b, index_b, out_grad):
    rows, depth = attn_out.shape
    width = frozen_weight.shape[1]
    half = width // 2
    levels, sublen = vector_bank.shape
    rank, per_row, _ = logits_a.shape
    vectors = rank * per_row
    own = logits_b.shape[1] * sublen
    factor = adapter_scale / (rows * dp_size)
    total = 2 * PIECES
    small = [v.transpose(1, 2, 0) for v in (logits_a, index_a, logits_b, index_b)]
    bf16, f32 = jnp.bfloat16, jnp.float32
    dma = pltpu.SemaphoreType.DMA
    hbm = pl.BlockSpec(memory_space=pl.ANY)
    vmem = pl.BlockSpec(memory_space=pltpu.VMEM)
    layer_out, attn_grad, _, bank_grad, slope_a, slope_b = pl.pallas_call(
        functools.partial(exchange_kernel, factor),
        name="exchange",
        out_shape=(
            jax.ShapeDtypeStruct((rows, own), bf16),
            jax.ShapeDtypeStruct((rows, depth), bf16),
            jax.ShapeDtypeStruct((2, 2, depth, half), bf16),
            jax.ShapeDtypeStruct((levels, sublen), f32),
            jax.ShapeDtypeStruct((per_row, 2, rank), f32),
            jax.ShapeDtypeStruct((per_row, 2, rank), f32),
        ),
        in_specs=[hbm, hbm, hbm, hbm, vmem, vmem, vmem, vmem],
        out_specs=(hbm, hbm, hbm, hbm, vmem, vmem),
        scratch_shapes=[
            pltpu.VMEM((8, depth, half), bf16),
            pltpu.VMEM((2, rows, depth), bf16),
            pltpu.VMEM((8, 2, rows, half), bf16),
            pltpu.VMEM((2, rows, depth), f32),
            pltpu.VMEM((8, 2, rows, half), bf16),
            pltpu.VMEM((4, 2, rows, half), bf16),
            pltpu.VMEM((rows, depth), bf16),
            pltpu.VMEM((rows, depth), bf16),
            pltpu.VMEM((2, 2, rows, half), f32),
            pltpu.VMEM((4, 2 * rank, rows), f32),
            pltpu.VMEM((rows, rank), bf16),
            pltpu.VMEM((rows, rank), bf16),
            pltpu.VMEM((rank, depth), bf16),
            pltpu.VMEM((rank, own), bf16),
            pltpu.VMEM((levels, sublen), f32),
            pltpu.VMEM((levels, sublen), f32),
            pltpu.VMEM((2, levels, vectors), f32),
            pltpu.VMEM((levels // 8 + 8, sublen), f32),
            pltpu.VMEM((2 * levels + 24, sublen), f32),
            dma((6,)), dma((1,)), dma((2, total)), dma((2,)), dma((total,)),
            dma((1,)), dma((total,)), dma((1,)), dma((total,)),
            dma((1,)), dma((2,)), dma((1,)), dma((1,)), dma((1,)), dma((1,)),
            dma((1,)), dma((1,)),
            dma((1,)), dma((8, 2)), dma((1,)), dma((4, 2)), dma((1,)), dma((4,)),
            dma((1,)), dma((PIECES,)), dma((1,)), dma((1,)), dma((8,)), dma((8,)),
        ],
        compiler_params=pltpu.CompilerParams(
            collective_id=0, has_side_effects=True, vmem_limit_bytes=67043328
        ),
    )(attn_out, frozen_weight, out_grad, vector_bank, *small)
    layer_out, attn_grad, bank_grad, slope_a, slope_b = pl.pallas_call(
        settle_kernel,
        name="settle",
        out_shape=[jax.ShapeDtypeStruct(v.shape, v.dtype) for v in (layer_out, attn_grad, bank_grad, slope_a, slope_b)],
        in_specs=[hbm, hbm, hbm, vmem, vmem],
        out_specs=[hbm, hbm, hbm, vmem, vmem],
        scratch_shapes=[
            pltpu.VMEM((2, rows, depth), bf16),
            pltpu.VMEM((levels, sublen), f32),
            dma((3, 4)),
            dma((3, 4)),
        ],
    )(layer_out, attn_grad, bank_grad, slope_a, slope_b)
    return (layer_out, attn_grad, bank_grad, slope_a.transpose(2, 0, 1), slope_b.transpose(2, 0, 1))


def solution(mesh):
    dp_size, tensor_size = mesh.shape["dp"], mesh.shape["tensor"]
    paired = dp_size == 2 * tensor_size and tensor_size % 2 == 0
    body = functools.partial(ring_local, dp_size, tensor_size) if paired else local
    if paired and tensor_size == 4:
        body = functools.partial(fused_local, dp_size)
    return jax.shard_map(
        body,
        mesh=mesh,
        in_specs=(
            P("dp", "tensor"),
            P("tensor", "dp"),
            P(),
            P(None, "tensor", None),
            P(None, "tensor", None),
            P(None, "tensor", None),
            P(None, "tensor", None),
            P("dp", None),
        ),
        out_specs=(
            P("dp", "tensor"),
            P("dp", "tensor"),
            P(),
            P(None, "tensor", None),
            P(None, "tensor", None),
        ),
        check_vma=False,
    )
```

```python
import functools

import jax
import jax.numpy as jnp
from jax import lax
from jax.experimental import pallas as pl
from jax.experimental.pallas import tpu as pltpu
from jax.sharding import PartitionSpec as P

adapter_scale = 2.0
ROW_PIECES = 4


def compose(logits, indices, vector_bank):
    weights = jax.nn.sigmoid(logits - logits[..., ::-1])
    levels = jnp.arange(vector_bank.shape[0], dtype=jnp.int32)
    picked = (indices[..., None] == levels).astype(jnp.float32)
    mixing = jnp.sum(picked * weights[..., None], axis=2)
    blocks = jnp.einsum("rjb,bc->rjc", mixing, vector_bank, precision=lax.Precision.HIGHEST)
    return (weights, picked, mixing, blocks.reshape(blocks.shape[0], -1))


def compose_back(grad_rows, weights, picked, mixing, vector_bank):
    blocks = grad_rows.reshape(mixing.shape[0], mixing.shape[1], -1)
    bank_part = jnp.einsum("rjb,rjc->bc", mixing, blocks, precision=lax.Precision.HIGHEST)
    projected = jnp.einsum("rjc,bc->rjb", blocks, vector_bank, precision=lax.Precision.HIGHEST)
    dots = jnp.sum(picked * projected[:, :, None, :], axis=3)
    logit_grad = weights * (dots - jnp.sum(weights * dots, axis=2, keepdims=True))
    return (bank_part, logit_grad)


def local(attn_out, frozen_weight, vector_bank, logits_a, index_a, logits_b, index_b, out_grad):
    weights_a, picked_a, mixing_a, rows_a = compose(logits_a, index_a, vector_bank)
    weights_b, picked_b, mixing_b, rows_b = compose(logits_b, index_b, vector_bank)
    down_a = rows_a.astype(jnp.bfloat16)
    up_b = rows_b.astype(jnp.bfloat16)
    own_width = up_b.shape[1]
    grad_cols = lax.dynamic_slice_in_dim(
        out_grad, lax.axis_index("tensor") * own_width, own_width, 1
    )
    low_part = jnp.dot(attn_out, down_a.T, preferred_element_type=jnp.float32)
    back_part = jnp.dot(grad_cols, up_b.T, preferred_element_type=jnp.float32)
    low_total = lax.psum(low_part, "tensor")
    low_bf = low_total.astype(jnp.bfloat16)
    gathered = lax.all_gather(frozen_weight, "dp", axis=1, tiled=True)
    partial_value = jnp.dot(attn_out, gathered, preferred_element_type=jnp.float32).astype(
        jnp.bfloat16
    )
    summed = lax.psum_scatter(partial_value, "tensor", scatter_dimension=1, tiled=True).astype(
        jnp.float32
    )
    layer_out = (
        summed + adapter_scale * jnp.dot(low_bf, up_b, preferred_element_type=jnp.float32)
    ).astype(jnp.bfloat16)
    back_total = lax.psum(back_part, "tensor")
    back_bf = back_total.astype(jnp.bfloat16)
    main = lax.dot_general(
        out_grad, gathered, (((1,), (1,)), ((), ())), preferred_element_type=jnp.float32
    )
    attn_grad = (
        main + adapter_scale * jnp.dot(back_bf, down_a, preferred_element_type=jnp.float32)
    ).astype(jnp.bfloat16)
    factor = adapter_scale / (attn_out.shape[0] * lax.axis_size("dp"))
    grad_a = factor * lax.dot_general(
        back_bf, attn_out, (((0,), (0,)), ((), ())), preferred_element_type=jnp.float32
    )
    grad_b = factor * lax.dot_general(
        low_bf, grad_cols, (((0,), (0,)), ((), ())), preferred_element_type=jnp.float32
    )
    bank_a, logit_grad_a = compose_back(grad_a, weights_a, picked_a, mixing_a, vector_bank)
    bank_b, logit_grad_b = compose_back(grad_b, weights_b, picked_b, mixing_b, vector_bank)
    bank_part = bank_a + bank_b
    bank_group = lax.psum(bank_part, "tensor")
    bank_grad, logits_a_grad, logits_b_grad = lax.psum(
        (bank_group, logit_grad_a, logit_grad_b), "dp"
    )
    return (layer_out, attn_grad, bank_grad, logits_a_grad, logits_b_grad)


def ring_local(dp_size, tensor_size, attn_out, frozen_weight, vector_bank, logits_a, index_a, logits_b, index_b, out_grad):
    depth = tensor_size
    chips = tensor_size // 2
    rows = attn_out.shape[0]
    own_width = attn_out.shape[1]
    width = frozen_weight.shape[1]
    half = width // 2
    part = own_width // ROW_PIECES
    place = lax.axis_index("dp")
    level, side = place // 2, place % 2
    tensor_index = lax.axis_index("tensor")

    ring = [(d, (d + 2) % dp_size) for d in range(dp_size)]
    swap = [(d, d ^ 1) for d in range(dp_size)]

    def hop(value):
        return lax.ppermute(value, "dp", ring)

    def cross(value):
        return lax.ppermute(value, "dp", swap)

    def collect(partial_value, step):
        target = (level - step + depth) % depth
        pairs = []
        for d in range(dp_size):
            goal = (d // 2 - step) % depth
            for chip in range(chips):
                core = 2 * chip + goal % 2
                pairs.append((d * tensor_size + (core ^ 1), d * tensor_size + core))
        other = lax.ppermute(partial_value, ("dp", "tensor"), pairs)
        paired = partial_value.astype(jnp.float32) + other.astype(jnp.float32)
        sent = paired.astype(jnp.bfloat16)
        total = paired
        for k in range(1, chips):
            pairs = []
            for d in range(dp_size):
                goal = (d // 2 - step) % depth
                source = ((goal // 2 + k) % chips) * 2 + goal % 2
                pairs.append((d * tensor_size + source, d * tensor_size + goal))
            total = total + lax.ppermute(sent, ("dp", "tensor"), pairs).astype(jnp.float32)
        return jnp.where(tensor_index == target, total, 0.0)

    first = frozen_weight[:, :half]
    later = [frozen_weight[r * part : (r + 1) * part, half:] for r in range(ROW_PIECES)]
    held = [(first, later)]
    for step in range(1, depth):
        first = hop(first)
        later = [hop(v) for v in later]
        held.append((first, later))

    attn_two = jnp.concatenate([attn_out, cross(attn_out)], axis=0)
    attn_parts = [attn_two[:, r * part : (r + 1) * part] for r in range(ROW_PIECES)]

    def grad_pair(step):
        origin = (level - step + depth) % depth
        mine = lax.dynamic_slice_in_dim(out_grad, (origin * 2 + side) * width, width, 1)
        theirs = lax.dynamic_slice_in_dim(out_grad, (origin * 2 + 1 - side) * width, width, 1)
        return jnp.concatenate([mine, cross(theirs)], axis=0)

    weights_a, picked_a, mixing_a, rows_a = compose(logits_a, index_a, vector_bank)
    weights_b, picked_b, mixing_b, rows_b = compose(logits_b, index_b, vector_bank)
    down_a = rows_a.astype(jnp.bfloat16)
    up_b = rows_b.astype(jnp.bfloat16)
    rank = down_a.shape[0]
    grad_cols = lax.dynamic_slice_in_dim(out_grad, tensor_index * own_width, own_width, 1)
    low_part = jnp.dot(attn_out, down_a.T, preferred_element_type=jnp.float32)
    back_part = jnp.dot(grad_cols, up_b.T, preferred_element_type=jnp.float32)
    both = lax.psum(jnp.concatenate([low_part, back_part], axis=1), "tensor")
    low_bf = both[:, :rank].astype(jnp.bfloat16)
    back_bf = both[:, rank:].astype(jnp.bfloat16)

    sums = [None] * ROW_PIECES
    own_total = jnp.zeros((rows, width), jnp.float32)
    cross_total = jnp.zeros((rows, width), jnp.float32)
    for step in range(depth):
        first, later = held[step]
        grads = grad_pair(step)
        out_first = jnp.dot(attn_two, first, preferred_element_type=jnp.float32)
        for r in range(ROW_PIECES):
            term = lax.dot_general(
                grads[:, :half],
                first[r * part : (r + 1) * part],
                (((1,), (1,)), ((), ())),
                preferred_element_type=jnp.float32,
            )
            sums[r] = term if sums[r] is None else sums[r] + term
        out_later = None
        for r in range(ROW_PIECES):
            term = jnp.dot(attn_parts[r], later[r], preferred_element_type=jnp.float32)
            out_later = term if out_later is None else out_later + term
            sums[r] = sums[r] + lax.dot_general(
                grads[:, half:],
                later[r],
                (((1,), (1,)), ((), ())),
                preferred_element_type=jnp.float32,
            )
        out_first = out_first.astype(jnp.bfloat16)
        out_later = out_later.astype(jnp.bfloat16)
        if step < depth - 1:
            block = collect(jnp.concatenate([out_first, out_later], axis=1), step)
            own_total = own_total + block[:rows]
            cross_total = cross_total + block[rows:]
        if step == depth - 2:
            came = cross(cross_total.astype(jnp.bfloat16)).astype(jnp.float32)
        if step == depth - 1:
            ends = [collect(out_first, step), collect(out_later, step)]
            own_end = jnp.concatenate([v[:rows] for v in ends], axis=1)
            came_end = jnp.concatenate(
                [cross(v[rows:].astype(jnp.bfloat16)) for v in ends], axis=1
            ).astype(jnp.float32)
    own_half = own_total + own_end
    other_half = came + came_end
    summed = jnp.concatenate(
        [
            jnp.where(side == 0, own_half, other_half),
            jnp.where(side == 0, other_half, own_half),
        ],
        axis=1,
    )
    layer_out = (
        summed + adapter_scale * jnp.dot(low_bf, up_b, preferred_element_type=jnp.float32)
    ).astype(jnp.bfloat16)

    adapter = adapter_scale * jnp.dot(back_bf, down_a, preferred_element_type=jnp.float32)
    pieces = []
    for r in range(ROW_PIECES):
        came_grad = cross(sums[r][rows:].astype(jnp.bfloat16)).astype(jnp.float32)
        pieces.append(sums[r][:rows] + came_grad + adapter[:, r * part : (r + 1) * part])
    attn_grad = jnp.concatenate(pieces, axis=1).astype(jnp.bfloat16)

    factor = adapter_scale / (rows * dp_size)
    grad_a = factor * lax.dot_general(
        back_bf, attn_out, (((0,), (0,)), ((), ())), preferred_element_type=jnp.float32
    )
    grad_b = factor * lax.dot_general(
        low_bf, grad_cols, (((0,), (0,)), ((), ())), preferred_element_type=jnp.float32
    )
    bank_a, logit_grad_a = compose_back(grad_a, weights_a, picked_a, mixing_a, vector_bank)
    bank_b, logit_grad_b = compose_back(grad_b, weights_b, picked_b, mixing_b, vector_bank)
    bank_grad = lax.psum(bank_a + bank_b, ("dp", "tensor"))
    logits_a_grad, logits_b_grad = lax.psum((logit_grad_a, logit_grad_b), "dp")
    return (layer_out, attn_grad, bank_grad, logits_a_grad, logits_b_grad)


MESH_ID = pl.DeviceIdType.MESH
PIECES = 8


def dot_nn(a, b):
    return jnp.dot(a, b, preferred_element_type=jnp.float32)


def dot_nt(a, b):
    return lax.dot_general(a, b, (((1,), (1,)), ((), ())), preferred_element_type=jnp.float32)


def exchange_kernel(
    factor,
    attn, weight, grad, bank_hbm, logits_a, index_a, logits_b, index_b,
    out_hbm, agrad_hbm, relay, bank_hbm_out, slope_a, slope_b,
    wbuf, abuf0, abuf1, gbuf0, gbuf1, dacc0, dacc1, cbuf0, cbuf1, ybuf0, ybuf1, dsend, drecv,
    cacc0, cacc1, lb, low, back,
    down, up, bank, bank_out, mixing, sums, came,
    load_sem, zs_send, relay_recv, relay_send, far_recv, xs_send, x_recv, xf_send, xf_recv,
    g_send, g_recv, gm_send, gm_recv, a_send, a_recv, mid_send, mid_recv, lb_send, lb_recv,
    c_send, c_recv, y_send, y_recv, zc_send, zc_recv, zm_recv, d_send, d_recv, dm_recv, out_sem, grad_sem,
    sum_send, sum_recv,
):
    rows, depth = attn.shape
    width = weight.shape[1]
    half = width // 2
    step = depth // PIECES
    few = rows // 16
    abufs, gbufs, daccs = (abuf0, abuf1), (gbuf0, gbuf1), (dacc0, dacc1)
    cbufs, caccs = (cbuf0, cbuf1), (cacc0, cacc1)
    rank = down.shape[0]
    own = up.shape[1]

    dp, t = lax.axis_index("dp"), lax.axis_index("tensor")
    z, x = dp // 2, dp % 2
    y, c = t // 2, t % 2
    zh, zl = z // 2, z % 2
    inner = (z == 1) | (z == 2)
    pz = zh * 2 + (1 - zl)
    mz = jnp.where(z == 1, 2, 1)
    x_dev = (z * 2 + (1 - x), t)
    p_dev = (pz * 2 + x, t)
    m_dev = (mz * 2 + x, t)
    c_dev = (dp, y * 2 + (1 - c))
    y_dev = (dp, (1 - y) * 2 + c)
    reduces = c == zl

    def remote(src, dst, send, recv, device):
        return pltpu.make_async_remote_copy(
            src_ref=src, dst_ref=dst, send_sem=send, recv_sem=recv,
            device_id=device, device_id_type=MESH_ID,
        )

    extra = pl.ds(rows, few)
    lead = pl.ds(0, few)

    def sent_rows(is_inner):
        return pl.ds(few, rows - few) if is_inner else pl.ds(0, rows)

    def taken_rows(is_inner):
        return sent_rows(not is_inner)

    def each_kind(act):
        for kind in (True, False):

            @pl.when(inner == kind)
            def _():
                act(kind)

    def rowsof(p):
        return pl.ds(pl.multiple_of(p * step, step), step)

    barrier = pltpu.get_barrier_semaphore()
    others = [(dp, (t + k) % 4) for k in (1, 2, 3)]
    for device in others + [x_dev, p_dev]:
        pl.semaphore_signal(barrier, inc=1, device_id=device, device_id_type=MESH_ID)

    @pl.when(inner)
    def _():
        pl.semaphore_signal(barrier, inc=1, device_id=m_dev, device_id_type=MESH_ID)

    def column_block(zz, b, xx):
        zb = jnp.where(b < 2, zz, (zz + 2) % 4)
        xb = jnp.where(b % 2 == 0, xx, 1 - xx)
        return zb * 2 + xb

    loads = [pltpu.make_async_copy(attn, abuf0, load_sem.at[0])]
    gq = pltpu.make_async_copy(
        grad.at[:, pl.ds(pl.multiple_of(t * own, own), own)], dsend.at[pl.ds(0, rows), pl.ds(0, own)], load_sem.at[1]
    )
    loads.append(gq)
    bank_load = pltpu.make_async_copy(bank_hbm, bank, load_sem.at[5])
    bank_load.start()
    for n in range(2):
        loads.append(
            pltpu.make_async_copy(weight.at[:, pl.ds(n * half, half)], wbuf.at[n], load_sem.at[2 + n])
        )
    for s in range(8):
        col = column_block(z, s // 2, x) * width + (s % 2) * half
        loads.append(
            pltpu.make_async_copy(
                grad.at[:, pl.ds(pl.multiple_of(col, half), half)], gbuf0.at[s], load_sem.at[4]
            )
        )
    for load in loads[:2]:
        load.start()

    @pl.when(inner)
    def _():
        pl.semaphore_wait(barrier, 6)

    @pl.when(jnp.logical_not(inner))
    def _():
        pl.semaphore_wait(barrier, 5)

    total = 2 * PIECES
    narrow = half // 2

    def area(n, p):
        return pl.ds(pl.multiple_of(p * step, step), step), pl.ds(0, half)

    def weight_area(n, p):
        return weight.at[area(n, p)[0], pl.ds(n * half, half)]

    def by_half(i, act):
        for n in range(2):

            @pl.when(i // PIECES == n)
            def _():
                act(n, i % PIECES)

    def x_own(n, p):
        i = n * PIECES + p
        return remote(weight_area(n, p), wbuf.at[(2 + n, *area(n, p))], xs_send.at[0], x_recv.at[i], x_dev)

    def z_own(n, p):
        i = n * PIECES + p
        stream = jnp.where(inner, 0, 1)
        device = (jnp.where(inner, mz, pz) * 2 + x, t)
        return remote(
            weight_area(n, p), relay.at[(stream, n, *area(n, p))],
            zs_send.at[0], relay_recv.at[stream, i], device,
        )

    def g_columns(zz, n):
        col = column_block(zz, t, x) * width + n * half
        return pl.ds(pl.multiple_of(col, half), half)

    def g_own(n, part):
        return remote(
            grad.at[part, g_columns(pz, n)], gbuf1.at[2 * t + n, part], g_send.at[0], g_recv.at[n], p_dev
        )

    def g_mid(n):
        return remote(
            grad.at[lead, g_columns(mz, n)], gbuf1.at[2 * t + n, extra], mid_send.at[n], mid_recv.at[n], m_dev
        )

    def a_own(part):
        return remote(attn.at[part], abuf1.at[part], a_send.at[0], a_recv.at[0], p_dev)

    a_mid = remote(attn.at[lead], abuf1.at[extra], mid_send.at[2], mid_recv.at[2], m_dev)
    early = PIECES // 2

    @pl.when(inner)
    def _():
        for n in range(2):
            g_own(n, sent_rows(True)).start()
            g_mid(n).start()
        a_own(sent_rows(True)).start()
        a_mid.start()

    @pl.when(jnp.logical_not(inner))
    def _():
        for n in range(2):
            g_own(n, sent_rows(False)).start()

        @pl.loop(0, early)
        def _(i):
            z_own(0, i).start()

        a_own(sent_rows(False)).start()

    @pl.loop(0, PIECES)
    def _(i):
        x_own(0, i).start()

        @pl.when(inner)
        def _():
            z_own(0, i).start()

    for load in loads[2:]:
        load.start()

    bank_load.wait()
    levels = bank.shape[0]
    sublen = bank.shape[1]
    vectors = mixing.shape[2]
    per_row = vectors // rank
    exact = dict(preferred_element_type=jnp.float32, precision=lax.Precision.HIGHEST)

    place = lax.broadcasted_iota(jnp.int32, (rank, vectors), 1)
    spread = (place % rank == lax.broadcasted_iota(jnp.int32, (rank, vectors), 0)).astype(jnp.float32)
    place = lax.broadcasted_iota(jnp.int32, (per_row, vectors), 1)
    keep = place // rank == lax.broadcasted_iota(jnp.int32, (per_row, vectors), 0)
    level = lax.broadcasted_iota(jnp.int32, (levels, vectors), 0)

    def as_row(value):
        wide_value = jnp.dot(value.astype(jnp.float32), spread, **exact)
        return jnp.sum(jnp.where(keep, wide_value, 0.0), axis=0, keepdims=True)

    def from_row(row):
        return lax.dot_general(jnp.where(keep, row, 0.0), spread, (((1,), (1,)), ((), ())), **exact)

    shares, found = [], []
    for k, (logits, indices) in enumerate(((logits_a, index_a), (logits_b, index_b))):
        first, second = as_row(logits[:, 0, :]), as_row(logits[:, 1, :])
        shares.append((1.0 / (1.0 + jnp.exp(second - first)), 1.0 / (1.0 + jnp.exp(first - second))))
        picks = [(as_row(indices[:, m, :]) + 0.5).astype(jnp.int32) for m in range(2)]
        found.append([level == pick for pick in picks])

    for k, target in enumerate((down, up)):
        mixing[k] = sum(jnp.where(found[k][m], shares[k][m], 0.0) for m in range(2))
        blocks = lax.dot_general(mixing[k], bank[...], (((0,), (0,)), ((), ())), **exact)
        for j in range(per_row):
            row = blocks[j * rank : (j + 1) * rank]
            target[:, j * sublen : (j + 1) * sublen] = row.astype(jnp.bfloat16)

    loads[0].wait()
    loads[1].wait()
    lb[t, :rank] = dot_nt(down[...], abuf0[...])
    lb[t, rank:] = dot_nt(up[...], dsend[:rows, :own])

    def lb_copy(k):
        device = (dp, (t + k) % 4)
        return remote(lb.at[t], lb.at[t], lb_send.at[0], lb_recv.at[0], device)

    for k in (1, 2, 3):
        lb_copy(k).start()
    for load in loads[2:4]:
        load.wait()
    pltpu.make_async_copy(gbuf0, gbuf0, load_sem.at[4]).wait()
    dacc0[...] = jnp.zeros_like(dacc0)
    dacc1[...] = jnp.zeros_like(dacc1)

    @pl.when(jnp.logical_not(inner))
    def _():
        for part in (lead, extra):
            abuf1[part] = jnp.zeros_like(abuf1[part])
            gbuf1[:, part] = jnp.zeros_like(gbuf1[:, part])

    three = lb.at[pl.ds(0, 3)]
    remote(three, three, lb_send.at[0], lb_recv.at[0], y_dev).wait()
    both = lb[0] + lb[1] + lb[2] + lb[3]
    low[...] = both[:rank].T.astype(jnp.bfloat16)
    back[...] = both[rank:].T.astype(jnp.bfloat16)
    both = both.astype(jnp.bfloat16)
    slopes = (
        factor * dot_nn(both[rank:], abuf0[...]),
        factor * dot_nn(both[:rank], dsend[:rows, :own]),
    )
    bank_out[...] = jnp.zeros_like(bank_out)
    dots = []
    for k in range(2):
        pieces = [slopes[k][:, j * sublen : (j + 1) * sublen] for j in range(per_row)]
        stacked = jnp.concatenate(pieces, axis=0)
        bank_out[...] += jnp.dot(mixing[k], stacked, **exact)
        projected = lax.dot_general(bank[...], stacked, (((1,), (1,)), ((), ())), **exact)
        for m in range(2):
            dots.append(jnp.sum(jnp.where(found[k][m], projected, 0.0), axis=0, keepdims=True))

    q1, q2, q3 = levels // 2, levels // 4, levels // 8
    pack = q3 + 8
    at_c = c * q1
    at_y = at_c + y * q2
    at_x = at_y + x * q3
    counts = (q1, q2, pack, pack, pack, q3, q2, q1)
    places = [pl.ds(sum(counts[:k]), counts[k]) for k in range(8)]

    def bank_rows(start, count):
        return pl.ds(pl.multiple_of(start, 8), count)

    def sum_copy(k, source, device):
        return remote(source, came.at[places[k]], sum_send.at[k], sum_recv.at[k], device)

    core_sum = sum_copy(0, bank_out.at[bank_rows((1 - c) * q1, q1)], c_dev)
    y_sum = sum_copy(1, bank_out.at[bank_rows(at_c + (1 - y) * q2, q2)], y_dev)
    x_sum = sum_copy(2, sums, x_dev)
    p_sum = sum_copy(3, sums, p_dev)
    m_sum = sum_copy(4, sums, m_dev)
    x_all = sum_copy(5, bank_out.at[bank_rows(at_x, q3)], x_dev)
    y_all = sum_copy(6, bank_out.at[bank_rows(at_y, q2)], y_dev)
    c_all = sum_copy(7, bank_out.at[bank_rows(at_c, q1)], c_dev)
    core_sum.start()
    core_sum.wait()
    bank_out[bank_rows(at_c, q1)] += came[places[0]]
    y_sum.start()
    y_sum.wait()
    bank_out[bank_rows(at_y, q2)] += came[places[1]]
    sums[:q3] = bank_out[bank_rows(at_y + (1 - x) * q3, q3)]
    sums[q3:] = jnp.zeros_like(sums[q3:])
    for k in range(4):
        sums[q3 + k : q3 + k + 1, :vectors] = dots[k]
    x_sum.start()

    @pl.loop(0, PIECES)
    def _(i):
        x_own(1, i).start()

    def relay_on(stream, n, p):
        i = n * PIECES + p
        device = (jnp.where(stream == 0, pz, mz) * 2 + x, t)
        return remote(
            relay.at[(stream, n, *area(n, p))], wbuf.at[(4 + n, *area(n, p))],
            relay_send.at[stream], far_recv.at[i], device,
        )

    def relay_wait(stream, n, p):
        i = n * PIECES + p
        piece = relay.at[(stream, n, *area(n, p))]
        remote(piece, piece, relay_send.at[stream], relay_recv.at[stream, i], p_dev).wait_recv()

    def x_far(n, p):
        i = n * PIECES + p
        return remote(
            wbuf.at[(4 + n, *area(n, p))], wbuf.at[(6 + n, *area(n, p))], xf_send.at[0], xf_recv.at[i], x_dev
        )

    def far_wait(n, p):
        i = n * PIECES + p
        piece = wbuf.at[(4 + n, *area(n, p))]
        remote(piece, piece, xf_send.at[0], far_recv.at[i], x_dev).wait_recv()

    def g_spread(k, n, is_inner):
        part = pl.ds(0, rows + few) if is_inner else taken_rows(False)
        piece = gbuf1.at[2 * t + n, part]
        return remote(piece, piece, gm_send.at[0], gm_recv.at[0], (dp, (t + k) % 4))

    def g_everything(is_inner):
        part = pl.ds(0, rows + few) if is_inner else taken_rows(False)
        return gbuf1.at[pl.ds(0, 6), part]

    ticks = 33

    def tick(i, carry):
        def near(n, p):
            x_own(n, p).wait_recv()

        @pl.when(i < total)
        def _():
            by_half(i, near)

        def outward(n, p):
            relay_wait(0, n, p)
            relay_on(0, n, p).start()

        @pl.when(inner & (i >= 2) & (i < 2 + PIECES))
        def _():
            outward(0, i - 2)

        @pl.when(inner & (i >= 15) & (i < 15 + PIECES))
        def _():
            outward(1, i - 15)

        def onward(n, p):
            relay_wait(1, n, p)
            relay_on(1, n, p).start()

        @pl.when(inner & (i >= 5) & (i < 5 + early))
        def _():
            onward(0, i - 5)

        @pl.when(inner & (i >= 16) & (i < 12 + total))
        def _():
            by_half(i - 12, onward)

        @pl.when(i == PIECES)
        def _():
            x_sum.wait()
            sums[:q3] = bank_out[bank_rows(at_x, q3)] + came[places[2]][:q3]
            sums[q3:] += came[places[2]][q3:]

            @pl.when(jnp.logical_not(inner))
            def _():
                p_sum.start()

                @pl.loop(early, PIECES)
                def _(k):
                    z_own(0, k).start()

            @pl.loop(0, PIECES)
            def _(k):
                z_own(1, k).start()

        @pl.when(i == 16)
        def _():
            @pl.when(jnp.logical_not(inner))
            def _():
                p_sum.wait_send()

            @pl.when(inner)
            def _():
                p_sum.wait_recv()
                sums[...] += came[places[3]]
                m_sum.start()

        @pl.when((i == 23) & inner)
        def _():
            m_sum.wait()
            sums[...] += came[places[4]]
            p_sum.start()

        @pl.when(i == 4)
        def _():
            def spread(is_inner):
                for n in range(2):
                    g_own(n, taken_rows(is_inner)).wait_recv()
                    if is_inner:
                        g_mid(n).wait_recv()
                    for k in (1, 2, 3):
                        g_spread(k, n, is_inner).start()

            each_kind(spread)

        def far(n, p):
            far_wait(n, p)
            x_far(n, p).start()

        wait = jnp.where(inner & (i >= 21), 17, 12)

        @pl.when((i >= 12) & (i - wait < total) & (jnp.logical_not(inner) | (i < 16) | (i >= 21)))
        def _():
            by_half(i - wait, far)

        return carry

    def c_copy(s, r):
        piece = cbufs[r].at[s]
        return remote(piece, piece, c_send.at[r], c_recv.at[s, r], c_dev)

    def y_copy(s, r):
        j = s % 4
        target = (ybuf0, ybuf1)[r].at[j]
        return remote(cbufs[r].at[s], target, y_send.at[r], y_recv.at[j, r], y_dev)

    def z_copy(s, part):
        j = s % 4
        return remote(cbuf1.at[s, part], ybuf0.at[j, part], zc_send.at[0], zc_recv.at[j], p_dev)

    def z_mid(s):
        j = s % 4
        return remote(cbuf1.at[s, extra], ybuf0.at[j, lead], zc_send.at[1], zm_recv.at[j], m_dev)

    def kept(s):
        return jnp.where(s < 4, zh, 1 - zh) == y

    def out_columns(j):
        xb = jnp.where(j < 2, x, 1 - x)
        return pl.ds(pl.multiple_of(xb * width + (j % 2) * half, half), half)

    def out_copy(j):
        return pltpu.make_async_copy(ybuf0.at[j], out_hbm.at[:, out_columns(j)], out_sem.at[0])

    def adapter_out(j):
        return 2.0 * dot_nn(low[...], up[:, out_columns(j)])

    def by_side(r, act):
        if isinstance(r, int):
            act(r)
            return
        for side in range(2):

            @pl.when(r == side)
            def _():
                act(side)

    def pass_core(s, r, k):
        @pl.when(jnp.logical_not(reduces))
        def _():
            cbufs[r][s] = caccs[r][k].astype(jnp.bfloat16)
            c_copy(s, r).start()

    def sum_core(s, r, k):
        def act(r):
            c_copy(s, r).wait_recv()
            cbufs[r][s] = (caccs[r][k] + cbufs[r][s].astype(jnp.float32)).astype(jnp.bfloat16)

            @pl.when(jnp.logical_not(kept(s)))
            def _():
                y_copy(s, r).start()

        @pl.when(reduces)
        def _():
            by_side(r, act)

    def sum_y(s, r):
        j = s % 4

        def act(r):
            y_copy(s, r).wait_recv()
            came_here = (ybuf0, ybuf1)[r][j].astype(jnp.float32)
            total_here = cbufs[r][s].astype(jnp.float32) + came_here
            if r == 0:
                ybuf0[j] = (total_here + adapter_out(j)).astype(jnp.bfloat16)
                out_copy(j).start()
            else:
                cbuf1[s] = total_here.astype(jnp.bfloat16)
                each_kind(lambda is_inner: z_copy(s, taken_rows(is_inner)).start())

                @pl.when(inner)
                def _():
                    z_mid(s).start()

        @pl.when(reduces & kept(s))
        def _():
            by_side(r, act)

    def finish_other(j):
        @pl.when(jnp.logical_not(reduces))
        def _():
            each_kind(lambda is_inner: z_copy(j, sent_rows(is_inner)).wait_recv())

            @pl.when(inner)
            def _():
                z_mid(j).wait_recv()

            ybuf0[j] = (ybuf0[j].astype(jnp.float32) + adapter_out(j)).astype(jnp.bfloat16)
            out_copy(j).start()

    slots = (0, 1, 2, 0, 1, 2, 3, 3, 4, 4, 6, 6)
    sides = (0, 0, 0, 1, 1, 1, 0, 1, 0, 1, 0, 1)

    def pick(table, u):
        if isinstance(u, int):
            return table[u]
        value = table[0]
        for k in range(1, len(table)):
            if table[k] != table[k - 1]:
                value = jnp.where(u >= k, table[k], value)
        return value

    def ready(u):
        value = jnp.where(u >= 2, PIECES, 0)
        value = jnp.where(u >= 3, 16, value)
        value = jnp.where(u >= 8, jnp.where(inner, 25, 20), value)
        return jnp.where(u >= 10, 26, value)

    def tiles(r):
        count = rows + few * r
        return [pl.ds(m * (count // 2), count // 2) for m in range(2)]

    def unit(u, carry):
        s, r = pick(slots, u), pick(sides, u)
        lax.fori_loop(ready(u - 1), ready(u), tick, 0)

        @pl.when(u == 3)
        def _():
            def arrived(is_inner):
                a_own(taken_rows(is_inner)).wait_recv()
                if is_inner:
                    a_mid.wait_recv()
                everything = g_everything(is_inner)
                remote(everything, everything, gm_send.at[0], gm_recv.at[0], y_dev).wait_recv()

            each_kind(arrived)

        @pl.when(u == 10)
        def _():
            for p in range(PIECES):
                x_far(0, p).wait_recv()


        def act(r):
            for part in tiles(r):
                caccs[r][u % 2, part] = dot_nn(abufs[r][part], wbuf[s])
                daccs[r][part] += dot_nt(gbufs[r][s, part], wbuf[s])
            pass_core(s, r, u % 2)

        by_side(r, act)

        @pl.when(u >= 1)
        def _():
            sum_core(pick(slots, u - 1), pick(sides, u - 1), (u - 1) % 2)

        @pl.when(u >= 4)
        def _():
            sum_y(pick(slots, u - 4), pick(sides, u - 4))

        return carry

    lax.fori_loop(0, 12, unit, 0)
    sum_core(slots[11], sides[11], 1)
    cacc0[...] = jnp.zeros_like(cacc0)
    cacc1[...] = jnp.zeros_like(cacc1)

    final = ((7, 1), (7, 0))

    def grad_part(p):
        return pl.ds(pl.multiple_of(p * step, step), step)

    def d_copy(p, part):
        columns = grad_part(p)
        return remote(dsend.at[part, columns], drecv.at[part, columns], d_send.at[0], d_recv.at[p], p_dev)

    def d_mid(p):
        columns = grad_part(p)
        return remote(dsend.at[extra, columns], drecv.at[lead, columns], d_send.at[1], dm_recv.at[p], m_dev)

    def last_piece(p, carry):
        done = 26 + p
        lax.fori_loop(jnp.minimum(done, ticks), jnp.minimum(done + 1, ticks), tick, 0)

        def ahead(p):
            columns = grad_part(p)
            for r in range(2):
                caccs[r][0] += dot_nn(abufs[r][:, columns], wbuf[5, columns])

        @pl.when(p == 0)
        def _():
            ahead(0)

        @pl.when(p < PIECES - 1)
        def _():
            ahead(p + 1)

        @pl.when(p == PIECES - 2)
        def _():
            for side in (1, 0):
                pass_core(5, side, 0)

        x_far(1, p).wait_recv()
        columns = grad_part(p)
        for r in (1, 0):
            for part in tiles(r):
                grown = daccs[r][part, columns]
                grown += dot_nt(gbufs[r][5, part], wbuf[5, columns])
                grown += dot_nt(gbufs[r][7, part], wbuf[7, columns])
                if r == 1:
                    dsend[part, columns] = grown.astype(jnp.bfloat16)
                else:
                    dacc0[part, columns] = grown
            if r == 1:
                each_kind(lambda is_inner: d_copy(p, taken_rows(is_inner)).start())

                @pl.when(inner)
                def _():
                    d_mid(p).start()

        for r in range(2):
            caccs[r][1] += dot_nn(abufs[r][:, columns], wbuf[7, columns])

        @pl.when(p == PIECES - 2)
        def _():
            for side in (1, 0):
                sum_core(5, side, 0)


        @pl.when(p == 1)
        def _():
            @pl.when(inner)
            def _():
                p_sum.wait_send()

            @pl.when(jnp.logical_not(inner))
            def _():
                p_sum.wait_recv()
                sums[...] = came[places[3]]

            bank_out[bank_rows(at_x, q3)] = sums[:q3]
            x_all.start()

        @pl.when(p == 3)
        def _():
            x_all.wait()
            bank_out[bank_rows(at_y + (1 - x) * q3, q3)] = came[places[5]]
            y_all.start()

        @pl.when((p >= 1) & (p < 5))
        def _():
            sum_y(pick(slots, 7 + p), (p - 1) % 2)

        @pl.when(p == 5)
        def _():
            y_all.wait()
            bank_out[bank_rows(at_c + (1 - y) * q2, q2)] = came[places[6]]
            c_all.start()

        return carry

    lax.fori_loop(0, PIECES, last_piece, 0)

    def agrad_copy(p):
        columns = grad_part(p)
        return pltpu.make_async_copy(drecv.at[:, columns], agrad_hbm.at[:, columns], grad_sem.at[0])

    def finish_grad(p, carry):
        columns = grad_part(p)
        each_kind(lambda is_inner: d_copy(p, sent_rows(is_inner)).wait_recv())

        @pl.when(inner)
        def _():
            d_mid(p).wait_recv()

        total_here = dacc0[:, columns] + drecv[:, columns].astype(jnp.float32)
        drecv[:, columns] = (total_here + 2.0 * dot_nn(back[...], down[:, columns])).astype(jnp.bfloat16)
        agrad_copy(p).start()
        return carry

    for slot, side in final:
        pass_core(slot, side, 1)
    for slot, side in final:
        sum_core(slot, side, 1)
    c_all.wait()
    bank_out[bank_rows((1 - c) * q1, q1)] = came[places[7]]
    bank_copy = pltpu.make_async_copy(bank_out, bank_hbm_out, load_sem.at[5])
    bank_copy.start()
    for k, target in enumerate((slope_a, slope_b)):
        values = [sums[q3 + 2 * k + m : q3 + 2 * k + m + 1, :vectors] for m in range(2)]
        mean = shares[k][0] * values[0] + shares[k][1] * values[1]
        for m in range(2):
            target[:, m, :] = from_row(shares[k][m] * (values[m] - mean))
    finish_other(0)
    finish_other(2)
    for slot, side in ((5, 1), (5, 0), (7, 1), (7, 0)):
        sum_y(slot, side)
    lax.fori_loop(0, PIECES, finish_grad, 0)
    finish_other(1)
    finish_other(3)
    def drain(buffer, semaphore):
        remote(buffer, buffer, semaphore, a_recv.at[0], p_dev).wait_send()

    def drain_kind(is_inner):
        a_own(sent_rows(is_inner)).wait_send()
        drain(gbuf1.at[pl.ds(0, 2), sent_rows(is_inner)], g_send.at[0])
        drain(g_everything(is_inner), gm_send.at[0])
        drain(dsend.at[taken_rows(is_inner)], d_send.at[0])
        if is_inner:
            a_mid.wait_send()
            for n in range(2):
                g_mid(n).wait_send()
                drain(relay.at[n], relay_send.at[n])
            drain(dsend.at[extra], d_send.at[1])

        @pl.when(reduces)
        def _():
            drain(gbuf1.at[pl.ds(0, 4), taken_rows(is_inner)], zc_send.at[0])
            if is_inner:
                drain(gbuf1.at[pl.ds(0, 4), extra], zc_send.at[1])

    each_kind(drain_kind)
    drain(weight, xs_send.at[0])
    drain(weight, zs_send.at[0])
    drain(weight, xf_send.at[0])

    @pl.when(jnp.logical_not(reduces))
    def _():
        for r in range(2):
            drain(cbufs[r], c_send.at[r])

    @pl.when(reduces)
    def _():
        for r in range(2):
            drain(cbufs[r].at[pl.ds(0, 4)], y_send.at[r])

    bank_copy.wait()
    pltpu.make_async_copy(drecv, agrad_hbm, grad_sem.at[0]).wait()
    pltpu.make_async_copy(out_hbm, out_hbm, out_sem.at[0]).wait()


def settle_kernel(*refs):
    sources, targets = refs[:5], refs[5:10]
    held, held_bank, sem_in, sem_out = refs[10:]
    pieces = sem_in.shape[1]
    part = held.shape[1] // pieces

    def copies(k, p):
        rows = pl.ds(p * part, part)
        return (
            pltpu.make_async_copy(sources[k].at[rows], held.at[k, rows], sem_in.at[k, p]),
            pltpu.make_async_copy(held.at[k, rows], targets[k].at[rows], sem_out.at[k, p]),
        )

    order = [copies(k, p) for p in range(pieces) for k in range(2)]
    order.append(
        (
            pltpu.make_async_copy(sources[2], held_bank, sem_in.at[2, 0]),
            pltpu.make_async_copy(held_bank, targets[2], sem_out.at[2, 0]),
        )
    )
    for inward, _ in order:
        inward.start()
    for source, target in zip(sources[3:], targets[3:]):
        target[...] = source[...]
    for inward, outward in order:
        inward.wait()
        outward.start()
    for _, outward in order:
        outward.wait()


def fused_local(dp_size, attn_out, frozen_weight, vector_bank, logits_a, index_a, logits_b, index_b, out_grad):
    rows, depth = attn_out.shape
    width = frozen_weight.shape[1]
    half = width // 2
    levels, sublen = vector_bank.shape
    rank, per_row, _ = logits_a.shape
    vectors = rank * per_row
    own = logits_b.shape[1] * sublen
    factor = adapter_scale / (rows * dp_size)
    total = 2 * PIECES
    more = rows + rows // 16
    small = [v.transpose(1, 2, 0) for v in (logits_a, index_a, logits_b, index_b)]
    bf16, f32 = jnp.bfloat16, jnp.float32
    dma = pltpu.SemaphoreType.DMA
    hbm = pl.BlockSpec(memory_space=pl.ANY)
    vmem = pl.BlockSpec(memory_space=pltpu.VMEM)
    layer_out, attn_grad, _, bank_grad, slope_a, slope_b = pl.pallas_call(
        functools.partial(exchange_kernel, factor),
        name="exchange",
        out_shape=(
            jax.ShapeDtypeStruct((rows, own), bf16),
            jax.ShapeDtypeStruct((rows, depth), bf16),
            jax.ShapeDtypeStruct((2, 2, depth, half), bf16),
            jax.ShapeDtypeStruct((levels, sublen), f32),
            jax.ShapeDtypeStruct((per_row, 2, rank), f32),
            jax.ShapeDtypeStruct((per_row, 2, rank), f32),
        ),
        in_specs=[hbm, hbm, hbm, hbm, vmem, vmem, vmem, vmem],
        out_specs=(hbm, hbm, hbm, hbm, vmem, vmem),
        scratch_shapes=[
            pltpu.VMEM((8, depth, half), bf16),
            pltpu.VMEM((rows, depth), bf16),
            pltpu.VMEM((more, depth), bf16),
            pltpu.VMEM((8, rows, half), bf16),
            pltpu.VMEM((8, more, half), bf16),
            pltpu.VMEM((rows, depth), f32),
            pltpu.VMEM((more, depth), f32),
            pltpu.VMEM((8, rows, half), bf16),
            pltpu.VMEM((8, more, half), bf16),
            pltpu.VMEM((4, rows, half), bf16),
            pltpu.VMEM((4, more, half), bf16),
            pltpu.VMEM((more, depth), bf16),
            pltpu.VMEM((rows, depth), bf16),
            pltpu.VMEM((2, rows, half), f32),
            pltpu.VMEM((2, more, half), f32),
            pltpu.VMEM((4, 2 * rank, rows), f32),
            pltpu.VMEM((rows, rank), bf16),
            pltpu.VMEM((rows, rank), bf16),
            pltpu.VMEM((rank, depth), bf16),
            pltpu.VMEM((rank, own), bf16),
            pltpu.VMEM((levels, sublen), f32),
            pltpu.VMEM((levels, sublen), f32),
            pltpu.VMEM((2, levels, vectors), f32),
            pltpu.VMEM((levels // 8 + 8, sublen), f32),
            pltpu.VMEM((2 * levels + 24, sublen), f32),
            dma((6,)), dma((1,)), dma((2, total)), dma((2,)), dma((total,)),
            dma((1,)), dma((total,)), dma((1,)), dma((total,)),
            dma((1,)), dma((2,)), dma((1,)), dma((1,)), dma((1,)), dma((1,)), dma((3,)), dma((3,)),
            dma((1,)), dma((1,)),
            dma((2,)), dma((8, 2)), dma((2,)), dma((4, 2)), dma((2,)), dma((4,)), dma((4,)),
            dma((2,)), dma((PIECES,)), dma((PIECES,)), dma((1,)), dma((1,)), dma((8,)), dma((8,)),
        ],
        compiler_params=pltpu.CompilerParams(
            collective_id=0, has_side_effects=True, vmem_limit_bytes=67043328
        ),
    )(attn_out, frozen_weight, out_grad, vector_bank, *small)
    layer_out, attn_grad, bank_grad, slope_a, slope_b = pl.pallas_call(
        settle_kernel,
        name="settle",
        out_shape=[jax.ShapeDtypeStruct(v.shape, v.dtype) for v in (layer_out, attn_grad, bank_grad, slope_a, slope_b)],
        in_specs=[hbm, hbm, hbm, vmem, vmem],
        out_specs=[hbm, hbm, hbm, vmem, vmem],
        scratch_shapes=[
            pltpu.VMEM((2, rows, depth), bf16),
            pltpu.VMEM((levels, sublen), f32),
            dma((3, 4)),
            dma((3, 4)),
        ],
    )(layer_out, attn_grad, bank_grad, slope_a, slope_b)
    return (layer_out, attn_grad, bank_grad, slope_a.transpose(2, 0, 1), slope_b.transpose(2, 0, 1))


def solution(mesh):
    dp_size, tensor_size = mesh.shape["dp"], mesh.shape["tensor"]
    paired = dp_size == 2 * tensor_size and tensor_size % 2 == 0
    body = functools.partial(ring_local, dp_size, tensor_size) if paired else local
    if paired and tensor_size == 4:
        body = functools.partial(fused_local, dp_size)
    return jax.shard_map(
        body,
        mesh=mesh,
        in_specs=(
            P("dp", "tensor"),
            P("tensor", "dp"),
            P(),
            P(None, "tensor", None),
            P(None, "tensor", None),
            P(None, "tensor", None),
            P(None, "tensor", None),
            P("dp", None),
        ),
        out_specs=(
            P("dp", "tensor"),
            P("dp", "tensor"),
            P(),
            P(None, "tensor", None),
            P(None, "tensor", None),
        ),
        check_vma=False,
    )
```

```python
import functools

import jax
import jax.numpy as jnp
from jax import lax
from jax.experimental import pallas as pl
from jax.experimental.pallas import tpu as pltpu
from jax.sharding import PartitionSpec as P

adapter_scale = 2.0
ROW_PIECES = 4


def compose(logits, indices, vector_bank):
    weights = jax.nn.sigmoid(logits - logits[..., ::-1])
    levels = jnp.arange(vector_bank.shape[0], dtype=jnp.int32)
    picked = (indices[..., None] == levels).astype(jnp.float32)
    mixing = jnp.sum(picked * weights[..., None], axis=2)
    blocks = jnp.einsum("rjb,bc->rjc", mixing, vector_bank, precision=lax.Precision.HIGHEST)
    return (weights, picked, mixing, blocks.reshape(blocks.shape[0], -1))


def compose_back(grad_rows, weights, picked, mixing, vector_bank):
    blocks = grad_rows.reshape(mixing.shape[0], mixing.shape[1], -1)
    bank_part = jnp.einsum("rjb,rjc->bc", mixing, blocks, precision=lax.Precision.HIGHEST)
    projected = jnp.einsum("rjc,bc->rjb", blocks, vector_bank, precision=lax.Precision.HIGHEST)
    dots = jnp.sum(picked * projected[:, :, None, :], axis=3)
    logit_grad = weights * (dots - jnp.sum(weights * dots, axis=2, keepdims=True))
    return (bank_part, logit_grad)


def local(attn_out, frozen_weight, vector_bank, logits_a, index_a, logits_b, index_b, out_grad):
    weights_a, picked_a, mixing_a, rows_a = compose(logits_a, index_a, vector_bank)
    weights_b, picked_b, mixing_b, rows_b = compose(logits_b, index_b, vector_bank)
    down_a = rows_a.astype(jnp.bfloat16)
    up_b = rows_b.astype(jnp.bfloat16)
    own_width = up_b.shape[1]
    grad_cols = lax.dynamic_slice_in_dim(
        out_grad, lax.axis_index("tensor") * own_width, own_width, 1
    )
    low_part = jnp.dot(attn_out, down_a.T, preferred_element_type=jnp.float32)
    back_part = jnp.dot(grad_cols, up_b.T, preferred_element_type=jnp.float32)
    low_total = lax.psum(low_part, "tensor")
    low_bf = low_total.astype(jnp.bfloat16)
    gathered = lax.all_gather(frozen_weight, "dp", axis=1, tiled=True)
    partial_value = jnp.dot(attn_out, gathered, preferred_element_type=jnp.float32).astype(
        jnp.bfloat16
    )
    summed = lax.psum_scatter(partial_value, "tensor", scatter_dimension=1, tiled=True).astype(
        jnp.float32
    )
    layer_out = (
        summed + adapter_scale * jnp.dot(low_bf, up_b, preferred_element_type=jnp.float32)
    ).astype(jnp.bfloat16)
    back_total = lax.psum(back_part, "tensor")
    back_bf = back_total.astype(jnp.bfloat16)
    main = lax.dot_general(
        out_grad, gathered, (((1,), (1,)), ((), ())), preferred_element_type=jnp.float32
    )
    attn_grad = (
        main + adapter_scale * jnp.dot(back_bf, down_a, preferred_element_type=jnp.float32)
    ).astype(jnp.bfloat16)
    factor = adapter_scale / (attn_out.shape[0] * lax.axis_size("dp"))
    grad_a = factor * lax.dot_general(
        back_bf, attn_out, (((0,), (0,)), ((), ())), preferred_element_type=jnp.float32
    )
    grad_b = factor * lax.dot_general(
        low_bf, grad_cols, (((0,), (0,)), ((), ())), preferred_element_type=jnp.float32
    )
    bank_a, logit_grad_a = compose_back(grad_a, weights_a, picked_a, mixing_a, vector_bank)
    bank_b, logit_grad_b = compose_back(grad_b, weights_b, picked_b, mixing_b, vector_bank)
    bank_part = bank_a + bank_b
    bank_group = lax.psum(bank_part, "tensor")
    bank_grad, logits_a_grad, logits_b_grad = lax.psum(
        (bank_group, logit_grad_a, logit_grad_b), "dp"
    )
    return (layer_out, attn_grad, bank_grad, logits_a_grad, logits_b_grad)


def ring_local(dp_size, tensor_size, attn_out, frozen_weight, vector_bank, logits_a, index_a, logits_b, index_b, out_grad):
    depth = tensor_size
    chips = tensor_size // 2
    rows = attn_out.shape[0]
    own_width = attn_out.shape[1]
    width = frozen_weight.shape[1]
    half = width // 2
    part = own_width // ROW_PIECES
    place = lax.axis_index("dp")
    level, side = place // 2, place % 2
    tensor_index = lax.axis_index("tensor")

    ring = [(d, (d + 2) % dp_size) for d in range(dp_size)]
    swap = [(d, d ^ 1) for d in range(dp_size)]

    def hop(value):
        return lax.ppermute(value, "dp", ring)

    def cross(value):
        return lax.ppermute(value, "dp", swap)

    def collect(partial_value, step):
        target = (level - step + depth) % depth
        pairs = []
        for d in range(dp_size):
            goal = (d // 2 - step) % depth
            for chip in range(chips):
                core = 2 * chip + goal % 2
                pairs.append((d * tensor_size + (core ^ 1), d * tensor_size + core))
        other = lax.ppermute(partial_value, ("dp", "tensor"), pairs)
        paired = partial_value.astype(jnp.float32) + other.astype(jnp.float32)
        sent = paired.astype(jnp.bfloat16)
        total = paired
        for k in range(1, chips):
            pairs = []
            for d in range(dp_size):
                goal = (d // 2 - step) % depth
                source = ((goal // 2 + k) % chips) * 2 + goal % 2
                pairs.append((d * tensor_size + source, d * tensor_size + goal))
            total = total + lax.ppermute(sent, ("dp", "tensor"), pairs).astype(jnp.float32)
        return jnp.where(tensor_index == target, total, 0.0)

    first = frozen_weight[:, :half]
    later = [frozen_weight[r * part : (r + 1) * part, half:] for r in range(ROW_PIECES)]
    held = [(first, later)]
    for step in range(1, depth):
        first = hop(first)
        later = [hop(v) for v in later]
        held.append((first, later))

    attn_two = jnp.concatenate([attn_out, cross(attn_out)], axis=0)
    attn_parts = [attn_two[:, r * part : (r + 1) * part] for r in range(ROW_PIECES)]

    def grad_pair(step):
        origin = (level - step + depth) % depth
        mine = lax.dynamic_slice_in_dim(out_grad, (origin * 2 + side) * width, width, 1)
        theirs = lax.dynamic_slice_in_dim(out_grad, (origin * 2 + 1 - side) * width, width, 1)
        return jnp.concatenate([mine, cross(theirs)], axis=0)

    weights_a, picked_a, mixing_a, rows_a = compose(logits_a, index_a, vector_bank)
    weights_b, picked_b, mixing_b, rows_b = compose(logits_b, index_b, vector_bank)
    down_a = rows_a.astype(jnp.bfloat16)
    up_b = rows_b.astype(jnp.bfloat16)
    rank = down_a.shape[0]
    grad_cols = lax.dynamic_slice_in_dim(out_grad, tensor_index * own_width, own_width, 1)
    low_part = jnp.dot(attn_out, down_a.T, preferred_element_type=jnp.float32)
    back_part = jnp.dot(grad_cols, up_b.T, preferred_element_type=jnp.float32)
    both = lax.psum(jnp.concatenate([low_part, back_part], axis=1), "tensor")
    low_bf = both[:, :rank].astype(jnp.bfloat16)
    back_bf = both[:, rank:].astype(jnp.bfloat16)

    sums = [None] * ROW_PIECES
    own_total = jnp.zeros((rows, width), jnp.float32)
    cross_total = jnp.zeros((rows, width), jnp.float32)
    for step in range(depth):
        first, later = held[step]
        grads = grad_pair(step)
        out_first = jnp.dot(attn_two, first, preferred_element_type=jnp.float32)
        for r in range(ROW_PIECES):
            term = lax.dot_general(
                grads[:, :half],
                first[r * part : (r + 1) * part],
                (((1,), (1,)), ((), ())),
                preferred_element_type=jnp.float32,
            )
            sums[r] = term if sums[r] is None else sums[r] + term
        out_later = None
        for r in range(ROW_PIECES):
            term = jnp.dot(attn_parts[r], later[r], preferred_element_type=jnp.float32)
            out_later = term if out_later is None else out_later + term
            sums[r] = sums[r] + lax.dot_general(
                grads[:, half:],
                later[r],
                (((1,), (1,)), ((), ())),
                preferred_element_type=jnp.float32,
            )
        out_first = out_first.astype(jnp.bfloat16)
        out_later = out_later.astype(jnp.bfloat16)
        if step < depth - 1:
            block = collect(jnp.concatenate([out_first, out_later], axis=1), step)
            own_total = own_total + block[:rows]
            cross_total = cross_total + block[rows:]
        if step == depth - 2:
            came = cross(cross_total.astype(jnp.bfloat16)).astype(jnp.float32)
        if step == depth - 1:
            ends = [collect(out_first, step), collect(out_later, step)]
            own_end = jnp.concatenate([v[:rows] for v in ends], axis=1)
            came_end = jnp.concatenate(
                [cross(v[rows:].astype(jnp.bfloat16)) for v in ends], axis=1
            ).astype(jnp.float32)
    own_half = own_total + own_end
    other_half = came + came_end
    summed = jnp.concatenate(
        [
            jnp.where(side == 0, own_half, other_half),
            jnp.where(side == 0, other_half, own_half),
        ],
        axis=1,
    )
    layer_out = (
        summed + adapter_scale * jnp.dot(low_bf, up_b, preferred_element_type=jnp.float32)
    ).astype(jnp.bfloat16)

    adapter = adapter_scale * jnp.dot(back_bf, down_a, preferred_element_type=jnp.float32)
    pieces = []
    for r in range(ROW_PIECES):
        came_grad = cross(sums[r][rows:].astype(jnp.bfloat16)).astype(jnp.float32)
        pieces.append(sums[r][:rows] + came_grad + adapter[:, r * part : (r + 1) * part])
    attn_grad = jnp.concatenate(pieces, axis=1).astype(jnp.bfloat16)

    factor = adapter_scale / (rows * dp_size)
    grad_a = factor * lax.dot_general(
        back_bf, attn_out, (((0,), (0,)), ((), ())), preferred_element_type=jnp.float32
    )
    grad_b = factor * lax.dot_general(
        low_bf, grad_cols, (((0,), (0,)), ((), ())), preferred_element_type=jnp.float32
    )
    bank_a, logit_grad_a = compose_back(grad_a, weights_a, picked_a, mixing_a, vector_bank)
    bank_b, logit_grad_b = compose_back(grad_b, weights_b, picked_b, mixing_b, vector_bank)
    bank_grad = lax.psum(bank_a + bank_b, ("dp", "tensor"))
    logits_a_grad, logits_b_grad = lax.psum((logit_grad_a, logit_grad_b), "dp")
    return (layer_out, attn_grad, bank_grad, logits_a_grad, logits_b_grad)


MESH_ID = pl.DeviceIdType.MESH
PIECES = 8


def dot_nn(a, b):
    return jnp.dot(a, b, preferred_element_type=jnp.float32)


def dot_nt(a, b):
    return lax.dot_general(a, b, (((1,), (1,)), ((), ())), preferred_element_type=jnp.float32)


def exchange_kernel(
    factor,
    attn, weight, grad, bank_hbm, logits_a, index_a, logits_b, index_b,
    ybuf0, drecv, relay, bank_out, slope_a, slope_b,
    wbuf, abuf0, abuf1, gbuf0, gbuf1, dacc0, dacc1, cbuf0, cbuf1, ybuf1, dsend,
    cacc0, cacc1, lb, low, back,
    down, up, bank, mixing, sums, came,
    load_sem, zs_send, relay_recv, relay_send, far_recv, xs_send, x_recv, xf_send, xf_recv,
    g_send, g_recv, gm_send, gm_recv, a_send, a_recv, mid_send, mid_recv, lb_send, lb_recv,
    c_send, c_recv, y_send, y_recv, zc_send, zc_recv, zm_recv, d_send, d_recv, dm_recv,
    sum_send, sum_recv,
):
    rows, depth = attn.shape
    width = weight.shape[1]
    half = width // 2
    step = depth // PIECES
    few = rows // 16
    abufs, gbufs, daccs = (abuf0, abuf1), (gbuf0, gbuf1), (dacc0, dacc1)
    cbufs, caccs = (cbuf0, cbuf1), (cacc0, cacc1)
    rank = down.shape[0]
    own = up.shape[1]

    dp, t = lax.axis_index("dp"), lax.axis_index("tensor")
    z, x = dp // 2, dp % 2
    y, c = t // 2, t % 2
    zh, zl = z // 2, z % 2
    inner = (z == 1) | (z == 2)
    pz = zh * 2 + (1 - zl)
    mz = jnp.where(z == 1, 2, 1)
    x_dev = (z * 2 + (1 - x), t)
    p_dev = (pz * 2 + x, t)
    m_dev = (mz * 2 + x, t)
    c_dev = (dp, y * 2 + (1 - c))
    y_dev = (dp, (1 - y) * 2 + c)
    reduces = c == zl

    def remote(src, dst, send, recv, device):
        return pltpu.make_async_remote_copy(
            src_ref=src, dst_ref=dst, send_sem=send, recv_sem=recv,
            device_id=device, device_id_type=MESH_ID,
        )

    extra = pl.ds(rows, few)
    lead = pl.ds(0, few)

    def sent_rows(is_inner):
        return pl.ds(few, rows - few) if is_inner else pl.ds(0, rows)

    def taken_rows(is_inner):
        return sent_rows(not is_inner)

    def each_kind(act):
        for kind in (True, False):

            @pl.when(inner == kind)
            def _():
                act(kind)

    def rowsof(p):
        return pl.ds(pl.multiple_of(p * step, step), step)

    barrier = pltpu.get_barrier_semaphore()
    others = [(dp, (t + k) % 4) for k in (1, 2, 3)]
    for device in others + [x_dev, p_dev]:
        pl.semaphore_signal(barrier, inc=1, device_id=device, device_id_type=MESH_ID)

    @pl.when(inner)
    def _():
        pl.semaphore_signal(barrier, inc=1, device_id=m_dev, device_id_type=MESH_ID)

    def column_block(zz, b, xx):
        zb = jnp.where(b < 2, zz, (zz + 2) % 4)
        xb = jnp.where(b % 2 == 0, xx, 1 - xx)
        return zb * 2 + xb

    loads = [pltpu.make_async_copy(attn, abuf0, load_sem.at[0])]
    gq = pltpu.make_async_copy(
        grad.at[:, pl.ds(pl.multiple_of(t * own, own), own)], dsend.at[pl.ds(0, rows), pl.ds(0, own)], load_sem.at[1]
    )
    loads.append(gq)
    bank_load = pltpu.make_async_copy(bank_hbm, bank, load_sem.at[5])
    bank_load.start()
    for n in range(2):
        loads.append(
            pltpu.make_async_copy(weight.at[:, pl.ds(n * half, half)], wbuf.at[n], load_sem.at[2 + n])
        )
    for s in range(8):
        col = column_block(z, s // 2, x) * width + (s % 2) * half
        loads.append(
            pltpu.make_async_copy(
                grad.at[:, pl.ds(pl.multiple_of(col, half), half)], gbuf0.at[s], load_sem.at[4]
            )
        )
    for load in loads[:2]:
        load.start()

    @pl.when(inner)
    def _():
        pl.semaphore_wait(barrier, 6)

    @pl.when(jnp.logical_not(inner))
    def _():
        pl.semaphore_wait(barrier, 5)

    total = 2 * PIECES
    narrow = half // 2

    def area(n, p):
        return pl.ds(pl.multiple_of(p * step, step), step), pl.ds(0, half)

    def weight_area(n, p):
        return weight.at[area(n, p)[0], pl.ds(n * half, half)]

    def by_half(i, act):
        for n in range(2):

            @pl.when(i // PIECES == n)
            def _():
                act(n, i % PIECES)

    def x_own(n, p):
        i = n * PIECES + p
        return remote(weight_area(n, p), wbuf.at[(2 + n, *area(n, p))], xs_send.at[0], x_recv.at[i], x_dev)

    def z_own(n, p):
        i = n * PIECES + p
        stream = jnp.where(inner, 0, 1)
        device = (jnp.where(inner, mz, pz) * 2 + x, t)
        return remote(
            weight_area(n, p), relay.at[(stream, n, *area(n, p))],
            zs_send.at[0], relay_recv.at[stream, i], device,
        )

    def g_columns(zz, n):
        col = column_block(zz, t, x) * width + n * half
        return pl.ds(pl.multiple_of(col, half), half)

    def g_own(n, part):
        return remote(
            grad.at[part, g_columns(pz, n)], gbuf1.at[2 * t + n, part], g_send.at[0], g_recv.at[n], p_dev
        )

    def g_mid(n):
        return remote(
            grad.at[lead, g_columns(mz, n)], gbuf1.at[2 * t + n, extra], mid_send.at[n], mid_recv.at[n], m_dev
        )

    def a_own(part):
        return remote(attn.at[part], abuf1.at[part], a_send.at[0], a_recv.at[0], p_dev)

    a_mid = remote(attn.at[lead], abuf1.at[extra], mid_send.at[2], mid_recv.at[2], m_dev)
    early = PIECES // 2

    @pl.when(inner)
    def _():
        for n in range(2):
            g_own(n, sent_rows(True)).start()
            g_mid(n).start()
        a_own(sent_rows(True)).start()
        a_mid.start()

    @pl.when(jnp.logical_not(inner))
    def _():
        for n in range(2):
            g_own(n, sent_rows(False)).start()

        @pl.loop(0, early)
        def _(i):
            z_own(0, i).start()

        a_own(sent_rows(False)).start()

    @pl.loop(0, PIECES)
    def _(i):
        x_own(0, i).start()

        @pl.when(inner)
        def _():
            z_own(0, i).start()

    for load in loads[2:]:
        load.start()

    bank_load.wait()
    levels = bank.shape[0]
    sublen = bank.shape[1]
    vectors = mixing.shape[2]
    per_row = vectors // rank
    exact = dict(preferred_element_type=jnp.float32, precision=lax.Precision.HIGHEST)

    place = lax.broadcasted_iota(jnp.int32, (rank, vectors), 1)
    spread = (place % rank == lax.broadcasted_iota(jnp.int32, (rank, vectors), 0)).astype(jnp.float32)
    place = lax.broadcasted_iota(jnp.int32, (per_row, vectors), 1)
    keep = place // rank == lax.broadcasted_iota(jnp.int32, (per_row, vectors), 0)
    level = lax.broadcasted_iota(jnp.int32, (levels, vectors), 0)

    def as_row(value):
        wide_value = jnp.dot(value.astype(jnp.float32), spread, **exact)
        return jnp.sum(jnp.where(keep, wide_value, 0.0), axis=0, keepdims=True)

    def from_row(row):
        return lax.dot_general(jnp.where(keep, row, 0.0), spread, (((1,), (1,)), ((), ())), **exact)

    shares, found = [], []
    for k, (logits, indices) in enumerate(((logits_a, index_a), (logits_b, index_b))):
        first, second = as_row(logits[:, 0, :]), as_row(logits[:, 1, :])
        shares.append((1.0 / (1.0 + jnp.exp(second - first)), 1.0 / (1.0 + jnp.exp(first - second))))
        picks = [(as_row(indices[:, m, :]) + 0.5).astype(jnp.int32) for m in range(2)]
        found.append([level == pick for pick in picks])

    for k, target in enumerate((down, up)):
        mixing[k] = sum(jnp.where(found[k][m], shares[k][m], 0.0) for m in range(2))
        blocks = lax.dot_general(mixing[k], bank[...], (((0,), (0,)), ((), ())), **exact)
        for j in range(per_row):
            row = blocks[j * rank : (j + 1) * rank]
            target[:, j * sublen : (j + 1) * sublen] = row.astype(jnp.bfloat16)

    loads[0].wait()
    loads[1].wait()
    lb[t, :rank] = dot_nt(down[...], abuf0[...])
    lb[t, rank:] = dot_nt(up[...], dsend[:rows, :own])

    def lb_copy(k):
        device = (dp, (t + k) % 4)
        return remote(lb.at[t], lb.at[t], lb_send.at[0], lb_recv.at[0], device)

    for k in (1, 2, 3):
        lb_copy(k).start()
    for load in loads[2:4]:
        load.wait()
    pltpu.make_async_copy(gbuf0, gbuf0, load_sem.at[4]).wait()
    dacc0[...] = jnp.zeros_like(dacc0)
    dacc1[...] = jnp.zeros_like(dacc1)

    @pl.when(jnp.logical_not(inner))
    def _():
        for part in (lead, extra):
            abuf1[part] = jnp.zeros_like(abuf1[part])
            gbuf1[:, part] = jnp.zeros_like(gbuf1[:, part])

    three = lb.at[pl.ds(0, 3)]
    remote(three, three, lb_send.at[0], lb_recv.at[0], y_dev).wait()
    both = lb[0] + lb[1] + lb[2] + lb[3]
    low[...] = both[:rank].T.astype(jnp.bfloat16)
    back[...] = both[rank:].T.astype(jnp.bfloat16)
    both = both.astype(jnp.bfloat16)
    slopes = (
        factor * dot_nn(both[rank:], abuf0[...]),
        factor * dot_nn(both[:rank], dsend[:rows, :own]),
    )
    bank_out[...] = jnp.zeros_like(bank_out)
    dots = []
    for k in range(2):
        pieces = [slopes[k][:, j * sublen : (j + 1) * sublen] for j in range(per_row)]
        stacked = jnp.concatenate(pieces, axis=0)
        bank_out[...] += jnp.dot(mixing[k], stacked, **exact)
        projected = lax.dot_general(bank[...], stacked, (((1,), (1,)), ((), ())), **exact)
        for m in range(2):
            dots.append(jnp.sum(jnp.where(found[k][m], projected, 0.0), axis=0, keepdims=True))

    q1, q2, q3 = levels // 2, levels // 4, levels // 8
    pack = q3 + 8
    at_c = c * q1
    at_y = at_c + y * q2
    at_x = at_y + x * q3
    counts = (q1, q2, pack, pack, pack, q3, q2, q1)
    places = [pl.ds(sum(counts[:k]), counts[k]) for k in range(8)]

    def bank_rows(start, count):
        return pl.ds(pl.multiple_of(start, 8), count)

    def sum_copy(k, source, device):
        return remote(source, came.at[places[k]], sum_send.at[k], sum_recv.at[k], device)

    core_sum = sum_copy(0, bank_out.at[bank_rows((1 - c) * q1, q1)], c_dev)
    y_sum = sum_copy(1, bank_out.at[bank_rows(at_c + (1 - y) * q2, q2)], y_dev)
    x_sum = sum_copy(2, sums, x_dev)
    p_sum = sum_copy(3, sums, p_dev)
    m_sum = sum_copy(4, sums, m_dev)
    x_all = sum_copy(5, bank_out.at[bank_rows(at_x, q3)], x_dev)
    y_all = sum_copy(6, bank_out.at[bank_rows(at_y, q2)], y_dev)
    c_all = sum_copy(7, bank_out.at[bank_rows(at_c, q1)], c_dev)
    core_sum.start()
    core_sum.wait()
    bank_out[bank_rows(at_c, q1)] += came[places[0]]
    y_sum.start()
    y_sum.wait()
    bank_out[bank_rows(at_y, q2)] += came[places[1]]
    sums[:q3] = bank_out[bank_rows(at_y + (1 - x) * q3, q3)]
    sums[q3:] = jnp.zeros_like(sums[q3:])
    for k in range(4):
        sums[q3 + k : q3 + k + 1, :vectors] = dots[k]
    x_sum.start()

    @pl.loop(0, PIECES)
    def _(i):
        x_own(1, i).start()

    def relay_on(stream, n, p):
        i = n * PIECES + p
        device = (jnp.where(stream == 0, pz, mz) * 2 + x, t)
        return remote(
            relay.at[(stream, n, *area(n, p))], wbuf.at[(4 + n, *area(n, p))],
            relay_send.at[stream], far_recv.at[i], device,
        )

    def relay_wait(stream, n, p):
        i = n * PIECES + p
        piece = relay.at[(stream, n, *area(n, p))]
        remote(piece, piece, relay_send.at[stream], relay_recv.at[stream, i], p_dev).wait_recv()

    def x_far(n, p):
        i = n * PIECES + p
        return remote(
            wbuf.at[(4 + n, *area(n, p))], wbuf.at[(6 + n, *area(n, p))], xf_send.at[0], xf_recv.at[i], x_dev
        )

    def far_wait(n, p):
        i = n * PIECES + p
        piece = wbuf.at[(4 + n, *area(n, p))]
        remote(piece, piece, xf_send.at[0], far_recv.at[i], x_dev).wait_recv()

    def g_spread(k, n, is_inner):
        part = pl.ds(0, rows + few) if is_inner else taken_rows(False)
        piece = gbuf1.at[2 * t + n, part]
        return remote(piece, piece, gm_send.at[0], gm_recv.at[0], (dp, (t + k) % 4))

    def g_everything(is_inner):
        part = pl.ds(0, rows + few) if is_inner else taken_rows(False)
        return gbuf1.at[pl.ds(0, 6), part]

    ticks = 33

    def tick(i, carry):
        def near(n, p):
            x_own(n, p).wait_recv()

        @pl.when(i < total)
        def _():
            by_half(i, near)

        def outward(n, p):
            relay_wait(0, n, p)
            relay_on(0, n, p).start()

        @pl.when(inner & (i >= 2) & (i < 2 + PIECES))
        def _():
            outward(0, i - 2)

        @pl.when(inner & (i >= 15) & (i < 15 + PIECES))
        def _():
            outward(1, i - 15)

        def onward(n, p):
            relay_wait(1, n, p)
            relay_on(1, n, p).start()

        @pl.when(inner & (i >= 5) & (i < 5 + early))
        def _():
            onward(0, i - 5)

        @pl.when(inner & (i >= 16) & (i < 12 + total))
        def _():
            by_half(i - 12, onward)

        @pl.when(i == PIECES)
        def _():
            x_sum.wait()
            sums[:q3] = bank_out[bank_rows(at_x, q3)] + came[places[2]][:q3]
            sums[q3:] += came[places[2]][q3:]

            @pl.when(jnp.logical_not(inner))
            def _():
                p_sum.start()

                @pl.loop(early, PIECES)
                def _(k):
                    z_own(0, k).start()

            @pl.loop(0, PIECES)
            def _(k):
                z_own(1, k).start()

        @pl.when(i == 16)
        def _():
            @pl.when(jnp.logical_not(inner))
            def _():
                p_sum.wait_send()

            @pl.when(inner)
            def _():
                p_sum.wait_recv()
                sums[...] += came[places[3]]
                m_sum.start()

        @pl.when((i == 23) & inner)
        def _():
            m_sum.wait()
            sums[...] += came[places[4]]
            p_sum.start()

        @pl.when(i == 4)
        def _():
            def spread(is_inner):
                for n in range(2):
                    g_own(n, taken_rows(is_inner)).wait_recv()
                    if is_inner:
                        g_mid(n).wait_recv()
                    for k in (1, 2, 3):
                        g_spread(k, n, is_inner).start()

            each_kind(spread)

        def far(n, p):
            far_wait(n, p)
            x_far(n, p).start()

        wait = jnp.where(inner & (i >= 21), 17, 12)

        @pl.when((i >= 12) & (i - wait < total) & (jnp.logical_not(inner) | (i < 16) | (i >= 21)))
        def _():
            by_half(i - wait, far)

        return carry

    def c_copy(s, r):
        piece = cbufs[r].at[s]
        return remote(piece, piece, c_send.at[r], c_recv.at[s, r], c_dev)

    def y_copy(s, r):
        j = s % 4
        target = (ybuf0, ybuf1)[r].at[j]
        return remote(cbufs[r].at[s], target, y_send.at[r], y_recv.at[j, r], y_dev)

    def z_copy(s, part):
        j = s % 4
        return remote(cbuf1.at[s, part], ybuf0.at[j, part], zc_send.at[0], zc_recv.at[j], p_dev)

    def z_mid(s):
        j = s % 4
        return remote(cbuf1.at[s, extra], ybuf0.at[j, lead], zc_send.at[1], zm_recv.at[j], m_dev)

    def kept(s):
        return jnp.where(s < 4, zh, 1 - zh) == y

    def out_columns(j):
        xb = jnp.where(j < 2, x, 1 - x)
        return pl.ds(pl.multiple_of(xb * width + (j % 2) * half, half), half)

    def adapter_out(j):
        return 2.0 * dot_nn(low[...], up[:, out_columns(j)])

    def by_side(r, act):
        if isinstance(r, int):
            act(r)
            return
        for side in range(2):

            @pl.when(r == side)
            def _():
                act(side)

    def pass_core(s, r, k):
        @pl.when(jnp.logical_not(reduces))
        def _():
            cbufs[r][s] = caccs[r][k].astype(jnp.bfloat16)
            c_copy(s, r).start()

    def sum_core(s, r, k):
        def act(r):
            c_copy(s, r).wait_recv()
            cbufs[r][s] = (caccs[r][k] + cbufs[r][s].astype(jnp.float32)).astype(jnp.bfloat16)

            @pl.when(jnp.logical_not(kept(s)))
            def _():
                y_copy(s, r).start()

        @pl.when(reduces)
        def _():
            by_side(r, act)

    def sum_y(s, r):
        j = s % 4

        def act(r):
            y_copy(s, r).wait_recv()
            came_here = (ybuf0, ybuf1)[r][j].astype(jnp.float32)
            total_here = cbufs[r][s].astype(jnp.float32) + came_here
            if r == 0:
                ybuf0[j] = (total_here + adapter_out(j)).astype(jnp.bfloat16)
            else:
                cbuf1[s] = total_here.astype(jnp.bfloat16)
                each_kind(lambda is_inner: z_copy(s, taken_rows(is_inner)).start())

                @pl.when(inner)
                def _():
                    z_mid(s).start()

        @pl.when(reduces & kept(s))
        def _():
            by_side(r, act)

    def finish_other(j):
        @pl.when(jnp.logical_not(reduces))
        def _():
            each_kind(lambda is_inner: z_copy(j, sent_rows(is_inner)).wait_recv())

            @pl.when(inner)
            def _():
                z_mid(j).wait_recv()

            ybuf0[j] = (ybuf0[j].astype(jnp.float32) + adapter_out(j)).astype(jnp.bfloat16)

    slots = (0, 1, 2, 0, 1, 2, 3, 3, 4, 4, 6, 6)
    sides = (0, 0, 0, 1, 1, 1, 0, 1, 0, 1, 0, 1)

    def pick(table, u):
        if isinstance(u, int):
            return table[u]
        value = table[0]
        for k in range(1, len(table)):
            if table[k] != table[k - 1]:
                value = jnp.where(u >= k, table[k], value)
        return value

    def ready(u):
        value = jnp.where(u >= 2, PIECES, 0)
        value = jnp.where(u >= 3, 16, value)
        value = jnp.where(u >= 8, jnp.where(inner, 25, 20), value)
        return jnp.where(u >= 10, 26, value)

    def tiles(r):
        count = rows + few * r
        return [pl.ds(m * (count // 2), count // 2) for m in range(2)]

    def unit(u, carry):
        s, r = pick(slots, u), pick(sides, u)
        lax.fori_loop(ready(u - 1), ready(u), tick, 0)

        @pl.when(u == 3)
        def _():
            def arrived(is_inner):
                a_own(taken_rows(is_inner)).wait_recv()
                if is_inner:
                    a_mid.wait_recv()
                everything = g_everything(is_inner)
                remote(everything, everything, gm_send.at[0], gm_recv.at[0], y_dev).wait_recv()

            each_kind(arrived)

        @pl.when(u == 10)
        def _():
            for p in range(PIECES):
                x_far(0, p).wait_recv()


        def act(r):
            for part in tiles(r):
                caccs[r][u % 2, part] = dot_nn(abufs[r][part], wbuf[s])
                daccs[r][part] += dot_nt(gbufs[r][s, part], wbuf[s])
            pass_core(s, r, u % 2)

        by_side(r, act)

        @pl.when(u >= 1)
        def _():
            sum_core(pick(slots, u - 1), pick(sides, u - 1), (u - 1) % 2)

        @pl.when(u >= 4)
        def _():
            sum_y(pick(slots, u - 4), pick(sides, u - 4))

        return carry

    lax.fori_loop(0, 12, unit, 0)
    sum_core(slots[11], sides[11], 1)
    cacc0[...] = jnp.zeros_like(cacc0)
    cacc1[...] = jnp.zeros_like(cacc1)

    final = ((7, 1), (7, 0))

    def grad_part(p):
        return pl.ds(pl.multiple_of(p * step, step), step)

    def d_copy(p, part):
        columns = grad_part(p)
        return remote(dsend.at[part, columns], drecv.at[part, columns], d_send.at[0], d_recv.at[p], p_dev)

    def d_mid(p):
        columns = grad_part(p)
        return remote(dsend.at[extra, columns], drecv.at[lead, columns], d_send.at[1], dm_recv.at[p], m_dev)

    def last_piece(p, carry):
        done = 26 + p
        lax.fori_loop(jnp.minimum(done, ticks), jnp.minimum(done + 1, ticks), tick, 0)

        def ahead(p):
            columns = grad_part(p)
            for r in range(2):
                caccs[r][0] += dot_nn(abufs[r][:, columns], wbuf[5, columns])

        @pl.when(p == 0)
        def _():
            ahead(0)

        @pl.when(p < PIECES - 1)
        def _():
            ahead(p + 1)

        @pl.when(p == PIECES - 2)
        def _():
            for side in (1, 0):
                pass_core(5, side, 0)

        x_far(1, p).wait_recv()
        columns = grad_part(p)
        for r in (1, 0):
            for part in tiles(r):
                grown = daccs[r][part, columns]
                grown += dot_nt(gbufs[r][5, part], wbuf[5, columns])
                grown += dot_nt(gbufs[r][7, part], wbuf[7, columns])
                if r == 1:
                    dsend[part, columns] = grown.astype(jnp.bfloat16)
                else:
                    dacc0[part, columns] = grown
            if r == 1:
                each_kind(lambda is_inner: d_copy(p, taken_rows(is_inner)).start())

                @pl.when(inner)
                def _():
                    d_mid(p).start()

        for r in range(2):
            caccs[r][1] += dot_nn(abufs[r][:, columns], wbuf[7, columns])

        @pl.when(p == PIECES - 2)
        def _():
            for side in (1, 0):
                sum_core(5, side, 0)


        @pl.when(p == 1)
        def _():
            @pl.when(inner)
            def _():
                p_sum.wait_send()

            @pl.when(jnp.logical_not(inner))
            def _():
                p_sum.wait_recv()
                sums[...] = came[places[3]]

            bank_out[bank_rows(at_x, q3)] = sums[:q3]
            x_all.start()

        @pl.when(p == 3)
        def _():
            x_all.wait()
            bank_out[bank_rows(at_y + (1 - x) * q3, q3)] = came[places[5]]
            y_all.start()

        @pl.when((p >= 1) & (p < 5))
        def _():
            sum_y(pick(slots, 7 + p), (p - 1) % 2)

        @pl.when(p == 5)
        def _():
            y_all.wait()
            bank_out[bank_rows(at_c + (1 - y) * q2, q2)] = came[places[6]]
            c_all.start()

        return carry

    lax.fori_loop(0, PIECES, last_piece, 0)

    def finish_grad(p, carry):
        columns = grad_part(p)
        each_kind(lambda is_inner: d_copy(p, sent_rows(is_inner)).wait_recv())

        @pl.when(inner)
        def _():
            d_mid(p).wait_recv()

        total_here = dacc0[:, columns] + drecv[:, columns].astype(jnp.float32)
        drecv[:, columns] = (total_here + 2.0 * dot_nn(back[...], down[:, columns])).astype(jnp.bfloat16)
        return carry

    for slot, side in final:
        pass_core(slot, side, 1)
    for slot, side in final:
        sum_core(slot, side, 1)
    c_all.wait()
    bank_out[bank_rows((1 - c) * q1, q1)] = came[places[7]]
    for k, target in enumerate((slope_a, slope_b)):
        values = [sums[q3 + 2 * k + m : q3 + 2 * k + m + 1, :vectors] for m in range(2)]
        mean = shares[k][0] * values[0] + shares[k][1] * values[1]
        for m in range(2):
            target[:, m, :] = from_row(shares[k][m] * (values[m] - mean))
    finish_other(0)
    finish_other(2)
    for slot, side in ((5, 1), (5, 0), (7, 1), (7, 0)):
        sum_y(slot, side)
    lax.fori_loop(0, PIECES, finish_grad, 0)
    finish_other(1)
    finish_other(3)
    def drain(buffer, semaphore):
        remote(buffer, buffer, semaphore, a_recv.at[0], p_dev).wait_send()

    def drain_kind(is_inner):
        a_own(sent_rows(is_inner)).wait_send()
        drain(gbuf1.at[pl.ds(0, 2), sent_rows(is_inner)], g_send.at[0])
        drain(g_everything(is_inner), gm_send.at[0])
        drain(dsend.at[taken_rows(is_inner)], d_send.at[0])
        if is_inner:
            a_mid.wait_send()
            for n in range(2):
                g_mid(n).wait_send()
                drain(relay.at[n], relay_send.at[n])
            drain(dsend.at[extra], d_send.at[1])

        @pl.when(reduces)
        def _():
            drain(gbuf1.at[pl.ds(0, 4), taken_rows(is_inner)], zc_send.at[0])
            if is_inner:
                drain(gbuf1.at[pl.ds(0, 4), extra], zc_send.at[1])

    each_kind(drain_kind)
    drain(weight, xs_send.at[0])
    drain(weight, zs_send.at[0])
    drain(weight, xf_send.at[0])

    @pl.when(jnp.logical_not(reduces))
    def _():
        for r in range(2):
            drain(cbufs[r], c_send.at[r])

    @pl.when(reduces)
    def _():
        for r in range(2):
            drain(cbufs[r].at[pl.ds(0, 4)], y_send.at[r])


def settle_kernel(width, *refs):
    sources, targets, sem = refs[:5], refs[5:10], refs[10]
    half = sources[0].shape[2]
    x = lax.axis_index("dp") % 2
    copies = []
    for j in range(4):
        col = (x if j < 2 else 1 - x) * width + (j % 2) * half
        columns = pl.ds(pl.multiple_of(col, half), half)
        copies.append(pltpu.make_async_copy(sources[0].at[j], targets[0].at[:, columns], sem.at[j]))
    for k in range(1, 5):
        copies.append(pltpu.make_async_copy(sources[k], targets[k], sem.at[3 + k]))
    for copy in copies:
        copy.start()
    for copy in copies:
        copy.wait()


def fused_local(dp_size, attn_out, frozen_weight, vector_bank, logits_a, index_a, logits_b, index_b, out_grad):
    rows, depth = attn_out.shape
    width = frozen_weight.shape[1]
    half = width // 2
    levels, sublen = vector_bank.shape
    rank, per_row, _ = logits_a.shape
    vectors = rank * per_row
    own = logits_b.shape[1] * sublen
    factor = adapter_scale / (rows * dp_size)
    total = 2 * PIECES
    more = rows + rows // 16
    small = [v.transpose(1, 2, 0) for v in (logits_a, index_a, logits_b, index_b)]
    bf16, f32 = jnp.bfloat16, jnp.float32
    dma = pltpu.SemaphoreType.DMA
    hbm = pl.BlockSpec(memory_space=pl.ANY)
    vmem = pl.BlockSpec(memory_space=pltpu.VMEM)
    layer_out, attn_grad, _, bank_grad, slope_a, slope_b = pl.pallas_call(
        functools.partial(exchange_kernel, factor),
        name="exchange",
        out_shape=(
            pltpu.VMEM((4, rows, half), bf16),
            pltpu.VMEM((rows, depth), bf16),
            jax.ShapeDtypeStruct((2, 2, depth, half), bf16),
            pltpu.VMEM((levels, sublen), f32),
            pltpu.VMEM((per_row, 2, rank), f32),
            pltpu.VMEM((per_row, 2, rank), f32),
        ),
        in_specs=[hbm, hbm, hbm, hbm, vmem, vmem, vmem, vmem],
        out_specs=(vmem, vmem, hbm, vmem, vmem, vmem),
        scratch_shapes=[
            pltpu.VMEM((8, depth, half), bf16),
            pltpu.VMEM((rows, depth), bf16),
            pltpu.VMEM((more, depth), bf16),
            pltpu.VMEM((8, rows, half), bf16),
            pltpu.VMEM((8, more, half), bf16),
            pltpu.VMEM((rows, depth), f32),
            pltpu.VMEM((more, depth), f32),
            pltpu.VMEM((8, rows, half), bf16),
            pltpu.VMEM((8, more, half), bf16),
            pltpu.VMEM((4, more, half), bf16),
            pltpu.VMEM((more, depth), bf16),
            pltpu.VMEM((2, rows, half), f32),
            pltpu.VMEM((2, more, half), f32),
            pltpu.VMEM((4, 2 * rank, rows), f32),
            pltpu.VMEM((rows, rank), bf16),
            pltpu.VMEM((rows, rank), bf16),
            pltpu.VMEM((rank, depth), bf16),
            pltpu.VMEM((rank, own), bf16),
            pltpu.VMEM((levels, sublen), f32),
            pltpu.VMEM((2, levels, vectors), f32),
            pltpu.VMEM((levels // 8 + 8, sublen), f32),
            pltpu.VMEM((2 * levels + 24, sublen), f32),
            dma((6,)), dma((1,)), dma((2, total)), dma((2,)), dma((total,)),
            dma((1,)), dma((total,)), dma((1,)), dma((total,)),
            dma((1,)), dma((2,)), dma((1,)), dma((1,)), dma((1,)), dma((1,)), dma((3,)), dma((3,)),
            dma((1,)), dma((1,)),
            dma((2,)), dma((8, 2)), dma((2,)), dma((4, 2)), dma((2,)), dma((4,)), dma((4,)),
            dma((2,)), dma((PIECES,)), dma((PIECES,)), dma((8,)), dma((8,)),
        ],
        compiler_params=pltpu.CompilerParams(
            collective_id=0, has_side_effects=True, vmem_limit_bytes=67043328 - 5 * 2**20
        ),
    )(attn_out, frozen_weight, out_grad, vector_bank, *small)
    targets = [((rows, own), bf16), ((rows, depth), bf16), ((levels, sublen), f32)]
    targets += [(v.shape, f32) for v in (slope_a, slope_b)]
    kept = [pltpu.with_memory_space_constraint(v, pltpu.VMEM) for v in (layer_out, attn_grad, bank_grad, slope_a, slope_b)]
    layer_out, attn_grad, bank_grad, slope_a, slope_b = pl.pallas_call(
        functools.partial(settle_kernel, width),
        name="settle",
        out_shape=[jax.ShapeDtypeStruct(*v) for v in targets],
        in_specs=[hbm] * 5,
        out_specs=[hbm] * 5,
        scratch_shapes=[dma((8,))],
        compiler_params=pltpu.CompilerParams(vmem_limit_bytes=16 * 2**20),
    )(*kept)
    return (layer_out, attn_grad, bank_grad, slope_a.transpose(2, 0, 1), slope_b.transpose(2, 0, 1))


def solution(mesh):
    dp_size, tensor_size = mesh.shape["dp"], mesh.shape["tensor"]
    paired = dp_size == 2 * tensor_size and tensor_size % 2 == 0
    body = functools.partial(ring_local, dp_size, tensor_size) if paired else local
    if paired and tensor_size == 4:
        body = functools.partial(fused_local, dp_size)
    return jax.shard_map(
        body,
        mesh=mesh,
        in_specs=(
            P("dp", "tensor"),
            P("tensor", "dp"),
            P(),
            P(None, "tensor", None),
            P(None, "tensor", None),
            P(None, "tensor", None),
            P(None, "tensor", None),
            P("dp", None),
        ),
        out_specs=(
            P("dp", "tensor"),
            P("dp", "tensor"),
            P(),
            P(None, "tensor", None),
            P(None, "tensor", None),
        ),
        check_vma=False,
    )
```

```python
import functools

import jax
import jax.numpy as jnp
from jax import lax
from jax.experimental import pallas as pl
from jax.experimental.pallas import tpu as pltpu
from jax.sharding import PartitionSpec as P

adapter_scale = 2.0
ROW_PIECES = 4


def compose(logits, indices, vector_bank):
    weights = jax.nn.sigmoid(logits - logits[..., ::-1])
    levels = jnp.arange(vector_bank.shape[0], dtype=jnp.int32)
    picked = (indices[..., None] == levels).astype(jnp.float32)
    mixing = jnp.sum(picked * weights[..., None], axis=2)
    blocks = jnp.einsum("rjb,bc->rjc", mixing, vector_bank, precision=lax.Precision.HIGHEST)
    return (weights, picked, mixing, blocks.reshape(blocks.shape[0], -1))


def compose_back(grad_rows, weights, picked, mixing, vector_bank):
    blocks = grad_rows.reshape(mixing.shape[0], mixing.shape[1], -1)
    bank_part = jnp.einsum("rjb,rjc->bc", mixing, blocks, precision=lax.Precision.HIGHEST)
    projected = jnp.einsum("rjc,bc->rjb", blocks, vector_bank, precision=lax.Precision.HIGHEST)
    dots = jnp.sum(picked * projected[:, :, None, :], axis=3)
    logit_grad = weights * (dots - jnp.sum(weights * dots, axis=2, keepdims=True))
    return (bank_part, logit_grad)


def local(attn_out, frozen_weight, vector_bank, logits_a, index_a, logits_b, index_b, out_grad):
    weights_a, picked_a, mixing_a, rows_a = compose(logits_a, index_a, vector_bank)
    weights_b, picked_b, mixing_b, rows_b = compose(logits_b, index_b, vector_bank)
    down_a = rows_a.astype(jnp.bfloat16)
    up_b = rows_b.astype(jnp.bfloat16)
    own_width = up_b.shape[1]
    grad_cols = lax.dynamic_slice_in_dim(
        out_grad, lax.axis_index("tensor") * own_width, own_width, 1
    )
    low_part = jnp.dot(attn_out, down_a.T, preferred_element_type=jnp.float32)
    back_part = jnp.dot(grad_cols, up_b.T, preferred_element_type=jnp.float32)
    low_total = lax.psum(low_part, "tensor")
    low_bf = low_total.astype(jnp.bfloat16)
    gathered = lax.all_gather(frozen_weight, "dp", axis=1, tiled=True)
    partial_value = jnp.dot(attn_out, gathered, preferred_element_type=jnp.float32).astype(
        jnp.bfloat16
    )
    summed = lax.psum_scatter(partial_value, "tensor", scatter_dimension=1, tiled=True).astype(
        jnp.float32
    )
    layer_out = (
        summed + adapter_scale * jnp.dot(low_bf, up_b, preferred_element_type=jnp.float32)
    ).astype(jnp.bfloat16)
    back_total = lax.psum(back_part, "tensor")
    back_bf = back_total.astype(jnp.bfloat16)
    main = lax.dot_general(
        out_grad, gathered, (((1,), (1,)), ((), ())), preferred_element_type=jnp.float32
    )
    attn_grad = (
        main + adapter_scale * jnp.dot(back_bf, down_a, preferred_element_type=jnp.float32)
    ).astype(jnp.bfloat16)
    factor = adapter_scale / (attn_out.shape[0] * lax.axis_size("dp"))
    grad_a = factor * lax.dot_general(
        back_bf, attn_out, (((0,), (0,)), ((), ())), preferred_element_type=jnp.float32
    )
    grad_b = factor * lax.dot_general(
        low_bf, grad_cols, (((0,), (0,)), ((), ())), preferred_element_type=jnp.float32
    )
    bank_a, logit_grad_a = compose_back(grad_a, weights_a, picked_a, mixing_a, vector_bank)
    bank_b, logit_grad_b = compose_back(grad_b, weights_b, picked_b, mixing_b, vector_bank)
    bank_part = bank_a + bank_b
    bank_group = lax.psum(bank_part, "tensor")
    bank_grad, logits_a_grad, logits_b_grad = lax.psum(
        (bank_group, logit_grad_a, logit_grad_b), "dp"
    )
    return (layer_out, attn_grad, bank_grad, logits_a_grad, logits_b_grad)


def ring_local(dp_size, tensor_size, attn_out, frozen_weight, vector_bank, logits_a, index_a, logits_b, index_b, out_grad):
    depth = tensor_size
    chips = tensor_size // 2
    rows = attn_out.shape[0]
    own_width = attn_out.shape[1]
    width = frozen_weight.shape[1]
    half = width // 2
    part = own_width // ROW_PIECES
    place = lax.axis_index("dp")
    level, side = place // 2, place % 2
    tensor_index = lax.axis_index("tensor")

    ring = [(d, (d + 2) % dp_size) for d in range(dp_size)]
    swap = [(d, d ^ 1) for d in range(dp_size)]

    def hop(value):
        return lax.ppermute(value, "dp", ring)

    def cross(value):
        return lax.ppermute(value, "dp", swap)

    def collect(partial_value, step):
        target = (level - step + depth) % depth
        pairs = []
        for d in range(dp_size):
            goal = (d // 2 - step) % depth
            for chip in range(chips):
                core = 2 * chip + goal % 2
                pairs.append((d * tensor_size + (core ^ 1), d * tensor_size + core))
        other = lax.ppermute(partial_value, ("dp", "tensor"), pairs)
        paired = partial_value.astype(jnp.float32) + other.astype(jnp.float32)
        sent = paired.astype(jnp.bfloat16)
        total = paired
        for k in range(1, chips):
            pairs = []
            for d in range(dp_size):
                goal = (d // 2 - step) % depth
                source = ((goal // 2 + k) % chips) * 2 + goal % 2
                pairs.append((d * tensor_size + source, d * tensor_size + goal))
            total = total + lax.ppermute(sent, ("dp", "tensor"), pairs).astype(jnp.float32)
        return jnp.where(tensor_index == target, total, 0.0)

    first = frozen_weight[:, :half]
    later = [frozen_weight[r * part : (r + 1) * part, half:] for r in range(ROW_PIECES)]
    held = [(first, later)]
    for step in range(1, depth):
        first = hop(first)
        later = [hop(v) for v in later]
        held.append((first, later))

    attn_two = jnp.concatenate([attn_out, cross(attn_out)], axis=0)
    attn_parts = [attn_two[:, r * part : (r + 1) * part] for r in range(ROW_PIECES)]

    def grad_pair(step):
        origin = (level - step + depth) % depth
        mine = lax.dynamic_slice_in_dim(out_grad, (origin * 2 + side) * width, width, 1)
        theirs = lax.dynamic_slice_in_dim(out_grad, (origin * 2 + 1 - side) * width, width, 1)
        return jnp.concatenate([mine, cross(theirs)], axis=0)

    weights_a, picked_a, mixing_a, rows_a = compose(logits_a, index_a, vector_bank)
    weights_b, picked_b, mixing_b, rows_b = compose(logits_b, index_b, vector_bank)
    down_a = rows_a.astype(jnp.bfloat16)
    up_b = rows_b.astype(jnp.bfloat16)
    rank = down_a.shape[0]
    grad_cols = lax.dynamic_slice_in_dim(out_grad, tensor_index * own_width, own_width, 1)
    low_part = jnp.dot(attn_out, down_a.T, preferred_element_type=jnp.float32)
    back_part = jnp.dot(grad_cols, up_b.T, preferred_element_type=jnp.float32)
    both = lax.psum(jnp.concatenate([low_part, back_part], axis=1), "tensor")
    low_bf = both[:, :rank].astype(jnp.bfloat16)
    back_bf = both[:, rank:].astype(jnp.bfloat16)

    sums = [None] * ROW_PIECES
    own_total = jnp.zeros((rows, width), jnp.float32)
    cross_total = jnp.zeros((rows, width), jnp.float32)
    for step in range(depth):
        first, later = held[step]
        grads = grad_pair(step)
        out_first = jnp.dot(attn_two, first, preferred_element_type=jnp.float32)
        for r in range(ROW_PIECES):
            term = lax.dot_general(
                grads[:, :half],
                first[r * part : (r + 1) * part],
                (((1,), (1,)), ((), ())),
                preferred_element_type=jnp.float32,
            )
            sums[r] = term if sums[r] is None else sums[r] + term
        out_later = None
        for r in range(ROW_PIECES):
            term = jnp.dot(attn_parts[r], later[r], preferred_element_type=jnp.float32)
            out_later = term if out_later is None else out_later + term
            sums[r] = sums[r] + lax.dot_general(
                grads[:, half:],
                later[r],
                (((1,), (1,)), ((), ())),
                preferred_element_type=jnp.float32,
            )
        out_first = out_first.astype(jnp.bfloat16)
        out_later = out_later.astype(jnp.bfloat16)
        if step < depth - 1:
            block = collect(jnp.concatenate([out_first, out_later], axis=1), step)
            own_total = own_total + block[:rows]
            cross_total = cross_total + block[rows:]
        if step == depth - 2:
            came = cross(cross_total.astype(jnp.bfloat16)).astype(jnp.float32)
        if step == depth - 1:
            ends = [collect(out_first, step), collect(out_later, step)]
            own_end = jnp.concatenate([v[:rows] for v in ends], axis=1)
            came_end = jnp.concatenate(
                [cross(v[rows:].astype(jnp.bfloat16)) for v in ends], axis=1
            ).astype(jnp.float32)
    own_half = own_total + own_end
    other_half = came + came_end
    summed = jnp.concatenate(
        [
            jnp.where(side == 0, own_half, other_half),
            jnp.where(side == 0, other_half, own_half),
        ],
        axis=1,
    )
    layer_out = (
        summed + adapter_scale * jnp.dot(low_bf, up_b, preferred_element_type=jnp.float32)
    ).astype(jnp.bfloat16)

    adapter = adapter_scale * jnp.dot(back_bf, down_a, preferred_element_type=jnp.float32)
    pieces = []
    for r in range(ROW_PIECES):
        came_grad = cross(sums[r][rows:].astype(jnp.bfloat16)).astype(jnp.float32)
        pieces.append(sums[r][:rows] + came_grad + adapter[:, r * part : (r + 1) * part])
    attn_grad = jnp.concatenate(pieces, axis=1).astype(jnp.bfloat16)

    factor = adapter_scale / (rows * dp_size)
    grad_a = factor * lax.dot_general(
        back_bf, attn_out, (((0,), (0,)), ((), ())), preferred_element_type=jnp.float32
    )
    grad_b = factor * lax.dot_general(
        low_bf, grad_cols, (((0,), (0,)), ((), ())), preferred_element_type=jnp.float32
    )
    bank_a, logit_grad_a = compose_back(grad_a, weights_a, picked_a, mixing_a, vector_bank)
    bank_b, logit_grad_b = compose_back(grad_b, weights_b, picked_b, mixing_b, vector_bank)
    bank_grad = lax.psum(bank_a + bank_b, ("dp", "tensor"))
    logits_a_grad, logits_b_grad = lax.psum((logit_grad_a, logit_grad_b), "dp")
    return (layer_out, attn_grad, bank_grad, logits_a_grad, logits_b_grad)


MESH_ID = pl.DeviceIdType.MESH
PIECES = 8


def dot_nn(a, b):
    return jnp.dot(a, b, preferred_element_type=jnp.float32)


def dot_nt(a, b):
    return lax.dot_general(a, b, (((1,), (1,)), ((), ())), preferred_element_type=jnp.float32)


def exchange_kernel(
    factor,
    attn, weight, grad, bank_hbm, logits_a, index_a, logits_b, index_b,
    ybuf0, drecv, relay, bank_out, slope_a, slope_b,
    wbuf, abuf0, abuf1, gbuf0, gbuf1, dacc0, dacc1, cbuf0, cbuf1, ybuf1, dsend,
    cacc0, cacc1, lb, low, back,
    down, up, bank, mixing, sums, came,
    load_sem, zs_send, relay_recv, relay_send, far_recv, xs_send, x_recv, xf_send, xf_recv,
    g_send, g_recv, gm_send, gm_recv, a_send, a_recv, mid_send, mid_recv, lb_send, lb_recv,
    c_send, c_recv, y_send, y_recv, zc_send, zc_recv, d_send, d_recv,
    sum_send, sum_recv,
):
    rows, depth = attn.shape
    width = weight.shape[1]
    half = width // 2
    step = depth // PIECES
    few = rows // 32
    abufs, gbufs, daccs = (abuf0, abuf1), (gbuf0, gbuf1), (dacc0, dacc1)
    cbufs, caccs = (cbuf0, cbuf1), (cacc0, cacc1)
    rank = down.shape[0]
    own = up.shape[1]

    dp, t = lax.axis_index("dp"), lax.axis_index("tensor")
    z, x = dp // 2, dp % 2
    y, c = t // 2, t % 2
    zh, zl = z // 2, z % 2
    inner = (z == 1) | (z == 2)
    pz = zh * 2 + (1 - zl)
    mz = jnp.where(z == 1, 2, 1)
    x_dev = (z * 2 + (1 - x), t)
    p_dev = (pz * 2 + x, t)
    m_dev = (mz * 2 + x, t)
    c_dev = (dp, y * 2 + (1 - c))
    y_dev = (dp, (1 - y) * 2 + c)
    reduces = c == zl

    def remote(src, dst, send, recv, device):
        return pltpu.make_async_remote_copy(
            src_ref=src, dst_ref=dst, send_sem=send, recv_sem=recv,
            device_id=device, device_id_type=MESH_ID,
        )

    extra = pl.ds(rows, few)
    lead = pl.ds(0, few)

    def sent_rows(is_inner):
        return pl.ds(few, rows - few) if is_inner else pl.ds(0, rows)

    def taken_rows(is_inner):
        return sent_rows(not is_inner)

    def each_kind(act):
        for kind in (True, False):

            @pl.when(inner == kind)
            def _():
                act(kind)

    def rowsof(p):
        return pl.ds(pl.multiple_of(p * step, step), step)

    barrier = pltpu.get_barrier_semaphore()
    others = [(dp, (t + k) % 4) for k in (1, 2, 3)]
    for device in others + [x_dev, p_dev]:
        pl.semaphore_signal(barrier, inc=1, device_id=device, device_id_type=MESH_ID)

    @pl.when(inner)
    def _():
        pl.semaphore_signal(barrier, inc=1, device_id=m_dev, device_id_type=MESH_ID)

    def column_block(zz, b, xx):
        zb = jnp.where(b < 2, zz, (zz + 2) % 4)
        xb = jnp.where(b % 2 == 0, xx, 1 - xx)
        return zb * 2 + xb

    loads = [pltpu.make_async_copy(attn, abuf0, load_sem.at[0])]
    gq = pltpu.make_async_copy(
        grad.at[:, pl.ds(pl.multiple_of(t * own, own), own)], dsend.at[pl.ds(0, rows), pl.ds(0, own)], load_sem.at[1]
    )
    loads.append(gq)
    bank_load = pltpu.make_async_copy(bank_hbm, bank, load_sem.at[5])
    bank_load.start()
    for n in range(2):
        loads.append(
            pltpu.make_async_copy(weight.at[:, pl.ds(n * half, half)], wbuf.at[n], load_sem.at[2 + n])
        )
    for s in range(8):
        col = column_block(z, s // 2, x) * width + (s % 2) * half
        loads.append(
            pltpu.make_async_copy(
                grad.at[:, pl.ds(pl.multiple_of(col, half), half)], gbuf0.at[s], load_sem.at[4]
            )
        )
    for load in loads[:2]:
        load.start()

    @pl.when(inner)
    def _():
        pl.semaphore_wait(barrier, 6)

    @pl.when(jnp.logical_not(inner))
    def _():
        pl.semaphore_wait(barrier, 5)

    total = 2 * PIECES
    narrow = half // 2

    def area(n, p):
        return pl.ds(pl.multiple_of(p * step, step), step), pl.ds(0, half)

    def weight_area(n, p):
        return weight.at[area(n, p)[0], pl.ds(n * half, half)]

    def by_half(i, act):
        for n in range(2):

            @pl.when(i // PIECES == n)
            def _():
                act(n, i % PIECES)

    def x_own(n, p):
        i = n * PIECES + p
        return remote(weight_area(n, p), wbuf.at[(2 + n, *area(n, p))], xs_send.at[0], x_recv.at[i], x_dev)

    def z_own(n, p):
        i = n * PIECES + p
        stream = jnp.where(inner, 0, 1)
        device = (jnp.where(inner, mz, pz) * 2 + x, t)
        return remote(
            weight_area(n, p), relay.at[(stream, n, *area(n, p))],
            zs_send.at[0], relay_recv.at[stream, i], device,
        )

    def g_columns(zz, n):
        col = column_block(zz, t, x) * width + n * half
        return pl.ds(pl.multiple_of(col, half), half)

    def g_own(n, part):
        return remote(
            grad.at[part, g_columns(pz, n)], gbuf1.at[2 * t + n, part], g_send.at[0], g_recv.at[n], p_dev
        )

    def g_mid(n):
        return remote(
            grad.at[lead, g_columns(mz, n)], gbuf1.at[2 * t + n, extra], mid_send.at[n], mid_recv.at[n], m_dev
        )

    def a_own(part):
        return remote(attn.at[part], abuf1.at[part], a_send.at[0], a_recv.at[0], p_dev)

    a_mid = remote(attn.at[lead], abuf1.at[extra], mid_send.at[2], mid_recv.at[2], m_dev)
    early = PIECES // 2

    @pl.when(inner)
    def _():
        for n in range(2):
            g_own(n, sent_rows(True)).start()
            g_mid(n).start()
        a_own(sent_rows(True)).start()
        a_mid.start()

    @pl.when(jnp.logical_not(inner))
    def _():
        for n in range(2):
            g_own(n, sent_rows(False)).start()

        @pl.loop(0, early)
        def _(i):
            z_own(0, i).start()

        a_own(sent_rows(False)).start()

    @pl.loop(0, PIECES)
    def _(i):
        x_own(0, i).start()

        @pl.when(inner)
        def _():
            z_own(0, i).start()

    for load in loads[2:]:
        load.start()

    bank_load.wait()
    levels = bank.shape[0]
    sublen = bank.shape[1]
    vectors = mixing.shape[2]
    per_row = vectors // rank
    exact = dict(preferred_element_type=jnp.float32, precision=lax.Precision.HIGHEST)

    place = lax.broadcasted_iota(jnp.int32, (rank, vectors), 1)
    spread = (place % rank == lax.broadcasted_iota(jnp.int32, (rank, vectors), 0)).astype(jnp.float32)
    place = lax.broadcasted_iota(jnp.int32, (per_row, vectors), 1)
    keep = place // rank == lax.broadcasted_iota(jnp.int32, (per_row, vectors), 0)
    level = lax.broadcasted_iota(jnp.int32, (levels, vectors), 0)

    def as_row(value):
        wide_value = jnp.dot(value.astype(jnp.float32), spread, **exact)
        return jnp.sum(jnp.where(keep, wide_value, 0.0), axis=0, keepdims=True)

    def from_row(row):
        return lax.dot_general(jnp.where(keep, row, 0.0), spread, (((1,), (1,)), ((), ())), **exact)

    shares, found = [], []
    for k, (logits, indices) in enumerate(((logits_a, index_a), (logits_b, index_b))):
        first, second = as_row(logits[:, 0, :]), as_row(logits[:, 1, :])
        shares.append((1.0 / (1.0 + jnp.exp(second - first)), 1.0 / (1.0 + jnp.exp(first - second))))
        picks = [(as_row(indices[:, m, :]) + 0.5).astype(jnp.int32) for m in range(2)]
        found.append([level == pick for pick in picks])

    for k, target in enumerate((down, up)):
        mixing[k] = sum(jnp.where(found[k][m], shares[k][m], 0.0) for m in range(2))
        blocks = lax.dot_general(mixing[k], bank[...], (((0,), (0,)), ((), ())), **exact)
        for j in range(per_row):
            row = blocks[j * rank : (j + 1) * rank]
            target[:, j * sublen : (j + 1) * sublen] = row.astype(jnp.bfloat16)

    loads[0].wait()
    loads[1].wait()
    lb[t, :rank] = dot_nt(down[...], abuf0[...])
    lb[t, rank:] = dot_nt(up[...], dsend[:rows, :own])

    def lb_copy(k):
        device = (dp, (t + k) % 4)
        return remote(lb.at[t], lb.at[t], lb_send.at[0], lb_recv.at[0], device)

    for k in (1, 2, 3):
        lb_copy(k).start()
    for load in loads[2:4]:
        load.wait()
    pltpu.make_async_copy(gbuf0, gbuf0, load_sem.at[4]).wait()
    dacc0[...] = jnp.zeros_like(dacc0)
    dacc1[...] = jnp.zeros_like(dacc1)

    @pl.when(jnp.logical_not(inner))
    def _():
        for part in (lead, extra):
            abuf1[part] = jnp.zeros_like(abuf1[part])
            gbuf1[:, part] = jnp.zeros_like(gbuf1[:, part])

    three = lb.at[pl.ds(0, 3)]
    remote(three, three, lb_send.at[0], lb_recv.at[0], y_dev).wait()
    both = lb[0] + lb[1] + lb[2] + lb[3]
    low[...] = both[:rank].T.astype(jnp.bfloat16)
    back[...] = both[rank:].T.astype(jnp.bfloat16)
    both = both.astype(jnp.bfloat16)
    slopes = (
        factor * dot_nn(both[rank:], abuf0[...]),
        factor * dot_nn(both[:rank], dsend[:rows, :own]),
    )
    bank_out[...] = jnp.zeros_like(bank_out)
    dots = []
    for k in range(2):
        pieces = [slopes[k][:, j * sublen : (j + 1) * sublen] for j in range(per_row)]
        stacked = jnp.concatenate(pieces, axis=0)
        bank_out[...] += jnp.dot(mixing[k], stacked, **exact)
        projected = lax.dot_general(bank[...], stacked, (((1,), (1,)), ((), ())), **exact)
        for m in range(2):
            dots.append(jnp.sum(jnp.where(found[k][m], projected, 0.0), axis=0, keepdims=True))

    q1, q2, q3 = levels // 2, levels // 4, levels // 8
    pack = q3 + 8
    at_c = c * q1
    at_y = at_c + y * q2
    at_x = at_y + x * q3
    counts = (q1, q2, pack, pack, pack, q3, q2, q1)
    places = [pl.ds(sum(counts[:k]), counts[k]) for k in range(8)]

    def bank_rows(start, count):
        return pl.ds(pl.multiple_of(start, 8), count)

    def sum_copy(k, source, device):
        return remote(source, came.at[places[k]], sum_send.at[0], sum_recv.at[k], device)

    core_sum = sum_copy(0, bank_out.at[bank_rows((1 - c) * q1, q1)], c_dev)
    y_sum = sum_copy(1, bank_out.at[bank_rows(at_c + (1 - y) * q2, q2)], y_dev)
    x_sum = sum_copy(2, sums, x_dev)
    p_sum = sum_copy(3, sums, p_dev)
    m_sum = sum_copy(4, sums, m_dev)
    x_all = sum_copy(5, bank_out.at[bank_rows(at_x, q3)], x_dev)
    y_all = sum_copy(6, bank_out.at[bank_rows(at_y, q2)], y_dev)
    c_all = sum_copy(7, bank_out.at[bank_rows(at_c, q1)], c_dev)
    core_sum.start()
    core_sum.wait()
    bank_out[bank_rows(at_c, q1)] += came[places[0]]
    y_sum.start()
    y_sum.wait()
    bank_out[bank_rows(at_y, q2)] += came[places[1]]
    sums[:q3] = bank_out[bank_rows(at_y + (1 - x) * q3, q3)]
    sums[q3:] = jnp.zeros_like(sums[q3:])
    for k in range(4):
        sums[q3 + k : q3 + k + 1, :vectors] = dots[k]
    x_sum.start()

    @pl.loop(0, PIECES)
    def _(i):
        x_own(1, i).start()

    def relay_on(stream, n, p):
        i = n * PIECES + p
        device = (jnp.where(stream == 0, pz, mz) * 2 + x, t)
        return remote(
            relay.at[(stream, n, *area(n, p))], wbuf.at[(4 + n, *area(n, p))],
            relay_send.at[stream], far_recv.at[i], device,
        )

    def relay_wait(stream, n, p):
        i = n * PIECES + p
        piece = relay.at[(stream, n, *area(n, p))]
        remote(piece, piece, relay_send.at[stream], relay_recv.at[stream, i], p_dev).wait_recv()

    def x_far(n, p):
        i = n * PIECES + p
        return remote(
            wbuf.at[(4 + n, *area(n, p))], wbuf.at[(6 + n, *area(n, p))], xf_send.at[0], xf_recv.at[i], x_dev
        )

    def far_wait(n, p):
        i = n * PIECES + p
        piece = wbuf.at[(4 + n, *area(n, p))]
        remote(piece, piece, xf_send.at[0], far_recv.at[i], x_dev).wait_recv()

    def g_spread(k, n, is_inner):
        part = pl.ds(0, rows + few) if is_inner else taken_rows(False)
        piece = gbuf1.at[2 * t + n, part]
        return remote(piece, piece, gm_send.at[0], gm_recv.at[0], (dp, (t + k) % 4))

    def g_everything(is_inner):
        part = pl.ds(0, rows + few) if is_inner else taken_rows(False)
        return gbuf1.at[pl.ds(0, 6), part]

    ticks = 33

    def tick(i, carry):
        def near(n, p):
            x_own(n, p).wait_recv()

        @pl.when(i < total)
        def _():
            by_half(i, near)

        def outward(n, p):
            relay_wait(0, n, p)
            relay_on(0, n, p).start()

        @pl.when(inner & (i >= 2) & (i < 2 + PIECES))
        def _():
            outward(0, i - 2)

        @pl.when(inner & (i >= 15) & (i < 15 + PIECES))
        def _():
            outward(1, i - 15)

        def onward(n, p):
            relay_wait(1, n, p)
            relay_on(1, n, p).start()

        @pl.when(inner & (i >= 5) & (i < 5 + early))
        def _():
            onward(0, i - 5)

        @pl.when(inner & (i >= 16) & (i < 12 + total))
        def _():
            by_half(i - 12, onward)

        @pl.when(i == PIECES)
        def _():
            x_sum.wait()
            sums[:q3] = bank_out[bank_rows(at_x, q3)] + came[places[2]][:q3]
            sums[q3:] += came[places[2]][q3:]

            @pl.when(jnp.logical_not(inner))
            def _():
                p_sum.start()

                @pl.loop(early, PIECES)
                def _(k):
                    z_own(0, k).start()

            @pl.loop(0, PIECES)
            def _(k):
                z_own(1, k).start()

        @pl.when(i == 16)
        def _():
            @pl.when(jnp.logical_not(inner))
            def _():
                p_sum.wait_send()

            @pl.when(inner)
            def _():
                p_sum.wait_recv()
                sums[...] += came[places[3]]
                m_sum.start()

        @pl.when((i == 23) & inner)
        def _():
            m_sum.wait()
            sums[...] += came[places[4]]
            p_sum.start()

        @pl.when(i == 4)
        def _():
            def spread(is_inner):
                for n in range(2):
                    g_own(n, taken_rows(is_inner)).wait_recv()
                    if is_inner:
                        g_mid(n).wait_recv()
                    for k in (1, 2, 3):
                        g_spread(k, n, is_inner).start()

            each_kind(spread)

        def far(n, p):
            far_wait(n, p)
            x_far(n, p).start()

        wait = jnp.where(inner & (i >= 21), 17, 12)

        @pl.when((i >= 12) & (i - wait < total) & (jnp.logical_not(inner) | (i < 16) | (i >= 21)))
        def _():
            by_half(i - wait, far)

        return carry

    def c_copy(s, r):
        piece = cbufs[r].at[s]
        return remote(piece, piece, c_send.at[r], c_recv.at[s, r], c_dev)

    def y_copy(s, r):
        j = s % 4
        target = (ybuf0, ybuf1)[r].at[j]
        return remote(cbufs[r].at[s], target, y_send.at[r], y_recv.at[j, r], y_dev)

    def z_copy(s, part):
        j = s % 4
        return remote(cbuf1.at[s, part], ybuf0.at[j, part], zc_send.at[0], zc_recv.at[j], p_dev)

    def z_mid(s):
        j = s % 4
        return remote(cbuf1.at[s, extra], ybuf0.at[j, lead], zc_send.at[1], zc_recv.at[j], m_dev)

    def kept(s):
        return jnp.where(s < 4, zh, 1 - zh) == y

    def out_columns(j):
        xb = jnp.where(j < 2, x, 1 - x)
        return pl.ds(pl.multiple_of(xb * width + (j % 2) * half, half), half)

    def adapter_out(j):
        return 2.0 * dot_nn(low[...], up[:, out_columns(j)])

    def by_side(r, act):
        if isinstance(r, int):
            act(r)
            return
        for side in range(2):

            @pl.when(r == side)
            def _():
                act(side)

    def pass_core(s, r, k):
        @pl.when(jnp.logical_not(reduces))
        def _():
            cbufs[r][s] = caccs[r][k].astype(jnp.bfloat16)
            c_copy(s, r).start()

    def sum_core(s, r, k):
        def act(r):
            c_copy(s, r).wait_recv()
            cbufs[r][s] = (caccs[r][k] + cbufs[r][s].astype(jnp.float32)).astype(jnp.bfloat16)

            @pl.when(jnp.logical_not(kept(s)))
            def _():
                y_copy(s, r).start()

        @pl.when(reduces)
        def _():
            by_side(r, act)

    def sum_y(s, r):
        j = s % 4

        def act(r):
            y_copy(s, r).wait_recv()
            came_here = (ybuf0, ybuf1)[r][j].astype(jnp.float32)
            total_here = cbufs[r][s].astype(jnp.float32) + came_here
            if r == 0:
                ybuf0[j] = (total_here + adapter_out(j)).astype(jnp.bfloat16)
            else:
                cbuf1[s] = total_here.astype(jnp.bfloat16)
                each_kind(lambda is_inner: z_copy(s, taken_rows(is_inner)).start())

                @pl.when(inner)
                def _():
                    z_mid(s).start()

        @pl.when(reduces & kept(s))
        def _():
            by_side(r, act)

    def finish_other(j):
        @pl.when(jnp.logical_not(reduces))
        def _():
            whole = ybuf0.at[j]
            remote(whole, whole, zc_send.at[0], zc_recv.at[j], p_dev).wait_recv()
            ybuf0[j] = (ybuf0[j].astype(jnp.float32) + adapter_out(j)).astype(jnp.bfloat16)

    slots = (0, 1, 2, 0, 1, 2, 3, 3, 4, 4, 6, 6)
    sides = (0, 0, 0, 1, 1, 1, 0, 1, 0, 1, 0, 1)

    def pick(table, u):
        if isinstance(u, int):
            return table[u]
        value = table[0]
        for k in range(1, len(table)):
            if table[k] != table[k - 1]:
                value = jnp.where(u >= k, table[k], value)
        return value

    def ready(u):
        value = jnp.where(u >= 2, PIECES, 0)
        value = jnp.where(u >= 3, 16, value)
        value = jnp.where(u >= 8, jnp.where(inner, 25, 20), value)
        return jnp.where(u >= 10, 26, value)

    def tiles(r):
        count = rows + few * r
        return [pl.ds(m * (count // 2), count // 2) for m in range(2)]

    def unit(u, carry):
        s, r = pick(slots, u), pick(sides, u)
        lax.fori_loop(ready(u - 1), ready(u), tick, 0)

        @pl.when(u == 3)
        def _():
            def arrived(is_inner):
                a_own(taken_rows(is_inner)).wait_recv()
                if is_inner:
                    a_mid.wait_recv()
                everything = g_everything(is_inner)
                remote(everything, everything, gm_send.at[0], gm_recv.at[0], y_dev).wait_recv()

            each_kind(arrived)

        @pl.when(u == 10)
        def _():
            for p in range(PIECES):
                x_far(0, p).wait_recv()


        def act(r):
            for part in tiles(r):
                caccs[r][u % 2, part] = dot_nn(abufs[r][part], wbuf[s])
                daccs[r][part] += dot_nt(gbufs[r][s, part], wbuf[s])
            pass_core(s, r, u % 2)

        by_side(r, act)

        @pl.when(u >= 1)
        def _():
            sum_core(pick(slots, u - 1), pick(sides, u - 1), (u - 1) % 2)

        @pl.when(u >= 4)
        def _():
            sum_y(pick(slots, u - 4), pick(sides, u - 4))

        return carry

    lax.fori_loop(0, 12, unit, 0)
    sum_core(slots[11], sides[11], 1)
    cacc0[...] = jnp.zeros_like(cacc0)
    cacc1[...] = jnp.zeros_like(cacc1)

    final = ((7, 1), (7, 0))

    def grad_part(p):
        return pl.ds(pl.multiple_of(p * step, step), step)

    def d_copy(p, part):
        columns = grad_part(p)
        return remote(dsend.at[part, columns], drecv.at[part, columns], d_send.at[0], d_recv.at[p], p_dev)

    def d_mid(p):
        columns = grad_part(p)
        return remote(dsend.at[extra, columns], drecv.at[lead, columns], d_send.at[1], d_recv.at[p], m_dev)

    def last_piece(p, carry):
        done = 26 + p
        lax.fori_loop(jnp.minimum(done, ticks), jnp.minimum(done + 1, ticks), tick, 0)

        def ahead(p):
            columns = grad_part(p)
            for r in range(2):
                caccs[r][0] += dot_nn(abufs[r][:, columns], wbuf[5, columns])

        @pl.when(p == 0)
        def _():
            ahead(0)

        @pl.when(p < PIECES - 1)
        def _():
            ahead(p + 1)

        @pl.when(p == PIECES - 2)
        def _():
            for side in (1, 0):
                pass_core(5, side, 0)

        x_far(1, p).wait_recv()
        columns = grad_part(p)
        for r in (1, 0):
            for part in tiles(r):
                grown = daccs[r][part, columns]
                grown += dot_nt(gbufs[r][5, part], wbuf[5, columns])
                grown += dot_nt(gbufs[r][7, part], wbuf[7, columns])
                if r == 1:
                    dsend[part, columns] = grown.astype(jnp.bfloat16)
                else:
                    dacc0[part, columns] = grown
            if r == 1:
                each_kind(lambda is_inner: d_copy(p, taken_rows(is_inner)).start())

                @pl.when(inner)
                def _():
                    d_mid(p).start()

        for r in range(2):
            caccs[r][1] += dot_nn(abufs[r][:, columns], wbuf[7, columns])

        @pl.when(p == PIECES - 2)
        def _():
            for side in (1, 0):
                sum_core(5, side, 0)


        @pl.when(p == 1)
        def _():
            @pl.when(inner)
            def _():
                p_sum.wait_send()

            @pl.when(jnp.logical_not(inner))
            def _():
                p_sum.wait_recv()
                sums[...] = came[places[3]]

            bank_out[bank_rows(at_x, q3)] = sums[:q3]
            x_all.start()

        @pl.when(p == 3)
        def _():
            x_all.wait()
            bank_out[bank_rows(at_y + (1 - x) * q3, q3)] = came[places[5]]
            y_all.start()

        @pl.when((p >= 1) & (p < 5))
        def _():
            sum_y(pick(slots, 7 + p), (p - 1) % 2)

        @pl.when(p == 5)
        def _():
            y_all.wait()
            bank_out[bank_rows(at_c + (1 - y) * q2, q2)] = came[places[6]]
            c_all.start()

        return carry

    lax.fori_loop(0, PIECES, last_piece, 0)

    def finish_grad(p, carry):
        columns = grad_part(p)
        whole = drecv.at[:, columns]
        remote(whole, whole, d_send.at[0], d_recv.at[p], p_dev).wait_recv()
        total_here = dacc0[:, columns] + drecv[:, columns].astype(jnp.float32)
        drecv[:, columns] = (total_here + 2.0 * dot_nn(back[...], down[:, columns])).astype(jnp.bfloat16)
        return carry

    for slot, side in final:
        pass_core(slot, side, 1)
    for slot, side in final:
        sum_core(slot, side, 1)
    c_all.wait()
    bank_out[bank_rows((1 - c) * q1, q1)] = came[places[7]]
    for k, target in enumerate((slope_a, slope_b)):
        values = [sums[q3 + 2 * k + m : q3 + 2 * k + m + 1, :vectors] for m in range(2)]
        mean = shares[k][0] * values[0] + shares[k][1] * values[1]
        for m in range(2):
            target[:, m, :] = from_row(shares[k][m] * (values[m] - mean))
    finish_other(0)
    finish_other(2)
    for slot, side in ((5, 1), (5, 0), (7, 1), (7, 0)):
        sum_y(slot, side)
    lax.fori_loop(0, PIECES, finish_grad, 0)
    finish_other(1)
    finish_other(3)
    def drain(buffer, semaphore):
        remote(buffer, buffer, semaphore, a_recv.at[0], p_dev).wait_send()

    def drain_kind(is_inner):
        a_own(sent_rows(is_inner)).wait_send()
        drain(gbuf1.at[pl.ds(0, 2), sent_rows(is_inner)], g_send.at[0])
        drain(g_everything(is_inner), gm_send.at[0])
        drain(dsend.at[taken_rows(is_inner)], d_send.at[0])
        if is_inner:
            a_mid.wait_send()
            for n in range(2):
                g_mid(n).wait_send()
                drain(relay.at[n], relay_send.at[n])
            drain(dsend.at[extra], d_send.at[1])

        @pl.when(reduces)
        def _():
            drain(gbuf1.at[pl.ds(0, 4), taken_rows(is_inner)], zc_send.at[0])
            if is_inner:
                drain(gbuf1.at[pl.ds(0, 4), extra], zc_send.at[1])

    each_kind(drain_kind)
    drain(weight, xs_send.at[0])
    drain(weight, zs_send.at[0])
    drain(weight, xf_send.at[0])

    @pl.when(jnp.logical_not(reduces))
    def _():
        for r in range(2):
            drain(cbufs[r], c_send.at[r])

    @pl.when(reduces)
    def _():
        for r in range(2):
            drain(cbufs[r].at[pl.ds(0, 4)], y_send.at[r])


def settle_kernel(width, *refs):
    sources, targets, sem = refs[:5], refs[5:10], refs[10]
    half = sources[0].shape[2]
    x = lax.axis_index("dp") % 2
    copies = []
    for j in range(4):
        col = (x if j < 2 else 1 - x) * width + (j % 2) * half
        columns = pl.ds(pl.multiple_of(col, half), half)
        copies.append(pltpu.make_async_copy(sources[0].at[j], targets[0].at[:, columns], sem.at[j]))
    for k in range(1, 5):
        copies.append(pltpu.make_async_copy(sources[k], targets[k], sem.at[3 + k]))
    for copy in copies:
        copy.start()
    for copy in copies:
        copy.wait()


def fused_local(dp_size, attn_out, frozen_weight, vector_bank, logits_a, index_a, logits_b, index_b, out_grad):
    rows, depth = attn_out.shape
    width = frozen_weight.shape[1]
    half = width // 2
    levels, sublen = vector_bank.shape
    rank, per_row, _ = logits_a.shape
    vectors = rank * per_row
    own = logits_b.shape[1] * sublen
    factor = adapter_scale / (rows * dp_size)
    total = 2 * PIECES
    more = rows + rows // 32
    small = [v.transpose(1, 2, 0) for v in (logits_a, index_a, logits_b, index_b)]
    bf16, f32 = jnp.bfloat16, jnp.float32
    dma = pltpu.SemaphoreType.DMA
    hbm = pl.BlockSpec(memory_space=pl.ANY)
    vmem = pl.BlockSpec(memory_space=pltpu.VMEM)
    layer_out, attn_grad, _, bank_grad, slope_a, slope_b = pl.pallas_call(
        functools.partial(exchange_kernel, factor),
        name="exchange",
        out_shape=(
            pltpu.VMEM((4, rows, half), bf16),
            pltpu.VMEM((rows, depth), bf16),
            jax.ShapeDtypeStruct((2, 2, depth, half), bf16),
            pltpu.VMEM((levels, sublen), f32),
            pltpu.VMEM((per_row, 2, rank), f32),
            pltpu.VMEM((per_row, 2, rank), f32),
        ),
        in_specs=[hbm, hbm, hbm, hbm, vmem, vmem, vmem, vmem],
        out_specs=(vmem, vmem, hbm, vmem, vmem, vmem),
        scratch_shapes=[
            pltpu.VMEM((8, depth, half), bf16),
            pltpu.VMEM((rows, depth), bf16),
            pltpu.VMEM((more, depth), bf16),
            pltpu.VMEM((8, rows, half), bf16),
            pltpu.VMEM((8, more, half), bf16),
            pltpu.VMEM((rows, depth), f32),
            pltpu.VMEM((more, depth), f32),
            pltpu.VMEM((8, rows, half), bf16),
            pltpu.VMEM((8, more, half), bf16),
            pltpu.VMEM((4, more, half), bf16),
            pltpu.VMEM((more, depth), bf16),
            pltpu.VMEM((2, rows, half), f32),
            pltpu.VMEM((2, more, half), f32),
            pltpu.VMEM((4, 2 * rank, rows), f32),
            pltpu.VMEM((rows, rank), bf16),
            pltpu.VMEM((rows, rank), bf16),
            pltpu.VMEM((rank, depth), bf16),
            pltpu.VMEM((rank, own), bf16),
            pltpu.VMEM((levels, sublen), f32),
            pltpu.VMEM((2, levels, vectors), f32),
            pltpu.VMEM((levels // 8 + 8, sublen), f32),
            pltpu.VMEM((2 * levels + 24, sublen), f32),
            dma((6,)), dma((1,)), dma((2, total)), dma((2,)), dma((total,)),
            dma((1,)), dma((total,)), dma((1,)), dma((total,)),
            dma((1,)), dma((2,)), dma((1,)), dma((1,)), dma((1,)), dma((1,)), dma((3,)), dma((3,)),
            dma((1,)), dma((1,)),
            dma((2,)), dma((8, 2)), dma((2,)), dma((4, 2)), dma((2,)), dma((4,)),
            dma((2,)), dma((PIECES,)), dma((1,)), dma((8,)),
        ],
        compiler_params=pltpu.CompilerParams(
            collective_id=0, has_side_effects=True, vmem_limit_bytes=67043328 - 5 * 2**20
        ),
    )(attn_out, frozen_weight, out_grad, vector_bank, *small)
    targets = [((rows, own), bf16), ((rows, depth), bf16), ((levels, sublen), f32)]
    targets += [(v.shape, f32) for v in (slope_a, slope_b)]
    kept = [pltpu.with_memory_space_constraint(v, pltpu.VMEM) for v in (layer_out, attn_grad, bank_grad, slope_a, slope_b)]
    layer_out, attn_grad, bank_grad, slope_a, slope_b = pl.pallas_call(
        functools.partial(settle_kernel, width),
        name="settle",
        out_shape=[jax.ShapeDtypeStruct(*v) for v in targets],
        in_specs=[hbm] * 5,
        out_specs=[hbm] * 5,
        scratch_shapes=[dma((8,))],
        compiler_params=pltpu.CompilerParams(vmem_limit_bytes=16 * 2**20),
    )(*kept)
    return (layer_out, attn_grad, bank_grad, slope_a.transpose(2, 0, 1), slope_b.transpose(2, 0, 1))


def solution(mesh):
    dp_size, tensor_size = mesh.shape["dp"], mesh.shape["tensor"]
    paired = dp_size == 2 * tensor_size and tensor_size % 2 == 0
    body = functools.partial(ring_local, dp_size, tensor_size) if paired else local
    if paired and tensor_size == 4:
        body = functools.partial(fused_local, dp_size)
    return jax.shard_map(
        body,
        mesh=mesh,
        in_specs=(
            P("dp", "tensor"),
            P("tensor", "dp"),
            P(),
            P(None, "tensor", None),
            P(None, "tensor", None),
            P(None, "tensor", None),
            P(None, "tensor", None),
            P("dp", None),
        ),
        out_specs=(
            P("dp", "tensor"),
            P("dp", "tensor"),
            P(),
            P(None, "tensor", None),
            P(None, "tensor", None),
        ),
        check_vma=False,
    )
```

```python
import functools

import jax
import jax.numpy as jnp
from jax import lax
from jax.experimental import pallas as pl
from jax.experimental.pallas import tpu as pltpu
from jax.sharding import PartitionSpec as P

adapter_scale = 2.0
ROW_PIECES = 4


def compose(logits, indices, vector_bank):
    weights = jax.nn.sigmoid(logits - logits[..., ::-1])
    levels = jnp.arange(vector_bank.shape[0], dtype=jnp.int32)
    picked = (indices[..., None] == levels).astype(jnp.float32)
    mixing = jnp.sum(picked * weights[..., None], axis=2)
    blocks = jnp.einsum("rjb,bc->rjc", mixing, vector_bank, precision=lax.Precision.HIGHEST)
    return (weights, picked, mixing, blocks.reshape(blocks.shape[0], -1))


def compose_back(grad_rows, weights, picked, mixing, vector_bank):
    blocks = grad_rows.reshape(mixing.shape[0], mixing.shape[1], -1)
    bank_part = jnp.einsum("rjb,rjc->bc", mixing, blocks, precision=lax.Precision.HIGHEST)
    projected = jnp.einsum("rjc,bc->rjb", blocks, vector_bank, precision=lax.Precision.HIGHEST)
    dots = jnp.sum(picked * projected[:, :, None, :], axis=3)
    logit_grad = weights * (dots - jnp.sum(weights * dots, axis=2, keepdims=True))
    return (bank_part, logit_grad)


def local(attn_out, frozen_weight, vector_bank, logits_a, index_a, logits_b, index_b, out_grad):
    weights_a, picked_a, mixing_a, rows_a = compose(logits_a, index_a, vector_bank)
    weights_b, picked_b, mixing_b, rows_b = compose(logits_b, index_b, vector_bank)
    down_a = rows_a.astype(jnp.bfloat16)
    up_b = rows_b.astype(jnp.bfloat16)
    own_width = up_b.shape[1]
    grad_cols = lax.dynamic_slice_in_dim(
        out_grad, lax.axis_index("tensor") * own_width, own_width, 1
    )
    low_part = jnp.dot(attn_out, down_a.T, preferred_element_type=jnp.float32)
    back_part = jnp.dot(grad_cols, up_b.T, preferred_element_type=jnp.float32)
    low_total = lax.psum(low_part, "tensor")
    low_bf = low_total.astype(jnp.bfloat16)
    gathered = lax.all_gather(frozen_weight, "dp", axis=1, tiled=True)
    partial_value = jnp.dot(attn_out, gathered, preferred_element_type=jnp.float32).astype(
        jnp.bfloat16
    )
    summed = lax.psum_scatter(partial_value, "tensor", scatter_dimension=1, tiled=True).astype(
        jnp.float32
    )
    layer_out = (
        summed + adapter_scale * jnp.dot(low_bf, up_b, preferred_element_type=jnp.float32)
    ).astype(jnp.bfloat16)
    back_total = lax.psum(back_part, "tensor")
    back_bf = back_total.astype(jnp.bfloat16)
    main = lax.dot_general(
        out_grad, gathered, (((1,), (1,)), ((), ())), preferred_element_type=jnp.float32
    )
    attn_grad = (
        main + adapter_scale * jnp.dot(back_bf, down_a, preferred_element_type=jnp.float32)
    ).astype(jnp.bfloat16)
    factor = adapter_scale / (attn_out.shape[0] * lax.axis_size("dp"))
    grad_a = factor * lax.dot_general(
        back_bf, attn_out, (((0,), (0,)), ((), ())), preferred_element_type=jnp.float32
    )
    grad_b = factor * lax.dot_general(
        low_bf, grad_cols, (((0,), (0,)), ((), ())), preferred_element_type=jnp.float32
    )
    bank_a, logit_grad_a = compose_back(grad_a, weights_a, picked_a, mixing_a, vector_bank)
    bank_b, logit_grad_b = compose_back(grad_b, weights_b, picked_b, mixing_b, vector_bank)
    bank_part = bank_a + bank_b
    bank_group = lax.psum(bank_part, "tensor")
    bank_grad, logits_a_grad, logits_b_grad = lax.psum(
        (bank_group, logit_grad_a, logit_grad_b), "dp"
    )
    return (layer_out, attn_grad, bank_grad, logits_a_grad, logits_b_grad)


def ring_local(dp_size, tensor_size, attn_out, frozen_weight, vector_bank, logits_a, index_a, logits_b, index_b, out_grad):
    depth = tensor_size
    chips = tensor_size // 2
    rows = attn_out.shape[0]
    own_width = attn_out.shape[1]
    width = frozen_weight.shape[1]
    half = width // 2
    part = own_width // ROW_PIECES
    place = lax.axis_index("dp")
    level, side = place // 2, place % 2
    tensor_index = lax.axis_index("tensor")

    ring = [(d, (d + 2) % dp_size) for d in range(dp_size)]
    swap = [(d, d ^ 1) for d in range(dp_size)]

    def hop(value):
        return lax.ppermute(value, "dp", ring)

    def cross(value):
        return lax.ppermute(value, "dp", swap)

    def collect(partial_value, step):
        target = (level - step + depth) % depth
        pairs = []
        for d in range(dp_size):
            goal = (d // 2 - step) % depth
            for chip in range(chips):
                core = 2 * chip + goal % 2
                pairs.append((d * tensor_size + (core ^ 1), d * tensor_size + core))
        other = lax.ppermute(partial_value, ("dp", "tensor"), pairs)
        paired = partial_value.astype(jnp.float32) + other.astype(jnp.float32)
        sent = paired.astype(jnp.bfloat16)
        total = paired
        for k in range(1, chips):
            pairs = []
            for d in range(dp_size):
                goal = (d // 2 - step) % depth
                source = ((goal // 2 + k) % chips) * 2 + goal % 2
                pairs.append((d * tensor_size + source, d * tensor_size + goal))
            total = total + lax.ppermute(sent, ("dp", "tensor"), pairs).astype(jnp.float32)
        return jnp.where(tensor_index == target, total, 0.0)

    first = frozen_weight[:, :half]
    later = [frozen_weight[r * part : (r + 1) * part, half:] for r in range(ROW_PIECES)]
    held = [(first, later)]
    for step in range(1, depth):
        first = hop(first)
        later = [hop(v) for v in later]
        held.append((first, later))

    attn_two = jnp.concatenate([attn_out, cross(attn_out)], axis=0)
    attn_parts = [attn_two[:, r * part : (r + 1) * part] for r in range(ROW_PIECES)]

    def grad_pair(step):
        origin = (level - step + depth) % depth
        mine = lax.dynamic_slice_in_dim(out_grad, (origin * 2 + side) * width, width, 1)
        theirs = lax.dynamic_slice_in_dim(out_grad, (origin * 2 + 1 - side) * width, width, 1)
        return jnp.concatenate([mine, cross(theirs)], axis=0)

    weights_a, picked_a, mixing_a, rows_a = compose(logits_a, index_a, vector_bank)
    weights_b, picked_b, mixing_b, rows_b = compose(logits_b, index_b, vector_bank)
    down_a = rows_a.astype(jnp.bfloat16)
    up_b = rows_b.astype(jnp.bfloat16)
    rank = down_a.shape[0]
    grad_cols = lax.dynamic_slice_in_dim(out_grad, tensor_index * own_width, own_width, 1)
    low_part = jnp.dot(attn_out, down_a.T, preferred_element_type=jnp.float32)
    back_part = jnp.dot(grad_cols, up_b.T, preferred_element_type=jnp.float32)
    both = lax.psum(jnp.concatenate([low_part, back_part], axis=1), "tensor")
    low_bf = both[:, :rank].astype(jnp.bfloat16)
    back_bf = both[:, rank:].astype(jnp.bfloat16)

    sums = [None] * ROW_PIECES
    own_total = jnp.zeros((rows, width), jnp.float32)
    cross_total = jnp.zeros((rows, width), jnp.float32)
    for step in range(depth):
        first, later = held[step]
        grads = grad_pair(step)
        out_first = jnp.dot(attn_two, first, preferred_element_type=jnp.float32)
        for r in range(ROW_PIECES):
            term = lax.dot_general(
                grads[:, :half],
                first[r * part : (r + 1) * part],
                (((1,), (1,)), ((), ())),
                preferred_element_type=jnp.float32,
            )
            sums[r] = term if sums[r] is None else sums[r] + term
        out_later = None
        for r in range(ROW_PIECES):
            term = jnp.dot(attn_parts[r], later[r], preferred_element_type=jnp.float32)
            out_later = term if out_later is None else out_later + term
            sums[r] = sums[r] + lax.dot_general(
                grads[:, half:],
                later[r],
                (((1,), (1,)), ((), ())),
                preferred_element_type=jnp.float32,
            )
        out_first = out_first.astype(jnp.bfloat16)
        out_later = out_later.astype(jnp.bfloat16)
        if step < depth - 1:
            block = collect(jnp.concatenate([out_first, out_later], axis=1), step)
            own_total = own_total + block[:rows]
            cross_total = cross_total + block[rows:]
        if step == depth - 2:
            came = cross(cross_total.astype(jnp.bfloat16)).astype(jnp.float32)
        if step == depth - 1:
            ends = [collect(out_first, step), collect(out_later, step)]
            own_end = jnp.concatenate([v[:rows] for v in ends], axis=1)
            came_end = jnp.concatenate(
                [cross(v[rows:].astype(jnp.bfloat16)) for v in ends], axis=1
            ).astype(jnp.float32)
    own_half = own_total + own_end
    other_half = came + came_end
    summed = jnp.concatenate(
        [
            jnp.where(side == 0, own_half, other_half),
            jnp.where(side == 0, other_half, own_half),
        ],
        axis=1,
    )
    layer_out = (
        summed + adapter_scale * jnp.dot(low_bf, up_b, preferred_element_type=jnp.float32)
    ).astype(jnp.bfloat16)

    adapter = adapter_scale * jnp.dot(back_bf, down_a, preferred_element_type=jnp.float32)
    pieces = []
    for r in range(ROW_PIECES):
        came_grad = cross(sums[r][rows:].astype(jnp.bfloat16)).astype(jnp.float32)
        pieces.append(sums[r][:rows] + came_grad + adapter[:, r * part : (r + 1) * part])
    attn_grad = jnp.concatenate(pieces, axis=1).astype(jnp.bfloat16)

    factor = adapter_scale / (rows * dp_size)
    grad_a = factor * lax.dot_general(
        back_bf, attn_out, (((0,), (0,)), ((), ())), preferred_element_type=jnp.float32
    )
    grad_b = factor * lax.dot_general(
        low_bf, grad_cols, (((0,), (0,)), ((), ())), preferred_element_type=jnp.float32
    )
    bank_a, logit_grad_a = compose_back(grad_a, weights_a, picked_a, mixing_a, vector_bank)
    bank_b, logit_grad_b = compose_back(grad_b, weights_b, picked_b, mixing_b, vector_bank)
    bank_grad = lax.psum(bank_a + bank_b, ("dp", "tensor"))
    logits_a_grad, logits_b_grad = lax.psum((logit_grad_a, logit_grad_b), "dp")
    return (layer_out, attn_grad, bank_grad, logits_a_grad, logits_b_grad)


MESH_ID = pl.DeviceIdType.MESH
PIECES = 8


def dot_nn(a, b):
    return jnp.dot(a, b, preferred_element_type=jnp.float32)


def dot_nt(a, b):
    return lax.dot_general(a, b, (((1,), (1,)), ((), ())), preferred_element_type=jnp.float32)


def exchange_kernel(
    factor,
    attn, weight, grad, bank_hbm, logits_a_hbm, index_a_hbm, logits_b_hbm, index_b_hbm,
    ybuf0, drecv, relay, bank_out, slope_a, slope_b,
    wbuf, abuf0, abuf1, gbuf0, gbuf1, dacc0, dacc1, cbuf0, cbuf1, ybuf1, dsend,
    cacc0, cacc1, lb, low, back,
    down, up, bank, logits_a, index_a, logits_b, index_b, mixing, sums, came,
    load_sem, zs_send, relay_recv, relay_send, far_recv, xs_send, x_recv, xf_send, xf_recv,
    g_send, g_recv, gm_send, gm_recv, a_send, a_recv, mid_send, mid_recv, lb_send, lb_recv,
    c_send, c_recv, y_send, y_recv, zc_send, zc_recv, d_send, d_recv,
    sum_send, sum_recv,
):
    rows, depth = attn.shape
    width = weight.shape[1]
    half = width // 2
    step = depth // PIECES
    few = rows // 32
    abufs, gbufs, daccs = (abuf0, abuf1), (gbuf0, gbuf1), (dacc0, dacc1)
    cbufs, caccs = (cbuf0, cbuf1), (cacc0, cacc1)
    rank = down.shape[0]
    own = up.shape[1]

    dp, t = lax.axis_index("dp"), lax.axis_index("tensor")
    z, x = dp // 2, dp % 2
    y, c = t // 2, t % 2
    zh, zl = z // 2, z % 2
    inner = (z == 1) | (z == 2)
    pz = zh * 2 + (1 - zl)
    mz = jnp.where(z == 1, 2, 1)
    x_dev = (z * 2 + (1 - x), t)
    p_dev = (pz * 2 + x, t)
    m_dev = (mz * 2 + x, t)
    c_dev = (dp, y * 2 + (1 - c))
    y_dev = (dp, (1 - y) * 2 + c)
    reduces = c == zl

    def remote(src, dst, send, recv, device):
        return pltpu.make_async_remote_copy(
            src_ref=src, dst_ref=dst, send_sem=send, recv_sem=recv,
            device_id=device, device_id_type=MESH_ID,
        )

    extra = pl.ds(rows, few)
    lead = pl.ds(0, few)

    def sent_rows(is_inner):
        return pl.ds(few, rows - few) if is_inner else pl.ds(0, rows)

    def taken_rows(is_inner):
        return sent_rows(not is_inner)

    def each_kind(act):
        for kind in (True, False):

            @pl.when(inner == kind)
            def _():
                act(kind)

    def rowsof(p):
        return pl.ds(pl.multiple_of(p * step, step), step)

    barrier = pltpu.get_barrier_semaphore()
    others = [(dp, (t + k) % 4) for k in (1, 2, 3)]
    for device in others + [x_dev, p_dev]:
        pl.semaphore_signal(barrier, inc=1, device_id=device, device_id_type=MESH_ID)

    @pl.when(inner)
    def _():
        pl.semaphore_signal(barrier, inc=1, device_id=m_dev, device_id_type=MESH_ID)

    def column_block(zz, b, xx):
        zb = jnp.where(b < 2, zz, (zz + 2) % 4)
        xb = jnp.where(b % 2 == 0, xx, 1 - xx)
        return zb * 2 + xb

    loads = [pltpu.make_async_copy(attn, abuf0, load_sem.at[0])]
    gq = pltpu.make_async_copy(
        grad.at[:, pl.ds(pl.multiple_of(t * own, own), own)], dsend.at[pl.ds(0, rows), pl.ds(0, own)], load_sem.at[1]
    )
    loads.append(gq)
    bank_load = pltpu.make_async_copy(bank_hbm, bank, load_sem.at[5])
    bank_load.start()
    small_loads = [
        pltpu.make_async_copy(source, target, load_sem.at[6 + k])
        for k, (source, target) in enumerate(
            (
                (logits_a_hbm, logits_a),
                (index_a_hbm, index_a),
                (logits_b_hbm, logits_b),
                (index_b_hbm, index_b),
            )
        )
    ]
    for load in small_loads:
        load.start()
    for n in range(2):
        loads.append(
            pltpu.make_async_copy(weight.at[:, pl.ds(n * half, half)], wbuf.at[n], load_sem.at[2 + n])
        )
    for s in range(8):
        col = column_block(z, s // 2, x) * width + (s % 2) * half
        loads.append(
            pltpu.make_async_copy(
                grad.at[:, pl.ds(pl.multiple_of(col, half), half)], gbuf0.at[s], load_sem.at[4]
            )
        )
    for load in loads[:2]:
        load.start()

    @pl.when(inner)
    def _():
        pl.semaphore_wait(barrier, 6)

    @pl.when(jnp.logical_not(inner))
    def _():
        pl.semaphore_wait(barrier, 5)

    total = 2 * PIECES
    narrow = half // 2

    def area(n, p):
        return pl.ds(pl.multiple_of(p * step, step), step), pl.ds(0, half)

    def weight_area(n, p):
        return weight.at[area(n, p)[0], pl.ds(n * half, half)]

    def by_half(i, act):
        for n in range(2):

            @pl.when(i // PIECES == n)
            def _():
                act(n, i % PIECES)

    def x_own(n, p):
        i = n * PIECES + p
        return remote(weight_area(n, p), wbuf.at[(2 + n, *area(n, p))], xs_send.at[0], x_recv.at[i], x_dev)

    def z_own(n, p):
        i = n * PIECES + p
        stream = jnp.where(inner, 0, 1)
        device = (jnp.where(inner, mz, pz) * 2 + x, t)
        return remote(
            weight_area(n, p), relay.at[(stream, n, *area(n, p))],
            zs_send.at[0], relay_recv.at[stream, i], device,
        )

    def g_columns(zz, n):
        col = column_block(zz, t, x) * width + n * half
        return pl.ds(pl.multiple_of(col, half), half)

    def g_own(n, part):
        return remote(
            grad.at[part, g_columns(pz, n)], gbuf1.at[2 * t + n, part], g_send.at[0], g_recv.at[n], p_dev
        )

    def g_mid(n):
        return remote(
            grad.at[lead, g_columns(mz, n)], gbuf1.at[2 * t + n, extra], mid_send.at[n], mid_recv.at[n], m_dev
        )

    def a_own(part):
        return remote(attn.at[part], abuf1.at[part], a_send.at[0], a_recv.at[0], p_dev)

    a_mid = remote(attn.at[lead], abuf1.at[extra], mid_send.at[2], mid_recv.at[2], m_dev)
    early = PIECES // 2

    @pl.when(inner)
    def _():
        for n in range(2):
            g_own(n, sent_rows(True)).start()
            g_mid(n).start()
        a_own(sent_rows(True)).start()
        a_mid.start()

    @pl.when(jnp.logical_not(inner))
    def _():
        for n in range(2):
            g_own(n, sent_rows(False)).start()

        @pl.loop(0, early)
        def _(i):
            z_own(0, i).start()

        a_own(sent_rows(False)).start()

    @pl.loop(0, PIECES)
    def _(i):
        x_own(0, i).start()

        @pl.when(inner)
        def _():
            z_own(0, i).start()

    for load in loads[2:]:
        load.start()

    bank_load.wait()
    for load in small_loads:
        load.wait()
    levels = bank.shape[0]
    sublen = bank.shape[1]
    vectors = mixing.shape[2]
    per_row = vectors // rank
    exact = dict(preferred_element_type=jnp.float32, precision=lax.Precision.HIGHEST)

    place = lax.broadcasted_iota(jnp.int32, (rank, vectors), 1)
    spread = (place % rank == lax.broadcasted_iota(jnp.int32, (rank, vectors), 0)).astype(jnp.float32)
    place = lax.broadcasted_iota(jnp.int32, (per_row, vectors), 1)
    keep = place // rank == lax.broadcasted_iota(jnp.int32, (per_row, vectors), 0)
    level = lax.broadcasted_iota(jnp.int32, (levels, vectors), 0)

    def as_row(value):
        wide_value = jnp.dot(value.astype(jnp.float32), spread, **exact)
        return jnp.sum(jnp.where(keep, wide_value, 0.0), axis=0, keepdims=True)

    def from_row(row):
        return lax.dot_general(jnp.where(keep, row, 0.0), spread, (((1,), (1,)), ((), ())), **exact)

    shares, found = [], []
    for k, (logits, indices) in enumerate(((logits_a, index_a), (logits_b, index_b))):
        first, second = as_row(logits[:, 0, :]), as_row(logits[:, 1, :])
        shares.append((1.0 / (1.0 + jnp.exp(second - first)), 1.0 / (1.0 + jnp.exp(first - second))))
        picks = [(as_row(indices[:, m, :]) + 0.5).astype(jnp.int32) for m in range(2)]
        found.append([level == pick for pick in picks])

    for k, target in enumerate((down, up)):
        mixing[k] = sum(jnp.where(found[k][m], shares[k][m], 0.0) for m in range(2))
        blocks = lax.dot_general(mixing[k], bank[...], (((0,), (0,)), ((), ())), **exact)
        for j in range(per_row):
            row = blocks[j * rank : (j + 1) * rank]
            target[:, j * sublen : (j + 1) * sublen] = row.astype(jnp.bfloat16)

    loads[0].wait()
    loads[1].wait()
    lb[t, :rank] = dot_nt(down[...], abuf0[...])
    lb[t, rank:] = dot_nt(up[...], dsend[:rows, :own])

    def lb_copy(k):
        device = (dp, (t + k) % 4)
        return remote(lb.at[t], lb.at[t], lb_send.at[0], lb_recv.at[0], device)

    for k in (1, 2, 3):
        lb_copy(k).start()
    for load in loads[2:4]:
        load.wait()
    pltpu.make_async_copy(gbuf0, gbuf0, load_sem.at[4]).wait()
    dacc0[...] = jnp.zeros_like(dacc0)
    dacc1[...] = jnp.zeros_like(dacc1)

    @pl.when(jnp.logical_not(inner))
    def _():
        for part in (lead, extra):
            abuf1[part] = jnp.zeros_like(abuf1[part])
            gbuf1[:, part] = jnp.zeros_like(gbuf1[:, part])

    three = lb.at[pl.ds(0, 3)]
    remote(three, three, lb_send.at[0], lb_recv.at[0], y_dev).wait()
    both = lb[0] + lb[1] + lb[2] + lb[3]
    low[...] = both[:rank].T.astype(jnp.bfloat16)
    back[...] = both[rank:].T.astype(jnp.bfloat16)
    both = both.astype(jnp.bfloat16)
    slopes = (
        factor * dot_nn(both[rank:], abuf0[...]),
        factor * dot_nn(both[:rank], dsend[:rows, :own]),
    )
    bank_out[...] = jnp.zeros_like(bank_out)
    dots = []
    for k in range(2):
        pieces = [slopes[k][:, j * sublen : (j + 1) * sublen] for j in range(per_row)]
        stacked = jnp.concatenate(pieces, axis=0)
        bank_out[...] += jnp.dot(mixing[k], stacked, **exact)
        projected = lax.dot_general(bank[...], stacked, (((1,), (1,)), ((), ())), **exact)
        for m in range(2):
            dots.append(jnp.sum(jnp.where(found[k][m], projected, 0.0), axis=0, keepdims=True))

    q1, q2, q3 = levels // 2, levels // 4, levels // 8
    pack = q3 + 8
    at_c = c * q1
    at_y = at_c + y * q2
    at_x = at_y + x * q3
    counts = (q1, q2, pack, pack, pack, q3, q2, q1)
    places = [pl.ds(sum(counts[:k]), counts[k]) for k in range(8)]

    def bank_rows(start, count):
        return pl.ds(pl.multiple_of(start, 8), count)

    def sum_copy(k, source, device):
        return remote(source, came.at[places[k]], sum_send.at[0], sum_recv.at[k], device)

    core_sum = sum_copy(0, bank_out.at[bank_rows((1 - c) * q1, q1)], c_dev)
    y_sum = sum_copy(1, bank_out.at[bank_rows(at_c + (1 - y) * q2, q2)], y_dev)
    x_sum = sum_copy(2, sums, x_dev)
    p_sum = sum_copy(3, sums, p_dev)
    m_sum = sum_copy(4, sums, m_dev)
    x_all = sum_copy(5, bank_out.at[bank_rows(at_x, q3)], x_dev)
    y_all = sum_copy(6, bank_out.at[bank_rows(at_y, q2)], y_dev)
    c_all = sum_copy(7, bank_out.at[bank_rows(at_c, q1)], c_dev)
    core_sum.start()
    core_sum.wait()
    bank_out[bank_rows(at_c, q1)] += came[places[0]]
    y_sum.start()
    y_sum.wait()
    bank_out[bank_rows(at_y, q2)] += came[places[1]]
    sums[:q3] = bank_out[bank_rows(at_y + (1 - x) * q3, q3)]
    sums[q3:] = jnp.zeros_like(sums[q3:])
    for k in range(4):
        sums[q3 + k : q3 + k + 1, :vectors] = dots[k]
    x_sum.start()

    @pl.loop(0, PIECES)
    def _(i):
        x_own(1, i).start()

    def relay_on(stream, n, p):
        i = n * PIECES + p
        device = (jnp.where(stream == 0, pz, mz) * 2 + x, t)
        return remote(
            relay.at[(stream, n, *area(n, p))], wbuf.at[(4 + n, *area(n, p))],
            relay_send.at[stream], far_recv.at[i], device,
        )

    def relay_wait(stream, n, p):
        i = n * PIECES + p
        piece = relay.at[(stream, n, *area(n, p))]
        remote(piece, piece, relay_send.at[stream], relay_recv.at[stream, i], p_dev).wait_recv()

    def x_far(n, p):
        i = n * PIECES + p
        return remote(
            wbuf.at[(4 + n, *area(n, p))], wbuf.at[(6 + n, *area(n, p))], xf_send.at[0], xf_recv.at[i], x_dev
        )

    def far_wait(n, p):
        i = n * PIECES + p
        piece = wbuf.at[(4 + n, *area(n, p))]
        remote(piece, piece, xf_send.at[0], far_recv.at[i], x_dev).wait_recv()

    def g_spread(k, n, is_inner):
        part = pl.ds(0, rows + few) if is_inner else taken_rows(False)
        piece = gbuf1.at[2 * t + n, part]
        return remote(piece, piece, gm_send.at[0], gm_recv.at[0], (dp, (t + k) % 4))

    def g_everything(is_inner):
        part = pl.ds(0, rows + few) if is_inner else taken_rows(False)
        return gbuf1.at[pl.ds(0, 6), part]

    ticks = 33

    def tick(i, carry):
        def near(n, p):
            x_own(n, p).wait_recv()

        @pl.when(i < total)
        def _():
            by_half(i, near)

        def outward(n, p):
            relay_wait(0, n, p)
            relay_on(0, n, p).start()

        @pl.when(inner & (i >= 2) & (i < 2 + PIECES))
        def _():
            outward(0, i - 2)

        @pl.when(inner & (i >= 15) & (i < 15 + PIECES))
        def _():
            outward(1, i - 15)

        def onward(n, p):
            relay_wait(1, n, p)
            relay_on(1, n, p).start()

        @pl.when(inner & (i >= 5) & (i < 5 + early))
        def _():
            onward(0, i - 5)

        @pl.when(inner & (i >= 16) & (i < 12 + total))
        def _():
            by_half(i - 12, onward)

        @pl.when(i == PIECES)
        def _():
            x_sum.wait()
            sums[:q3] = bank_out[bank_rows(at_x, q3)] + came[places[2]][:q3]
            sums[q3:] += came[places[2]][q3:]

            @pl.when(jnp.logical_not(inner))
            def _():
                p_sum.start()

                @pl.loop(early, PIECES)
                def _(k):
                    z_own(0, k).start()

            @pl.loop(0, PIECES)
            def _(k):
                z_own(1, k).start()

        @pl.when(i == 16)
        def _():
            @pl.when(jnp.logical_not(inner))
            def _():
                p_sum.wait_send()

            @pl.when(inner)
            def _():
                p_sum.wait_recv()
                sums[...] += came[places[3]]
                m_sum.start()

        @pl.when((i == 23) & inner)
        def _():
            m_sum.wait()
            sums[...] += came[places[4]]
            p_sum.start()

        @pl.when(i == 4)
        def _():
            def spread(is_inner):
                for n in range(2):
                    g_own(n, taken_rows(is_inner)).wait_recv()
                    if is_inner:
                        g_mid(n).wait_recv()
                    for k in (1, 2, 3):
                        g_spread(k, n, is_inner).start()

            each_kind(spread)

        def far(n, p):
            far_wait(n, p)
            x_far(n, p).start()

        wait = jnp.where(inner & (i >= 21), 17, 12)

        @pl.when((i >= 12) & (i - wait < total) & (jnp.logical_not(inner) | (i < 16) | (i >= 21)))
        def _():
            by_half(i - wait, far)

        return carry

    def c_copy(s, r):
        piece = cbufs[r].at[s]
        return remote(piece, piece, c_send.at[r], c_recv.at[s, r], c_dev)

    def y_copy(s, r):
        j = s % 4
        target = (ybuf0, ybuf1)[r].at[j]
        return remote(cbufs[r].at[s], target, y_send.at[r], y_recv.at[j, r], y_dev)

    def z_copy(s, part):
        j = s % 4
        return remote(cbuf1.at[s, part], ybuf0.at[j, part], zc_send.at[0], zc_recv.at[j], p_dev)

    def z_mid(s):
        j = s % 4
        return remote(cbuf1.at[s, extra], ybuf0.at[j, lead], zc_send.at[1], zc_recv.at[j], m_dev)

    def kept(s):
        return jnp.where(s < 4, zh, 1 - zh) == y

    def out_columns(j):
        xb = jnp.where(j < 2, x, 1 - x)
        return pl.ds(pl.multiple_of(xb * width + (j % 2) * half, half), half)

    def adapter_out(j):
        return 2.0 * dot_nn(low[...], up[:, out_columns(j)])

    def by_side(r, act):
        if isinstance(r, int):
            act(r)
            return
        for side in range(2):

            @pl.when(r == side)
            def _():
                act(side)

    def pass_core(s, r, k):
        @pl.when(jnp.logical_not(reduces))
        def _():
            cbufs[r][s] = caccs[r][k].astype(jnp.bfloat16)
            c_copy(s, r).start()

    def sum_core(s, r, k):
        def act(r):
            c_copy(s, r).wait_recv()
            cbufs[r][s] = (caccs[r][k] + cbufs[r][s].astype(jnp.float32)).astype(jnp.bfloat16)

            @pl.when(jnp.logical_not(kept(s)))
            def _():
                y_copy(s, r).start()

        @pl.when(reduces)
        def _():
            by_side(r, act)

    def sum_y(s, r):
        j = s % 4

        def act(r):
            y_copy(s, r).wait_recv()
            came_here = (ybuf0, ybuf1)[r][j].astype(jnp.float32)
            total_here = cbufs[r][s].astype(jnp.float32) + came_here
            if r == 0:
                ybuf0[j] = (total_here + adapter_out(j)).astype(jnp.bfloat16)
            else:
                cbuf1[s] = total_here.astype(jnp.bfloat16)
                each_kind(lambda is_inner: z_copy(s, taken_rows(is_inner)).start())

                @pl.when(inner)
                def _():
                    z_mid(s).start()

        @pl.when(reduces & kept(s))
        def _():
            by_side(r, act)

    def finish_other(j):
        @pl.when(jnp.logical_not(reduces))
        def _():
            whole = ybuf0.at[j]
            remote(whole, whole, zc_send.at[0], zc_recv.at[j], p_dev).wait_recv()
            ybuf0[j] = (ybuf0[j].astype(jnp.float32) + adapter_out(j)).astype(jnp.bfloat16)

    slots = (0, 1, 2, 0, 1, 2, 3, 3, 4, 4, 6, 6)
    sides = (0, 0, 0, 1, 1, 1, 0, 1, 0, 1, 0, 1)

    def pick(table, u):
        if isinstance(u, int):
            return table[u]
        value = table[0]
        for k in range(1, len(table)):
            if table[k] != table[k - 1]:
                value = jnp.where(u >= k, table[k], value)
        return value

    def ready(u):
        value = jnp.where(u >= 2, PIECES, 0)
        value = jnp.where(u >= 3, 16, value)
        value = jnp.where(u >= 8, jnp.where(inner, 25, 20), value)
        return jnp.where(u >= 10, 26, value)

    def tiles(r):
        count = rows + few * r
        return [pl.ds(m * (count // 2), count // 2) for m in range(2)]

    def unit(u, carry):
        s, r = pick(slots, u), pick(sides, u)
        lax.fori_loop(ready(u - 1), ready(u), tick, 0)

        @pl.when(u == 3)
        def _():
            def arrived(is_inner):
                a_own(taken_rows(is_inner)).wait_recv()
                if is_inner:
                    a_mid.wait_recv()
                everything = g_everything(is_inner)
                remote(everything, everything, gm_send.at[0], gm_recv.at[0], y_dev).wait_recv()

            each_kind(arrived)

        @pl.when(u == 10)
        def _():
            for p in range(PIECES):
                x_far(0, p).wait_recv()


        def act(r):
            for part in tiles(r):
                caccs[r][u % 2, part] = dot_nn(abufs[r][part], wbuf[s])
                daccs[r][part] += dot_nt(gbufs[r][s, part], wbuf[s])
            pass_core(s, r, u % 2)

        by_side(r, act)

        @pl.when(u >= 1)
        def _():
            sum_core(pick(slots, u - 1), pick(sides, u - 1), (u - 1) % 2)

        @pl.when(u >= 4)
        def _():
            sum_y(pick(slots, u - 4), pick(sides, u - 4))

        return carry

    lax.fori_loop(0, 12, unit, 0)
    sum_core(slots[11], sides[11], 1)
    cacc0[...] = jnp.zeros_like(cacc0)
    cacc1[...] = jnp.zeros_like(cacc1)

    final = ((7, 1), (7, 0))

    def grad_part(p):
        return pl.ds(pl.multiple_of(p * step, step), step)

    def d_copy(p, part):
        columns = grad_part(p)
        return remote(dsend.at[part, columns], drecv.at[part, columns], d_send.at[0], d_recv.at[p], p_dev)

    def d_mid(p):
        columns = grad_part(p)
        return remote(dsend.at[extra, columns], drecv.at[lead, columns], d_send.at[1], d_recv.at[p], m_dev)

    def last_piece(p, carry):
        done = 26 + p
        lax.fori_loop(jnp.minimum(done, ticks), jnp.minimum(done + 1, ticks), tick, 0)

        def ahead(p):
            columns = grad_part(p)
            for r in range(2):
                caccs[r][0] += dot_nn(abufs[r][:, columns], wbuf[5, columns])

        @pl.when(p == 0)
        def _():
            ahead(0)

        @pl.when(p < PIECES - 1)
        def _():
            ahead(p + 1)

        @pl.when(p == PIECES - 2)
        def _():
            for side in (1, 0):
                pass_core(5, side, 0)

        x_far(1, p).wait_recv()
        columns = grad_part(p)
        for r in (1, 0):
            for part in tiles(r):
                grown = daccs[r][part, columns]
                grown += dot_nt(gbufs[r][5, part], wbuf[5, columns])
                grown += dot_nt(gbufs[r][7, part], wbuf[7, columns])
                if r == 1:
                    dsend[part, columns] = grown.astype(jnp.bfloat16)
                else:
                    dacc0[part, columns] = grown
            if r == 1:
                each_kind(lambda is_inner: d_copy(p, taken_rows(is_inner)).start())

                @pl.when(inner)
                def _():
                    d_mid(p).start()

        for r in range(2):
            caccs[r][1] += dot_nn(abufs[r][:, columns], wbuf[7, columns])

        @pl.when(p == PIECES - 2)
        def _():
            for side in (1, 0):
                sum_core(5, side, 0)


        @pl.when(p == 1)
        def _():
            @pl.when(inner)
            def _():
                p_sum.wait_send()

            @pl.when(jnp.logical_not(inner))
            def _():
                p_sum.wait_recv()
                sums[...] = came[places[3]]

            bank_out[bank_rows(at_x, q3)] = sums[:q3]
            x_all.start()

        @pl.when(p == 3)
        def _():
            x_all.wait()
            bank_out[bank_rows(at_y + (1 - x) * q3, q3)] = came[places[5]]
            y_all.start()

        @pl.when((p >= 1) & (p < 5))
        def _():
            sum_y(pick(slots, 7 + p), (p - 1) % 2)

        @pl.when(p == 5)
        def _():
            y_all.wait()
            bank_out[bank_rows(at_c + (1 - y) * q2, q2)] = came[places[6]]
            c_all.start()

        return carry

    lax.fori_loop(0, PIECES, last_piece, 0)

    def finish_grad(p, carry):
        columns = grad_part(p)
        whole = drecv.at[:, columns]
        remote(whole, whole, d_send.at[0], d_recv.at[p], p_dev).wait_recv()
        total_here = dacc0[:, columns] + drecv[:, columns].astype(jnp.float32)
        drecv[:, columns] = (total_here + 2.0 * dot_nn(back[...], down[:, columns])).astype(jnp.bfloat16)
        return carry

    for slot, side in final:
        pass_core(slot, side, 1)
    for slot, side in final:
        sum_core(slot, side, 1)
    c_all.wait()
    bank_out[bank_rows((1 - c) * q1, q1)] = came[places[7]]
    for k, target in enumerate((slope_a, slope_b)):
        values = [sums[q3 + 2 * k + m : q3 + 2 * k + m + 1, :vectors] for m in range(2)]
        mean = shares[k][0] * values[0] + shares[k][1] * values[1]
        for m in range(2):
            target[:, m, :] = from_row(shares[k][m] * (values[m] - mean))
    finish_other(0)
    finish_other(2)
    for slot, side in ((5, 1), (5, 0), (7, 1), (7, 0)):
        sum_y(slot, side)
    lax.fori_loop(0, PIECES, finish_grad, 0)
    finish_other(1)
    finish_other(3)
    def drain(buffer, semaphore):
        remote(buffer, buffer, semaphore, a_recv.at[0], p_dev).wait_send()

    def drain_kind(is_inner):
        a_own(sent_rows(is_inner)).wait_send()
        drain(gbuf1.at[pl.ds(0, 2), sent_rows(is_inner)], g_send.at[0])
        drain(g_everything(is_inner), gm_send.at[0])
        drain(dsend.at[taken_rows(is_inner)], d_send.at[0])
        if is_inner:
            a_mid.wait_send()
            for n in range(2):
                g_mid(n).wait_send()
                drain(relay.at[n], relay_send.at[n])
            drain(dsend.at[extra], d_send.at[1])

        @pl.when(reduces)
        def _():
            drain(gbuf1.at[pl.ds(0, 4), taken_rows(is_inner)], zc_send.at[0])
            if is_inner:
                drain(gbuf1.at[pl.ds(0, 4), extra], zc_send.at[1])

    each_kind(drain_kind)
    drain(weight, xs_send.at[0])
    drain(weight, zs_send.at[0])
    drain(weight, xf_send.at[0])

    @pl.when(jnp.logical_not(reduces))
    def _():
        for r in range(2):
            drain(cbufs[r], c_send.at[r])

    @pl.when(reduces)
    def _():
        for r in range(2):
            drain(cbufs[r].at[pl.ds(0, 4)], y_send.at[r])


def settle_kernel(width, *refs):
    sources, targets, sem = refs[:5], refs[5:10], refs[10]
    half = sources[0].shape[2]
    x = lax.axis_index("dp") % 2
    copies = []
    for j in range(4):
        col = (x if j < 2 else 1 - x) * width + (j % 2) * half
        columns = pl.ds(pl.multiple_of(col, half), half)
        copies.append(pltpu.make_async_copy(sources[0].at[j], targets[0].at[:, columns], sem.at[j]))
    for k in range(1, 5):
        copies.append(pltpu.make_async_copy(sources[k], targets[k], sem.at[3 + k]))
    for copy in copies:
        copy.start()
    for copy in copies:
        copy.wait()


def fused_local(dp_size, attn_out, frozen_weight, vector_bank, logits_a, index_a, logits_b, index_b, out_grad):
    rows, depth = attn_out.shape
    width = frozen_weight.shape[1]
    half = width // 2
    levels, sublen = vector_bank.shape
    rank, per_row, _ = logits_a.shape
    vectors = rank * per_row
    own = logits_b.shape[1] * sublen
    factor = adapter_scale / (rows * dp_size)
    total = 2 * PIECES
    more = rows + rows // 32
    small = [v.transpose(1, 2, 0) for v in (logits_a, index_a, logits_b, index_b)]
    bf16, f32 = jnp.bfloat16, jnp.float32
    dma = pltpu.SemaphoreType.DMA
    hbm = pl.BlockSpec(memory_space=pl.ANY)
    vmem = pl.BlockSpec(memory_space=pltpu.VMEM)
    layer_out, attn_grad, _, bank_grad, slope_a, slope_b = pl.pallas_call(
        functools.partial(exchange_kernel, factor),
        name="exchange",
        out_shape=(
            pltpu.VMEM((4, rows, half), bf16),
            pltpu.VMEM((rows, depth), bf16),
            jax.ShapeDtypeStruct((2, 2, depth, half), bf16),
            pltpu.VMEM((levels, sublen), f32),
            pltpu.VMEM((per_row, 2, rank), f32),
            pltpu.VMEM((per_row, 2, rank), f32),
        ),
        in_specs=[hbm] * 8,
        out_specs=(vmem, vmem, hbm, vmem, vmem, vmem),
        scratch_shapes=[
            pltpu.VMEM((8, depth, half), bf16),
            pltpu.VMEM((rows, depth), bf16),
            pltpu.VMEM((more, depth), bf16),
            pltpu.VMEM((8, rows, half), bf16),
            pltpu.VMEM((8, more, half), bf16),
            pltpu.VMEM((rows, depth), f32),
            pltpu.VMEM((more, depth), f32),
            pltpu.VMEM((8, rows, half), bf16),
            pltpu.VMEM((8, more, half), bf16),
            pltpu.VMEM((4, more, half), bf16),
            pltpu.VMEM((more, depth), bf16),
            pltpu.VMEM((2, rows, half), f32),
            pltpu.VMEM((2, more, half), f32),
            pltpu.VMEM((4, 2 * rank, rows), f32),
            pltpu.VMEM((rows, rank), bf16),
            pltpu.VMEM((rows, rank), bf16),
            pltpu.VMEM((rank, depth), bf16),
            pltpu.VMEM((rank, own), bf16),
            pltpu.VMEM((levels, sublen), f32),
            *[pltpu.VMEM(v.shape, v.dtype) for v in small],
            pltpu.VMEM((2, levels, vectors), f32),
            pltpu.VMEM((levels // 8 + 8, sublen), f32),
            pltpu.VMEM((2 * levels + 24, sublen), f32),
            dma((10,)), dma((1,)), dma((2, total)), dma((2,)), dma((total,)),
            dma((1,)), dma((total,)), dma((1,)), dma((total,)),
            dma((1,)), dma((2,)), dma((1,)), dma((1,)), dma((1,)), dma((1,)), dma((3,)), dma((3,)),
            dma((1,)), dma((1,)),
            dma((2,)), dma((8, 2)), dma((2,)), dma((4, 2)), dma((2,)), dma((4,)),
            dma((2,)), dma((PIECES,)), dma((1,)), dma((8,)),
        ],
        compiler_params=pltpu.CompilerParams(
            collective_id=0, has_side_effects=True, vmem_limit_bytes=67043328 - 5 * 2**20
        ),
    )(attn_out, frozen_weight, out_grad, vector_bank, *small)
    targets = [((rows, own), bf16), ((rows, depth), bf16), ((levels, sublen), f32)]
    targets += [(v.shape, f32) for v in (slope_a, slope_b)]
    kept = [pltpu.with_memory_space_constraint(v, pltpu.VMEM) for v in (layer_out, attn_grad, bank_grad, slope_a, slope_b)]
    layer_out, attn_grad, bank_grad, slope_a, slope_b = pl.pallas_call(
        functools.partial(settle_kernel, width),
        name="settle",
        out_shape=[jax.ShapeDtypeStruct(*v) for v in targets],
        in_specs=[hbm] * 5,
        out_specs=[hbm] * 5,
        scratch_shapes=[dma((8,))],
        compiler_params=pltpu.CompilerParams(vmem_limit_bytes=16 * 2**20),
    )(*kept)
    return (layer_out, attn_grad, bank_grad, slope_a.transpose(2, 0, 1), slope_b.transpose(2, 0, 1))


def solution(mesh):
    dp_size, tensor_size = mesh.shape["dp"], mesh.shape["tensor"]
    paired = dp_size == 2 * tensor_size and tensor_size % 2 == 0
    body = functools.partial(ring_local, dp_size, tensor_size) if paired else local
    if paired and tensor_size == 4:
        body = functools.partial(fused_local, dp_size)
    return jax.shard_map(
        body,
        mesh=mesh,
        in_specs=(
            P("dp", "tensor"),
            P("tensor", "dp"),
            P(),
            P(None, "tensor", None),
            P(None, "tensor", None),
            P(None, "tensor", None),
            P(None, "tensor", None),
            P("dp", None),
        ),
        out_specs=(
            P("dp", "tensor"),
            P("dp", "tensor"),
            P(),
            P(None, "tensor", None),
            P(None, "tensor", None),
        ),
        check_vma=False,
    )
```

```python
import functools

import jax
import jax.numpy as jnp
from jax import lax
from jax.experimental import pallas as pl
from jax.experimental.pallas import tpu as pltpu
from jax.sharding import PartitionSpec as P

adapter_scale = 2.0
ROW_PIECES = 4


def compose(logits, indices, vector_bank):
    weights = jax.nn.sigmoid(logits - logits[..., ::-1])
    levels = jnp.arange(vector_bank.shape[0], dtype=jnp.int32)
    picked = (indices[..., None] == levels).astype(jnp.float32)
    mixing = jnp.sum(picked * weights[..., None], axis=2)
    blocks = jnp.einsum("rjb,bc->rjc", mixing, vector_bank, precision=lax.Precision.HIGHEST)
    return (weights, picked, mixing, blocks.reshape(blocks.shape[0], -1))


def compose_back(grad_rows, weights, picked, mixing, vector_bank):
    blocks = grad_rows.reshape(mixing.shape[0], mixing.shape[1], -1)
    bank_part = jnp.einsum("rjb,rjc->bc", mixing, blocks, precision=lax.Precision.HIGHEST)
    projected = jnp.einsum("rjc,bc->rjb", blocks, vector_bank, precision=lax.Precision.HIGHEST)
    dots = jnp.sum(picked * projected[:, :, None, :], axis=3)
    logit_grad = weights * (dots - jnp.sum(weights * dots, axis=2, keepdims=True))
    return (bank_part, logit_grad)


def local(attn_out, frozen_weight, vector_bank, logits_a, index_a, logits_b, index_b, out_grad):
    weights_a, picked_a, mixing_a, rows_a = compose(logits_a, index_a, vector_bank)
    weights_b, picked_b, mixing_b, rows_b = compose(logits_b, index_b, vector_bank)
    down_a = rows_a.astype(jnp.bfloat16)
    up_b = rows_b.astype(jnp.bfloat16)
    own_width = up_b.shape[1]
    grad_cols = lax.dynamic_slice_in_dim(
        out_grad, lax.axis_index("tensor") * own_width, own_width, 1
    )
    low_part = jnp.dot(attn_out, down_a.T, preferred_element_type=jnp.float32)
    back_part = jnp.dot(grad_cols, up_b.T, preferred_element_type=jnp.float32)
    low_total = lax.psum(low_part, "tensor")
    low_bf = low_total.astype(jnp.bfloat16)
    gathered = lax.all_gather(frozen_weight, "dp", axis=1, tiled=True)
    partial_value = jnp.dot(attn_out, gathered, preferred_element_type=jnp.float32).astype(
        jnp.bfloat16
    )
    summed = lax.psum_scatter(partial_value, "tensor", scatter_dimension=1, tiled=True).astype(
        jnp.float32
    )
    layer_out = (
        summed + adapter_scale * jnp.dot(low_bf, up_b, preferred_element_type=jnp.float32)
    ).astype(jnp.bfloat16)
    back_total = lax.psum(back_part, "tensor")
    back_bf = back_total.astype(jnp.bfloat16)
    main = lax.dot_general(
        out_grad, gathered, (((1,), (1,)), ((), ())), preferred_element_type=jnp.float32
    )
    attn_grad = (
        main + adapter_scale * jnp.dot(back_bf, down_a, preferred_element_type=jnp.float32)
    ).astype(jnp.bfloat16)
    factor = adapter_scale / (attn_out.shape[0] * lax.axis_size("dp"))
    grad_a = factor * lax.dot_general(
        back_bf, attn_out, (((0,), (0,)), ((), ())), preferred_element_type=jnp.float32
    )
    grad_b = factor * lax.dot_general(
        low_bf, grad_cols, (((0,), (0,)), ((), ())), preferred_element_type=jnp.float32
    )
    bank_a, logit_grad_a = compose_back(grad_a, weights_a, picked_a, mixing_a, vector_bank)
    bank_b, logit_grad_b = compose_back(grad_b, weights_b, picked_b, mixing_b, vector_bank)
    bank_part = bank_a + bank_b
    bank_group = lax.psum(bank_part, "tensor")
    bank_grad, logits_a_grad, logits_b_grad = lax.psum(
        (bank_group, logit_grad_a, logit_grad_b), "dp"
    )
    return (layer_out, attn_grad, bank_grad, logits_a_grad, logits_b_grad)


def ring_local(dp_size, tensor_size, attn_out, frozen_weight, vector_bank, logits_a, index_a, logits_b, index_b, out_grad):
    depth = tensor_size
    chips = tensor_size // 2
    rows = attn_out.shape[0]
    own_width = attn_out.shape[1]
    width = frozen_weight.shape[1]
    half = width // 2
    part = own_width // ROW_PIECES
    place = lax.axis_index("dp")
    level, side = place // 2, place % 2
    tensor_index = lax.axis_index("tensor")

    ring = [(d, (d + 2) % dp_size) for d in range(dp_size)]
    swap = [(d, d ^ 1) for d in range(dp_size)]

    def hop(value):
        return lax.ppermute(value, "dp", ring)

    def cross(value):
        return lax.ppermute(value, "dp", swap)

    def collect(partial_value, step):
        target = (level - step + depth) % depth
        pairs = []
        for d in range(dp_size):
            goal = (d // 2 - step) % depth
            for chip in range(chips):
                core = 2 * chip + goal % 2
                pairs.append((d * tensor_size + (core ^ 1), d * tensor_size + core))
        other = lax.ppermute(partial_value, ("dp", "tensor"), pairs)
        paired = partial_value.astype(jnp.float32) + other.astype(jnp.float32)
        sent = paired.astype(jnp.bfloat16)
        total = paired
        for k in range(1, chips):
            pairs = []
            for d in range(dp_size):
                goal = (d // 2 - step) % depth
                source = ((goal // 2 + k) % chips) * 2 + goal % 2
                pairs.append((d * tensor_size + source, d * tensor_size + goal))
            total = total + lax.ppermute(sent, ("dp", "tensor"), pairs).astype(jnp.float32)
        return jnp.where(tensor_index == target, total, 0.0)

    first = frozen_weight[:, :half]
    later = [frozen_weight[r * part : (r + 1) * part, half:] for r in range(ROW_PIECES)]
    held = [(first, later)]
    for step in range(1, depth):
        first = hop(first)
        later = [hop(v) for v in later]
        held.append((first, later))

    attn_two = jnp.concatenate([attn_out, cross(attn_out)], axis=0)
    attn_parts = [attn_two[:, r * part : (r + 1) * part] for r in range(ROW_PIECES)]

    def grad_pair(step):
        origin = (level - step + depth) % depth
        mine = lax.dynamic_slice_in_dim(out_grad, (origin * 2 + side) * width, width, 1)
        theirs = lax.dynamic_slice_in_dim(out_grad, (origin * 2 + 1 - side) * width, width, 1)
        return jnp.concatenate([mine, cross(theirs)], axis=0)

    weights_a, picked_a, mixing_a, rows_a = compose(logits_a, index_a, vector_bank)
    weights_b, picked_b, mixing_b, rows_b = compose(logits_b, index_b, vector_bank)
    down_a = rows_a.astype(jnp.bfloat16)
    up_b = rows_b.astype(jnp.bfloat16)
    rank = down_a.shape[0]
    grad_cols = lax.dynamic_slice_in_dim(out_grad, tensor_index * own_width, own_width, 1)
    low_part = jnp.dot(attn_out, down_a.T, preferred_element_type=jnp.float32)
    back_part = jnp.dot(grad_cols, up_b.T, preferred_element_type=jnp.float32)
    both = lax.psum(jnp.concatenate([low_part, back_part], axis=1), "tensor")
    low_bf = both[:, :rank].astype(jnp.bfloat16)
    back_bf = both[:, rank:].astype(jnp.bfloat16)

    sums = [None] * ROW_PIECES
    own_total = jnp.zeros((rows, width), jnp.float32)
    cross_total = jnp.zeros((rows, width), jnp.float32)
    for step in range(depth):
        first, later = held[step]
        grads = grad_pair(step)
        out_first = jnp.dot(attn_two, first, preferred_element_type=jnp.float32)
        for r in range(ROW_PIECES):
            term = lax.dot_general(
                grads[:, :half],
                first[r * part : (r + 1) * part],
                (((1,), (1,)), ((), ())),
                preferred_element_type=jnp.float32,
            )
            sums[r] = term if sums[r] is None else sums[r] + term
        out_later = None
        for r in range(ROW_PIECES):
            term = jnp.dot(attn_parts[r], later[r], preferred_element_type=jnp.float32)
            out_later = term if out_later is None else out_later + term
            sums[r] = sums[r] + lax.dot_general(
                grads[:, half:],
                later[r],
                (((1,), (1,)), ((), ())),
                preferred_element_type=jnp.float32,
            )
        out_first = out_first.astype(jnp.bfloat16)
        out_later = out_later.astype(jnp.bfloat16)
        if step < depth - 1:
            block = collect(jnp.concatenate([out_first, out_later], axis=1), step)
            own_total = own_total + block[:rows]
            cross_total = cross_total + block[rows:]
        if step == depth - 2:
            came = cross(cross_total.astype(jnp.bfloat16)).astype(jnp.float32)
        if step == depth - 1:
            ends = [collect(out_first, step), collect(out_later, step)]
            own_end = jnp.concatenate([v[:rows] for v in ends], axis=1)
            came_end = jnp.concatenate(
                [cross(v[rows:].astype(jnp.bfloat16)) for v in ends], axis=1
            ).astype(jnp.float32)
    own_half = own_total + own_end
    other_half = came + came_end
    summed = jnp.concatenate(
        [
            jnp.where(side == 0, own_half, other_half),
            jnp.where(side == 0, other_half, own_half),
        ],
        axis=1,
    )
    layer_out = (
        summed + adapter_scale * jnp.dot(low_bf, up_b, preferred_element_type=jnp.float32)
    ).astype(jnp.bfloat16)

    adapter = adapter_scale * jnp.dot(back_bf, down_a, preferred_element_type=jnp.float32)
    pieces = []
    for r in range(ROW_PIECES):
        came_grad = cross(sums[r][rows:].astype(jnp.bfloat16)).astype(jnp.float32)
        pieces.append(sums[r][:rows] + came_grad + adapter[:, r * part : (r + 1) * part])
    attn_grad = jnp.concatenate(pieces, axis=1).astype(jnp.bfloat16)

    factor = adapter_scale / (rows * dp_size)
    grad_a = factor * lax.dot_general(
        back_bf, attn_out, (((0,), (0,)), ((), ())), preferred_element_type=jnp.float32
    )
    grad_b = factor * lax.dot_general(
        low_bf, grad_cols, (((0,), (0,)), ((), ())), preferred_element_type=jnp.float32
    )
    bank_a, logit_grad_a = compose_back(grad_a, weights_a, picked_a, mixing_a, vector_bank)
    bank_b, logit_grad_b = compose_back(grad_b, weights_b, picked_b, mixing_b, vector_bank)
    bank_grad = lax.psum(bank_a + bank_b, ("dp", "tensor"))
    logits_a_grad, logits_b_grad = lax.psum((logit_grad_a, logit_grad_b), "dp")
    return (layer_out, attn_grad, bank_grad, logits_a_grad, logits_b_grad)


MESH_ID = pl.DeviceIdType.MESH
PIECES = 8


def dot_nn(a, b):
    return jnp.dot(a, b, preferred_element_type=jnp.float32)


def dot_nt(a, b):
    return lax.dot_general(a, b, (((1,), (1,)), ((), ())), preferred_element_type=jnp.float32)


def exchange_kernel(
    factor,
    attn, weight, grad, bank_hbm, logits_a_hbm, index_a_hbm, logits_b_hbm, index_b_hbm,
    ybuf0, drecv, relay, bank_out, slope_a, slope_b,
    wbuf, abuf0, abuf1, gbuf0, gbuf1, dacc0, dacc1, cbuf0, cbuf1, ybuf1, dsend,
    cacc0, cacc1, lb, low, back,
    down, up, bank, logits_a, index_a, logits_b, index_b, mixing, sums, came,
    load_sem, zs_send, relay_recv, relay_send, far_recv, xs_send, x_recv, xf_send, xf_recv,
    g_send, g_recv, gm_send, gm_recv, a_send, a_recv, mid_send, mid_recv, lb_send, lb_recv,
    c_send, c_recv, y_send, y_recv, zc_send, zc_recv, d_send, d_recv,
    sum_send, sum_recv,
):
    rows, depth = attn.shape
    width = weight.shape[1]
    half = width // 2
    step = depth // PIECES
    few = rows // 32
    abufs, gbufs, daccs = (abuf0, abuf1), (gbuf0, gbuf1), (dacc0, dacc1)
    cbufs, caccs = (cbuf0, cbuf1), (cacc0, cacc1)
    rank = down.shape[0]
    own = up.shape[1]

    dp, t = lax.axis_index("dp"), lax.axis_index("tensor")
    z, x = dp // 2, dp % 2
    y, c = t // 2, t % 2
    zh, zl = z // 2, z % 2
    inner = (z == 1) | (z == 2)
    pz = zh * 2 + (1 - zl)
    mz = jnp.where(z == 1, 2, 1)
    x_dev = (z * 2 + (1 - x), t)
    p_dev = (pz * 2 + x, t)
    m_dev = (mz * 2 + x, t)
    c_dev = (dp, y * 2 + (1 - c))
    y_dev = (dp, (1 - y) * 2 + c)
    reduces = c == zl

    def remote(src, dst, send, recv, device):
        return pltpu.make_async_remote_copy(
            src_ref=src, dst_ref=dst, send_sem=send, recv_sem=recv,
            device_id=device, device_id_type=MESH_ID,
        )

    extra = pl.ds(rows, few)
    lead = pl.ds(0, few)

    def sent_rows(is_inner):
        return pl.ds(few, rows - few) if is_inner else pl.ds(0, rows)

    def taken_rows(is_inner):
        return sent_rows(not is_inner)

    def each_kind(act):
        for kind in (True, False):

            @pl.when(inner == kind)
            def _():
                act(kind)

    def rowsof(p):
        return pl.ds(pl.multiple_of(p * step, step), step)

    barrier = pltpu.get_barrier_semaphore()
    others = [(dp, (t + k) % 4) for k in (1, 2, 3)]
    for device in others + [x_dev, p_dev]:
        pl.semaphore_signal(barrier, inc=1, device_id=device, device_id_type=MESH_ID)

    @pl.when(inner)
    def _():
        pl.semaphore_signal(barrier, inc=1, device_id=m_dev, device_id_type=MESH_ID)

    def column_block(zz, b, xx):
        zb = jnp.where(b < 2, zz, (zz + 2) % 4)
        xb = jnp.where(b % 2 == 0, xx, 1 - xx)
        return zb * 2 + xb

    loads = [pltpu.make_async_copy(attn, abuf0, load_sem.at[0])]
    gq = pltpu.make_async_copy(
        grad.at[:, pl.ds(pl.multiple_of(t * own, own), own)], dsend.at[pl.ds(0, rows), pl.ds(0, own)], load_sem.at[1]
    )
    loads.append(gq)
    bank_load = pltpu.make_async_copy(bank_hbm, bank, load_sem.at[5])
    bank_load.start()
    small_loads = [
        pltpu.make_async_copy(source, target, load_sem.at[6 + k])
        for k, (source, target) in enumerate(
            (
                (logits_a_hbm, logits_a),
                (index_a_hbm, index_a),
                (logits_b_hbm, logits_b),
                (index_b_hbm, index_b),
            )
        )
    ]
    for load in small_loads:
        load.start()
    for n in range(2):
        loads.append(
            pltpu.make_async_copy(weight.at[:, pl.ds(n * half, half)], wbuf.at[n], load_sem.at[2 + n])
        )
    for s in range(8):
        col = column_block(z, s // 2, x) * width + (s % 2) * half
        loads.append(
            pltpu.make_async_copy(
                grad.at[:, pl.ds(pl.multiple_of(col, half), half)], gbuf0.at[s], load_sem.at[4]
            )
        )
    for load in loads[:2]:
        load.start()

    @pl.when(inner)
    def _():
        pl.semaphore_wait(barrier, 6)

    @pl.when(jnp.logical_not(inner))
    def _():
        pl.semaphore_wait(barrier, 5)

    total = 2 * PIECES
    narrow = half // 2

    def area(n, p):
        return pl.ds(pl.multiple_of(p * step, step), step), pl.ds(0, half)

    def weight_area(n, p):
        return weight.at[area(n, p)[0], pl.ds(n * half, half)]

    def by_half(i, act):
        for n in range(2):

            @pl.when(i // PIECES == n)
            def _():
                act(n, i % PIECES)

    def x_own(n, p):
        i = n * PIECES + p
        return remote(weight_area(n, p), wbuf.at[(2 + n, *area(n, p))], xs_send.at[0], x_recv.at[i], x_dev)

    def z_own(n, p):
        i = n * PIECES + p
        stream = jnp.where(inner, 0, 1)
        device = (jnp.where(inner, mz, pz) * 2 + x, t)
        return remote(
            weight_area(n, p), relay.at[(stream, n, *area(n, p))],
            zs_send.at[0], relay_recv.at[stream, i], device,
        )

    def g_columns(zz, n):
        col = column_block(zz, t, x) * width + n * half
        return pl.ds(pl.multiple_of(col, half), half)

    def g_own(n, part):
        return remote(
            grad.at[part, g_columns(pz, n)], gbuf1.at[2 * t + n, part], g_send.at[0], g_recv.at[n], p_dev
        )

    def g_mid(n):
        return remote(
            grad.at[lead, g_columns(mz, n)], gbuf1.at[2 * t + n, extra], mid_send.at[n], mid_recv.at[n], m_dev
        )

    def a_own(part):
        return remote(attn.at[part], abuf1.at[part], a_send.at[0], a_recv.at[0], p_dev)

    a_mid = remote(attn.at[lead], abuf1.at[extra], mid_send.at[2], mid_recv.at[2], m_dev)
    early = PIECES // 2

    @pl.when(inner)
    def _():
        for n in range(2):
            g_own(n, sent_rows(True)).start()
            g_mid(n).start()
        a_own(sent_rows(True)).start()
        a_mid.start()

    @pl.when(jnp.logical_not(inner))
    def _():
        for n in range(2):
            g_own(n, sent_rows(False)).start()

        @pl.loop(0, early)
        def _(i):
            z_own(0, i).start()

        a_own(sent_rows(False)).start()

    @pl.loop(0, PIECES)
    def _(i):
        x_own(0, i).start()

        @pl.when(inner)
        def _():
            z_own(0, i).start()

    for load in loads[2:]:
        load.start()

    bank_load.wait()
    for load in small_loads:
        load.wait()
    levels = bank.shape[0]
    sublen = bank.shape[1]
    vectors = mixing.shape[2]
    per_row = vectors // rank
    exact = dict(preferred_element_type=jnp.float32, precision=lax.Precision.HIGHEST)

    place = lax.broadcasted_iota(jnp.int32, (rank, vectors), 1)
    spread = (place % rank == lax.broadcasted_iota(jnp.int32, (rank, vectors), 0)).astype(jnp.float32)
    place = lax.broadcasted_iota(jnp.int32, (per_row, vectors), 1)
    keep = place // rank == lax.broadcasted_iota(jnp.int32, (per_row, vectors), 0)
    level = lax.broadcasted_iota(jnp.int32, (levels, vectors), 0)

    def as_row(value):
        wide_value = jnp.dot(value.astype(jnp.float32), spread, **exact)
        return jnp.sum(jnp.where(keep, wide_value, 0.0), axis=0, keepdims=True)

    def from_row(row):
        return lax.dot_general(jnp.where(keep, row, 0.0), spread, (((1,), (1,)), ((), ())), **exact)

    shares, found = [], []
    for k, (logits, indices) in enumerate(((logits_a, index_a), (logits_b, index_b))):
        first, second = as_row(logits[:, 0, :]), as_row(logits[:, 1, :])
        shares.append((1.0 / (1.0 + jnp.exp(second - first)), 1.0 / (1.0 + jnp.exp(first - second))))
        picks = [(as_row(indices[:, m, :]) + 0.5).astype(jnp.int32) for m in range(2)]
        found.append([level == pick for pick in picks])

    for k, target in enumerate((down, up)):
        mixing[k] = sum(jnp.where(found[k][m], shares[k][m], 0.0) for m in range(2))
        blocks = lax.dot_general(mixing[k], bank[...], (((0,), (0,)), ((), ())), **exact)
        for j in range(per_row):
            row = blocks[j * rank : (j + 1) * rank]
            target[:, j * sublen : (j + 1) * sublen] = row.astype(jnp.bfloat16)

    loads[0].wait()
    loads[1].wait()
    lb[t, :rank] = dot_nt(down[...], abuf0[...])
    lb[t, rank:] = dot_nt(up[...], dsend[:rows, :own])

    def lb_copy(k):
        device = (dp, (t + k) % 4)
        return remote(lb.at[t], lb.at[t], lb_send.at[0], lb_recv.at[0], device)

    for k in (1, 2, 3):
        lb_copy(k).start()
    for load in loads[2:4]:
        load.wait()
    pltpu.make_async_copy(gbuf0, gbuf0, load_sem.at[4]).wait()
    dacc0[...] = jnp.zeros_like(dacc0)
    dacc1[...] = jnp.zeros_like(dacc1)

    @pl.when(jnp.logical_not(inner))
    def _():
        for part in (lead, extra):
            abuf1[part] = jnp.zeros_like(abuf1[part])
            gbuf1[:, part] = jnp.zeros_like(gbuf1[:, part])

    three = lb.at[pl.ds(0, 3)]
    remote(three, three, lb_send.at[0], lb_recv.at[0], y_dev).wait()
    both = lb[0] + lb[1] + lb[2] + lb[3]
    low[...] = both[:rank].T.astype(jnp.bfloat16)
    back[...] = both[rank:].T.astype(jnp.bfloat16)
    both = both.astype(jnp.bfloat16)
    slopes = (
        factor * dot_nn(both[rank:], abuf0[...]),
        factor * dot_nn(both[:rank], dsend[:rows, :own]),
    )
    bank_out[...] = jnp.zeros_like(bank_out)
    dots = []
    for k in range(2):
        pieces = [slopes[k][:, j * sublen : (j + 1) * sublen] for j in range(per_row)]
        stacked = jnp.concatenate(pieces, axis=0)
        bank_out[...] += jnp.dot(mixing[k], stacked, **exact)
        projected = lax.dot_general(bank[...], stacked, (((1,), (1,)), ((), ())), **exact)
        for m in range(2):
            dots.append(jnp.sum(jnp.where(found[k][m], projected, 0.0), axis=0, keepdims=True))

    q1, q2, q3 = levels // 2, levels // 4, levels // 8
    pack = q3 + 8
    at_c = c * q1
    at_y = at_c + y * q2
    at_x = at_y + x * q3
    counts = (q1, q2, pack, pack, pack, q3, q2, q1)
    places = [pl.ds(sum(counts[:k]), counts[k]) for k in range(8)]

    def bank_rows(start, count):
        return pl.ds(pl.multiple_of(start, 8), count)

    def sum_copy(k, source, device):
        return remote(source, came.at[places[k]], sum_send.at[0], sum_recv.at[k], device)

    core_sum = sum_copy(0, bank_out.at[bank_rows((1 - c) * q1, q1)], c_dev)
    y_sum = sum_copy(1, bank_out.at[bank_rows(at_c + (1 - y) * q2, q2)], y_dev)
    x_sum = sum_copy(2, sums, x_dev)
    p_sum = sum_copy(3, sums, p_dev)
    m_sum = sum_copy(4, sums, m_dev)
    x_all = sum_copy(5, bank_out.at[bank_rows(at_x, q3)], x_dev)
    y_all = sum_copy(6, bank_out.at[bank_rows(at_y, q2)], y_dev)
    c_all = sum_copy(7, bank_out.at[bank_rows(at_c, q1)], c_dev)
    core_sum.start()
    core_sum.wait()
    bank_out[bank_rows(at_c, q1)] += came[places[0]]
    y_sum.start()
    y_sum.wait()
    bank_out[bank_rows(at_y, q2)] += came[places[1]]
    sums[:q3] = bank_out[bank_rows(at_y + (1 - x) * q3, q3)]
    sums[q3:] = jnp.zeros_like(sums[q3:])
    for k in range(4):
        sums[q3 + k : q3 + k + 1, :vectors] = dots[k]
    x_sum.start()

    @pl.loop(0, PIECES)
    def _(i):
        x_own(1, i).start()

    def relay_on(stream, n, p):
        i = n * PIECES + p
        device = (jnp.where(stream == 0, pz, mz) * 2 + x, t)
        return remote(
            relay.at[(stream, n, *area(n, p))], wbuf.at[(4 + n, *area(n, p))],
            relay_send.at[stream], far_recv.at[i], device,
        )

    def relay_wait(stream, n, p):
        i = n * PIECES + p
        piece = relay.at[(stream, n, *area(n, p))]
        remote(piece, piece, relay_send.at[stream], relay_recv.at[stream, i], p_dev).wait_recv()

    def x_far(n, p):
        i = n * PIECES + p
        return remote(
            wbuf.at[(4 + n, *area(n, p))], wbuf.at[(6 + n, *area(n, p))], xf_send.at[0], xf_recv.at[n * (p + 1)], x_dev
        )

    def far_wait(n, p):
        i = n * PIECES + p
        piece = wbuf.at[(4 + n, *area(n, p))]
        remote(piece, piece, xf_send.at[0], far_recv.at[i], x_dev).wait_recv()

    def g_spread(k, n, is_inner):
        part = pl.ds(0, rows + few) if is_inner else taken_rows(False)
        piece = gbuf1.at[2 * t + n, part]
        return remote(piece, piece, gm_send.at[0], gm_recv.at[0], (dp, (t + k) % 4))

    def g_everything(is_inner):
        part = pl.ds(0, rows + few) if is_inner else taken_rows(False)
        return gbuf1.at[pl.ds(0, 6), part]

    ticks = 33

    def tick(i, carry):
        def near(n, p):
            x_own(n, p).wait_recv()

        @pl.when(i < total)
        def _():
            by_half(i, near)

        def outward(n, p):
            relay_wait(0, n, p)
            relay_on(0, n, p).start()

        @pl.when(inner & (i >= 2) & (i < 2 + PIECES))
        def _():
            outward(0, i - 2)

        @pl.when(inner & (i >= 15) & (i < 15 + PIECES))
        def _():
            outward(1, i - 15)

        def onward(n, p):
            relay_wait(1, n, p)
            relay_on(1, n, p).start()

        @pl.when(inner & (i >= 5) & (i < 5 + early))
        def _():
            onward(0, i - 5)

        @pl.when(inner & (i >= 16) & (i < 12 + total))
        def _():
            by_half(i - 12, onward)

        @pl.when(i == PIECES)
        def _():
            x_sum.wait()
            sums[:q3] = bank_out[bank_rows(at_x, q3)] + came[places[2]][:q3]
            sums[q3:] += came[places[2]][q3:]

            @pl.when(jnp.logical_not(inner))
            def _():
                p_sum.start()

                @pl.loop(early, PIECES)
                def _(k):
                    z_own(0, k).start()

            @pl.loop(0, PIECES)
            def _(k):
                z_own(1, k).start()

        @pl.when(i == 16)
        def _():
            @pl.when(jnp.logical_not(inner))
            def _():
                p_sum.wait_send()

            @pl.when(inner)
            def _():
                p_sum.wait_recv()
                sums[...] += came[places[3]]
                m_sum.start()

        @pl.when((i == 23) & inner)
        def _():
            m_sum.wait()
            sums[...] += came[places[4]]
            p_sum.start()

        @pl.when(i == 4)
        def _():
            def spread(is_inner):
                for n in range(2):
                    g_own(n, taken_rows(is_inner)).wait_recv()
                    if is_inner:
                        g_mid(n).wait_recv()
                    for k in (1, 2, 3):
                        g_spread(k, n, is_inner).start()

            each_kind(spread)

        def far(n, p):
            far_wait(n, p)
            x_far(n, p).start()

        wait = jnp.where(inner & (i >= 21), 17, 12)

        @pl.when((i >= 12) & (i - wait < total) & (jnp.logical_not(inner) | (i < 16) | (i >= 21)))
        def _():
            by_half(i - wait, far)

        return carry

    def c_copy(s, r):
        piece = cbufs[r].at[s]
        return remote(piece, piece, c_send.at[r], c_recv.at[s, r], c_dev)

    def y_copy(s, r):
        j = s % 4
        target = (ybuf0, ybuf1)[r].at[j]
        return remote(cbufs[r].at[s], target, y_send.at[r], y_recv.at[j, r], y_dev)

    def z_copy(s, part):
        j = s % 4
        return remote(cbuf1.at[s, part], ybuf0.at[j, part], zc_send.at[0], zc_recv.at[j], p_dev)

    def z_mid(s):
        j = s % 4
        return remote(cbuf1.at[s, extra], ybuf0.at[j, lead], zc_send.at[1], zc_recv.at[j], m_dev)

    def kept(s):
        return jnp.where(s < 4, zh, 1 - zh) == y

    def out_columns(j):
        xb = jnp.where(j < 2, x, 1 - x)
        return pl.ds(pl.multiple_of(xb * width + (j % 2) * half, half), half)

    def adapter_out(j):
        return 2.0 * dot_nn(low[...], up[:, out_columns(j)])

    def by_side(r, act):
        if isinstance(r, int):
            act(r)
            return
        for side in range(2):

            @pl.when(r == side)
            def _():
                act(side)

    def pass_core(s, r, k):
        @pl.when(jnp.logical_not(reduces))
        def _():
            cbufs[r][s] = caccs[r][k].astype(jnp.bfloat16)
            c_copy(s, r).start()

    def sum_core(s, r, k):
        def act(r):
            c_copy(s, r).wait_recv()
            cbufs[r][s] = (caccs[r][k] + cbufs[r][s].astype(jnp.float32)).astype(jnp.bfloat16)

            @pl.when(jnp.logical_not(kept(s)))
            def _():
                y_copy(s, r).start()

        @pl.when(reduces)
        def _():
            by_side(r, act)

    def sum_y(s, r):
        j = s % 4

        def act(r):
            y_copy(s, r).wait_recv()
            came_here = (ybuf0, ybuf1)[r][j].astype(jnp.float32)
            total_here = cbufs[r][s].astype(jnp.float32) + came_here
            if r == 0:
                ybuf0[j] = (total_here + adapter_out(j)).astype(jnp.bfloat16)
            else:
                cbuf1[s] = total_here.astype(jnp.bfloat16)
                each_kind(lambda is_inner: z_copy(s, taken_rows(is_inner)).start())

                @pl.when(inner)
                def _():
                    z_mid(s).start()

        @pl.when(reduces & kept(s))
        def _():
            by_side(r, act)

    def finish_other(j):
        @pl.when(jnp.logical_not(reduces))
        def _():
            whole = ybuf0.at[j]
            remote(whole, whole, zc_send.at[0], zc_recv.at[j], p_dev).wait_recv()
            ybuf0[j] = (ybuf0[j].astype(jnp.float32) + adapter_out(j)).astype(jnp.bfloat16)

    slots = (0, 1, 2, 0, 1, 2, 3, 3, 4, 4, 6, 6)
    sides = (0, 0, 0, 1, 1, 1, 0, 1, 0, 1, 0, 1)

    def pick(table, u):
        if isinstance(u, int):
            return table[u]
        value = table[0]
        for k in range(1, len(table)):
            if table[k] != table[k - 1]:
                value = jnp.where(u >= k, table[k], value)
        return value

    def ready(u):
        value = jnp.where(u >= 2, PIECES, 0)
        value = jnp.where(u >= 3, 16, value)
        value = jnp.where(u >= 8, jnp.where(inner, 25, 20), value)
        return jnp.where(u >= 10, 26, value)

    def tiles(r):
        count = rows + few * r
        return [pl.ds(m * (count // 2), count // 2) for m in range(2)]

    def unit(u, carry):
        s, r = pick(slots, u), pick(sides, u)
        lax.fori_loop(ready(u - 1), ready(u), tick, 0)

        @pl.when(u == 3)
        def _():
            def arrived(is_inner):
                a_own(taken_rows(is_inner)).wait_recv()
                if is_inner:
                    a_mid.wait_recv()
                everything = g_everything(is_inner)
                remote(everything, everything, gm_send.at[0], gm_recv.at[0], y_dev).wait_recv()

            each_kind(arrived)

        @pl.when(u == 10)
        def _():
            whole = wbuf.at[6]
            remote(whole, whole, xf_send.at[0], xf_recv.at[0], x_dev).wait_recv()


        def act(r):
            for part in tiles(r):
                caccs[r][u % 2, part] = dot_nn(abufs[r][part], wbuf[s])
                daccs[r][part] += dot_nt(gbufs[r][s, part], wbuf[s])
            pass_core(s, r, u % 2)

        by_side(r, act)

        @pl.when(u >= 1)
        def _():
            sum_core(pick(slots, u - 1), pick(sides, u - 1), (u - 1) % 2)

        @pl.when(u >= 4)
        def _():
            sum_y(pick(slots, u - 4), pick(sides, u - 4))

        return carry

    lax.fori_loop(0, 12, unit, 0)
    sum_core(slots[11], sides[11], 1)
    cacc0[...] = jnp.zeros_like(cacc0)
    cacc1[...] = jnp.zeros_like(cacc1)

    final = ((7, 1), (7, 0))

    def grad_part(p):
        return pl.ds(pl.multiple_of(p * step, step), step)

    def d_copy(p, part):
        columns = grad_part(p)
        return remote(dsend.at[part, columns], drecv.at[part, columns], d_send.at[0], d_recv.at[p], p_dev)

    def d_mid(p):
        columns = grad_part(p)
        return remote(dsend.at[extra, columns], drecv.at[lead, columns], d_send.at[1], d_recv.at[p], m_dev)

    def last_piece(p, carry):
        done = 26 + p
        lax.fori_loop(jnp.minimum(done, ticks), jnp.minimum(done + 1, ticks), tick, 0)

        def ahead(p):
            columns = grad_part(p)
            for r in range(2):
                caccs[r][0] += dot_nn(abufs[r][:, columns], wbuf[5, columns])

        @pl.when(p == 0)
        def _():
            ahead(0)

        @pl.when(p < PIECES - 1)
        def _():
            ahead(p + 1)

        @pl.when(p == PIECES - 2)
        def _():
            for side in (1, 0):
                pass_core(5, side, 0)

        x_far(1, p).wait_recv()
        columns = grad_part(p)
        for r in (1, 0):
            for part in tiles(r):
                grown = daccs[r][part, columns]
                grown += dot_nt(gbufs[r][5, part], wbuf[5, columns])
                grown += dot_nt(gbufs[r][7, part], wbuf[7, columns])
                if r == 1:
                    dsend[part, columns] = grown.astype(jnp.bfloat16)
                else:
                    dacc0[part, columns] = grown
            if r == 1:
                each_kind(lambda is_inner: d_copy(p, taken_rows(is_inner)).start())

                @pl.when(inner)
                def _():
                    d_mid(p).start()

        for r in range(2):
            caccs[r][1] += dot_nn(abufs[r][:, columns], wbuf[7, columns])

        @pl.when(p == PIECES - 2)
        def _():
            for side in (1, 0):
                sum_core(5, side, 0)


        @pl.when(p == 1)
        def _():
            @pl.when(inner)
            def _():
                p_sum.wait_send()

            @pl.when(jnp.logical_not(inner))
            def _():
                p_sum.wait_recv()
                sums[...] = came[places[3]]

            bank_out[bank_rows(at_x, q3)] = sums[:q3]
            x_all.start()

        @pl.when(p == 3)
        def _():
            x_all.wait()
            bank_out[bank_rows(at_y + (1 - x) * q3, q3)] = came[places[5]]
            y_all.start()

        @pl.when((p >= 1) & (p < 5))
        def _():
            sum_y(pick(slots, 7 + p), (p - 1) % 2)

        @pl.when(p == 5)
        def _():
            y_all.wait()
            bank_out[bank_rows(at_c + (1 - y) * q2, q2)] = came[places[6]]
            c_all.start()

        return carry

    lax.fori_loop(0, PIECES, last_piece, 0)

    def finish_grad(p, carry):
        columns = grad_part(p)
        whole = drecv.at[:, columns]
        remote(whole, whole, d_send.at[0], d_recv.at[p], p_dev).wait_recv()
        total_here = dacc0[:, columns] + drecv[:, columns].astype(jnp.float32)
        drecv[:, columns] = (total_here + 2.0 * dot_nn(back[...], down[:, columns])).astype(jnp.bfloat16)
        return carry

    for slot, side in final:
        pass_core(slot, side, 1)
    for slot, side in final:
        sum_core(slot, side, 1)
    c_all.wait()
    bank_out[bank_rows((1 - c) * q1, q1)] = came[places[7]]
    for k, target in enumerate((slope_a, slope_b)):
        values = [sums[q3 + 2 * k + m : q3 + 2 * k + m + 1, :vectors] for m in range(2)]
        mean = shares[k][0] * values[0] + shares[k][1] * values[1]
        for m in range(2):
            target[:, m, :] = from_row(shares[k][m] * (values[m] - mean))
    finish_other(0)
    finish_other(2)
    for slot, side in ((5, 1), (5, 0), (7, 1), (7, 0)):
        sum_y(slot, side)
    lax.fori_loop(0, PIECES, finish_grad, 0)
    finish_other(1)
    finish_other(3)
    def drain(buffer, semaphore):
        remote(buffer, buffer, semaphore, a_recv.at[0], p_dev).wait_send()

    def drain_kind(is_inner):
        a_own(sent_rows(is_inner)).wait_send()
        drain(gbuf1.at[pl.ds(0, 2), sent_rows(is_inner)], g_send.at[0])
        drain(g_everything(is_inner), gm_send.at[0])
        drain(dsend.at[taken_rows(is_inner)], d_send.at[0])
        if is_inner:
            a_mid.wait_send()
            for n in range(2):
                g_mid(n).wait_send()
                drain(relay.at[n], relay_send.at[n])
            drain(dsend.at[extra], d_send.at[1])

        @pl.when(reduces)
        def _():
            drain(gbuf1.at[pl.ds(0, 4), taken_rows(is_inner)], zc_send.at[0])
            if is_inner:
                drain(gbuf1.at[pl.ds(0, 4), extra], zc_send.at[1])

    each_kind(drain_kind)
    drain(weight, xs_send.at[0])
    drain(weight, zs_send.at[0])
    drain(weight, xf_send.at[0])

    @pl.when(jnp.logical_not(reduces))
    def _():
        for r in range(2):
            drain(cbufs[r], c_send.at[r])

    @pl.when(reduces)
    def _():
        for r in range(2):
            drain(cbufs[r].at[pl.ds(0, 4)], y_send.at[r])


def settle_kernel(width, *refs):
    sources, targets, sem = refs[:5], refs[5:10], refs[10]
    half = sources[0].shape[2]
    x = lax.axis_index("dp") % 2
    copies = []
    for j in range(4):
        col = (x if j < 2 else 1 - x) * width + (j % 2) * half
        columns = pl.ds(pl.multiple_of(col, half), half)
        copies.append(pltpu.make_async_copy(sources[0].at[j], targets[0].at[:, columns], sem.at[j]))
    for k in range(1, 5):
        copies.append(pltpu.make_async_copy(sources[k], targets[k], sem.at[3 + k]))
    for copy in copies:
        copy.start()
    for copy in copies:
        copy.wait()


def fused_local(dp_size, attn_out, frozen_weight, vector_bank, logits_a, index_a, logits_b, index_b, out_grad):
    rows, depth = attn_out.shape
    width = frozen_weight.shape[1]
    half = width // 2
    levels, sublen = vector_bank.shape
    rank, per_row, _ = logits_a.shape
    vectors = rank * per_row
    own = logits_b.shape[1] * sublen
    factor = adapter_scale / (rows * dp_size)
    total = 2 * PIECES
    more = rows + rows // 32
    small = [v.transpose(1, 2, 0) for v in (logits_a, index_a, logits_b, index_b)]
    bf16, f32 = jnp.bfloat16, jnp.float32
    dma = pltpu.SemaphoreType.DMA
    hbm = pl.BlockSpec(memory_space=pl.ANY)
    vmem = pl.BlockSpec(memory_space=pltpu.VMEM)
    layer_out, attn_grad, _, bank_grad, slope_a, slope_b = pl.pallas_call(
        functools.partial(exchange_kernel, factor),
        name="exchange",
        out_shape=(
            pltpu.VMEM((4, rows, half), bf16),
            pltpu.VMEM((rows, depth), bf16),
            jax.ShapeDtypeStruct((2, 2, depth, half), bf16),
            pltpu.VMEM((levels, sublen), f32),
            pltpu.VMEM((per_row, 2, rank), f32),
            pltpu.VMEM((per_row, 2, rank), f32),
        ),
        in_specs=[hbm] * 8,
        out_specs=(vmem, vmem, hbm, vmem, vmem, vmem),
        scratch_shapes=[
            pltpu.VMEM((8, depth, half), bf16),
            pltpu.VMEM((rows, depth), bf16),
            pltpu.VMEM((more, depth), bf16),
            pltpu.VMEM((8, rows, half), bf16),
            pltpu.VMEM((8, more, half), bf16),
            pltpu.VMEM((rows, depth), f32),
            pltpu.VMEM((more, depth), f32),
            pltpu.VMEM((8, rows, half), bf16),
            pltpu.VMEM((8, more, half), bf16),
            pltpu.VMEM((4, more, half), bf16),
            pltpu.VMEM((more, depth), bf16),
            pltpu.VMEM((2, rows, half), f32),
            pltpu.VMEM((2, more, half), f32),
            pltpu.VMEM((4, 2 * rank, rows), f32),
            pltpu.VMEM((rows, rank), bf16),
            pltpu.VMEM((rows, rank), bf16),
            pltpu.VMEM((rank, depth), bf16),
            pltpu.VMEM((rank, own), bf16),
            pltpu.VMEM((levels, sublen), f32),
            *[pltpu.VMEM(v.shape, v.dtype) for v in small],
            pltpu.VMEM((2, levels, vectors), f32),
            pltpu.VMEM((levels // 8 + 8, sublen), f32),
            pltpu.VMEM((2 * levels + 24, sublen), f32),
            dma((10,)), dma((1,)), dma((2, total)), dma((2,)), dma((total,)),
            dma((1,)), dma((total,)), dma((1,)), dma((PIECES + 1,)),
            dma((1,)), dma((2,)), dma((1,)), dma((1,)), dma((1,)), dma((1,)), dma((3,)), dma((3,)),
            dma((1,)), dma((1,)),
            dma((2,)), dma((8, 2)), dma((2,)), dma((4, 2)), dma((2,)), dma((4,)),
            dma((2,)), dma((PIECES,)), dma((1,)), dma((8,)),
        ],
        compiler_params=pltpu.CompilerParams(
            collective_id=0, has_side_effects=True, vmem_limit_bytes=67043328 - 5 * 2**20
        ),
    )(attn_out, frozen_weight, out_grad, vector_bank, *small)
    targets = [((rows, own), bf16), ((rows, depth), bf16), ((levels, sublen), f32)]
    targets += [(v.shape, f32) for v in (slope_a, slope_b)]
    kept = [pltpu.with_memory_space_constraint(v, pltpu.VMEM) for v in (layer_out, attn_grad, bank_grad, slope_a, slope_b)]
    layer_out, attn_grad, bank_grad, slope_a, slope_b = pl.pallas_call(
        functools.partial(settle_kernel, width),
        name="settle",
        out_shape=[jax.ShapeDtypeStruct(*v) for v in targets],
        in_specs=[hbm] * 5,
        out_specs=[hbm] * 5,
        scratch_shapes=[dma((8,))],
        compiler_params=pltpu.CompilerParams(vmem_limit_bytes=16 * 2**20),
    )(*kept)
    return (layer_out, attn_grad, bank_grad, slope_a.transpose(2, 0, 1), slope_b.transpose(2, 0, 1))


def solution(mesh):
    dp_size, tensor_size = mesh.shape["dp"], mesh.shape["tensor"]
    paired = dp_size == 2 * tensor_size and tensor_size % 2 == 0
    body = functools.partial(ring_local, dp_size, tensor_size) if paired else local
    if paired and tensor_size == 4:
        body = functools.partial(fused_local, dp_size)
    return jax.shard_map(
        body,
        mesh=mesh,
        in_specs=(
            P("dp", "tensor"),
            P("tensor", "dp"),
            P(),
            P(None, "tensor", None),
            P(None, "tensor", None),
            P(None, "tensor", None),
            P(None, "tensor", None),
            P("dp", None),
        ),
        out_specs=(
            P("dp", "tensor"),
            P("dp", "tensor"),
            P(),
            P(None, "tensor", None),
            P(None, "tensor", None),
        ),
        check_vma=False,
    )
```
